32 devices in a mesh: fsdp: 4 (over y, x), ctx: 2 (over core), tp: 4 (over z).
Axes of the slice: x: 2, y: 2, z: 4, core: 2. Of those that a mesh axis runs over, the one named last changes fastest.
Arguments:
- tokens: bfloat16 [2, 4, 1024, 768], P(None, 'fsdp', 'ctx'), may hold values from -6 to 6
- cotangent: bfloat16 [2, 4, 1024, 768], P(None, 'fsdp', 'ctx'), may hold values from -6 to 6
- lengths: int32 [2, 4], P(None, 'fsdp'), may hold values from 513 to 1024
- routes: int32 [2, 2, 4, 1024, 2], P(None, None, 'fsdp', 'ctx'), may hold values from 0 to 11, all different within a row; in each aligned block of 512 rows (0 to 511, 512 to 1023, ..., all dimensions but the last counted through in order) at most 128 rows name the same one
- norm_attn: bfloat16 [2, 768], P(None, ('fsdp', 'ctx')), may hold values from 0.5 to 1.5
- w_qkv: bfloat16 [2, 768, 2304], P(None, ('fsdp', 'ctx'), 'tp'), may hold values from -0.21875 to 0.21875
- w_out: bfloat16 [2, 768, 768], P(None, 'tp', ('fsdp', 'ctx')), may hold values from -1.25 to 1.25
- norm_moe: bfloat16 [2, 768], P(None, ('fsdp', 'ctx')), may hold values from 0.5 to 1.5
- w_router: bfloat16 [2, 768, 12], P(None, ('fsdp', 'ctx')), may hold values from -0.15625 to 0.15625
- w_resid: bfloat16 [12, 12], replicated, may hold values from -1.75 to 1.75
- w_const: bfloat16 [2, 2, 768, 2], P(None, None, ('fsdp', 'ctx')), may hold values from -0.21875 to 0.21875
- v_const: bfloat16 [2, 2, 768], P(None, None, ('fsdp', 'ctx')), may hold values from -6 to 6
- w_gate_up: bfloat16 [2, 8, 768, 2, 2048], P(None, None, ('fsdp', 'ctx'), None, 'tp'), may hold values from -0.21875 to 0.21875
- w_down: bfloat16 [2, 8, 2048, 768], P(None, None, 'tp', ('fsdp', 'ctx')), may hold values from -0.1875 to 0.1875
Outputs:
- mixed: bfloat16 [2, 4, 1024, 768], P(None, 'fsdp', 'ctx')
- grad_tokens: float32 [2, 4, 1024, 768], P(None, 'fsdp', 'ctx')
- grad_norm_attn: float32 [2, 768], P(None, ('fsdp', 'ctx'))
- grad_w_qkv: float32 [2, 768, 2304], P(None, ('fsdp', 'ctx'), 'tp')
- grad_w_out: float32 [2, 768, 768], P(None, 'tp', ('fsdp', 'ctx'))
- grad_norm_moe: float32 [2, 768], P(None, ('fsdp', 'ctx'))
- grad_w_router: float32 [2, 768, 12], P(None, ('fsdp', 'ctx'))
- grad_w_resid: float32 [12, 12], replicated
- grad_w_const: float32 [2, 2, 768, 2], P(None, None, ('fsdp', 'ctx'))
- grad_v_const: float32 [2, 2, 768], P(None, None, ('fsdp', 'ctx'))
- grad_w_gate_up: float32 [2, 8, 768, 2, 2048], P(None, None, ('fsdp', 'ctx'), None, 'tp')
- grad_w_down: float32 [2, 8, 2048, 768], P(None, None, 'tp', ('fsdp', 'ctx'))
The draws below stay inside these ranges and needn't reach their ends.
Inputs may be any that keep to these rules, and one draw needn't show every extreme that they name: In each aligned block of 512 slots of routes (one context block of one sequence in one layer and micro-batch), no expert is named by more than 128 of the block's routes, a bound that some block reaches; the two routes of a slot name different experts; every expert is named somewhere.
All inputs are finite; a program needn't handle non-finite values.
Results may differ from the reference program's by a relative error of at most 0.025.
Values may be sent and summed in bfloat16 or wider, within the bound.
No kernel may reach another device: no remote copies, remote signals or barrier semaphores. Data moves between devices by JAX's collectives and lax.ppermute only.
A program may use at most 384 MiB of HBM per device.

```python
import math
import jax
import jax.numpy as jnp
import numpy as np
from jax import lax

D = 768
H = 12
HD = 64
FF = 2048
NF = 8
NE = 12
LAYERS = 2
MICRO = 2
SEQLEN = 1024
NSEQ = 4
BLOCK = 512
CAP = 128


def place_ends(array, key, smallest, high):
    place = [jax.random.randint(jax.random.fold_in(key, axis), (), 0, length) for axis, length in enumerate(array.shape)]
    widest = array.shape.index(max(array.shape))
    neighbour = place[:widest] + [(place[widest] + 1) % array.shape[widest]] + place[widest + 1:]
    return array.at[tuple(place)].set(smallest).at[tuple(neighbour)].set(high)


def levels(key, shape, cuts, low, top_value):
    loudness, own = 1.0, jax.random.fold_in(key, 6)
    for position, blocks in cuts:
        heights = jnp.exp(jax.random.uniform(jax.random.fold_in(own, position), (blocks,), jnp.float32, low / len(cuts), top_value / len(cuts)))
        loudness = loudness * jnp.repeat(heights, shape[position] // blocks).reshape([-1 if axis == position else 1 for axis in range(len(shape))])
    return loudness


def shared_out(own_key, own, number, rows, number_of, top, bound, slope):
    ranking = jax.random.permutation(own_key, number_of)
    packed, common = portions_of(number_of, rows * top, bound, slope, True), portions_of(number_of, rows * top, bound, slope, False)
    places = jnp.arange(number_of)

    def named(sizes, offset_by):
        used = int((sizes > 0).sum())
        fixed = max(1, used // 4)
        moved = fixed + (places - fixed + offset_by * (used - fixed)) % max(1, number_of - fixed)
        return jnp.zeros((number_of,), jnp.int32).at[ranking[jnp.where(places < fixed, places, moved)]].set(jnp.asarray(sizes, jnp.int32))

    sizes = jnp.where(number % 4 == 0, named(packed, number // 4), named(common, number - number // 4 - 1))
    mixed = jax.random.permutation(jax.random.fold_in(own, 3), number_of)
    donor, receiver = mixed[0:number_of // 2 * 2:2], mixed[1:number_of // 2 * 2:2]
    slack = jnp.minimum(sizes[donor] - 1, bound - sizes[receiver]) // 2
    slack = jnp.where((donor == ranking[0]) | (receiver == ranking[0]) | (sizes[receiver] == 0), 0, jnp.maximum(slack, 0))
    moved = jax.random.randint(jax.random.fold_in(own, 4), (number_of // 2,), 0, 1 << 20) % (slack + 1)
    sizes = sizes.at[donor].add(-moved).at[receiver].add(moved)
    members = jnp.searchsorted(jnp.cumsum(sizes), jnp.arange(rows * top), side="right").astype(jnp.int32)
    listing = members.reshape(top, rows).T
    listing = listing[jax.random.permutation(jax.random.fold_in(own, 1), rows)]
    offset_by = jax.random.randint(jax.random.fold_in(own, 2), (rows, 1), 0, top)
    return jnp.take_along_axis(listing, (jnp.arange(top)[None, :] + offset_by) % top, axis=1)


def portions_of(number_of, total, bound, skew, full):
    portions = [(1 << 20) // math.isqrt(standing ** skew) + 1 for standing in range(1, number_of + 1)]
    largest = bound if full else min(bound, max(-(-total // number_of), total * portions[0] // sum(portions)))
    least = 1 if total - largest >= number_of - 1 else 0
    holding, surplus = [largest] + [least] * (number_of - 1), total - largest - least * (number_of - 1)
    while surplus > 0:
        movable = [i for i in range(1, number_of) if holding[i] < largest] or [i for i in range(1, number_of) if holding[i] < bound]
        mass, remaining = sum([portions[i] for i in movable]), surplus
        for i in movable:
            addition = min(bound - holding[i], max(1, remaining * portions[i] // mass), surplus)
            holding[i] = holding[i] + addition
            surplus = surplus - addition
    return np.array(holding)


def gaussian(own_key, dims, spread, most, shards=(), kind=jnp.bfloat16):
    loudness = levels(own_key, dims, shards, -0.22, 0.18) if shards else 1.0
    array = jax.random.normal(own_key, dims, jnp.float32) * spread * loudness
    return jnp.minimum(jnp.maximum(array, -most), most).astype(kind)


def setup_inputs(seed: int = 0) -> dict:
    arg_keys = jax.random.split(jax.random.key(seed), 15)
    tokens = gaussian(arg_keys[0], (MICRO, NSEQ, SEQLEN, D), 1.0, 6.0, ((1, 4), (2, 2)))
    cotangent = gaussian(arg_keys[1], (MICRO, NSEQ, SEQLEN, D), 1.0, 6.0, ((1, 4), (2, 2)))
    lengths = place_ends(jax.random.randint(arg_keys[2], (MICRO, NSEQ), SEQLEN // 2 + 1, SEQLEN + 1), jax.random.fold_in(arg_keys[2], 1), SEQLEN // 2 + 1, SEQLEN).astype(jnp.int32)
    routes_keys = jax.random.split(jax.random.fold_in(arg_keys[3], 1), LAYERS * MICRO * NSEQ * SEQLEN // BLOCK)
    routes_turns = jax.random.permutation(jax.random.fold_in(arg_keys[3], 3), LAYERS * MICRO * NSEQ * SEQLEN // BLOCK)
    routes = jax.vmap(lambda own, number: shared_out(jax.random.fold_in(arg_keys[3], 2), own, number, BLOCK, NE, 2, CAP, 1))(routes_keys, routes_turns).reshape((LAYERS, MICRO, NSEQ, SEQLEN, 2))
    norm_attn = jnp.clip(1.0 + 0.1 * jax.random.normal(arg_keys[4], (LAYERS, D), jnp.float32), 0.5, 1.5).astype(jnp.bfloat16)
    w_qkv = gaussian(arg_keys[5], (LAYERS, D, 3 * H * HD), D ** -0.5, 0.21875, ((1, 8), (2, 4)))
    w_out = gaussian(arg_keys[6], (LAYERS, H * HD, D), (H * HD // 32) ** -0.5, 1.25, ((1, 4), (2, 8)))
    norm_moe = jnp.clip(1.0 + 0.1 * jax.random.normal(arg_keys[7], (LAYERS, D), jnp.float32), 0.5, 1.5).astype(jnp.bfloat16)
    w_router = gaussian(arg_keys[8], (LAYERS, D, NE), (2 * D) ** -0.5, 0.15625, ((1, 8),))
    w_resid = gaussian(arg_keys[9], (NE, NE), NE ** -0.5, 1.75)
    w_const = gaussian(arg_keys[10], (LAYERS, 2, D, 2), D ** -0.5, 0.21875, ((2, 8),))
    v_const = gaussian(arg_keys[11], (LAYERS, 2, D), 1.0, 6.0, ((2, 8),))
    w_gate_up = gaussian(arg_keys[12], (LAYERS, NF, D, 2, FF), D ** -0.5, 0.21875, ((2, 8), (4, 4)))
    w_down = gaussian(arg_keys[13], (LAYERS, NF, FF, D), (FF // 2) ** -0.5, 0.1875, ((2, 4), (3, 8)))
    return dict(tokens=tokens, cotangent=cotangent, lengths=lengths, routes=routes, norm_attn=norm_attn, w_qkv=w_qkv, w_out=w_out, norm_moe=norm_moe, w_router=w_router, w_resid=w_resid, w_const=w_const, v_const=v_const, w_gate_up=w_gate_up, w_down=w_down)


PRECISE = lax.Precision.HIGHEST
EPSILON = 1e-06
MASKED = -1e+30

@jax.custom_vjp
def low(v):
    return lax.optimization_barrier(v.astype(jnp.bfloat16)).astype(jnp.float32)

@jax.custom_vjp
def low_back(v):
    return v

def low_keep(v):
    return (low(v), None)

def low_pass(kept, grad):
    return (grad,)

def back_keep(v):
    return (v, None)

def back_low(kept, grad):
    return (low(grad),)
low.defvjp(low_keep, low_pass)
low_back.defvjp(back_keep, back_low)

def rms_norm(operand, norm_gain):
    return operand * lax.rsqrt(lax.optimization_barrier(jnp.mean(operand * operand, axis=-1, keepdims=True)) + EPSILON) * norm_gain

def pair_softmax(operand):
    row_max = lax.optimization_barrier(jnp.max(operand, axis=-1, keepdims=True))
    exp_terms = jnp.exp(operand - row_max)
    return exp_terms / lax.optimization_barrier(jnp.sum(exp_terms, axis=-1, keepdims=True))

def gate_terms(xm_wide, normed, logits_prev, w_router, w_resid, w_const, v_const, route_flat):
    logits = jnp.dot(xm_wide, w_router, precision=PRECISE) + jnp.dot(logits_prev, w_resid, precision=PRECISE)
    expert_ids = jnp.arange(NE, dtype=jnp.int32)
    one_hot = (route_flat[:, :, None] == expert_ids[None, None, :]).astype(jnp.float32)
    chosen = lax.optimization_barrier(jnp.sum(one_hot * logits[:, None, :], axis=-1))
    gate_vals = pair_softmax(chosen)
    const_terms = []
    for const_idx in range(2):
        alpha_pair = pair_softmax(jnp.dot(xm_wide, w_const[const_idx], precision=PRECISE))
        const_terms.append(alpha_pair[:, 0:1] * normed + alpha_pair[:, 1:2] * v_const[const_idx][None, :])
    slot_terms = one_hot[:, :, NF + 1:NF + 2] * normed[:, None, :] + one_hot[:, :, NF + 2:NF + 3] * const_terms[0][:, None, :] + one_hot[:, :, NF + 3:NF + 4] * const_terms[1][:, None, :]
    fixed_terms = lax.optimization_barrier(jnp.sum(gate_vals[:, :, None] * slot_terms, axis=1))
    return (gate_vals, fixed_terms, logits)

def slot_tables(route_block):
    slot_routes = route_block.reshape(-1)
    slot_count = slot_routes.shape[0]
    expert_hits = (slot_routes[:, None] == jnp.arange(NF, dtype=jnp.int32)[None, :]).astype(jnp.int32)
    slot_place = lax.optimization_barrier(jnp.sum((jnp.cumsum(expert_hits, axis=0) - expert_hits) * expert_hits, axis=1)).astype(jnp.int32)
    is_ffn = slot_routes < NF
    slot_table = jnp.full((NF, CAP), slot_count, jnp.int32).at[jnp.where(is_ffn, slot_routes, NF), slot_place].set(jnp.arange(slot_count, dtype=jnp.int32), mode='drop')
    target = jnp.where(is_ffn, slot_routes * CAP + slot_place, NF * CAP).astype(jnp.int32)
    return (slot_table, target)

def experts_block(xm_block, route_block, gate_block, w_gate_up, w_down):
    slot_table, target = slot_tables(route_block)
    padded = jnp.concatenate([xm_block, jnp.zeros((1, D), jnp.float32)], axis=0)
    picked = padded[slot_table // 2]
    gate_up = low_back(jnp.einsum('ecd,edkf->eckf', picked, w_gate_up, precision=PRECISE))
    hidden = low(gate_up[:, :, 0] * lax.logistic(gate_up[:, :, 0]) * gate_up[:, :, 1])
    result = low_back(jnp.einsum('ecf,efd->ecd', hidden, w_down, precision=PRECISE))
    flat_result = jnp.concatenate([result.reshape(NF * CAP, D), jnp.zeros((1, D), jnp.float32)], axis=0)
    per_slot = flat_result[target].reshape(BLOCK, 2, D)
    return lax.optimization_barrier(jnp.sum(gate_block[:, :, None] * per_slot, axis=1))

def attend(qkv_seq, seq_length):
    positions = jnp.arange(SEQLEN, dtype=jnp.int32)
    scores = low_back(jnp.einsum('qhe,khe->hqk', qkv_seq[:, :, 0], qkv_seq[:, :, 1], precision=PRECISE) * HD ** (-0.5))
    allowed = (positions[None, :] <= positions[:, None]) & (positions[None, :] < seq_length)
    masked = jnp.where(allowed[None], scores, MASKED)
    row_max = lax.optimization_barrier(jnp.max(masked, axis=-1, keepdims=True))
    exp_terms = jnp.exp(masked - row_max)
    prob_low = low(exp_terms / lax.optimization_barrier(jnp.sum(exp_terms, axis=-1, keepdims=True)))
    return low(low_back(jnp.einsum('hqk,khe->qhe', prob_low, qkv_seq[:, :, 2], precision=PRECISE)))

def attend_pair(seq_items):
    return attend(seq_items[0], seq_items[1])

def group_forward(token_in, weight_set, route_grp, length_grp):
    norm_attn, w_qkv, w_out, norm_moe, w_router, w_resid, w_const, v_const, w_gate_up, w_down = weight_set
    group_size = token_in.shape[0]
    block_count = group_size * SEQLEN // BLOCK
    residual = token_in
    logits_prev = jnp.zeros((group_size * SEQLEN, NE), jnp.float32)
    for layer_idx in range(LAYERS):
        attn_in = low(rms_norm(residual, norm_attn[layer_idx]))
        qkv_low = low_back(low(jnp.einsum('gsd,dc->gsc', attn_in, w_qkv[layer_idx], precision=PRECISE)))
        context = lax.map(jax.checkpoint(attend_pair), (qkv_low.reshape(group_size, SEQLEN, H, 3, HD), length_grp))
        attn_out = low_back(jnp.einsum('gsc,cd->gsd', context.reshape(group_size, SEQLEN, H * HD), w_out[layer_idx], precision=PRECISE))
        middle = residual + attn_out
        normed = rms_norm(middle, norm_moe[layer_idx])
        xm_low = low(normed)
        route_layer = route_grp[layer_idx]
        gate_vals, fixed_terms, logits = gate_terms(xm_low.reshape(-1, D), normed.reshape(-1, D), logits_prev, w_router[layer_idx], w_resid, w_const[layer_idx], v_const[layer_idx], route_layer.reshape(-1, 2))
        gate_weight = w_gate_up[layer_idx]
        down_weight = w_down[layer_idx]

        def expert_pass(block_items):
            return experts_block(block_items[0], block_items[1], block_items[2], gate_weight, down_weight)
        ffn_out = lax.map(jax.checkpoint(expert_pass), (xm_low.reshape(block_count, BLOCK, D), route_layer.reshape(block_count, BLOCK, 2), gate_vals.reshape(block_count, BLOCK, 2)))
        residual = middle + ffn_out.reshape(group_size, SEQLEN, D) + fixed_terms.reshape(group_size, SEQLEN, D)
        logits_prev = logits
    return residual

def reference(tokens, cotangent, lengths, routes, norm_attn, w_qkv, w_out, norm_moe, w_router, w_resid, w_const, v_const, w_gate_up, w_down):
    weights = tuple((weight.astype(jnp.float32) for weight in (norm_attn, w_qkv, w_out, norm_moe, w_router, w_resid, w_const, v_const, w_gate_up, w_down)))
    seq_total = MICRO * NSEQ
    group_limit = max(1, 4096 // SEQLEN)
    group_size = 1
    for candidate in range(1, seq_total + 1):
        if seq_total % candidate == 0 and candidate <= group_limit:
            group_size = candidate
    group_count = seq_total // group_size
    positions = jnp.arange(SEQLEN, dtype=jnp.int32)
    valid_mask = (positions[None, None, :] < lengths[:, :, None]).astype(jnp.float32)
    masked_cot = cotangent.astype(jnp.float32) * valid_mask[:, :, :, None]
    token_groups = tokens.astype(jnp.float32).reshape(group_count, group_size, SEQLEN, D)
    cot_groups = masked_cot.reshape(group_count, group_size, SEQLEN, D)
    length_groups = lengths.reshape(group_count, group_size)
    route_groups = jnp.moveaxis(routes.reshape(LAYERS, group_count, group_size, SEQLEN, 2), 1, 0)

    def scan_step(totals, group_items):
        token_grp, cot_grp, length_grp, route_grp = group_items

        def forward(token_in, weight_set):
            return group_forward(token_in, weight_set, route_grp, length_grp)
        outputs, pull_back = jax.vjp(forward, token_grp, weights)
        grad_input, grad_weights = pull_back(cot_grp)
        return (jax.tree.map(jnp.add, totals, grad_weights), (outputs.astype(jnp.bfloat16), grad_input))
    zero_totals = jax.tree.map(jnp.zeros_like, weights)
    totals, (out_groups, grad_groups) = lax.scan(scan_step, zero_totals, (token_groups, cot_groups, length_groups, route_groups))
    mixed = out_groups.reshape(MICRO, NSEQ, SEQLEN, D)
    grad_tokens = grad_groups.reshape(MICRO, NSEQ, SEQLEN, D)
    return (mixed, grad_tokens, totals[0], totals[1], totals[2], totals[3], totals[4], totals[5], totals[6], totals[7], totals[8], totals[9])
```

```python
import functools

import jax
import jax.numpy as jnp
from jax import lax
from jax.experimental import pallas as pl
from jax.experimental.pallas import tpu as pltpu
from jax.sharding import PartitionSpec as P

HD = 64
NF = 8
NE = 12
BLOCK = 512
CAP = 128
TILE = 256
EPSILON = 1e-06
MASKED = -1e30
F32 = jnp.float32
BF16 = jnp.bfloat16
HIGH = lax.Precision.HIGHEST
ROW_CONST, ROW_VEC, ROW_GA, ROW_GM = 16, 20, 22, 23
VMEM_LIMIT = 58 * 1024 * 1024

NN = (((1,), (0,)), ((), ()))
NT = (((1,), (1,)), ((), ()))
TN = (((0,), (0,)), ((), ()))


def mm(left, right, dims=NN, precision=None):
    return lax.dot_general(left, right, dims, precision=precision, preferred_element_type=F32)


def kernel_params():
    return pltpu.CompilerParams(vmem_limit_bytes=VMEM_LIMIT)


def cost(flops, nbytes, trans=0):
    return pl.CostEstimate(flops=int(flops), bytes_accessed=int(nbytes), transcendentals=int(trans))


def iota(shape, dim):
    return lax.broadcasted_iota(jnp.int32, shape, dim)


def full_spec(shape):
    zeros = (0,) * len(shape)
    return pl.BlockSpec(shape, lambda *idx: zeros)


SMEM_SPEC = pl.BlockSpec(memory_space=pltpu.SMEM)


def pad_rows(rows, count, width):
    row_id = iota((count, width), 0)
    out = jnp.zeros((count, width), F32)
    for place, row in rows:
        out = jnp.where(row_id == place, row, out)
    return out


def prep_kernel(count, rows, offs_ref, *refs):
    in_a, in_w = refs[:count], refs[count : 2 * count]
    qkv_ref, wo_ref, vec_ref = refs[2 * count :]
    cols = qkv_ref.shape[1]
    vec_cols = []
    for piece in range(count):
        start = pl.multiple_of(offs_ref[piece] * rows, rows)
        block = in_a[piece][...]
        qkv_ref[pl.ds(start, rows), :] = block[:, :cols]
        vec_ref[pl.ds(start, rows), :] = block[:, cols:]
        for rank in range(wo_ref.shape[0]):
            wo_ref[rank, pl.ds(start, rows), :] = in_w[piece][rank]
    del vec_cols


def prep_weights(pieces_a, pieces_w, offs, feature_dim, qkv_cols):
    count = len(pieces_a)
    rows = feature_dim // count
    tp_count, _, out_cols = pieces_w[0].shape
    vec_cols = pieces_a[0].shape[1] - qkv_cols
    return pl.pallas_call(
        functools.partial(prep_kernel, count, rows),
        out_shape=(
            jax.ShapeDtypeStruct((feature_dim, qkv_cols), BF16),
            jax.ShapeDtypeStruct((tp_count, feature_dim, out_cols), BF16),
            jax.ShapeDtypeStruct((feature_dim, vec_cols), BF16),
        ),
        in_specs=[SMEM_SPEC] + [pl.BlockSpec(memory_space=pltpu.VMEM)] * (2 * count),
        out_specs=tuple([pl.BlockSpec(memory_space=pltpu.VMEM)] * 3),
        compiler_params=kernel_params(),
        cost_estimate=cost(1e6, 5e6),
        name="prep",
    )(offs, *pieces_a, *pieces_w)


def qkv_kernel(with_ffn, *refs):
    if with_ffn:
        base_ref, ffn_ref, vec_ref, w_ref, h_ref, qkv_ref = refs
        hidden = base_ref[...] + ffn_ref[...].astype(F32)
        h_ref[...] = hidden
    else:
        base_ref, vec_ref, w_ref, qkv_ref = refs
        hidden = base_ref[...].astype(F32)
    gain = vec_ref[ROW_GA : ROW_GA + 1, :]
    scale = lax.rsqrt(jnp.mean(hidden * hidden, axis=-1, keepdims=True) + EPSILON)
    attn_in = (hidden * scale * gain).astype(BF16)
    qkv_ref[...] = mm(attn_in, w_ref[...]).astype(BF16)


def qkv_part(base, ffn, vecs, w_qkv):
    rows, feature_dim = base.shape
    cols = w_qkv.shape[1]
    row_spec = pl.BlockSpec((TILE, feature_dim), lambda i: (i, 0))
    with_ffn = ffn is not None
    out_shape = [jax.ShapeDtypeStruct((rows, cols), BF16)]
    out_specs = [pl.BlockSpec((TILE, cols), lambda i: (i, 0))]
    if with_ffn:
        out_shape = [jax.ShapeDtypeStruct((rows, feature_dim), F32)] + out_shape
        out_specs = [row_spec] + out_specs
    ins = [base] + ([ffn] if with_ffn else []) + [vecs, w_qkv]
    in_specs = [row_spec] * (2 if with_ffn else 1) + [full_spec(vecs.shape), full_spec(w_qkv.shape)]
    return pl.pallas_call(
        functools.partial(qkv_kernel, with_ffn),
        grid=(rows // TILE,),
        out_shape=tuple(out_shape),
        in_specs=in_specs,
        out_specs=tuple(out_specs),
        compiler_params=kernel_params(),
        cost_estimate=cost(2 * rows * feature_dim * cols, rows * feature_dim * 10),
        name="qkv_part",
    )(*ins)


def attn_masks(ctx, length, tile, width):
    row = iota((TILE, width), 0) + tile * TILE
    col = iota((TILE, width), 1)
    return (col <= row) & (col + ctx * BLOCK < length)


def attn_fwd_kernel(heads, info_ref, own_ref, other_ref, ctx_ref, lse_ref):
    ctx = info_ref[0]
    length = info_ref[1 + pl.program_id(0)]
    own = own_ref[...]
    other = other_ref[...]
    for head in range(heads):
        col = head * 3 * HD
        k_own = own[:, col + HD : col + 2 * HD]
        v_own = own[:, col + 2 * HD : col + 3 * HD]
        k_oth = other[:, col + HD : col + 2 * HD]
        v_oth = other[:, col + 2 * HD : col + 3 * HD]
        for tile in range(BLOCK // TILE):
            width = (tile + 1) * TILE
            query = own[tile * TILE : (tile + 1) * TILE, col : col + HD] * BF16(HD**-0.5)
            s_own = mm(query, k_own[:width], NT)
            s_own = jnp.where(attn_masks(ctx, length, tile, width), s_own, MASKED)
            s_oth = jnp.where(ctx > 0, mm(query, k_oth, NT), MASKED)
            top = jnp.maximum(
                jnp.max(s_own, axis=-1, keepdims=True), jnp.max(s_oth, axis=-1, keepdims=True)
            )
            p_own = jnp.exp(s_own - top)
            p_oth = jnp.exp(s_oth - top)
            total = jnp.sum(p_own, axis=-1, keepdims=True) + jnp.sum(p_oth, axis=-1, keepdims=True)
            out = mm(p_own.astype(BF16), v_own[:width]) + mm(p_oth.astype(BF16), v_oth)
            out = out / total
            rows = slice(tile * TILE, (tile + 1) * TILE)
            ctx_ref[rows, head * HD : (head + 1) * HD] = out.astype(BF16)
            lse_ref[rows, head : head + 1] = top + jnp.log(total)


def attend_forward(qkv, other, info, heads):
    rows, cols = qkv.shape
    count = rows // BLOCK
    spec = pl.BlockSpec((BLOCK, cols), lambda i: (i, 0))
    return pl.pallas_call(
        functools.partial(attn_fwd_kernel, heads),
        grid=(count,),
        out_shape=(
            jax.ShapeDtypeStruct((rows, heads * HD), BF16),
            jax.ShapeDtypeStruct((rows, 8), F32),
        ),
        in_specs=[SMEM_SPEC, spec, spec],
        out_specs=(
            pl.BlockSpec((BLOCK, heads * HD), lambda i: (i, 0)),
            pl.BlockSpec((BLOCK, 8), lambda i: (i, 0)),
        ),
        compiler_params=kernel_params(),
        cost_estimate=cost(rows * 1024 * heads * HD * 16, rows * cols * 6, rows * heads * 1024),
        name="attend_forward",
    )(info, qkv, other)


def attn_bwd_kernel(heads, info_ref, own_ref, other_ref, lse_ref, gctx_ref, gown_ref, goth_ref):
    ctx = info_ref[0]
    length = info_ref[1 + pl.program_id(0)]
    own = own_ref[...]
    other = other_ref[...]
    scale = BF16(HD**-0.5)
    for head in range(heads):
        col = head * 3 * HD
        k_own = own[:, col + HD : col + 2 * HD]
        v_own = own[:, col + 2 * HD : col + 3 * HD]
        k_oth = other[:, col + HD : col + 2 * HD]
        v_oth = other[:, col + 2 * HD : col + 3 * HD]
        goth_ref[:, col : col + HD] = jnp.zeros((BLOCK, HD), BF16)
        gk_own, gv_own, gk_oth, gv_oth = [], [], [], []
        for tile in range(BLOCK // TILE):
            width = (tile + 1) * TILE
            rows = slice(tile * TILE, (tile + 1) * TILE)
            query = own[rows, col : col + HD] * scale
            gout = gctx_ref[rows, head * HD : (head + 1) * HD]
            lse = lse_ref[rows, head : head + 1]
            s_own = mm(query, k_own[:width], NT)
            s_own = jnp.where(attn_masks(ctx, length, tile, width), s_own, MASKED)
            s_oth = jnp.where(ctx > 0, mm(query, k_oth, NT), MASKED)
            p_own = jnp.exp(s_own - lse)
            p_oth = jnp.exp(s_oth - lse)
            d_own = mm(gout, v_own[:width], NT)
            d_oth = mm(gout, v_oth, NT)
            inner = jnp.sum(p_own * d_own, axis=-1, keepdims=True) + jnp.sum(
                p_oth * d_oth, axis=-1, keepdims=True
            )
            ds_own = (p_own * (d_own - inner)).astype(BF16)
            ds_oth = (p_oth * (d_oth - inner)).astype(BF16)
            p_own = p_own.astype(BF16)
            p_oth = p_oth.astype(BF16)
            gown_ref[rows, col : col + HD] = (mm(ds_own, k_own[:width]) + mm(ds_oth, k_oth)) * (
                HD**-0.5
            )
            gk_own.append(mm(ds_own, query, TN))
            gv_own.append(mm(p_own, gout, TN))
            gk_oth.append(mm(ds_oth, query, TN))
            gv_oth.append(mm(p_oth, gout, TN))
        gown_ref[:TILE, col + HD : col + 2 * HD] = gk_own[0] + gk_own[1][:TILE]
        gown_ref[TILE:, col + HD : col + 2 * HD] = gk_own[1][TILE:]
        gown_ref[:TILE, col + 2 * HD : col + 3 * HD] = gv_own[0] + gv_own[1][:TILE]
        gown_ref[TILE:, col + 2 * HD : col + 3 * HD] = gv_own[1][TILE:]
        goth_ref[:, col + HD : col + 2 * HD] = (gk_oth[0] + gk_oth[1]).astype(BF16)
        goth_ref[:, col + 2 * HD : col + 3 * HD] = (gv_oth[0] + gv_oth[1]).astype(BF16)


def attend_backward(qkv, other, lse, grad_context, info, heads):
    rows, cols = qkv.shape
    spec = pl.BlockSpec((BLOCK, cols), lambda i: (i, 0))
    return pl.pallas_call(
        functools.partial(attn_bwd_kernel, heads),
        grid=(rows // BLOCK,),
        out_shape=(
            jax.ShapeDtypeStruct((rows, cols), F32),
            jax.ShapeDtypeStruct((rows, cols), BF16),
        ),
        in_specs=[
            SMEM_SPEC,
            spec,
            spec,
            pl.BlockSpec((BLOCK, 8), lambda i: (i, 0)),
            pl.BlockSpec((BLOCK, heads * HD), lambda i: (i, 0)),
        ],
        out_specs=(spec, spec),
        compiler_params=kernel_params(),
        cost_estimate=cost(rows * 1024 * heads * HD * 40, rows * cols * 12, rows * heads * 1024),
        name="attend_backward",
    )(info, qkv, other, lse, grad_context)


def alpha_rows(gate_in, const_idx):
    first = gate_in[ROW_CONST + 2 * const_idx : ROW_CONST + 2 * const_idx + 1]
    second = gate_in[ROW_CONST + 2 * const_idx + 1 : ROW_CONST + 2 * const_idx + 2]
    return pair(first, second)


def pair(first, second):
    top = jnp.maximum(first, second)
    exp_first = jnp.exp(first - top)
    exp_second = jnp.exp(second - top)
    total = exp_first + exp_second
    return exp_first / total, exp_second / total


def picks(route, value):
    return (route == value).astype(F32)


def gate_coefs(routes, gates, alphas):
    copy = picks(routes[0], NF + 1) * gates[0] + picks(routes[1], NF + 1) * gates[1]
    const = [
        picks(routes[0], NF + 2 + j) * gates[0] + picks(routes[1], NF + 2 + j) * gates[1]
        for j in range(2)
    ]
    on_normed = copy + const[0] * alphas[0][0] + const[1] * alphas[1][0]
    on_vec = [const[j] * alphas[j][1] for j in range(2)]
    return const, on_normed, on_vec


def to_columns(rows):
    width = rows[0].shape[1]
    return pad_rows(list(enumerate(rows)), 128, width).T


def middle_kernel(with_prev, *refs):
    if with_prev:
        h_ref, ctx_ref, wo_ref, vec_ref, route_ref, prev_ref, resid_ref = refs[:7]
        refs = refs[7:]
    else:
        h_ref, ctx_ref, wo_ref, vec_ref, route_ref = refs[:5]
        refs = refs[5:]
    mid_ref, base_ref, xm_ref, gate_ref, logit_ref = refs
    attn_out = mm(ctx_ref[0], wo_ref[0], NT)
    for rank in range(1, ctx_ref.shape[0]):
        attn_out += mm(ctx_ref[rank], wo_ref[rank], NT)
    middle = h_ref[...].astype(F32) + attn_out
    mid_ref[...] = middle
    vecs = vec_ref[...]
    scale = lax.rsqrt(jnp.mean(middle * middle, axis=-1, keepdims=True) + EPSILON)
    normed = middle * scale * vecs[ROW_GM : ROW_GM + 1]
    xm_low = normed.astype(BF16)
    xm_ref[...] = xm_low
    gate_in = mm(vecs[:32].astype(BF16), xm_low, NT)
    logits = gate_in[:16]
    if with_prev:
        logits = logits + mm(resid_ref[...], prev_ref[...], TN, HIGH)
    logit_ref[...] = logits
    routes = (route_ref[0:1], route_ref[1:2])
    expert = iota(logits.shape, 0)
    chosen = [
        jnp.sum(jnp.where(expert == route, logits, 0.0), axis=0, keepdims=True) for route in routes
    ]
    gates = pair(chosen[0], chosen[1])
    gate_ref[...] = pad_rows(list(enumerate(gates)), 8, logits.shape[1])
    alphas = [alpha_rows(gate_in, j) for j in range(2)]
    const, on_normed, on_vec = gate_coefs(routes, gates, alphas)
    cols = to_columns([on_normed, on_vec[0], on_vec[1]])
    base_ref[...] = (
        middle
        + cols[:, 0:1] * normed
        + cols[:, 1:2] * vecs[ROW_VEC : ROW_VEC + 1]
        + cols[:, 2:3] * vecs[ROW_VEC + 1 : ROW_VEC + 2]
    )


def middle_part(h, ctx_all, wo_all, vecs, routes_t, prev_t, resid):
    rows, feature_dim = h.shape
    tp_count, _, out_cols = ctx_all.shape
    row_spec = pl.BlockSpec((TILE, feature_dim), lambda i: (i, 0))
    lane8 = pl.BlockSpec((8, TILE), lambda i: (0, i))
    lane16 = pl.BlockSpec((16, TILE), lambda i: (0, i))
    ins = [h, ctx_all, wo_all, vecs, routes_t]
    in_specs = [
        row_spec,
        pl.BlockSpec((tp_count, TILE, out_cols), lambda i: (0, i, 0)),
        full_spec(wo_all.shape),
        full_spec(vecs.shape),
        lane8,
    ]
    with_prev = prev_t is not None
    if with_prev:
        ins += [prev_t, resid]
        in_specs += [lane16, full_spec(resid.shape)]
    return pl.pallas_call(
        functools.partial(middle_kernel, with_prev),
        grid=(rows // TILE,),
        out_shape=(
            jax.ShapeDtypeStruct((rows, feature_dim), F32),
            jax.ShapeDtypeStruct((rows, feature_dim), F32),
            jax.ShapeDtypeStruct((rows, feature_dim), BF16),
            jax.ShapeDtypeStruct((8, rows), F32),
            jax.ShapeDtypeStruct((16, rows), F32),
        ),
        in_specs=in_specs,
        out_specs=(row_spec, row_spec, row_spec, lane8, lane16),
        compiler_params=kernel_params(),
        cost_estimate=cost(2 * rows * feature_dim * feature_dim, rows * feature_dim * 16),
        name="middle_part",
    )(*ins)


def split(value):
    high = value.astype(BF16)
    return high, (value - high.astype(F32)).astype(BF16)


def gate_bwd_kernel(with_prev, rank_ref, *refs):
    del rank_ref
    gh_ref, mid_ref, gxm_ref, vec_ref, route_ref, gate_ref, gg_ref, ctx_ref, wo_ref = refs[:9]
    refs = refs[9:]
    if with_prev:
        prev_ref, resid_ref = refs[:2]
        gmid_ref, gctx_ref, dwo_ref, dvec_ref, gprev_ref, dres_ref = refs[2:]
    else:
        gl_ref = refs[0]
        gmid_ref, gctx_ref, dwo_ref, dvec_ref = refs[1:]
    step = pl.program_id(0)
    grad = gh_ref[...].astype(F32)
    middle = mid_ref[...]
    vecs = vec_ref[...]
    gain = vecs[ROW_GM : ROW_GM + 1]
    scale = lax.rsqrt(jnp.mean(middle * middle, axis=-1, keepdims=True) + EPSILON)
    unit = middle * scale
    normed = unit * gain
    xm_low = normed.astype(BF16)
    low_vecs = vecs[:32].astype(BF16)
    gate_in = mm(low_vecs, xm_low, NT)
    alphas = [alpha_rows(gate_in, j) for j in range(2)]
    routes = (route_ref[0:1], route_ref[1:2])
    gates = (gate_ref[0:1], gate_ref[1:2])
    const, on_normed, on_vec = gate_coefs(routes, gates, alphas)
    grad_hi, grad_lo = split(grad)
    vec_dots = mm(low_vecs[16:32], grad_hi, NT) + mm(low_vecs[16:32], grad_lo, NT)
    dot_vec = [vec_dots[ROW_VEC - 16 + j : ROW_VEC - 15 + j] for j in range(2)]
    dot_col = jnp.sum(grad * normed, axis=-1, keepdims=True)
    dot_normed = jnp.broadcast_to(dot_col, (dot_col.shape[0], 128)).T[0:1]
    term = [alphas[j][0] * dot_normed + alphas[j][1] * dot_vec[j] for j in range(2)]
    gate_grads = []
    for slot in range(2):
        fixed = (
            picks(routes[slot], NF + 1) * dot_normed
            + picks(routes[slot], NF + 2) * term[0]
            + picks(routes[slot], NF + 3) * term[1]
        )
        gate_grads.append(jnp.where(routes[slot] < NF, gg_ref[slot : slot + 1], fixed))
    inner = gates[0] * gate_grads[0] + gates[1] * gate_grads[1]
    chosen_grads = [gates[slot] * (gate_grads[slot] - inner) for slot in range(2)]
    expert = iota((16, TILE), 0)
    grad_logits = jnp.where(expert == routes[0], chosen_grads[0], 0.0) + jnp.where(
        expert == routes[1], chosen_grads[1], 0.0
    )
    if not with_prev:
        grad_logits = grad_logits + gl_ref[...]
    alpha_grads = []
    for j in range(2):
        grad_first = const[j] * dot_normed
        grad_second = const[j] * dot_vec[j]
        mean = alphas[j][0] * grad_first + alphas[j][1] * grad_second
        alpha_grads.append((2 * j, alphas[j][0] * (grad_first - mean)))
        alpha_grads.append((2 * j + 1, alphas[j][1] * (grad_second - mean)))
    grad_in = jnp.concatenate([grad_logits, pad_rows(alpha_grads, 16, TILE)], axis=0)
    in_hi, in_lo = split(grad_in)
    low_gate = jnp.where(iota(low_vecs.shape, 0) < ROW_VEC, low_vecs, 0)
    grad_xm = mm(in_hi, low_gate, TN) + mm(in_lo, low_gate, TN)
    cols = to_columns([on_normed])
    grad_y = cols[:, 0:1] * grad + grad_xm + gxm_ref[...].astype(F32)
    weighted = grad_y * gain
    mean = jnp.mean(weighted * unit, axis=-1, keepdims=True)
    grad_mid = grad + scale * (weighted - unit * mean)
    gmid_ref[...] = grad_mid
    low_mid = grad_mid.astype(BF16)
    gctx_ref[...] = mm(low_mid, wo_ref[...]).astype(BF16)
    dwo = mm(low_mid, ctx_ref[...], TN)
    vec_rows = pad_rows([(ROW_VEC - 16 + j, on_vec[j]) for j in range(2)], 16, TILE)
    vec_hi, vec_lo = split(vec_rows)
    dvec_low = mm(vec_hi, grad_hi) + mm(vec_lo, grad_hi)
    dvec_gate = mm(in_hi, xm_low) + mm(in_lo, xm_low)
    dgain = jnp.sum(grad_y * unit, axis=0, keepdims=True)
    row_id = iota(dvec_gate.shape, 0)
    dvec = dvec_gate + jnp.concatenate([jnp.zeros_like(dvec_low), dvec_low], axis=0)
    dvec = jnp.where(row_id == ROW_GM, dgain, dvec)

    @pl.when(step == 0)
    def _():
        dwo_ref[...] = dwo
        dvec_ref[...] = dvec

    @pl.when(step > 0)
    def _():
        dwo_ref[...] += dwo
        dvec_ref[...] += dvec

    if with_prev:
        gprev_ref[...] = mm(resid_ref[...], grad_logits, NN, HIGH)
        dres = mm(prev_ref[...], grad_logits, NT, HIGH)

        @pl.when(step == 0)
        def _():
            dres_ref[...] = dres

        @pl.when(step > 0)
        def _():
            dres_ref[...] += dres


def gate_backward(grad, middle, gxm, vecs, routes_t, gates_t, gg_t, context, wo_all, rank, extra):
    rows, feature_dim = middle.shape
    out_cols = context.shape[1]
    with_prev = len(extra) == 2
    row_spec = pl.BlockSpec((TILE, feature_dim), lambda i, r: (i, 0))
    lane8 = pl.BlockSpec((8, TILE), lambda i, r: (0, i))
    lane16 = pl.BlockSpec((16, TILE), lambda i, r: (0, i))
    ctx_spec = pl.BlockSpec((TILE, out_cols), lambda i, r: (i, 0))
    wo_spec = pl.BlockSpec((pl.Squeezed(), feature_dim, out_cols), lambda i, r: (r[0], 0, 0))
    in_specs = [row_spec, row_spec, row_spec, full_spec(vecs.shape), lane8, lane8, lane8]
    in_specs += [ctx_spec, wo_spec, lane16]
    out_shape = [
        jax.ShapeDtypeStruct((rows, feature_dim), F32),
        jax.ShapeDtypeStruct((rows, out_cols), BF16),
        jax.ShapeDtypeStruct((feature_dim, out_cols), F32),
        jax.ShapeDtypeStruct((32, feature_dim), F32),
    ]
    out_specs = [row_spec, ctx_spec, full_spec((feature_dim, out_cols)), full_spec((32, feature_dim))]
    if with_prev:
        in_specs.append(full_spec(extra[1].shape))
        out_shape += [jax.ShapeDtypeStruct((16, rows), F32), jax.ShapeDtypeStruct((16, 16), F32)]
        out_specs += [lane16, full_spec((16, 16))]
    return pl.pallas_call(
        functools.partial(gate_bwd_kernel, with_prev),
        grid_spec=pltpu.PrefetchScalarGridSpec(
            num_scalar_prefetch=1,
            grid=(rows // TILE,),
            in_specs=in_specs,
            out_specs=tuple(out_specs),
        ),
        out_shape=tuple(out_shape),
        compiler_params=kernel_params(),
        cost_estimate=cost(4 * rows * feature_dim * out_cols, rows * feature_dim * 18),
        name="gate_backward",
    )(rank, grad, middle, gxm, vecs, routes_t, gates_t, gg_t, context, wo_all, *extra)


def qkv_bwd_kernel(gown_ref, goth_ref, h_ref, vec_ref, w_ref, part_ref, dw_ref):
    step = pl.program_id(0)
    grad = (gown_ref[...] + goth_ref[...].astype(F32)).astype(BF16)
    part_ref[...] = mm(grad, w_ref[...], NT).astype(BF16)
    hidden = h_ref[...].astype(F32)
    gain = vec_ref[ROW_GA : ROW_GA + 1, :]
    scale = lax.rsqrt(jnp.mean(hidden * hidden, axis=-1, keepdims=True) + EPSILON)
    attn_in = (hidden * scale * gain).astype(BF16)
    dw = mm(attn_in, grad, TN)

    @pl.when(step == 0)
    def _():
        dw_ref[...] = dw

    @pl.when(step > 0)
    def _():
        dw_ref[...] += dw


def qkv_backward(gown, goth, h, vecs, w_qkv):
    rows, feature_dim = h.shape
    cols = w_qkv.shape[1]
    row_spec = pl.BlockSpec((TILE, feature_dim), lambda i: (i, 0))
    col_spec = pl.BlockSpec((TILE, cols), lambda i: (i, 0))
    return pl.pallas_call(
        qkv_bwd_kernel,
        grid=(rows // TILE,),
        out_shape=(
            jax.ShapeDtypeStruct((rows, feature_dim), BF16),
            jax.ShapeDtypeStruct((feature_dim, cols), F32),
        ),
        in_specs=[col_spec, col_spec, row_spec, full_spec(vecs.shape), full_spec(w_qkv.shape)],
        out_specs=(row_spec, full_spec((feature_dim, cols))),
        compiler_params=kernel_params(),
        cost_estimate=cost(4 * rows * feature_dim * cols, rows * feature_dim * 10),
        name="qkv_backward",
    )(gown, goth, h, vecs, w_qkv)


def norm_bwd_kernel(with_low, gmid_ref, ga_ref, h_ref, vec_ref, out_ref, *rest):
    step = pl.program_id(0)
    hidden = h_ref[...].astype(F32)
    gain = vec_ref[ROW_GA : ROW_GA + 1, :]
    scale = lax.rsqrt(jnp.mean(hidden * hidden, axis=-1, keepdims=True) + EPSILON)
    unit = hidden * scale
    grad_y = ga_ref[...].astype(F32)
    weighted = grad_y * gain
    mean = jnp.mean(weighted * unit, axis=-1, keepdims=True)
    grad = gmid_ref[...] + scale * (weighted - unit * mean)
    out_ref[...] = grad
    if with_low:
        rest[0][...] = grad.astype(BF16)
    dgain_ref = rest[-1]
    dgain = jnp.broadcast_to(jnp.sum(grad_y * unit, axis=0, keepdims=True), dgain_ref.shape)

    @pl.when(step == 0)
    def _():
        dgain_ref[...] = dgain

    @pl.when(step > 0)
    def _():
        dgain_ref[...] += dgain


def norm_backward(gmid, ga, h, vecs, with_low):
    rows, feature_dim = gmid.shape
    row_spec = pl.BlockSpec((TILE, feature_dim), lambda i: (i, 0))
    out_shape = [jax.ShapeDtypeStruct((rows, feature_dim), F32)]
    out_specs = [row_spec]
    if with_low:
        out_shape.append(jax.ShapeDtypeStruct((rows, feature_dim), BF16))
        out_specs.append(row_spec)
    out_shape.append(jax.ShapeDtypeStruct((8, feature_dim), F32))
    out_specs.append(full_spec((8, feature_dim)))
    return pl.pallas_call(
        functools.partial(norm_bwd_kernel, with_low),
        grid=(rows // TILE,),
        out_shape=tuple(out_shape),
        in_specs=[row_spec, row_spec, row_spec, full_spec(vecs.shape)],
        out_specs=tuple(out_specs),
        compiler_params=kernel_params(),
        cost_estimate=cost(rows * feature_dim * 10, rows * feature_dim * 16),
        name="norm_backward",
    )(gmid, ga, h, vecs)


def experts_kernel(fwd, bwd, blocks, count, halves, rows, offs_ref, *refs):
    refs = list(refs)
    xm_ref = refs.pop(0)
    gh_ref = refs.pop(0) if bwd else None
    route_ref, gate_ref = refs.pop(0), refs.pop(0)
    w_refs = [refs.pop(0) for _ in range(count * halves)]
    ffn_ref = refs.pop(0) if fwd else None
    if bwd:
        gx_ref = refs.pop(0)
        dw_refs = [refs.pop(0) for _ in range(count * halves)]
    w_scr, place_scr, pick_scr = refs.pop(0), refs.pop(0), refs.pop(0)
    acc_ref = refs.pop(0) if fwd else None
    if bwd:
        gacc_ref, raw_scr, gg_scr, dw_scr = refs
    expert = pl.program_id(0)
    last = pl.num_programs(0) - 1
    width = w_scr.shape[1]
    units = width // 3
    half = NF // halves

    @pl.when(expert == 0)
    def _():
        order = (iota((BLOCK, BLOCK), 0) < iota((BLOCK, BLOCK), 1)).astype(BF16)
        for block in range(blocks):
            lanes = slice(block * BLOCK, (block + 1) * BLOCK)
            ids = iota((8, BLOCK), 0)
            hits = (ids == route_ref[0:1, lanes]) | (ids == route_ref[1:2, lanes])
            earlier = mm(hits.astype(BF16), order)
            place_scr[block] = jnp.where(hits, earlier, -1.0)
        if fwd:
            acc_ref[...] = jnp.zeros_like(acc_ref)
        if bwd:
            gacc_ref[...] = jnp.zeros_like(gacc_ref)
            gg_scr[...] = jnp.zeros_like(gg_scr)

    for part in range(halves):

        @pl.when((expert >= part * half) & (expert < (part + 1) * half))
        def _(part=part):
            for piece in range(count):
                start = pl.multiple_of(offs_ref[piece] * rows, rows)
                w_scr[pl.ds(start, rows), :] = w_refs[part * count + piece][0]

    hot, gate_cols, masks = [], [], []
    for block in range(blocks):
        lanes = slice(block * BLOCK, (block + 1) * BLOCK)
        place = place_scr[block, pl.ds(expert, 1), :]
        one_hot = (iota((CAP, BLOCK), 0).astype(F32) == place).astype(F32)
        mask = [route_ref[slot : slot + 1, lanes] == expert for slot in range(2)]
        gate_row = jnp.where(mask[0], gate_ref[0:1, lanes], 0.0) + jnp.where(
            mask[1], gate_ref[1:2, lanes], 0.0
        )
        gate_cols.append(jnp.sum(one_hot * gate_row, axis=1, keepdims=True))
        one_hot = one_hot.astype(BF16)
        pick_scr[block * CAP : (block + 1) * CAP, :] = mm(one_hot, xm_ref[lanes, :]).astype(BF16)
        if bwd:
            raw_scr[block * CAP : (block + 1) * CAP, :] = mm(one_hot, gh_ref[lanes, :]).astype(BF16)
        hot.append(one_hot)
        masks.append(mask)
    gate_col = jnp.concatenate(gate_cols, axis=0)
    picked = pick_scr[...]
    gate_up = mm(picked, w_scr[:, : 2 * units])
    gate_in, up_in = gate_up[:, :units], gate_up[:, units:]
    sigmoid = lax.logistic(gate_in)
    silu = gate_in * sigmoid
    hidden = (silu * up_in).astype(BF16)
    if fwd:
        scaled = (mm(hidden, w_scr[:, 2 * units :], NT) * gate_col).astype(BF16)
        for block in range(blocks):
            acc_ref[block * BLOCK : (block + 1) * BLOCK, :] += mm(
                hot[block], scaled[block * CAP : (block + 1) * CAP], TN
            )

        @pl.when(expert == last)
        def _():
            ffn_ref[...] = acc_ref[...].astype(BF16)

    if bwd:
        raw = raw_scr[...]
        grad_raw = mm(raw, w_scr[:, 2 * units :])
        gate_dot = jnp.sum(hidden.astype(F32) * grad_raw, axis=1, keepdims=True)
        for block in range(blocks):
            row = jnp.sum(
                hot[block].astype(F32) * gate_dot[block * CAP : (block + 1) * CAP],
                axis=0,
                keepdims=True,
            )
            for slot in range(2):
                gg_scr[8 * block + slot : 8 * block + slot + 1, :] += jnp.where(
                    masks[block][slot], row, 0.0
                )
        grad_hidden = grad_raw * gate_col
        grad_gate = grad_hidden * up_in * sigmoid * (1.0 + gate_in * (1.0 - sigmoid))
        grad_up = grad_hidden * silu
        grad_gu = jnp.concatenate([grad_gate.astype(BF16), grad_up.astype(BF16)], axis=1)
        grad_pick = mm(grad_gu, w_scr[:, : 2 * units], NT).astype(BF16)
        for block in range(blocks):
            gacc_ref[block * BLOCK : (block + 1) * BLOCK, :] += mm(
                hot[block], grad_pick[block * CAP : (block + 1) * CAP], TN
            )
        grad_result = (raw.astype(F32) * gate_col).astype(BF16)
        dw_scr[:, : 2 * units] = mm(picked, grad_gu, TN).astype(BF16)
        dw_scr[:, 2 * units :] = mm(grad_result, hidden, TN).astype(BF16)
        for part in range(halves):

            @pl.when((expert >= part * half) & (expert < (part + 1) * half))
            def _(part=part):
                for piece in range(count):
                    start = pl.multiple_of(offs_ref[piece] * rows, rows)
                    dw_refs[part * count + piece][0] = dw_scr[pl.ds(start, rows), :]

        @pl.when(expert == last)
        def _():
            total = blocks * BLOCK
            gx_ref[:total, :] = gacc_ref[...].astype(BF16)
            gx_ref[total:, :] = jnp.zeros((gx_ref.shape[0] - total, gx_ref.shape[1]), BF16)
            gx_ref[total : total + gg_scr.shape[0], :BLOCK] = gg_scr[...].astype(BF16)


def experts(fwd, bwd, xm, gh, routes_t, gates_t, pieces, offs):
    rows, feature_dim = xm.shape
    blocks = rows // BLOCK
    halves, count = len(pieces), len(pieces[0])
    half = NF // halves
    piece_rows = pieces[0][0].shape[1]
    width = pieces[0][0].shape[2]
    units = width // 3

    def piece_specs():
        specs = []
        for part in range(halves):
            for _ in range(count):
                specs.append(
                    pl.BlockSpec(
                        (1, piece_rows, width),
                        lambda e, part=part: (jnp.clip(e - part * half, 0, half - 1), 0, 0),
                    )
                )
        return specs

    ins = [xm] + ([gh] if bwd else []) + [routes_t, gates_t]
    in_specs = [SMEM_SPEC] + [full_spec(item.shape) for item in ins] + piece_specs()
    flat = [piece for part in pieces for piece in part]
    out_shape, out_specs, scratch = [], [], []
    scratch += [
        pltpu.VMEM((feature_dim, width), BF16),
        pltpu.VMEM((blocks, 8, BLOCK), F32),
        pltpu.VMEM((blocks * CAP, feature_dim), BF16),
    ]
    flops = 0
    if fwd:
        out_shape.append(jax.ShapeDtypeStruct((rows, feature_dim), BF16))
        out_specs.append(full_spec((rows, feature_dim)))
        scratch.append(pltpu.VMEM((rows, feature_dim), F32))
        flops += 1.0e9 * NF * blocks / 2
    if bwd:
        out_shape.append(jax.ShapeDtypeStruct((rows + 16, feature_dim), BF16))
        out_specs.append(full_spec((rows + 16, feature_dim)))
        for piece in flat:
            out_shape.append(jax.ShapeDtypeStruct(piece.shape, BF16))
        out_specs += piece_specs()
        scratch += [
            pltpu.VMEM((rows, feature_dim), F32),
            pltpu.VMEM((blocks * CAP, feature_dim), BF16),
            pltpu.VMEM((blocks * 8, BLOCK), F32),
            pltpu.VMEM((feature_dim, width), BF16),
        ]
        flops += 2.2e9 * NF * blocks / 2
    outs = pl.pallas_call(
        functools.partial(experts_kernel, fwd, bwd, blocks, count, halves, piece_rows),
        grid=(NF,),
        out_shape=tuple(out_shape),
        in_specs=in_specs,
        out_specs=tuple(out_specs),
        scratch_shapes=scratch,
        compiler_params=kernel_params(),
        cost_estimate=cost(flops, 20e6 * (2 if bwd else 1), rows * units * 8),
        name="experts",
    )(offs, *ins, *flat)
    outs = list(outs)
    ffn = outs.pop(0) if fwd else None
    if not bwd:
        return ffn
    gx = outs.pop(0)
    grads = [outs[part * count : (part + 1) * count] for part in range(halves)]
    return ffn, gx, grads


def hop(value, step):
    return lax.ppermute(value, "fsdp", [(i, i ^ step) for i in range(4)])


def swap(value):
    return lax.ppermute(value, "ctx", [(0, 1), (1, 0)])


def gather_small(value):
    by_x, by_y = hop(value, 1), hop(value, 2)
    by_d = hop(value, 3)
    out = []
    for item in (value, by_x, by_y, by_d):
        out += [item, swap(item)]
    return out


def gather_halves(low, high):
    x_low, y_high = hop(low, 1), hop(high, 2)
    x_high, y_low = hop(high, 1), hop(low, 2)
    d_low, d_high = hop(y_low, 1), hop(x_high, 2)
    lows, highs = [], []
    for item in (low, x_low, y_low, d_low):
        lows += [item, swap(item)]
    for item in (high, x_high, y_high, d_high):
        highs += [item, swap(item)]
    return lows, highs


def add_low(first, second):
    return (first.astype(F32) + second.astype(F32)).astype(BF16)


def sum_cores(pieces):
    return [add_low(pieces[2 * chip], swap(pieces[2 * chip + 1])) for chip in range(4)]


def sum_chips(sums, first):
    second = 3 - first
    mine = add_low(sums[0], hop(sums[first], first))
    beside = add_low(sums[second], hop(sums[3], first))
    return mine.astype(F32) + hop(beside, second).astype(F32)


def per_device(
    hyper,
    axes,
    tokens,
    cotangent,
    lengths,
    routes,
    norm_attn,
    w_qkv,
    w_out,
    norm_moe,
    w_router,
    w_resid,
    w_const,
    v_const,
    w_gate_up,
    w_down,
):
    micro_count, seq_count, block_len, feature_dim = tokens.shape
    rows = micro_count * seq_count * block_len
    layer_count, shard_rows, qkv_cols = w_qkv.shape
    heads = qkv_cols // (3 * HD)
    units = w_gate_up.shape[-1]
    groups = ("fsdp", "ctx")
    shard_count = feature_dim // shard_rows
    ctx = lax.axis_index("ctx")
    me = lax.axis_index("fsdp") * axes["ctx"] + ctx
    rank = lax.axis_index("tp").reshape(1)
    if hyper:
        offs = me ^ jnp.arange(shard_count, dtype=jnp.int32)
    else:
        offs = jnp.zeros((1,), jnp.int32)
    info = jnp.concatenate([ctx.reshape(1), lengths.reshape(-1)]).astype(jnp.int32)
    resid = jnp.zeros((16, 16), F32).at[:NE, :NE].set(w_resid.astype(F32))

    small, wide, outer = [], [], []
    for layer in range(layer_count):
        vec = jnp.concatenate(
            [
                w_router[layer],
                jnp.zeros((shard_rows, ROW_CONST - NE), BF16),
                w_const[layer, 0],
                w_const[layer, 1],
                v_const[layer].T,
                norm_attn[layer][:, None],
                norm_moe[layer][:, None],
                jnp.zeros((shard_rows, 128 - ROW_GM - 1), BF16),
            ],
            axis=1,
        )
        small.append(jnp.concatenate([w_qkv[layer], vec], axis=1))
        wide.append(
            jnp.concatenate(
                [
                    w_gate_up[layer].reshape(NF, shard_rows, 2 * units),
                    jnp.transpose(w_down[layer], (0, 2, 1)),
                ],
                axis=2,
            )
        )
    outer = lax.all_gather(jnp.transpose(w_out, (0, 2, 1)), "tp", axis=1)

    weights = []
    token = None
    for layer in range(layer_count):
        if hyper:
            low, high = wide[layer][: NF // 2], wide[layer][NF // 2 :]
            own_small, own_outer = small[layer], outer[layer]
            if token is not None:
                own_small, low, high, _ = lax.optimization_barrier((own_small, low, high, token))
            pieces_small = gather_small(own_small)
            pieces_outer = gather_small(own_outer)
            pieces = gather_halves(low, high)
            token = (pieces[0][6], pieces[1][6])
        else:
            pieces_small = [lax.all_gather(small[layer], groups, axis=0, tiled=True)]
            pieces_outer = [lax.all_gather(outer[layer], groups, axis=1, tiled=True)]
            pieces = [[lax.all_gather(wide[layer], groups, axis=1, tiled=True)]]
        qkv_full, wo_all, vec_cols = prep_weights(
            pieces_small, pieces_outer, offs, feature_dim, qkv_cols
        )
        weights.append((qkv_full, wo_all, vec_cols[:, :32].T.astype(F32), pieces))

    routes_t = jnp.moveaxis(routes.reshape(layer_count, rows, 2), 2, 1)
    routes_t = jnp.concatenate(
        [routes_t, jnp.full((layer_count, 6, rows), -1, jnp.int32)], axis=1
    )
    position = ctx * block_len + jnp.arange(block_len, dtype=jnp.int32)
    valid = position[None, None, :] < lengths[:, :, None]
    cot = jnp.where(valid[..., None], cotangent, 0).reshape(rows, feature_dim)

    base, ffn, prev_t = tokens.reshape(rows, feature_dim), None, None
    saved = []
    for layer in range(layer_count):
        qkv_full, wo_all, vecs, pieces = weights[layer]
        outs = qkv_part(base, ffn, vecs, qkv_full)
        h_in, qkv = outs if ffn is not None else (base, outs[0])
        other = swap(qkv)
        context, lse = attend_forward(qkv, other, info, heads)
        ctx_all = lax.all_gather(context, "tp", axis=0)
        middle, base, xm_low, gates_t, logits_t = middle_part(
            h_in, ctx_all, wo_all, vecs, routes_t[layer], prev_t, resid
        )
        saved.append((h_in, qkv, other, context, lse, middle, xm_low, gates_t, prev_t))
        prev_t = logits_t
        if layer < layer_count - 1:
            part = experts(True, False, xm_low, None, routes_t[layer], gates_t, pieces, offs)
            ffn = lax.psum(part, "tp")

    grad, grad_low = cot, cot
    grad_logits = None
    finals = [None] * layer_count
    for layer in reversed(range(layer_count)):
        qkv_full, wo_all, vecs, pieces = weights[layer]
        h_in, qkv, other, context, lse, middle, xm_low, gates_t, prev_t = saved[layer]
        top = layer == layer_count - 1
        part, gx, grads = experts(
            top, True, xm_low, grad_low, routes_t[layer], gates_t, pieces, offs
        )
        gx = lax.psum(gx, "tp")
        if top:
            ffn = lax.psum(part, "tp")
            mixed = (base + ffn.astype(F32)).astype(BF16)
        gg_t = gx[rows : rows + 16, :block_len].astype(F32)
        gg_t = jnp.moveaxis(gg_t.reshape(2, 8, block_len)[: rows // BLOCK], 0, 1).reshape(8, rows)
        extra = (prev_t, resid) if prev_t is not None else (grad_logits,)
        outs = gate_backward(
            grad, middle, gx, vecs, routes_t[layer], gates_t, gg_t, context, wo_all, rank, extra
        )
        gmid, gctx, dwo, dvec = outs[:4]
        if prev_t is not None:
            grad_logits, dres = outs[4:]
        gown, goth = attend_backward(qkv, other, lse, gctx, info, heads)
        ga_part, dqkv = qkv_backward(gown, swap(goth), h_in, vecs, qkv_full)
        ga = lax.psum(ga_part, "tp")
        outs = norm_backward(gmid, ga, h_in, vecs, layer > 0)
        grad, dgain = outs[0], outs[-1]
        grad_low = outs[1]
        finals[layer] = (grads, dqkv, dwo, dvec, dgain)

    results = []
    gain_rows = jnp.concatenate([item[4][:1] for item in finals] + [dres[:NE + 4].reshape(1, -1)], axis=1)
    if hyper:
        total = gain_rows + swap(gain_rows)
        total = total + hop(total, 1)
        total = total + hop(total, 2)
    else:
        total = lax.psum(gain_rows, groups)
    gain_total = total[0, : layer_count * feature_dim].reshape(layer_count, feature_dim)
    resid_total = total[0, layer_count * feature_dim :].reshape(16, 16)[:NE, :NE]
    gain_own = lax.dynamic_slice(gain_total, (0, me * shard_rows), (layer_count, shard_rows))
    for layer in range(layer_count):
        grads, dqkv, dwo, dvec, _ = finals[layer]
        packed = jnp.concatenate([dqkv, dwo, dvec.T], axis=1).astype(BF16)
        if hyper:
            packed = packed.reshape(shard_count, shard_rows, -1)
            packed = [
                lax.dynamic_index_in_dim(packed, me ^ off, 0, keepdims=False)
                for off in range(shard_count)
            ]
            own = sum_chips(sum_cores(packed), 1)
            low = sum_chips(sum_cores(grads[0]), 1)
            high = sum_chips(sum_cores(grads[1]), 2)
            wide_own = jnp.concatenate([low, high], axis=0)
        else:
            own = lax.psum_scatter(packed, groups, scatter_dimension=0, tiled=True).astype(F32)
            wide_own = lax.psum_scatter(
                grads[0][0], groups, scatter_dimension=1, tiled=True
            ).astype(F32)
        out_cols = dwo.shape[1]
        vec = own[:, qkv_cols + out_cols :]
        results.append(
            (
                own[:, :qkv_cols],
                own[:, qkv_cols : qkv_cols + out_cols].T,
                vec[:, ROW_GM],
                vec[:, :NE],
                jnp.stack([vec[:, ROW_CONST : ROW_CONST + 2], vec[:, ROW_CONST + 2 : ROW_CONST + 4]]),
                vec[:, ROW_VEC : ROW_VEC + 2].T,
                wide_own[:, :, : 2 * units].reshape(NF, shard_rows, 2, units),
                jnp.transpose(wide_own[:, :, 2 * units :], (0, 2, 1)),
            )
        )
    stacked = [jnp.stack([item[member] for item in results]) for member in range(8)]
    return (
        mixed.reshape(tokens.shape),
        grad.reshape(tokens.shape),
        gain_own,
        stacked[0],
        stacked[1],
        stacked[2],
        stacked[3],
        resid_total,
        stacked[4],
        stacked[5],
        stacked[6],
        stacked[7],
    )


def solution(mesh):
    axes = dict(mesh.shape)
    hyper = axes["fsdp"] == 4 and axes["ctx"] == 2
    in_specs = (
        P(None, "fsdp", "ctx", None),
        P(None, "fsdp", "ctx", None),
        P(None, "fsdp"),
        P(None, None, "fsdp", "ctx", None),
        P(None, ("fsdp", "ctx")),
        P(None, ("fsdp", "ctx"), "tp"),
        P(None, "tp", ("fsdp", "ctx")),
        P(None, ("fsdp", "ctx")),
        P(None, ("fsdp", "ctx"), None),
        P(),
        P(None, None, ("fsdp", "ctx"), None),
        P(None, None, ("fsdp", "ctx")),
        P(None, None, ("fsdp", "ctx"), None, "tp"),
        P(None, None, "tp", ("fsdp", "ctx")),
    )
    out_specs = (
        P(None, "fsdp", "ctx", None),
        P(None, "fsdp", "ctx", None),
        P(None, ("fsdp", "ctx")),
        P(None, ("fsdp", "ctx"), "tp"),
        P(None, "tp", ("fsdp", "ctx")),
        P(None, ("fsdp", "ctx")),
        P(None, ("fsdp", "ctx"), None),
        P(),
        P(None, None, ("fsdp", "ctx"), None),
        P(None, None, ("fsdp", "ctx")),
        P(None, None, ("fsdp", "ctx"), None, "tp"),
        P(None, None, "tp", ("fsdp", "ctx")),
    )
    return jax.shard_map(
        functools.partial(per_device, hyper, axes),
        mesh=mesh,
        in_specs=in_specs,
        out_specs=out_specs,
        check_vma=False,
    )
```

```python
import functools

import jax
import jax.numpy as jnp
from jax import lax
from jax.experimental import pallas as pl
from jax.experimental.pallas import tpu as pltpu
from jax.sharding import PartitionSpec as P

HD = 64
NF = 8
NE = 12
BLOCK = 512
CAP = 128
TILE = 256
EPSILON = 1e-06
MASKED = -1e30
F32 = jnp.float32
BF16 = jnp.bfloat16
HIGH = lax.Precision.HIGHEST
ROW_CONST, ROW_VEC, ROW_GA, ROW_GM, ROW_UP = 16, 20, 22, 23, 24
VMEM_LIMIT = 58 * 1024 * 1024
SCALE = 0.05
PACK = 128
LATE = 512

NN = (((1,), (0,)), ((), ()))
NT = (((1,), (1,)), ((), ()))
TN = (((0,), (0,)), ((), ()))


def mm(left, right, dims=NN, precision=None):
    return lax.dot_general(left, right, dims, precision=precision, preferred_element_type=F32)


def kernel_params():
    return pltpu.CompilerParams(vmem_limit_bytes=VMEM_LIMIT)


def cost(flops, nbytes, trans=0):
    return pl.CostEstimate(
        flops=int(flops * SCALE), bytes_accessed=int(nbytes * SCALE), transcendentals=int(trans * SCALE)
    )


def iota(shape, dim):
    return lax.broadcasted_iota(jnp.int32, shape, dim)


def full_spec(shape):
    zeros = (0,) * len(shape)
    return pl.BlockSpec(shape, lambda *idx: zeros)


SMEM_SPEC = pl.BlockSpec(memory_space=pltpu.SMEM)


def pad_rows(rows, count, width):
    row_id = iota((count, width), 0)
    out = jnp.zeros((count, width), F32)
    for place, row in rows:
        out = jnp.where(row_id == place, row, out)
    return out


def round_up(value, unit):
    return -(-value // unit) * unit


def prep_kernel(count, rows, offs_ref, *refs):
    qkv_ref, wo_ref, vec_ref, scr_ref = refs[count:]
    cols, out_cols = qkv_ref.shape[1], wo_ref.shape[2]
    for piece in range(count):
        start = pl.multiple_of(offs_ref[piece] * rows, rows)
        block = refs[piece][...]
        qkv_ref[pl.ds(start, rows), :] = block[:, :cols]
        scr_ref[pl.ds(start, rows), :] = block[:, cols : cols + PACK].astype(F32)
        for rank in range(wo_ref.shape[0]):
            first = cols + PACK + rank * out_cols
            wo_ref[rank, pl.ds(start, rows), :] = block[:, first : first + out_cols]
    vec_ref[...] = scr_ref[...].T[:32]


def prep_weights(pieces, offs, feature_dim, qkv_cols, tp_count):
    count = len(pieces)
    cols = round_up(qkv_cols, 128)
    out_cols = (pieces[0].shape[1] - cols - PACK) // tp_count
    vmem = pl.BlockSpec(memory_space=pltpu.VMEM)
    return pl.pallas_call(
        functools.partial(prep_kernel, count, feature_dim // count),
        out_shape=(
            jax.ShapeDtypeStruct((feature_dim, cols), BF16),
            jax.ShapeDtypeStruct((tp_count, feature_dim, out_cols), BF16),
            jax.ShapeDtypeStruct((32, feature_dim), F32),
        ),
        in_specs=[SMEM_SPEC] + [vmem] * count,
        out_specs=(vmem, vmem, vmem),
        scratch_shapes=[pltpu.VMEM((feature_dim, PACK), F32)],
        compiler_params=kernel_params(),
        cost_estimate=cost(1e6, 3e6),
        name="prep",
    )(offs, *pieces)


def pack_kernel(count, rows, offs_ref, dqkv_ref, dwo_ref, dvec_ref, *refs):
    outs, scr_ref = refs[:-1], refs[-1]
    cols, out_cols = dqkv_ref.shape[1], dwo_ref.shape[1]
    scr_ref[:, :cols] = dqkv_ref[...]
    scr_ref[:, cols : cols + out_cols] = dwo_ref[...]
    wide = jnp.concatenate([dvec_ref[...], jnp.zeros((96, dvec_ref.shape[1]), F32)], axis=0).T
    scr_ref[:, cols + out_cols :] = wide
    for piece in range(count):
        start = pl.multiple_of(offs_ref[piece] * rows, rows)
        block = scr_ref[pl.ds(start, rows), :].astype(BF16)
        if count > 1:
            outs[piece % 2][piece // 2] = block
        else:
            outs[0][...] = block


def pack_grads(dqkv, dwo, dvec, offs):
    feature_dim = dqkv.shape[0]
    count = offs.shape[0]
    rows = feature_dim // count
    width = dqkv.shape[1] + dwo.shape[1] + PACK
    shape = (count // 2, rows, width) if count > 1 else (feature_dim, width)
    vmem = pl.BlockSpec(memory_space=pltpu.VMEM)
    outs = 2 if count > 1 else 1
    return pl.pallas_call(
        functools.partial(pack_kernel, count, rows),
        out_shape=tuple([jax.ShapeDtypeStruct(shape, BF16)] * outs),
        in_specs=[SMEM_SPEC, vmem, vmem, vmem],
        out_specs=tuple([vmem] * outs),
        scratch_shapes=[pltpu.VMEM((feature_dim, width), F32)],
        compiler_params=kernel_params(),
        cost_estimate=cost(1e6, 6e6),
        name="pack_grads",
    )(offs, dqkv, dwo, dvec)


def pack_wide_kernel(gu_ref, down_ref, low_ref, high_ref):
    units = down_ref.shape[-1]

    def write(ref):
        ref[0, :, :units] = gu_ref[0, 0, :, 0, :]
        ref[0, :, units : 2 * units] = gu_ref[0, 0, :, 1, :]
        ref[0, :, 2 * units :] = down_ref[0, 0]

    @pl.when(pl.program_id(0) < NF // 2)
    def _():
        write(low_ref)

    @pl.when(pl.program_id(0) >= NF // 2)
    def _():
        write(high_ref)


def pack_wide(w_gate_up, w_down_t, layer):
    _, _, rows, _, units = w_gate_up.shape
    half = NF // 2
    specs = [
        pl.BlockSpec(
            (1, rows, 3 * units), lambda e, part=part: (jnp.clip(e - part * half, 0, half - 1), 0, 0)
        )
        for part in range(2)
    ]
    return pl.pallas_call(
        pack_wide_kernel,
        grid=(NF,),
        out_shape=tuple([jax.ShapeDtypeStruct((half, rows, 3 * units), BF16)] * 2),
        in_specs=[
            pl.BlockSpec((1, 1, rows, 2, units), lambda e: (layer, e, 0, 0, 0)),
            pl.BlockSpec((1, 1, rows, units), lambda e: (layer, e, 0, 0)),
        ],
        out_specs=tuple(specs),
        compiler_params=kernel_params(),
        cost_estimate=cost(1e6, 5e6),
        name="pack_wide",
    )(w_gate_up, w_down_t)


def qkv_kernel(with_ffn, *refs):
    if with_ffn:
        base_ref, ffn_ref, vec_ref, w_ref, h_ref, qkv_ref = refs
        hidden = base_ref[...] + ffn_ref[...].astype(F32)
        h_ref[...] = hidden
    else:
        base_ref, vec_ref, w_ref, qkv_ref = refs
        hidden = base_ref[...].astype(F32)
    gain = vec_ref[ROW_GA : ROW_GA + 1, :]
    scale = lax.rsqrt(jnp.mean(hidden * hidden, axis=-1, keepdims=True) + EPSILON)
    attn_in = (hidden * scale * gain).astype(BF16)
    qkv_ref[...] = mm(attn_in, w_ref[...]).astype(BF16)


def qkv_part(base, ffn, vecs, w_qkv):
    rows, feature_dim = base.shape
    cols = round_up(w_qkv.shape[1], 128)
    row_spec = pl.BlockSpec((TILE, feature_dim), lambda i: (i, 0))
    with_ffn = ffn is not None
    out_shape = [jax.ShapeDtypeStruct((rows, cols), BF16)]
    out_specs = [pl.BlockSpec((TILE, cols), lambda i: (i, 0))]
    if with_ffn:
        out_shape = [jax.ShapeDtypeStruct((rows, feature_dim), F32)] + out_shape
        out_specs = [row_spec] + out_specs
    ins = [base] + ([ffn] if with_ffn else []) + [vecs, w_qkv]
    in_specs = [row_spec] * (2 if with_ffn else 1) + [full_spec(vecs.shape), full_spec(w_qkv.shape)]
    return pl.pallas_call(
        functools.partial(qkv_kernel, with_ffn),
        grid=(rows // TILE,),
        out_shape=tuple(out_shape),
        in_specs=in_specs,
        out_specs=tuple(out_specs),
        compiler_params=kernel_params(),
        cost_estimate=cost(2 * rows * feature_dim * cols, rows * feature_dim * 10),
        name="qkv_part",
    )(*ins)


def attn_masks(ctx, length, tile, width):
    row = iota((TILE, width), 0) + tile * TILE
    col = iota((TILE, width), 1)
    return (col <= row) & (col + ctx * BLOCK < length)


def attn_fwd_kernel(heads, info_ref, own_ref, other_ref, ctx_ref, lse_ref):
    ctx = info_ref[0]
    length = info_ref[1 + pl.program_id(0)]
    own = own_ref[...]
    other = other_ref[...]
    for head in range(heads):
        col = head * 3 * HD
        k_own = own[:, col + HD : col + 2 * HD]
        v_own = own[:, col + 2 * HD : col + 3 * HD]
        k_oth = other[:, col + HD : col + 2 * HD]
        v_oth = other[:, col + 2 * HD : col + 3 * HD]
        for tile in range(BLOCK // TILE):
            width = (tile + 1) * TILE
            query = own[tile * TILE : (tile + 1) * TILE, col : col + HD] * BF16(HD**-0.5)
            s_own = mm(query, k_own[:width], NT)
            s_own = jnp.where(attn_masks(ctx, length, tile, width), s_own, MASKED)
            s_oth = jnp.where(ctx > 0, mm(query, k_oth, NT), MASKED)
            top = jnp.maximum(
                jnp.max(s_own, axis=-1, keepdims=True), jnp.max(s_oth, axis=-1, keepdims=True)
            )
            p_own = jnp.exp(s_own - top)
            p_oth = jnp.exp(s_oth - top)
            total = jnp.sum(p_own, axis=-1, keepdims=True) + jnp.sum(p_oth, axis=-1, keepdims=True)
            out = mm(p_own.astype(BF16), v_own[:width]) + mm(p_oth.astype(BF16), v_oth)
            out = out / total
            rows = slice(tile * TILE, (tile + 1) * TILE)
            ctx_ref[head * TILE : (head + 1) * TILE, tile * HD : (tile + 1) * HD] = out.astype(BF16)
            lse_ref[rows, head : head + 1] = top + jnp.log(total)


def attend_forward(qkv, other, info, heads):
    rows, cols = qkv.shape
    count = rows // BLOCK
    spec = pl.BlockSpec((BLOCK, cols), lambda i: (i, 0))
    return pl.pallas_call(
        functools.partial(attn_fwd_kernel, heads),
        grid=(count,),
        out_shape=(
            jax.ShapeDtypeStruct((count * heads * TILE, 2 * HD), BF16),
            jax.ShapeDtypeStruct((rows, 8), F32),
        ),
        in_specs=[SMEM_SPEC, spec, spec],
        out_specs=(
            pl.BlockSpec((heads * TILE, 2 * HD), lambda i: (i, 0)),
            pl.BlockSpec((BLOCK, 8), lambda i: (i, 0)),
        ),
        compiler_params=kernel_params(),
        cost_estimate=cost(rows * 1024 * heads * HD * 16, rows * cols * 6, rows * heads * 1024),
        name="attend_forward",
    )(info, qkv, other)


def attn_bwd_kernel(heads, info_ref, own_ref, other_ref, lse_ref, gctx_ref, gown_ref, goth_ref):
    ctx = info_ref[0]
    length = info_ref[1 + pl.program_id(0)]
    own = own_ref[...]
    other = other_ref[...]
    scale = BF16(HD**-0.5)
    for head in range(heads):
        col = head * 3 * HD
        k_own = own[:, col + HD : col + 2 * HD]
        v_own = own[:, col + 2 * HD : col + 3 * HD]
        k_oth = other[:, col + HD : col + 2 * HD]
        v_oth = other[:, col + 2 * HD : col + 3 * HD]
        goth_ref[:, col : col + HD] = jnp.zeros((BLOCK, HD), BF16)
        gk_own, gv_own, gk_oth, gv_oth = [], [], [], []
        for tile in range(BLOCK // TILE):
            width = (tile + 1) * TILE
            rows = slice(tile * TILE, (tile + 1) * TILE)
            query = own[rows, col : col + HD] * scale
            gout = gctx_ref[rows, head * HD : (head + 1) * HD]
            lse = lse_ref[rows, head : head + 1]
            s_own = mm(query, k_own[:width], NT)
            s_own = jnp.where(attn_masks(ctx, length, tile, width), s_own, MASKED)
            s_oth = jnp.where(ctx > 0, mm(query, k_oth, NT), MASKED)
            p_own = jnp.exp(s_own - lse)
            p_oth = jnp.exp(s_oth - lse)
            d_own = mm(gout, v_own[:width], NT)
            d_oth = mm(gout, v_oth, NT)
            inner = jnp.sum(p_own * d_own, axis=-1, keepdims=True) + jnp.sum(
                p_oth * d_oth, axis=-1, keepdims=True
            )
            ds_own = (p_own * (d_own - inner)).astype(BF16)
            ds_oth = (p_oth * (d_oth - inner)).astype(BF16)
            p_own = p_own.astype(BF16)
            p_oth = p_oth.astype(BF16)
            gown_ref[rows, col : col + HD] = (mm(ds_own, k_own[:width]) + mm(ds_oth, k_oth)) * (
                HD**-0.5
            )
            gk_own.append(mm(ds_own, query, TN))
            gv_own.append(mm(p_own, gout, TN))
            gk_oth.append(mm(ds_oth, query, TN))
            gv_oth.append(mm(p_oth, gout, TN))
        gown_ref[:TILE, col + HD : col + 2 * HD] = gk_own[0] + gk_own[1][:TILE]
        gown_ref[TILE:, col + HD : col + 2 * HD] = gk_own[1][TILE:]
        gown_ref[:TILE, col + 2 * HD : col + 3 * HD] = gv_own[0] + gv_own[1][:TILE]
        gown_ref[TILE:, col + 2 * HD : col + 3 * HD] = gv_own[1][TILE:]
        goth_ref[:, col + HD : col + 2 * HD] = (gk_oth[0] + gk_oth[1]).astype(BF16)
        goth_ref[:, col + 2 * HD : col + 3 * HD] = (gv_oth[0] + gv_oth[1]).astype(BF16)


def attend_backward(qkv, other, lse, grad_context, info, heads):
    rows, width = qkv.shape
    cols = heads * 3 * HD
    spec = pl.BlockSpec((BLOCK, width), lambda i: (i, 0))
    return pl.pallas_call(
        functools.partial(attn_bwd_kernel, heads),
        grid=(rows // BLOCK,),
        out_shape=(
            jax.ShapeDtypeStruct((rows, cols), F32),
            jax.ShapeDtypeStruct((rows, width), BF16),
        ),
        in_specs=[
            SMEM_SPEC,
            spec,
            spec,
            pl.BlockSpec((BLOCK, 8), lambda i: (i, 0)),
            pl.BlockSpec((BLOCK, heads * HD), lambda i: (i, 0)),
        ],
        out_specs=(pl.BlockSpec((BLOCK, cols), lambda i: (i, 0)), spec),
        compiler_params=kernel_params(),
        cost_estimate=cost(rows * 1024 * heads * HD * 40, rows * cols * 12, rows * heads * 1024),
        name="attend_backward",
    )(info, qkv, other, lse, grad_context)


def alpha_rows(gate_in, const_idx):
    first = gate_in[ROW_CONST + 2 * const_idx : ROW_CONST + 2 * const_idx + 1]
    second = gate_in[ROW_CONST + 2 * const_idx + 1 : ROW_CONST + 2 * const_idx + 2]
    return pair(first, second)


def pair(first, second):
    top = jnp.maximum(first, second)
    exp_first = jnp.exp(first - top)
    exp_second = jnp.exp(second - top)
    total = exp_first + exp_second
    return exp_first / total, exp_second / total


def picks(route, value):
    return (route == value).astype(F32)


def gate_coefs(routes, gates, alphas):
    copy = picks(routes[0], NF + 1) * gates[0] + picks(routes[1], NF + 1) * gates[1]
    const = [
        picks(routes[0], NF + 2 + j) * gates[0] + picks(routes[1], NF + 2 + j) * gates[1]
        for j in range(2)
    ]
    on_normed = copy + const[0] * alphas[0][0] + const[1] * alphas[1][0]
    on_vec = [const[j] * alphas[j][1] for j in range(2)]
    return const, on_normed, on_vec


def to_columns(rows):
    width = rows[0].shape[1]
    return pad_rows(list(enumerate(rows)), 128, width).T


def unpack_context(both):
    heads = both.shape[0] // TILE
    side = lax.rem(pl.program_id(0), 2) == 0
    both = jnp.where(side, both[:, :HD], both[:, HD:])
    parts = [both[head * TILE : (head + 1) * TILE] for head in range(heads)]
    return jnp.concatenate(parts, axis=1)


def middle_kernel(with_prev, rank_ref, *refs):
    if with_prev:
        h_ref, ctx_ref, wo_ref, vec_ref, route_ref, prev_ref, resid_ref = refs[:7]
        refs = refs[7:]
    else:
        h_ref, ctx_ref, wo_ref, vec_ref, route_ref = refs[:5]
        refs = refs[5:]
    mid_ref, base_ref, xm_ref, gate_ref, logit_ref = refs
    count = ctx_ref.shape[0]
    attn_out = mm(unpack_context(ctx_ref[rank_ref[0]]), wo_ref[0], NT)
    for back in range(1, count):
        owner = lax.rem(rank_ref[0] + count - back, count)
        attn_out += mm(unpack_context(ctx_ref[owner]), wo_ref[back], NT)
    middle = h_ref[...].astype(F32) + attn_out
    mid_ref[...] = middle
    vecs = vec_ref[...]
    scale = lax.rsqrt(jnp.mean(middle * middle, axis=-1, keepdims=True) + EPSILON)
    normed = middle * scale * vecs[ROW_GM : ROW_GM + 1]
    xm_low = normed.astype(BF16)
    xm_ref[...] = xm_low
    gate_in = mm(vecs[:32].astype(BF16), xm_low, NT)
    logits = gate_in[:16]
    if with_prev:
        logits = logits + mm(resid_ref[...], prev_ref[...], TN, HIGH)
    logit_ref[...] = logits
    routes = (route_ref[0:1], route_ref[1:2])
    expert = iota(logits.shape, 0)
    chosen = [
        jnp.sum(jnp.where(expert == route, logits, 0.0), axis=0, keepdims=True) for route in routes
    ]
    gates = pair(chosen[0], chosen[1])
    gate_ref[...] = pad_rows(list(enumerate(gates)), 8, logits.shape[1])
    alphas = [alpha_rows(gate_in, j) for j in range(2)]
    const, on_normed, on_vec = gate_coefs(routes, gates, alphas)
    cols = to_columns([on_normed, on_vec[0], on_vec[1]])
    base_ref[...] = (
        middle
        + cols[:, 0:1] * normed
        + cols[:, 1:2] * vecs[ROW_VEC : ROW_VEC + 1]
        + cols[:, 2:3] * vecs[ROW_VEC + 1 : ROW_VEC + 2]
    )


def middle_part(h, ctx_all, wo_all, vecs, routes_t, prev_t, resid, rank):
    rows, feature_dim = h.shape
    tp_count, packed, lanes = ctx_all.shape
    packed = packed * BLOCK // rows
    row_spec = pl.BlockSpec((TILE, feature_dim), lambda i: (i, 0))
    lane8 = pl.BlockSpec((8, TILE), lambda i: (0, i))
    lane16 = pl.BlockSpec((16, TILE), lambda i: (0, i))
    ins = [rank, h, ctx_all, wo_all, vecs, routes_t]
    in_specs = [
        SMEM_SPEC,
        row_spec,
        pl.BlockSpec((tp_count, packed, lanes), lambda i: (0, i // 2, 0)),
        full_spec(wo_all.shape),
        full_spec(vecs.shape),
        lane8,
    ]
    with_prev = prev_t is not None
    if with_prev:
        ins += [prev_t, resid]
        in_specs += [lane16, full_spec(resid.shape)]
    return pl.pallas_call(
        functools.partial(middle_kernel, with_prev),
        grid=(rows // TILE,),
        out_shape=(
            jax.ShapeDtypeStruct((rows, feature_dim), F32),
            jax.ShapeDtypeStruct((rows, feature_dim), F32),
            jax.ShapeDtypeStruct((rows, feature_dim), BF16),
            jax.ShapeDtypeStruct((8, rows), F32),
            jax.ShapeDtypeStruct((16, rows), F32),
        ),
        in_specs=in_specs,
        out_specs=(row_spec, row_spec, row_spec, lane8, lane16),
        compiler_params=kernel_params(),
        cost_estimate=cost(2 * rows * feature_dim * feature_dim, rows * feature_dim * 16),
        name="middle_part",
    )(*ins)


def split(value):
    high = value.astype(BF16)
    return high, (value - high.astype(F32)).astype(BF16)


def gate_bwd_kernel(with_prev, *refs):
    gh_ref, mid_ref, gxm_ref, vec_ref, route_ref, gate_ref, gg_ref, ctx_ref, wo_ref = refs[:9]
    refs = refs[9:]
    if with_prev:
        prev_ref, resid_ref = refs[:2]
        gmid_ref, gctx_ref, dwo_ref, dvec_ref, gprev_ref, dres_ref = refs[2:]
    else:
        gl_ref = refs[0]
        gmid_ref, gctx_ref, dwo_ref, dvec_ref = refs[1:]
    step = pl.program_id(0)
    grad = gh_ref[...].astype(F32)
    middle = mid_ref[...]
    vecs = vec_ref[...]
    gain = vecs[ROW_GM : ROW_GM + 1]
    scale = lax.rsqrt(jnp.mean(middle * middle, axis=-1, keepdims=True) + EPSILON)
    unit = middle * scale
    normed = unit * gain
    xm_low = normed.astype(BF16)
    low_vecs = vecs[:32].astype(BF16)
    gate_in = mm(low_vecs, xm_low, NT)
    alphas = [alpha_rows(gate_in, j) for j in range(2)]
    routes = (route_ref[0:1], route_ref[1:2])
    gates = (gate_ref[0:1], gate_ref[1:2])
    const, on_normed, on_vec = gate_coefs(routes, gates, alphas)
    grad_hi, grad_lo = split(grad)
    vec_dots = mm(low_vecs[16:32], grad_hi, NT) + mm(low_vecs[16:32], grad_lo, NT)
    dot_vec = [vec_dots[ROW_VEC - 16 + j : ROW_VEC - 15 + j] for j in range(2)]
    dot_col = jnp.sum(grad * normed, axis=-1, keepdims=True)
    dot_normed = jnp.broadcast_to(dot_col, (dot_col.shape[0], 128)).T[0:1]
    term = [alphas[j][0] * dot_normed + alphas[j][1] * dot_vec[j] for j in range(2)]
    gate_grads = []
    for slot in range(2):
        fixed = (
            picks(routes[slot], NF + 1) * dot_normed
            + picks(routes[slot], NF + 2) * term[0]
            + picks(routes[slot], NF + 3) * term[1]
        )
        gate_grads.append(jnp.where(routes[slot] < NF, gg_ref[slot : slot + 1], fixed))
    inner = gates[0] * gate_grads[0] + gates[1] * gate_grads[1]
    chosen_grads = [gates[slot] * (gate_grads[slot] - inner) for slot in range(2)]
    expert = iota((16, TILE), 0)
    grad_logits = jnp.where(expert == routes[0], chosen_grads[0], 0.0) + jnp.where(
        expert == routes[1], chosen_grads[1], 0.0
    )
    if not with_prev:
        grad_logits = grad_logits + gl_ref[...]
    alpha_grads = []
    for j in range(2):
        grad_first = const[j] * dot_normed
        grad_second = const[j] * dot_vec[j]
        mean = alphas[j][0] * grad_first + alphas[j][1] * grad_second
        alpha_grads.append((2 * j, alphas[j][0] * (grad_first - mean)))
        alpha_grads.append((2 * j + 1, alphas[j][1] * (grad_second - mean)))
    grad_in = jnp.concatenate([grad_logits, pad_rows(alpha_grads, 16, TILE)], axis=0)
    in_hi, in_lo = split(grad_in)
    low_gate = jnp.where(iota(low_vecs.shape, 0) < ROW_VEC, low_vecs, 0)
    grad_xm = mm(in_hi, low_gate, TN) + mm(in_lo, low_gate, TN)
    cols = to_columns([on_normed])
    grad_y = cols[:, 0:1] * grad + grad_xm + gxm_ref[...].astype(F32)
    weighted = grad_y * gain
    mean = jnp.mean(weighted * unit, axis=-1, keepdims=True)
    grad_mid = grad + scale * (weighted - unit * mean)
    gmid_ref[...] = grad_mid
    low_mid = grad_mid.astype(BF16)
    gctx_ref[...] = mm(low_mid, wo_ref[...]).astype(BF16)
    dwo = mm(low_mid, unpack_context(ctx_ref[...]), TN)
    vec_rows = pad_rows([(ROW_VEC - 16 + j, on_vec[j]) for j in range(2)], 16, TILE)
    vec_hi, vec_lo = split(vec_rows)
    dvec_low = mm(vec_hi, grad_hi) + mm(vec_lo, grad_hi)
    dvec_gate = mm(in_hi, xm_low) + mm(in_lo, xm_low)
    dgain = jnp.sum(grad_y * unit, axis=0, keepdims=True)
    row_id = iota(dvec_gate.shape, 0)
    dvec = dvec_gate + jnp.concatenate([jnp.zeros_like(dvec_low), dvec_low], axis=0)
    dvec = jnp.where(row_id == ROW_GM, dgain, dvec)

    @pl.when(step == 0)
    def _():
        dwo_ref[...] = dwo
        dvec_ref[...] = dvec

    @pl.when(step > 0)
    def _():
        dwo_ref[...] += dwo
        dvec_ref[...] += dvec

    if with_prev:
        gprev_ref[...] = mm(resid_ref[...], grad_logits, NN, HIGH)
        dres = mm(prev_ref[...], grad_logits, NT, HIGH)

        @pl.when(step == 0)
        def _():
            dres_ref[...] = dres

        @pl.when(step > 0)
        def _():
            dres_ref[...] += dres


def gate_backward(grad, middle, gxm, vecs, routes_t, gates_t, gg_t, context, wo_all, extra):
    rows, feature_dim = middle.shape
    out_cols = wo_all.shape[2]
    with_prev = len(extra) == 2
    row_spec = pl.BlockSpec((TILE, feature_dim), lambda i: (i, 0))
    lane8 = pl.BlockSpec((8, TILE), lambda i: (0, i))
    lane16 = pl.BlockSpec((16, TILE), lambda i: (0, i))
    ctx_spec = pl.BlockSpec((context.shape[0] * BLOCK // rows, 2 * HD), lambda i: (i // 2, 0))
    out_spec = pl.BlockSpec((TILE, out_cols), lambda i: (i, 0))
    wo_spec = pl.BlockSpec((pl.Squeezed(), feature_dim, out_cols), lambda i: (0, 0, 0))
    in_specs = [row_spec, row_spec, row_spec, full_spec(vecs.shape), lane8, lane8, lane8]
    in_specs += [ctx_spec, wo_spec, lane16]
    out_shape = [
        jax.ShapeDtypeStruct((rows, feature_dim), F32),
        jax.ShapeDtypeStruct((rows, out_cols), BF16),
        jax.ShapeDtypeStruct((feature_dim, out_cols), F32),
        jax.ShapeDtypeStruct((32, feature_dim), F32),
    ]
    out_specs = [row_spec, out_spec, full_spec((feature_dim, out_cols)), full_spec((32, feature_dim))]
    if with_prev:
        in_specs.append(full_spec(extra[1].shape))
        out_shape += [jax.ShapeDtypeStruct((16, rows), F32), jax.ShapeDtypeStruct((16, 16), F32)]
        out_specs += [lane16, full_spec((16, 16))]
    return pl.pallas_call(
        functools.partial(gate_bwd_kernel, with_prev),
        grid=(rows // TILE,),
        out_shape=tuple(out_shape),
        in_specs=in_specs,
        out_specs=tuple(out_specs),
        compiler_params=kernel_params(),
        cost_estimate=cost(4 * rows * feature_dim * out_cols, rows * feature_dim * 18),
        name="gate_backward",
    )(grad, middle, gxm, vecs, routes_t, gates_t, gg_t, context, wo_all, *extra)


def qkv_bwd_kernel(gown_ref, goth_ref, h_ref, vec_ref, w_ref, part_ref, dw_ref):
    step = pl.program_id(0)
    cols = gown_ref.shape[1]
    grad = (gown_ref[...] + goth_ref[:, :cols].astype(F32)).astype(BF16)
    part_ref[...] = mm(grad, w_ref[:, :cols], NT).astype(BF16)
    hidden = h_ref[...].astype(F32)
    gain = vec_ref[ROW_GA : ROW_GA + 1, :]
    scale = lax.rsqrt(jnp.mean(hidden * hidden, axis=-1, keepdims=True) + EPSILON)
    attn_in = (hidden * scale * gain).astype(BF16)
    dw = mm(attn_in, grad, TN)

    @pl.when(step == 0)
    def _():
        dw_ref[...] = dw

    @pl.when(step > 0)
    def _():
        dw_ref[...] += dw


def qkv_backward(gown, goth, h, vecs, w_qkv):
    rows, feature_dim = h.shape
    cols = gown.shape[1]
    row_spec = pl.BlockSpec((TILE, feature_dim), lambda i: (i, 0))
    col_spec = pl.BlockSpec((TILE, cols), lambda i: (i, 0))
    oth_spec = pl.BlockSpec((TILE, goth.shape[1]), lambda i: (i, 0))
    return pl.pallas_call(
        qkv_bwd_kernel,
        grid=(rows // TILE,),
        out_shape=(
            jax.ShapeDtypeStruct((rows, feature_dim), BF16),
            jax.ShapeDtypeStruct((feature_dim, cols), F32),
        ),
        in_specs=[col_spec, oth_spec, row_spec, full_spec(vecs.shape), full_spec(w_qkv.shape)],
        out_specs=(row_spec, full_spec((feature_dim, cols))),
        compiler_params=kernel_params(),
        cost_estimate=cost(4 * rows * feature_dim * cols, rows * feature_dim * 10),
        name="qkv_backward",
    )(gown, goth, h, vecs, w_qkv)


def norm_bwd_kernel(with_low, gmid_ref, ga_ref, h_ref, vec_ref, out_ref, *rest):
    step = pl.program_id(0)
    hidden = h_ref[...].astype(F32)
    gain = vec_ref[ROW_GA : ROW_GA + 1, :]
    scale = lax.rsqrt(jnp.mean(hidden * hidden, axis=-1, keepdims=True) + EPSILON)
    unit = hidden * scale
    grad_y = ga_ref[...].astype(F32)
    weighted = grad_y * gain
    mean = jnp.mean(weighted * unit, axis=-1, keepdims=True)
    grad = gmid_ref[...] + scale * (weighted - unit * mean)
    out_ref[...] = grad
    if with_low:
        rest[0][...] = grad.astype(BF16)
    dgain_ref = rest[-1]
    dgain = jnp.broadcast_to(jnp.sum(grad_y * unit, axis=0, keepdims=True), dgain_ref.shape)

    @pl.when(step == 0)
    def _():
        dgain_ref[...] = dgain

    @pl.when(step > 0)
    def _():
        dgain_ref[...] += dgain


def norm_backward(gmid, ga, h, vecs, with_low):
    rows, feature_dim = gmid.shape
    row_spec = pl.BlockSpec((TILE, feature_dim), lambda i: (i, 0))
    out_shape = [jax.ShapeDtypeStruct((rows, feature_dim), F32)]
    out_specs = [row_spec]
    if with_low:
        out_shape.append(jax.ShapeDtypeStruct((rows, feature_dim), BF16))
        out_specs.append(row_spec)
    out_shape.append(jax.ShapeDtypeStruct((8, feature_dim), F32))
    out_specs.append(full_spec((8, feature_dim)))
    return pl.pallas_call(
        functools.partial(norm_bwd_kernel, with_low),
        grid=(rows // TILE,),
        out_shape=tuple(out_shape),
        in_specs=[row_spec, row_spec, row_spec, full_spec(vecs.shape)],
        out_specs=tuple(out_specs),
        compiler_params=kernel_params(),
        cost_estimate=cost(rows * feature_dim * 10, rows * feature_dim * 16),
        name="norm_backward",
    )(gmid, ga, h, vecs)


def experts_kernel(fwd, bwd, blocks, plan, out_count, rows, offs_ref, *refs):
    refs = list(refs)
    xm_ref = refs.pop(0)
    gh_ref = refs.pop(0) if bwd else None
    route_ref, gate_ref = refs.pop(0), refs.pop(0)
    w_refs = [refs.pop(0) for _ in plan]
    ffn_ref = refs.pop(0) if fwd else None
    if bwd:
        gx_ref = refs.pop(0)
        dw_refs = [refs.pop(0) for _ in range(out_count)]
    w_scr, place_scr, pick_scr = refs.pop(0), refs.pop(0), refs.pop(0)
    acc_ref = refs.pop(0) if fwd else None
    if bwd:
        gacc_ref, raw_scr, gg_scr, dw_scr = refs
    expert = pl.program_id(0)
    last = pl.num_programs(0) - 1
    width = w_scr.shape[1]
    units = width // 3

    @pl.when(expert == 0)
    def _():
        order = (iota((BLOCK, BLOCK), 0) < iota((BLOCK, BLOCK), 1)).astype(BF16)
        for block in range(blocks):
            lanes = slice(block * BLOCK, (block + 1) * BLOCK)
            ids = iota((8, BLOCK), 0)
            hits = (ids == route_ref[0:1, lanes]) | (ids == route_ref[1:2, lanes])
            earlier = mm(hits.astype(BF16), order)
            place_scr[block] = jnp.where(hits, earlier, -1.0)
        if fwd:
            acc_ref[...] = jnp.zeros_like(acc_ref)
        if bwd:
            gacc_ref[...] = jnp.zeros_like(gacc_ref)
            gg_scr[...] = jnp.zeros_like(gg_scr)

    def fill(ref, off):
        start = pl.multiple_of(offs_ref[off] * rows, rows)
        w_scr[pl.ds(start, rows), :] = ref[0]

    for ref, (off, first, number) in zip(w_refs, plan):
        if number == NF:
            fill(ref, off)
        else:
            pl.when((expert >= first) & (expert < first + number))(
                functools.partial(fill, ref, off)
            )

    hot, gate_cols, masks = [], [], []
    for block in range(blocks):
        lanes = slice(block * BLOCK, (block + 1) * BLOCK)
        place = place_scr[block, pl.ds(expert, 1), :]
        one_hot = (iota((CAP, BLOCK), 0).astype(F32) == place).astype(F32)
        mask = [route_ref[slot : slot + 1, lanes] == expert for slot in range(2)]
        gate_row = jnp.where(mask[0], gate_ref[0:1, lanes], 0.0) + jnp.where(
            mask[1], gate_ref[1:2, lanes], 0.0
        )
        gate_cols.append(jnp.sum(one_hot * gate_row, axis=1, keepdims=True))
        one_hot = one_hot.astype(BF16)
        pick_scr[block * CAP : (block + 1) * CAP, :] = mm(one_hot, xm_ref[lanes, :]).astype(BF16)
        if bwd:
            raw_scr[block * CAP : (block + 1) * CAP, :] = mm(one_hot, gh_ref[lanes, :]).astype(BF16)
        hot.append(one_hot)
        masks.append(mask)
    gate_col = jnp.concatenate(gate_cols, axis=0)
    picked = pick_scr[...]
    gate_up = mm(picked, w_scr[:, : 2 * units])
    gate_in, up_in = gate_up[:, :units], gate_up[:, units:]
    sigmoid = lax.logistic(gate_in)
    silu = gate_in * sigmoid
    hidden = (silu * up_in).astype(BF16)
    if fwd:
        scaled = (mm(hidden, w_scr[:, 2 * units :], NT) * gate_col).astype(BF16)
        for block in range(blocks):
            acc_ref[block * BLOCK : (block + 1) * BLOCK, :] += mm(
                hot[block], scaled[block * CAP : (block + 1) * CAP], TN
            )

        @pl.when(expert == last)
        def _():
            if bwd:
                late_rows = ffn_ref.shape[0]
                ffn_ref[...] = acc_ref[acc_ref.shape[0] - late_rows :, :].astype(BF16)
                rest = acc_ref.shape[0] - late_rows
                gx_ref[gx_ref.shape[0] - rest :, :] = acc_ref[:rest, :].astype(BF16)
            else:
                ffn_ref[...] = acc_ref[...].astype(BF16)

    if bwd:
        raw = raw_scr[...]
        grad_raw = mm(raw, w_scr[:, 2 * units :])
        gate_dot = jnp.sum(hidden.astype(F32) * grad_raw, axis=1, keepdims=True)
        for block in range(blocks):
            row = jnp.sum(
                hot[block].astype(F32) * gate_dot[block * CAP : (block + 1) * CAP],
                axis=0,
                keepdims=True,
            )
            for slot in range(2):
                gg_scr[8 * block + slot : 8 * block + slot + 1, :] += jnp.where(
                    masks[block][slot], row, 0.0
                )
        grad_hidden = grad_raw * gate_col
        grad_gate = grad_hidden * up_in * sigmoid * (1.0 + gate_in * (1.0 - sigmoid))
        grad_up = grad_hidden * silu
        grad_gu = jnp.concatenate([grad_gate.astype(BF16), grad_up.astype(BF16)], axis=1)
        grad_pick = mm(grad_gu, w_scr[:, : 2 * units], NT).astype(BF16)
        for block in range(blocks):
            gacc_ref[block * BLOCK : (block + 1) * BLOCK, :] += mm(
                hot[block], grad_pick[block * CAP : (block + 1) * CAP], TN
            )
        grad_result = (raw.astype(F32) * gate_col).astype(BF16)
        if out_count == 1:
            dw_refs[0][0, :, : 2 * units] = mm(picked, grad_gu, TN).astype(BF16)
            dw_refs[0][0, :, 2 * units :] = mm(grad_result, hidden, TN).astype(BF16)
        else:
            dw_scr[:, : 2 * units] = mm(picked, grad_gu, TN).astype(BF16)
            dw_scr[:, 2 * units :] = mm(grad_result, hidden, TN).astype(BF16)
            half = NF // 2
            for part in range(2):

                @pl.when((expert >= part * half) & (expert < (part + 1) * half))
                def _(part=part):
                    for off in range(8):
                        start = pl.multiple_of(offs_ref[off] * rows, rows)
                        dw_refs[2 * part + off % 2][off // 2, 0] = dw_scr[pl.ds(start, rows), :]

        @pl.when(expert == last)
        def _():
            total = blocks * BLOCK
            gx_ref[:total, :] = gacc_ref[...].astype(BF16)
            gx_ref[total : total + 16, :] = jnp.zeros((16, gx_ref.shape[1]), BF16)
            gx_ref[total : total + gg_scr.shape[0], :BLOCK] = gg_scr[...].astype(BF16)


def experts(fwd, bwd, xm, gh, routes_t, gates_t, pieces, offs):
    rows, feature_dim = xm.shape
    blocks = rows // BLOCK
    arrays = [item[0] for item in pieces]
    plan = [item[1:] for item in pieces]
    _, piece_rows, width = arrays[0].shape
    units = width // 3
    split_out = len(pieces) > 1
    half = NF // 2

    ins = [xm] + ([gh] if bwd else []) + [routes_t, gates_t]
    in_specs = [SMEM_SPEC] + [full_spec(item.shape) for item in ins]
    for _, first, number in plan:
        in_specs.append(
            pl.BlockSpec(
                (1, piece_rows, width),
                lambda e, first=first, number=number: (jnp.clip(e - first, 0, number - 1), 0, 0),
            )
        )
    out_shape, out_specs, scratch = [], [], []
    scratch += [
        pltpu.VMEM((feature_dim, width), BF16),
        pltpu.VMEM((blocks, 8, BLOCK), F32),
        pltpu.VMEM((blocks * CAP, feature_dim), BF16),
    ]
    flops = 0
    out_count = 4 if split_out else 1
    if fwd:
        ffn_rows = LATE if bwd else rows
        out_shape.append(jax.ShapeDtypeStruct((ffn_rows, feature_dim), BF16))
        out_specs.append(full_spec((ffn_rows, feature_dim)))
        scratch.append(pltpu.VMEM((rows, feature_dim), F32))
        flops += 1.0e9 * NF * blocks / 2
    if bwd:
        gx_rows = rows + 16 + (rows - LATE if fwd else 0)
        out_shape.append(jax.ShapeDtypeStruct((gx_rows, feature_dim), BF16))
        out_specs.append(full_spec((gx_rows, feature_dim)))
        if split_out:
            for part in range(2):
                for _ in range(2):
                    out_shape.append(jax.ShapeDtypeStruct((4, half, piece_rows, width), BF16))
                    out_specs.append(
                        pl.BlockSpec(
                            (4, 1, piece_rows, width),
                            lambda e, part=part: (0, jnp.clip(e - part * half, 0, half - 1), 0, 0),
                        )
                    )
        else:
            out_shape.append(jax.ShapeDtypeStruct((NF, feature_dim, width), BF16))
            out_specs.append(pl.BlockSpec((1, feature_dim, width), lambda e: (e, 0, 0)))
        scratch += [
            pltpu.VMEM((rows, feature_dim), F32),
            pltpu.VMEM((blocks * CAP, feature_dim), BF16),
            pltpu.VMEM((blocks * 8, BLOCK), F32),
            pltpu.VMEM((feature_dim, width) if split_out else (8, 128), BF16),
        ]
        flops += 2.2e9 * NF * blocks / 2
    outs = pl.pallas_call(
        functools.partial(experts_kernel, fwd, bwd, blocks, plan, out_count, piece_rows),
        grid=(NF,),
        out_shape=tuple(out_shape),
        in_specs=in_specs,
        out_specs=tuple(out_specs),
        scratch_shapes=scratch,
        compiler_params=kernel_params(),
        cost_estimate=cost(flops, 20e6 * (2 if bwd else 1), rows * units * 8),
        name="experts",
    )(offs, *ins, *arrays)
    outs = list(outs)
    ffn = outs.pop(0) if fwd else None
    return (ffn, outs[0], outs[1:]) if bwd else (ffn, None, None)


def final_kernel(with_old, count, *refs):
    parts = refs[:count]
    gu_ref, dn_ref = refs[-2:]
    del with_old
    half = count // 2
    units = gu_ref.shape[-1]

    def write(group):
        total = group[0][...].reshape(group[0].shape[-2:]).astype(F32)
        for ref in group[1:]:
            total += ref[...].reshape(ref.shape[-2:]).astype(F32)
        gu_ref[0, 0, :, 0, :] = total[:, :units]
        gu_ref[0, 0, :, 1, :] = total[:, units : 2 * units]
        dn_ref[0, 0] = total[:, 2 * units :]

    @pl.when(pl.program_id(0) < NF // 2)
    def _():
        write(parts[:half])

    @pl.when(pl.program_id(0) >= NF // 2)
    def _():
        write(parts[half:])


def final_sums(lows, highs, old, layer, layer_count):
    half = NF // 2
    specs, arrays = [], []
    for part, group in enumerate((lows, highs)):
        for item in group:
            lead = (1,) * (item.ndim - 3)
            specs.append(
                pl.BlockSpec(
                    lead + (1,) + item.shape[-2:],
                    lambda e, part=part, lead=lead: (0,) * len(lead)
                    + (jnp.clip(e - part * half, 0, half - 1), 0, 0),
                )
            )
            arrays.append(item)
    count = len(arrays)
    rows, width = arrays[0].shape[-2:]
    units = width // 3
    aliases = {}
    if old is not None:
        specs += [pl.BlockSpec(memory_space=pl.ANY)] * 2
        arrays += list(old)
        aliases = {count: 0, count + 1: 1}
    return pl.pallas_call(
        functools.partial(final_kernel, old is not None, count),
        grid=(NF,),
        out_shape=(
            jax.ShapeDtypeStruct((layer_count, NF, rows, 2, units), F32),
            jax.ShapeDtypeStruct((layer_count, NF, rows, units), F32),
        ),
        in_specs=specs,
        out_specs=(
            pl.BlockSpec((1, 1, rows, 2, units), lambda e: (layer, e, 0, 0, 0)),
            pl.BlockSpec((1, 1, rows, units), lambda e: (layer, e, 0, 0)),
        ),
        input_output_aliases=aliases,
        compiler_params=kernel_params(),
        cost_estimate=cost(1e7, NF * rows * width * 12),
        name="final_sums",
    )(*arrays)


def hop(value, step):
    return lax.ppermute(value, "fsdp", [(i, i ^ step) for i in range(4)])


def swap(value):
    return lax.ppermute(value, "ctx", [(0, 1), (1, 0)])


def gather_small(value):
    by_x, by_y, by_d = hop(value, 1), hop(value, 2), hop(value, 3)
    out = []
    for item in (value, by_x, by_y, by_d):
        out += [item, swap(item)]
    return out


def gather_rest(own, x_high, y_low):
    low, high = own
    x_low, y_high = hop(low, 1), hop(high, 2)
    d_low, d_high = hop(y_low, 1), hop(x_high, 2)
    return (low, x_low, y_low, d_low), (high, x_high, y_high, d_high)


def gather_cores(lows, highs):
    half = NF // 2
    out = []
    for first, items in ((0, lows), (half, highs)):
        for chip, item in enumerate(items):
            out += [(item, 2 * chip, first, half), (swap(item), 2 * chip + 1, first, half)]
    return out


def tie(*values):
    return lax.optimization_barrier(values)


def add_low(*terms):
    total = terms[0].astype(F32)
    for term in terms[1:]:
        total = total + term.astype(F32)
    return total.astype(BF16)


def scatter_cores(keep, send, first):
    other = swap(send)
    if first == 1:
        out = add_low(keep[1::2], other[1::2])
    else:
        out = add_low(keep[2:], other[2:])
    return keep, other, out


def scatter_first(keep, other, out, first):
    got = hop(out, first)
    return keep[:1], other[:1], got[:1], add_low(keep[3 - first], other[3 - first], got[1])


def scatter_second(terms, first):
    return terms[:3] + (hop(terms[3], 3 - first),)


def per_device(
    hyper,
    axes,
    tokens,
    cotangent,
    lengths,
    routes,
    norm_attn,
    w_qkv,
    w_out,
    norm_moe,
    w_router,
    w_resid,
    w_const,
    v_const,
    w_gate_up,
    w_down,
):
    micro_count, seq_count, block_len, feature_dim = tokens.shape
    rows = micro_count * seq_count * block_len
    layer_count, shard_rows, qkv_cols = w_qkv.shape
    heads = qkv_cols // (3 * HD)
    units = w_gate_up.shape[-1]
    groups = ("fsdp", "ctx")
    shard_count = feature_dim // shard_rows
    ctx = lax.axis_index("ctx")
    me = lax.axis_index("fsdp") * axes["ctx"] + ctx
    rank = lax.axis_index("tp").reshape(1)
    if hyper:
        offs = me ^ jnp.arange(shard_count, dtype=jnp.int32)
    else:
        offs = jnp.zeros((1,), jnp.int32)
    info = jnp.concatenate([ctx.reshape(1), lengths.reshape(-1)]).astype(jnp.int32)
    resid = jnp.zeros((16, 16), F32).at[:NE, :NE].set(w_resid.astype(F32))

    small, wide = [], []
    for layer in range(layer_count):
        vec = jnp.concatenate(
            [
                w_router[layer],
                jnp.zeros((shard_rows, ROW_CONST - NE), BF16),
                w_const[layer, 0],
                w_const[layer, 1],
                v_const[layer].T,
                norm_attn[layer][:, None],
                norm_moe[layer][:, None],
                jnp.zeros((shard_rows, PACK - ROW_GM - 1), BF16),
            ],
            axis=1,
        )
        pad = jnp.zeros((shard_rows, round_up(qkv_cols, 128) - qkv_cols), BF16)
        small.append(jnp.concatenate([w_qkv[layer], pad, vec], axis=1))
        wide.append(pack_wide(w_gate_up, jnp.swapaxes(w_down, 2, 3), layer))
    tp_count = axes["tp"]
    outer = jnp.transpose(w_out, (0, 2, 1))
    outer = [outer] + [
        lax.ppermute(outer, "tp", [(i, (i + k) % tp_count) for i in range(tp_count)])
        for k in range(1, tp_count)
    ]
    small = [
        jnp.concatenate([small[layer]] + [item[layer] for item in outer], axis=1)
        for layer in range(layer_count)
    ]

    weights, wide_first = [None] * layer_count, [None] * layer_count

    def fetch_small(layer, after):
        own = small[layer]
        if hyper:
            own, _ = tie(own, after)
            pieces = gather_small(own)
            first = [pieces[k] for k in (2, 4, 6)]
            if layer == 0:
                fetch_first(0, info)
                pieces, wide_first[0] = tie(pieces, wide_first[0])
            else:
                fetch_first(layer, first)
        else:
            pieces = [lax.all_gather(own, groups, axis=0, tiled=True)]
        weights[layer] = list(prep_weights(pieces, offs, feature_dim, qkv_cols, tp_count))

    def fetch_first(layer, after):
        own, _ = tie(wide[layer], after)
        wide_first[layer] = (own, hop(own[1], 1), hop(own[0], 2))

    def fetch_rest(layer, value):
        if hyper:
            own, x_high, y_low = wide_first[layer]
            value, own, x_high, y_low = tie(value, own, x_high, y_low)
            rests[layer] = gather_rest(own, x_high, y_low)
        return value

    def fetch_cores(layer, after):
        if hyper:
            lows, highs = rests[layer]
            early = (lows[0], lows[2], highs[0], highs[1])
            early, _ = tie(early, after)
            lows = (early[0], lows[1], early[1], lows[3])
            highs = (early[2], early[3], highs[2], highs[3])
            ends[layer] = (lows[1], lows[3], highs[2], highs[3])
            weights[layer].append(gather_cores(lows, highs))
        else:
            both = jnp.concatenate(wide[layer], axis=0)
            full = lax.all_gather(both, groups, axis=1, tiled=True)
            weights[layer].append([(full, 0, 0, NF)])

    ends, rests = [None] * layer_count, [None] * layer_count
    fetch_small(0, info)

    routes_t = jnp.moveaxis(routes.reshape(layer_count, rows, 2), 2, 1)
    routes_t = jnp.concatenate(
        [routes_t, jnp.full((layer_count, 6, rows), -1, jnp.int32)], axis=1
    )
    position = ctx * block_len + jnp.arange(block_len, dtype=jnp.int32)
    valid = position[None, None, :] < lengths[:, :, None]
    cot = jnp.where(valid[..., None], cotangent, 0).reshape(rows, feature_dim)

    base, ffn, prev_t = tokens.reshape(rows, feature_dim), None, None
    saved = []
    for layer in range(layer_count):
        qkv_full, wo_all, vecs = weights[layer][:3]
        outs = qkv_part(base, ffn, vecs, qkv_full)
        h_in, qkv = outs if ffn is not None else (base, outs[0])
        other = fetch_rest(layer, swap(qkv))
        context, lse = attend_forward(qkv, other, info, heads)
        ctx_all = lax.all_gather(context, "tp", axis=0)
        fetch_cores(layer, context)
        pieces = weights[layer][3]
        middle, base, xm_low, gates_t, logits_t = middle_part(
            h_in, ctx_all, wo_all, vecs, routes_t[layer], prev_t, resid, rank
        )
        saved.append((h_in, qkv, other, context, lse, middle, xm_low, gates_t, prev_t))
        prev_t = logits_t
        if layer < layer_count - 1:
            fetch_small(layer + 1, ends[layer] if hyper else ctx_all)
            part, _, _ = experts(True, False, xm_low, None, routes_t[layer], gates_t, pieces, offs)
            ffn = lax.psum(part, "tp")
            if hyper:
                ffn, wide_first[layer + 1] = tie(ffn, wide_first[layer + 1])

    grad, grad_low = cot, cot
    upper_gain = None
    grad_logits, wide_out, pending, small_terms, late = None, None, None, None, None
    finals = [None] * layer_count
    for layer in reversed(range(layer_count)):
        qkv_full, wo_all, vecs, pieces = weights[layer]
        h_in, qkv, other, context, lse, middle, xm_low, gates_t, prev_t = saved[layer]
        top = layer == layer_count - 1
        part, gx, grads = experts(
            top, True, xm_low, grad_low, routes_t[layer], gates_t, pieces, offs
        )
        if not top and late is not None:
            late = lax.psum(late, "tp")
            gx, grads, late, pending = tie(gx, grads, late, pending)
            mixed = (base_top + jnp.concatenate([early, late], axis=0).astype(F32)).astype(BF16)
        gx = lax.psum(gx, "tp")
        if hyper:
            sums = [scatter_cores(grads[2 * k], grads[2 * k + 1], k + 1) for k in range(2)]
            if pending is not None:
                wide_terms, small_sums, dres = pending
                terms = [scatter_second(wide_terms[k], k + 1) for k in range(2)]
                wide_out = final_sums(terms[0], terms[1], wide_out, layer + 1, layer_count)
                small_terms = scatter_first(*small_sums, 1)
                gx, sums, wide_out, small_terms = tie(gx, sums, wide_out, small_terms)
            else:
                gx, sums = tie(gx, sums)
            grads = [scatter_first(*sums[k], k + 1) for k in range(2)]
        if top:
            base_top, early = base, gx[rows + 16 :]
        gg_t = gx[rows : rows + 16, :block_len].astype(F32)
        gg_t = jnp.moveaxis(gg_t.reshape(2, 8, block_len)[: rows // BLOCK], 0, 1).reshape(8, rows)
        extra = (prev_t, resid) if prev_t is not None else (grad_logits,)
        outs = gate_backward(
            grad, middle, gx, vecs, routes_t[layer], gates_t, gg_t, context, wo_all, extra
        )
        gmid, gctx, dwo, dvec = outs[:4]
        if prev_t is not None:
            grad_logits, dres = outs[4:]
        gown, goth = attend_backward(qkv, other, lse, gctx, info, heads)
        goth = swap(goth)
        if hyper and layer == 0:
            goth, grads = tie(goth, grads)
        ga_part, dqkv = qkv_backward(gown, goth, h_in, vecs, qkv_full)
        if upper_gain is not None:
            dvec = dvec.at[ROW_UP].set(upper_gain)
        packed = pack_grads(dqkv, dwo, dvec, offs)
        ga = lax.psum(ga_part, "tp")
        own = None
        if hyper:
            small_sums = scatter_cores(*packed, 1)
            if layer > 0:
                dres = dres + swap(dres)
                dres = dres + hop(dres, 1)
                ga, grads, small_sums, dres = tie(ga, grads, small_sums, dres)
                dres = dres + hop(dres, 2)
                pending = (grads, small_sums, dres)
            else:
                small_terms = scatter_second(small_terms, 1)
                ga, small_terms = tie(ga, small_terms)
                terms = [scatter_second(grads[k], k + 1) for k in range(2)]
                wide_out = final_sums(terms[0], terms[1], wide_out, layer, layer_count)
                own = scatter_second(scatter_first(*small_sums, 1), 1)
        if top:
            late, ga = tie(part, ga)
        outs = norm_backward(gmid, ga, h_in, vecs, layer > 0)
        grad, dgain = outs[0], outs[-1]
        upper_gain = dgain[0]
        grad_low = outs[1]
        finals[layer] = (grads, packed, own if hyper else None, dgain)

    gain_first = finals[0][3][:1]
    if hyper:
        gain_first = gain_first + swap(gain_first)
        gain_first = (
            gain_first + hop(gain_first, 1) + (hop(gain_first, 2) + hop(gain_first, 3))
        )
        resid_total = dres[:NE, :NE]
    else:
        gain_first = lax.psum(gain_first, groups)
        resid_total = lax.psum(dres, groups)[:NE, :NE]
    gain_first = lax.dynamic_slice(gain_first[0], (me * shard_rows,), (shard_rows,))
    results = [None] * layer_count
    for layer in reversed(range(layer_count)):
        grads, packed, own, _ = finals[layer]
        if hyper:
            own = own if layer == 0 else small_terms
            own = sum(term.reshape(shard_rows, -1).astype(F32) for term in own)
        else:
            own = lax.psum_scatter(packed[0], groups, scatter_dimension=0, tiled=True).astype(F32)
            wide_own = lax.psum_scatter(
                grads[0], groups, scatter_dimension=1, tiled=True
            ).astype(F32)
            here = (
                wide_own[:, :, : 2 * units].reshape(NF, shard_rows, 2, units),
                wide_own[:, :, 2 * units :],
            )
            if wide_out is None:
                wide_out = ([], [])
            wide_out[0].insert(0, here[0])
            wide_out[1].insert(0, here[1])
        out_cols = heads * HD
        vec = own[:, qkv_cols + out_cols :]
        results[layer] = (
            own[:, :qkv_cols],
            own[:, qkv_cols : qkv_cols + out_cols].T,
            vec[:, ROW_GM],
            vec[:, :NE],
            jnp.stack([vec[:, ROW_CONST : ROW_CONST + 2], vec[:, ROW_CONST + 2 : ROW_CONST + 4]]),
            vec[:, ROW_VEC : ROW_VEC + 2].T,
            vec[:, ROW_UP],
        )
    if not hyper:
        wide_out = (jnp.stack(wide_out[0]), jnp.stack(wide_out[1]))
    stacked = [jnp.stack([item[member] for item in results]) for member in range(6)]
    return (
        mixed.reshape(tokens.shape),
        grad.reshape(tokens.shape),
        jnp.stack([gain_first] + [item[6] for item in results[: layer_count - 1]]),
        stacked[0],
        stacked[1],
        stacked[2],
        stacked[3],
        resid_total,
        stacked[4],
        stacked[5],
        wide_out[0],
        jnp.swapaxes(wide_out[1], 2, 3),
    )


def solution(mesh):
    axes = dict(mesh.shape)
    hyper = axes["fsdp"] == 4 and axes["ctx"] == 2
    in_specs = (
        P(None, "fsdp", "ctx", None),
        P(None, "fsdp", "ctx", None),
        P(None, "fsdp"),
        P(None, None, "fsdp", "ctx", None),
        P(None, ("fsdp", "ctx")),
        P(None, ("fsdp", "ctx"), "tp"),
        P(None, "tp", ("fsdp", "ctx")),
        P(None, ("fsdp", "ctx")),
        P(None, ("fsdp", "ctx"), None),
        P(),
        P(None, None, ("fsdp", "ctx"), None),
        P(None, None, ("fsdp", "ctx")),
        P(None, None, ("fsdp", "ctx"), None, "tp"),
        P(None, None, "tp", ("fsdp", "ctx")),
    )
    out_specs = (
        P(None, "fsdp", "ctx", None),
        P(None, "fsdp", "ctx", None),
        P(None, ("fsdp", "ctx")),
        P(None, ("fsdp", "ctx"), "tp"),
        P(None, "tp", ("fsdp", "ctx")),
        P(None, ("fsdp", "ctx")),
        P(None, ("fsdp", "ctx"), None),
        P(),
        P(None, None, ("fsdp", "ctx"), None),
        P(None, None, ("fsdp", "ctx")),
        P(None, None, ("fsdp", "ctx"), None, "tp"),
        P(None, None, "tp", ("fsdp", "ctx")),
    )
    return jax.shard_map(
        functools.partial(per_device, hyper, axes),
        mesh=mesh,
        in_specs=in_specs,
        out_specs=out_specs,
        check_vma=False,
    )
```

```python
import functools

import jax
import jax.numpy as jnp
from jax import lax
from jax.experimental import pallas as pl
from jax.experimental.pallas import tpu as pltpu
from jax.sharding import PartitionSpec as P

HD = 64
NF = 8
NE = 12
BLOCK = 512
CAP = 128
TILE = 256
EPSILON = 1e-06
MASKED = -1e30
F32 = jnp.float32
BF16 = jnp.bfloat16
HIGH = lax.Precision.HIGHEST
ROW_CONST, ROW_VEC, ROW_GA, ROW_GM = 16, 20, 22, 23
VMEM_LIMIT = 58 * 1024 * 1024
SCALE = 0.05
PACK = 128

NN = (((1,), (0,)), ((), ()))
NT = (((1,), (1,)), ((), ()))
TN = (((0,), (0,)), ((), ()))


def mm(left, right, dims=NN, precision=None):
    return lax.dot_general(left, right, dims, precision=precision, preferred_element_type=F32)


def kernel_params():
    return pltpu.CompilerParams(vmem_limit_bytes=VMEM_LIMIT)


def cost(flops, nbytes, trans=0):
    return pl.CostEstimate(
        flops=int(flops * SCALE), bytes_accessed=int(nbytes * SCALE), transcendentals=int(trans * SCALE)
    )


def iota(shape, dim):
    return lax.broadcasted_iota(jnp.int32, shape, dim)


def full_spec(shape):
    zeros = (0,) * len(shape)
    return pl.BlockSpec(shape, lambda *idx: zeros)


SMEM_SPEC = pl.BlockSpec(memory_space=pltpu.SMEM)


def pad_rows(rows, count, width):
    row_id = iota((count, width), 0)
    out = jnp.zeros((count, width), F32)
    for place, row in rows:
        out = jnp.where(row_id == place, row, out)
    return out


def round_up(value, unit):
    return -(-value // unit) * unit


def prep_kernel(count, rows, out_cols, offs_ref, *refs):
    qkv_ref, vec_ref, wo_refs = refs[count], refs[count + 1], refs[count + 2 : -2]
    scr_ref, wo_scr = refs[-2:]
    cols = qkv_ref.shape[1]
    for piece in range(count):
        start = pl.multiple_of(offs_ref[piece] * rows, rows)
        block = refs[piece][...]
        qkv_ref[pl.ds(start, rows), :] = block[:, :cols]
        scr_ref[pl.ds(start, rows), :] = block[:, cols : cols + PACK].astype(F32)
        for rank in range(len(wo_refs)):
            first = cols + PACK + rank * out_cols
            wo_scr[rank, pl.ds(start, rows), :out_cols] = block[:, first : first + out_cols]
    vec_ref[...] = scr_ref[...].T[:32]
    total = wo_scr.shape[1]
    rest = out_cols - 128
    for rank, ref in enumerate(wo_refs):
        ref[:total, :] = wo_scr[rank, :, :128]
        ref[total:, :rest] = wo_scr[rank, : total // 2, 128:out_cols]
        ref[total:, rest:] = wo_scr[rank, total // 2 :, 128:out_cols]


def prep_weights(pieces, offs, feature_dim, qkv_cols, out_cols, out_count):
    count = len(pieces)
    cols = round_up(qkv_cols, 128)
    vmem = pl.BlockSpec(memory_space=pltpu.VMEM)
    outs = pl.pallas_call(
        functools.partial(prep_kernel, count, feature_dim // count, out_cols),
        out_shape=tuple(
            [
                jax.ShapeDtypeStruct((feature_dim, cols), BF16),
                jax.ShapeDtypeStruct((32, feature_dim), F32),
            ]
            + [jax.ShapeDtypeStruct((feature_dim * 3 // 2, 128), BF16)] * out_count
        ),
        in_specs=[SMEM_SPEC] + [vmem] * count,
        out_specs=tuple([vmem] * (2 + out_count)),
        scratch_shapes=[
            pltpu.VMEM((feature_dim, PACK), F32),
            pltpu.VMEM((out_count, feature_dim, 256), BF16),
        ],
        compiler_params=kernel_params(),
        cost_estimate=cost(1e6, 3e6),
        name="prep",
    )(offs, *pieces)
    return outs[0], outs[1], list(outs[2:])


def pack_kernel(count, rows, offs_ref, dqkv_ref, dwo_ref, dvec_ref, dgain_ref, *refs):
    outs, scr_ref = refs[:-1], refs[-1]
    cols, out_cols = dqkv_ref.shape[1], dwo_ref.shape[1]
    scr_ref[:, :cols] = dqkv_ref[...]
    scr_ref[:, cols : cols + out_cols] = dwo_ref[...]
    vec = dvec_ref[...]
    vec = jnp.where(iota(vec.shape, 0) == ROW_GA, dgain_ref[0:1, :], vec)
    wide = jnp.concatenate([vec, jnp.zeros((PACK - vec.shape[0], vec.shape[1]), F32)], axis=0).T
    scr_ref[:, cols + out_cols :] = wide
    for piece in range(count):
        start = pl.multiple_of(offs_ref[piece] * rows, rows)
        block = scr_ref[pl.ds(start, rows), :].astype(BF16)
        if count > 1:
            outs[piece % 2][piece // 2] = block
        else:
            outs[0][...] = block


def pack_grads(dqkv, dwo, dvec, dgain, offs):
    feature_dim = dqkv.shape[0]
    count = offs.shape[0]
    rows = feature_dim // count
    width = dqkv.shape[1] + dwo.shape[1] + PACK
    shape = (count // 2, rows, width) if count > 1 else (feature_dim, width)
    vmem = pl.BlockSpec(memory_space=pltpu.VMEM)
    outs = 2 if count > 1 else 1
    return pl.pallas_call(
        functools.partial(pack_kernel, count, rows),
        out_shape=tuple([jax.ShapeDtypeStruct(shape, BF16)] * outs),
        in_specs=[SMEM_SPEC, vmem, vmem, vmem, vmem],
        out_specs=tuple([vmem] * outs),
        scratch_shapes=[pltpu.VMEM((feature_dim, width), F32)],
        compiler_params=kernel_params(),
        cost_estimate=cost(1e6, 6e6),
        name="pack_grads",
    )(offs, dqkv, dwo, dvec, dgain)


def pack_wide_kernel(gu_ref, down_ref, low_ref, high_ref):
    units = down_ref.shape[-1]

    def write(ref):
        ref[0, :, :units] = gu_ref[0, 0, :, 0, :]
        ref[0, :, units : 2 * units] = gu_ref[0, 0, :, 1, :]
        ref[0, :, 2 * units :] = down_ref[0, 0]

    @pl.when(pl.program_id(0) < NF // 2)
    def _():
        write(low_ref)

    @pl.when(pl.program_id(0) >= NF // 2)
    def _():
        write(high_ref)


def pack_wide(w_gate_up, w_down_t, layer):
    _, _, rows, _, units = w_gate_up.shape
    half = NF // 2
    specs = [
        pl.BlockSpec(
            (1, rows, 3 * units), lambda e, part=part: (jnp.clip(e - part * half, 0, half - 1), 0, 0)
        )
        for part in range(2)
    ]
    return pl.pallas_call(
        pack_wide_kernel,
        grid=(NF,),
        out_shape=tuple([jax.ShapeDtypeStruct((half, rows, 3 * units), BF16)] * 2),
        in_specs=[
            pl.BlockSpec((1, 1, rows, 2, units), lambda e: (layer, e, 0, 0, 0)),
            pl.BlockSpec((1, 1, rows, units), lambda e: (layer, e, 0, 0)),
        ],
        out_specs=tuple(specs),
        compiler_params=kernel_params(),
        cost_estimate=cost(1e6, 5e6),
        name="pack_wide",
    )(w_gate_up, w_down_t)


def qkv_kernel(with_ffn, *refs):
    if with_ffn:
        base_ref, ffn_ref, vec_ref, w_ref, h_ref, qkv_ref = refs
        hidden = base_ref[...] + ffn_ref[...].astype(F32)
        h_ref[...] = hidden
    else:
        base_ref, vec_ref, w_ref, qkv_ref = refs
        hidden = base_ref[...].astype(F32)
    gain = vec_ref[ROW_GA : ROW_GA + 1, :]
    scale = lax.rsqrt(jnp.mean(hidden * hidden, axis=-1, keepdims=True) + EPSILON)
    attn_in = (hidden * scale * gain).astype(BF16)
    qkv_ref[...] = mm(attn_in, w_ref[...]).astype(BF16)


def qkv_part(base, ffn, vecs, w_qkv):
    rows, feature_dim = base.shape
    cols = round_up(w_qkv.shape[1], 128)
    row_spec = pl.BlockSpec((TILE, feature_dim), lambda i: (i, 0))
    with_ffn = ffn is not None
    out_shape = [jax.ShapeDtypeStruct((rows, cols), BF16)]
    out_specs = [pl.BlockSpec((TILE, cols), lambda i: (i, 0))]
    if with_ffn:
        out_shape = [jax.ShapeDtypeStruct((rows, feature_dim), F32)] + out_shape
        out_specs = [row_spec] + out_specs
    ins = [base] + ([ffn] if with_ffn else []) + [vecs, w_qkv]
    in_specs = [row_spec] * (2 if with_ffn else 1) + [full_spec(vecs.shape), full_spec(w_qkv.shape)]
    return pl.pallas_call(
        functools.partial(qkv_kernel, with_ffn),
        grid=(rows // TILE,),
        out_shape=tuple(out_shape),
        in_specs=in_specs,
        out_specs=tuple(out_specs),
        compiler_params=kernel_params(),
        cost_estimate=cost(2 * rows * feature_dim * cols, rows * feature_dim * 10),
        name="qkv_part",
    )(*ins)


def attn_masks(ctx, length, tile, width):
    row = iota((TILE, width), 0) + tile * TILE
    col = iota((TILE, width), 1)
    return (col <= row) & (col + ctx * BLOCK < length)


def attn_fwd_kernel(heads, info_ref, own_ref, other_ref, ctx_ref, lse_ref):
    ctx = info_ref[0]
    length = info_ref[1 + pl.program_id(0)]
    own = own_ref[...]
    other = other_ref[...]
    for head in range(heads):
        col = head * 3 * HD
        k_own = own[:, col + HD : col + 2 * HD]
        v_own = own[:, col + 2 * HD : col + 3 * HD]
        k_oth = other[:, col + HD : col + 2 * HD]
        v_oth = other[:, col + 2 * HD : col + 3 * HD]
        for tile in range(BLOCK // TILE):
            width = (tile + 1) * TILE
            query = own[tile * TILE : (tile + 1) * TILE, col : col + HD] * BF16(HD**-0.5)
            s_own = mm(query, k_own[:width], NT)
            s_own = jnp.where(attn_masks(ctx, length, tile, width), s_own, MASKED)
            s_oth = jnp.where(ctx > 0, mm(query, k_oth, NT), MASKED)
            top = jnp.maximum(
                jnp.max(s_own, axis=-1, keepdims=True), jnp.max(s_oth, axis=-1, keepdims=True)
            )
            p_own = jnp.exp(s_own - top)
            p_oth = jnp.exp(s_oth - top)
            total = jnp.sum(p_own, axis=-1, keepdims=True) + jnp.sum(p_oth, axis=-1, keepdims=True)
            out = mm(p_own.astype(BF16), v_own[:width]) + mm(p_oth.astype(BF16), v_oth)
            out = out / total
            rows = slice(tile * TILE, (tile + 1) * TILE)
            ctx_ref[head * TILE : (head + 1) * TILE, tile * HD : (tile + 1) * HD] = out.astype(BF16)
            lse_ref[rows, head : head + 1] = top + jnp.log(total)


def attend_forward(qkv, other, info, heads):
    rows, cols = qkv.shape
    count = rows // BLOCK
    spec = pl.BlockSpec((BLOCK, cols), lambda i: (i, 0))
    return pl.pallas_call(
        functools.partial(attn_fwd_kernel, heads),
        grid=(count,),
        out_shape=(
            jax.ShapeDtypeStruct((count * heads * TILE, 2 * HD), BF16),
            jax.ShapeDtypeStruct((rows, 8), F32),
        ),
        in_specs=[SMEM_SPEC, spec, spec],
        out_specs=(
            pl.BlockSpec((heads * TILE, 2 * HD), lambda i: (i, 0)),
            pl.BlockSpec((BLOCK, 8), lambda i: (i, 0)),
        ),
        compiler_params=kernel_params(),
        cost_estimate=cost(rows * 1024 * heads * HD * 16, rows * cols * 6, rows * heads * 1024),
        name="attend_forward",
    )(info, qkv, other)


def attn_bwd_kernel(heads, info_ref, own_ref, other_ref, lse_ref, gctx_ref, gown_ref, goth_ref):
    ctx = info_ref[0]
    length = info_ref[1 + pl.program_id(0)]
    own = own_ref[...]
    other = other_ref[...]
    scale = BF16(HD**-0.5)
    for head in range(heads):
        col = head * 3 * HD
        k_own = own[:, col + HD : col + 2 * HD]
        v_own = own[:, col + 2 * HD : col + 3 * HD]
        k_oth = other[:, col + HD : col + 2 * HD]
        v_oth = other[:, col + 2 * HD : col + 3 * HD]
        goth_ref[:, col : col + HD] = jnp.zeros((BLOCK, HD), BF16)
        gk_own, gv_own, gk_oth, gv_oth = [], [], [], []
        for tile in range(BLOCK // TILE):
            width = (tile + 1) * TILE
            rows = slice(tile * TILE, (tile + 1) * TILE)
            query = own[rows, col : col + HD] * scale
            gout = gctx_ref[rows, head * HD : (head + 1) * HD]
            lse = lse_ref[rows, head : head + 1]
            s_own = mm(query, k_own[:width], NT)
            s_own = jnp.where(attn_masks(ctx, length, tile, width), s_own, MASKED)
            s_oth = jnp.where(ctx > 0, mm(query, k_oth, NT), MASKED)
            p_own = jnp.exp(s_own - lse)
            p_oth = jnp.exp(s_oth - lse)
            d_own = mm(gout, v_own[:width], NT)
            d_oth = mm(gout, v_oth, NT)
            inner = jnp.sum(p_own * d_own, axis=-1, keepdims=True) + jnp.sum(
                p_oth * d_oth, axis=-1, keepdims=True
            )
            ds_own = (p_own * (d_own - inner)).astype(BF16)
            ds_oth = (p_oth * (d_oth - inner)).astype(BF16)
            p_own = p_own.astype(BF16)
            p_oth = p_oth.astype(BF16)
            gown_ref[rows, col : col + HD] = (mm(ds_own, k_own[:width]) + mm(ds_oth, k_oth)) * (
                HD**-0.5
            )
            gk_own.append(mm(ds_own, query, TN))
            gv_own.append(mm(p_own, gout, TN))
            gk_oth.append(mm(ds_oth, query, TN))
            gv_oth.append(mm(p_oth, gout, TN))
        gown_ref[:TILE, col + HD : col + 2 * HD] = gk_own[0] + gk_own[1][:TILE]
        gown_ref[TILE:, col + HD : col + 2 * HD] = gk_own[1][TILE:]
        gown_ref[:TILE, col + 2 * HD : col + 3 * HD] = gv_own[0] + gv_own[1][:TILE]
        gown_ref[TILE:, col + 2 * HD : col + 3 * HD] = gv_own[1][TILE:]
        goth_ref[:, col + HD : col + 2 * HD] = (gk_oth[0] + gk_oth[1]).astype(BF16)
        goth_ref[:, col + 2 * HD : col + 3 * HD] = (gv_oth[0] + gv_oth[1]).astype(BF16)


def attend_backward(qkv, other, lse, grad_context, info, heads):
    rows, width = qkv.shape
    cols = heads * 3 * HD
    spec = pl.BlockSpec((BLOCK, width), lambda i: (i, 0))
    return pl.pallas_call(
        functools.partial(attn_bwd_kernel, heads),
        grid=(rows // BLOCK,),
        out_shape=(
            jax.ShapeDtypeStruct((rows, cols), F32),
            jax.ShapeDtypeStruct((rows, width), BF16),
        ),
        in_specs=[
            SMEM_SPEC,
            spec,
            spec,
            pl.BlockSpec((BLOCK, 8), lambda i: (i, 0)),
            pl.BlockSpec((BLOCK, heads * HD), lambda i: (i, 0)),
        ],
        out_specs=(pl.BlockSpec((BLOCK, cols), lambda i: (i, 0)), spec),
        compiler_params=kernel_params(),
        cost_estimate=cost(rows * 1024 * heads * HD * 40, rows * cols * 12, rows * heads * 1024),
        name="attend_backward",
    )(info, qkv, other, lse, grad_context)


def alpha_rows(gate_in, const_idx):
    first = gate_in[ROW_CONST + 2 * const_idx : ROW_CONST + 2 * const_idx + 1]
    second = gate_in[ROW_CONST + 2 * const_idx + 1 : ROW_CONST + 2 * const_idx + 2]
    return pair(first, second)


def pair(first, second):
    top = jnp.maximum(first, second)
    exp_first = jnp.exp(first - top)
    exp_second = jnp.exp(second - top)
    total = exp_first + exp_second
    return exp_first / total, exp_second / total


def picks(route, value):
    return (route == value).astype(F32)


def gate_coefs(routes, gates, alphas):
    copy = picks(routes[0], NF + 1) * gates[0] + picks(routes[1], NF + 1) * gates[1]
    const = [
        picks(routes[0], NF + 2 + j) * gates[0] + picks(routes[1], NF + 2 + j) * gates[1]
        for j in range(2)
    ]
    on_normed = copy + const[0] * alphas[0][0] + const[1] * alphas[1][0]
    on_vec = [const[j] * alphas[j][1] for j in range(2)]
    return const, on_normed, on_vec


def to_columns(rows):
    width = rows[0].shape[1]
    return pad_rows(list(enumerate(rows)), 128, width).T


def unpack_context(both):
    heads = both.shape[0] // TILE
    side = lax.rem(pl.program_id(0), 2) == 0
    both = jnp.where(side, both[:, :HD], both[:, HD:])
    parts = [both[head * TILE : (head + 1) * TILE] for head in range(heads)]
    return jnp.concatenate(parts, axis=1)


def middle_kernel(with_prev, rank_ref, *refs):
    h_ref, ctx_ref, refs = refs[0], refs[1], refs[2:]
    count = ctx_ref.shape[0]
    wo_refs, refs = refs[:count], refs[count:]
    if with_prev:
        vec_ref, route_ref, prev_ref, resid_ref = refs[:4]
        refs = refs[4:]
    else:
        vec_ref, route_ref = refs[:2]
        refs = refs[2:]
    mid_ref, base_ref, xm_ref, gate_ref, logit_ref = refs
    attn_out = 0.0
    for back, ref in enumerate(wo_refs):
        context = unpack_context(ctx_ref[lax.rem(rank_ref[0] + count - back, count)])
        total = ref.shape[0] * 2 // 3
        rest = context[:, 128:]
        attn_out += mm(context[:, :128], ref[:total], NT) + jnp.concatenate(
            [mm(rest, ref[total:, :HD], NT), mm(rest, ref[total:, HD:], NT)], axis=1
        )
    middle = h_ref[...].astype(F32) + attn_out
    mid_ref[...] = middle
    vecs = vec_ref[...]
    scale = lax.rsqrt(jnp.mean(middle * middle, axis=-1, keepdims=True) + EPSILON)
    normed = middle * scale * vecs[ROW_GM : ROW_GM + 1]
    xm_low = normed.astype(BF16)
    xm_ref[...] = xm_low
    gate_in = mm(vecs[:32].astype(BF16), xm_low, NT)
    logits = gate_in[:16]
    if with_prev:
        logits = logits + mm(resid_ref[...], prev_ref[...], TN, HIGH)
    logit_ref[...] = logits
    routes = (route_ref[0:1], route_ref[1:2])
    expert = iota(logits.shape, 0)
    chosen = [
        jnp.sum(jnp.where(expert == route, logits, 0.0), axis=0, keepdims=True) for route in routes
    ]
    gates = pair(chosen[0], chosen[1])
    gate_ref[...] = pad_rows(list(enumerate(gates)), 8, logits.shape[1])
    alphas = [alpha_rows(gate_in, j) for j in range(2)]
    const, on_normed, on_vec = gate_coefs(routes, gates, alphas)
    cols = to_columns([on_normed, on_vec[0], on_vec[1]])
    base_ref[...] = (
        middle
        + cols[:, 0:1] * normed
        + cols[:, 1:2] * vecs[ROW_VEC : ROW_VEC + 1]
        + cols[:, 2:3] * vecs[ROW_VEC + 1 : ROW_VEC + 2]
    )


def middle_part(h, ctx_all, wo_all, vecs, routes_t, prev_t, resid, rank):
    rows, feature_dim = h.shape
    tp_count, packed, lanes = ctx_all.shape
    packed = packed * BLOCK // rows
    row_spec = pl.BlockSpec((TILE, feature_dim), lambda i: (i, 0))
    lane8 = pl.BlockSpec((8, TILE), lambda i: (0, i))
    lane16 = pl.BlockSpec((16, TILE), lambda i: (0, i))
    ins = [rank, h, ctx_all, *wo_all, vecs, routes_t]
    in_specs = [
        SMEM_SPEC,
        row_spec,
        pl.BlockSpec((tp_count, packed, lanes), lambda i: (0, i // 2, 0)),
        *[full_spec(item.shape) for item in wo_all],
        full_spec(vecs.shape),
        lane8,
    ]
    with_prev = prev_t is not None
    if with_prev:
        ins += [prev_t, resid]
        in_specs += [lane16, full_spec(resid.shape)]
    return pl.pallas_call(
        functools.partial(middle_kernel, with_prev),
        grid=(rows // TILE,),
        out_shape=(
            jax.ShapeDtypeStruct((rows, feature_dim), F32),
            jax.ShapeDtypeStruct((rows, feature_dim), F32),
            jax.ShapeDtypeStruct((rows, feature_dim), BF16),
            jax.ShapeDtypeStruct((8, rows), F32),
            jax.ShapeDtypeStruct((16, rows), F32),
        ),
        in_specs=in_specs,
        out_specs=(row_spec, row_spec, row_spec, lane8, lane16),
        compiler_params=kernel_params(),
        cost_estimate=cost(2 * rows * feature_dim * feature_dim, rows * feature_dim * 16),
        name="middle_part",
    )(*ins)


def split(value):
    high = value.astype(BF16)
    return high, (value - high.astype(F32)).astype(BF16)


def gate_bwd_kernel(with_prev, *refs):
    gh_ref, mid_ref, gxm_ref, vec_ref, route_ref, gate_ref, gg_ref, ctx_ref, wo_ref = refs[:9]
    refs = refs[9:]
    if with_prev:
        prev_ref, resid_ref = refs[:2]
        gmid_ref, gctx_ref, dwo_ref, dvec_ref, gprev_ref, dres_ref = refs[2:]
    else:
        gl_ref = refs[0]
        gmid_ref, gctx_ref, dwo_ref, dvec_ref = refs[1:]
    step = pl.program_id(0)
    grad = gh_ref[...].astype(F32)
    middle = mid_ref[...]
    vecs = vec_ref[...]
    gain = vecs[ROW_GM : ROW_GM + 1]
    scale = lax.rsqrt(jnp.mean(middle * middle, axis=-1, keepdims=True) + EPSILON)
    unit = middle * scale
    normed = unit * gain
    xm_low = normed.astype(BF16)
    low_vecs = vecs[:32].astype(BF16)
    gate_in = mm(low_vecs, xm_low, NT)
    alphas = [alpha_rows(gate_in, j) for j in range(2)]
    routes = (route_ref[0:1], route_ref[1:2])
    gates = (gate_ref[0:1], gate_ref[1:2])
    const, on_normed, on_vec = gate_coefs(routes, gates, alphas)
    grad_hi, grad_lo = split(grad)
    vec_dots = mm(low_vecs[16:32], grad_hi, NT) + mm(low_vecs[16:32], grad_lo, NT)
    dot_vec = [vec_dots[ROW_VEC - 16 + j : ROW_VEC - 15 + j] for j in range(2)]
    dot_col = jnp.sum(grad * normed, axis=-1, keepdims=True)
    dot_normed = jnp.broadcast_to(dot_col, (dot_col.shape[0], 128)).T[0:1]
    term = [alphas[j][0] * dot_normed + alphas[j][1] * dot_vec[j] for j in range(2)]
    gate_grads = []
    for slot in range(2):
        fixed = (
            picks(routes[slot], NF + 1) * dot_normed
            + picks(routes[slot], NF + 2) * term[0]
            + picks(routes[slot], NF + 3) * term[1]
        )
        gate_grads.append(jnp.where(routes[slot] < NF, gg_ref[slot : slot + 1], fixed))
    inner = gates[0] * gate_grads[0] + gates[1] * gate_grads[1]
    chosen_grads = [gates[slot] * (gate_grads[slot] - inner) for slot in range(2)]
    expert = iota((16, TILE), 0)
    grad_logits = jnp.where(expert == routes[0], chosen_grads[0], 0.0) + jnp.where(
        expert == routes[1], chosen_grads[1], 0.0
    )
    if not with_prev:
        grad_logits = grad_logits + gl_ref[...]
    alpha_grads = []
    for j in range(2):
        grad_first = const[j] * dot_normed
        grad_second = const[j] * dot_vec[j]
        mean = alphas[j][0] * grad_first + alphas[j][1] * grad_second
        alpha_grads.append((2 * j, alphas[j][0] * (grad_first - mean)))
        alpha_grads.append((2 * j + 1, alphas[j][1] * (grad_second - mean)))
    grad_in = jnp.concatenate([grad_logits, pad_rows(alpha_grads, 16, TILE)], axis=0)
    in_hi, in_lo = split(grad_in)
    low_gate = jnp.where(iota(low_vecs.shape, 0) < ROW_VEC, low_vecs, 0)
    grad_xm = mm(in_hi, low_gate, TN) + mm(in_lo, low_gate, TN)
    cols = to_columns([on_normed])
    grad_y = cols[:, 0:1] * grad + grad_xm + gxm_ref[...].astype(F32)
    weighted = grad_y * gain
    mean = jnp.mean(weighted * unit, axis=-1, keepdims=True)
    grad_mid = grad + scale * (weighted - unit * mean)
    gmid_ref[...] = grad_mid
    low_mid = grad_mid.astype(BF16)
    total = low_mid.shape[1]
    gctx_ref[:, :128] = mm(low_mid, wo_ref[:total]).astype(BF16)
    gctx_ref[:, 128:] = (
        mm(low_mid[:, : total // 2], wo_ref[total:, :HD])
        + mm(low_mid[:, total // 2 :], wo_ref[total:, HD:])
    ).astype(BF16)
    dwo = mm(low_mid, unpack_context(ctx_ref[...]), TN)
    vec_rows = pad_rows([(ROW_VEC - 16 + j, on_vec[j]) for j in range(2)], 16, TILE)
    vec_hi, vec_lo = split(vec_rows)
    dvec_low = mm(vec_hi, grad_hi) + mm(vec_lo, grad_hi)
    dvec_gate = mm(in_hi, xm_low) + mm(in_lo, xm_low)
    dgain = jnp.sum(grad_y * unit, axis=0, keepdims=True)
    row_id = iota(dvec_gate.shape, 0)
    dvec = dvec_gate + jnp.concatenate([jnp.zeros_like(dvec_low), dvec_low], axis=0)
    dvec = jnp.where(row_id == ROW_GM, dgain, dvec)

    @pl.when(step == 0)
    def _():
        dwo_ref[...] = dwo
        dvec_ref[...] = dvec

    @pl.when(step > 0)
    def _():
        dwo_ref[...] += dwo
        dvec_ref[...] += dvec

    if with_prev:
        gprev_ref[...] = mm(resid_ref[...], grad_logits, NN, HIGH)
        dres = mm(prev_ref[...], grad_logits, NT, HIGH)

        @pl.when(step == 0)
        def _():
            dres_ref[...] = dres

        @pl.when(step > 0)
        def _():
            dres_ref[...] += dres


def gate_backward(grad, middle, gxm, vecs, routes_t, gates_t, gg_t, context, wo_own, extra):
    rows, feature_dim = middle.shape
    out_cols = context.shape[0] * BLOCK // rows // TILE * HD
    with_prev = len(extra) == 2
    row_spec = pl.BlockSpec((TILE, feature_dim), lambda i: (i, 0))
    lane8 = pl.BlockSpec((8, TILE), lambda i: (0, i))
    lane16 = pl.BlockSpec((16, TILE), lambda i: (0, i))
    ctx_spec = pl.BlockSpec((context.shape[0] * BLOCK // rows, 2 * HD), lambda i: (i // 2, 0))
    out_spec = pl.BlockSpec((TILE, out_cols), lambda i: (i, 0))
    wo_spec = full_spec(wo_own.shape)
    in_specs = [row_spec, row_spec, row_spec, full_spec(vecs.shape), lane8, lane8, lane8]
    in_specs += [ctx_spec, wo_spec, lane16]
    out_shape = [
        jax.ShapeDtypeStruct((rows, feature_dim), F32),
        jax.ShapeDtypeStruct((rows, out_cols), BF16),
        jax.ShapeDtypeStruct((feature_dim, out_cols), F32),
        jax.ShapeDtypeStruct((32, feature_dim), F32),
    ]
    out_specs = [row_spec, out_spec, full_spec((feature_dim, out_cols)), full_spec((32, feature_dim))]
    if with_prev:
        in_specs.append(full_spec(extra[1].shape))
        out_shape += [jax.ShapeDtypeStruct((16, rows), F32), jax.ShapeDtypeStruct((16, 16), F32)]
        out_specs += [lane16, full_spec((16, 16))]
    return pl.pallas_call(
        functools.partial(gate_bwd_kernel, with_prev),
        grid=(rows // TILE,),
        out_shape=tuple(out_shape),
        in_specs=in_specs,
        out_specs=tuple(out_specs),
        compiler_params=kernel_params(),
        cost_estimate=cost(4 * rows * feature_dim * out_cols, rows * feature_dim * 18),
        name="gate_backward",
    )(grad, middle, gxm, vecs, routes_t, gates_t, gg_t, context, wo_own, *extra)


def qkv_bwd_kernel(gown_ref, goth_ref, h_ref, vec_ref, w_ref, part_ref, dw_ref, dgain_ref):
    step = pl.program_id(0)
    cols = gown_ref.shape[1]
    grad = (gown_ref[...] + goth_ref[:, :cols].astype(F32)).astype(BF16)
    part = mm(grad, w_ref[:, :cols], NT)
    part_ref[...] = part.astype(BF16)
    hidden = h_ref[...].astype(F32)
    gain = vec_ref[ROW_GA : ROW_GA + 1, :]
    scale = lax.rsqrt(jnp.mean(hidden * hidden, axis=-1, keepdims=True) + EPSILON)
    unit = hidden * scale
    attn_in = (unit * gain).astype(BF16)
    dw = mm(attn_in, grad, TN)
    dgain = jnp.broadcast_to(jnp.sum(part * unit, axis=0, keepdims=True), dgain_ref.shape)

    @pl.when(step == 0)
    def _():
        dw_ref[...] = dw
        dgain_ref[...] = dgain

    @pl.when(step > 0)
    def _():
        dw_ref[...] += dw
        dgain_ref[...] += dgain


def qkv_backward(gown, goth, h, vecs, w_qkv):
    rows, feature_dim = h.shape
    cols = gown.shape[1]
    row_spec = pl.BlockSpec((TILE, feature_dim), lambda i: (i, 0))
    col_spec = pl.BlockSpec((TILE, cols), lambda i: (i, 0))
    oth_spec = pl.BlockSpec((TILE, goth.shape[1]), lambda i: (i, 0))
    return pl.pallas_call(
        qkv_bwd_kernel,
        grid=(rows // TILE,),
        out_shape=(
            jax.ShapeDtypeStruct((rows, feature_dim), BF16),
            jax.ShapeDtypeStruct((feature_dim, cols), F32),
            jax.ShapeDtypeStruct((8, feature_dim), F32),
        ),
        in_specs=[col_spec, oth_spec, row_spec, full_spec(vecs.shape), full_spec(w_qkv.shape)],
        out_specs=(row_spec, full_spec((feature_dim, cols)), full_spec((8, feature_dim))),
        compiler_params=kernel_params(),
        cost_estimate=cost(4 * rows * feature_dim * cols, rows * feature_dim * 10),
        name="qkv_backward",
    )(gown, goth, h, vecs, w_qkv)


def norm_bwd_kernel(with_low, gmid_ref, ga_ref, h_ref, vec_ref, out_ref, *rest):
    hidden = h_ref[...].astype(F32)
    gain = vec_ref[ROW_GA : ROW_GA + 1, :]
    scale = lax.rsqrt(jnp.mean(hidden * hidden, axis=-1, keepdims=True) + EPSILON)
    unit = hidden * scale
    grad_y = ga_ref[...].astype(F32)
    weighted = grad_y * gain
    mean = jnp.mean(weighted * unit, axis=-1, keepdims=True)
    grad = gmid_ref[...] + scale * (weighted - unit * mean)
    out_ref[...] = grad
    if with_low:
        rest[0][...] = grad.astype(BF16)


def norm_backward(gmid, ga, h, vecs, with_low):
    rows, feature_dim = gmid.shape
    row_spec = pl.BlockSpec((TILE, feature_dim), lambda i: (i, 0))
    out_shape = [jax.ShapeDtypeStruct((rows, feature_dim), F32)]
    out_specs = [row_spec]
    if with_low:
        out_shape.append(jax.ShapeDtypeStruct((rows, feature_dim), BF16))
        out_specs.append(row_spec)
    return pl.pallas_call(
        functools.partial(norm_bwd_kernel, with_low),
        grid=(rows // TILE,),
        out_shape=tuple(out_shape),
        in_specs=[row_spec, row_spec, row_spec, full_spec(vecs.shape)],
        out_specs=tuple(out_specs),
        compiler_params=kernel_params(),
        cost_estimate=cost(rows * feature_dim * 10, rows * feature_dim * 16),
        name="norm_backward",
    )(gmid, ga, h, vecs)


def experts_kernel(fwd, bwd, blocks, plan, out_count, rows, offs_ref, *refs):
    refs = list(refs)
    xm_ref = refs.pop(0)
    gh_ref = refs.pop(0) if bwd else None
    route_ref, gate_ref = refs.pop(0), refs.pop(0)
    w_refs = [refs.pop(0) for _ in plan]
    ffn_ref = refs.pop(0) if fwd else None
    if bwd:
        gx_ref = refs.pop(0)
        dw_refs = [refs.pop(0) for _ in range(out_count)]
    w_scr, hot_scr, pick_scr = refs.pop(0), refs.pop(0), refs.pop(0)
    part_scr = refs.pop(0) if fwd else None
    if bwd:
        gpart_scr, raw_scr, gg_scr, dw_scr = refs
    expert = pl.program_id(0)
    last = pl.num_programs(0) - 1
    width = w_scr.shape[1]
    units = width // 3

    @pl.when(expert == 0)
    def _():
        order = (iota((BLOCK, BLOCK), 0) < iota((BLOCK, BLOCK), 1)).astype(BF16)
        ids = iota((NF, BLOCK), 0)
        row_ids = iota((CAP, BLOCK), 0).astype(F32)
        for block in range(blocks):
            lanes = slice(block * BLOCK, (block + 1) * BLOCK)
            hits = (ids == route_ref[0:1, lanes]) | (ids == route_ref[1:2, lanes])
            place = jnp.where(hits, mm(hits.astype(BF16), order), -1.0)
            for each in range(NF):
                hot_scr[block, each * CAP : (each + 1) * CAP, :] = (
                    (row_ids == place[each : each + 1]).astype(F32).astype(BF16)
                )
            hot = hot_scr[block]
            for source, target in ((xm_ref, pick_scr),) + (((gh_ref, raw_scr),) if bwd else ()):
                rows_all = mm(hot, source[lanes, :]).astype(BF16)
                for each in range(NF):
                    target[each, block * CAP : (block + 1) * CAP, :] = rows_all[
                        each * CAP : (each + 1) * CAP
                    ]
        if bwd:
            gg_scr[...] = jnp.zeros_like(gg_scr)

    def combine(source, block):
        return mm(hot_scr[block], source[block], TN)

    def fill(ref, off):
        start = pl.multiple_of(offs_ref[off] * rows, rows)
        w_scr[pl.ds(start, rows), :] = ref[0]

    for ref, (off, first, number) in zip(w_refs, plan):
        if number == NF:
            fill(ref, off)
        else:
            pl.when((expert >= first) & (expert < first + number))(
                functools.partial(fill, ref, off)
            )

    hot, gate_cols, masks = [], [], []
    first_row = pl.multiple_of(expert * CAP, CAP)
    for block in range(blocks):
        lanes = slice(block * BLOCK, (block + 1) * BLOCK)
        one_hot = hot_scr[block, pl.ds(first_row, CAP), :].astype(F32)
        mask = [route_ref[slot : slot + 1, lanes] == expert for slot in range(2)]
        gate_row = jnp.where(mask[0], gate_ref[0:1, lanes], 0.0) + jnp.where(
            mask[1], gate_ref[1:2, lanes], 0.0
        )
        gate_cols.append(jnp.sum(one_hot * gate_row, axis=1, keepdims=True))
        hot.append(one_hot)
        masks.append(mask)
    gate_col = jnp.concatenate(gate_cols, axis=0)
    picked = pick_scr[expert]
    gate_up = mm(picked, w_scr[:, : 2 * units])
    gate_in, up_in = gate_up[:, :units], gate_up[:, units:]
    sigmoid = lax.logistic(gate_in)
    silu = gate_in * sigmoid
    hidden = (silu * up_in).astype(BF16)
    if fwd:
        scaled = (mm(hidden, w_scr[:, 2 * units :], NT) * gate_col).astype(BF16)
        for block in range(blocks):
            part_scr[block, pl.ds(first_row, CAP), :] = scaled[block * CAP : (block + 1) * CAP]

        @pl.when(expert == last)
        def _():
            for block in range(blocks):
                ffn_ref[block * BLOCK : (block + 1) * BLOCK, :] = combine(part_scr, block).astype(
                    BF16
                )

    if bwd:
        raw = raw_scr[expert]
        grad_raw = mm(raw, w_scr[:, 2 * units :])
        gate_dot = jnp.sum(hidden.astype(F32) * grad_raw, axis=1, keepdims=True)
        for block in range(blocks):
            row = jnp.sum(
                hot[block] * gate_dot[block * CAP : (block + 1) * CAP],
                axis=0,
                keepdims=True,
            )
            for slot in range(2):
                gg_scr[8 * block + slot : 8 * block + slot + 1, :] += jnp.where(
                    masks[block][slot], row, 0.0
                )
        grad_hidden = grad_raw * gate_col
        grad_gate = grad_hidden * up_in * sigmoid * (1.0 + gate_in * (1.0 - sigmoid))
        grad_up = grad_hidden * silu
        grad_gu = jnp.concatenate([grad_gate.astype(BF16), grad_up.astype(BF16)], axis=1)
        grad_pick = mm(grad_gu, w_scr[:, : 2 * units], NT).astype(BF16)
        for block in range(blocks):
            gpart_scr[block, pl.ds(first_row, CAP), :] = grad_pick[block * CAP : (block + 1) * CAP]
        grad_result = (raw.astype(F32) * gate_col).astype(BF16)
        if out_count == 1:
            dw_refs[0][0, :, : 2 * units] = mm(picked, grad_gu, TN).astype(BF16)
            dw_refs[0][0, :, 2 * units :] = mm(grad_result, hidden, TN).astype(BF16)
        else:
            dw_scr[:, : 2 * units] = mm(picked, grad_gu, TN).astype(BF16)
            dw_scr[:, 2 * units :] = mm(grad_result, hidden, TN).astype(BF16)
            half = NF // 2
            for part in range(2):

                @pl.when((expert >= part * half) & (expert < (part + 1) * half))
                def _(part=part):
                    for off in range(8):
                        start = pl.multiple_of(offs_ref[off] * rows, rows)
                        dw_refs[2 * part + off % 2][off // 2, 0] = dw_scr[pl.ds(start, rows), :]

        @pl.when(expert == last)
        def _():
            total = blocks * BLOCK
            for block in range(blocks):
                gx_ref[block * BLOCK : (block + 1) * BLOCK, :] = combine(gpart_scr, block).astype(
                    BF16
                )
            gx_ref[total : total + 16, :] = jnp.zeros((16, gx_ref.shape[1]), BF16)
            gx_ref[total : total + gg_scr.shape[0], :BLOCK] = gg_scr[...].astype(BF16)


def experts(fwd, bwd, xm, gh, routes_t, gates_t, pieces, offs):
    rows, feature_dim = xm.shape
    blocks = rows // BLOCK
    arrays = [item[0] for item in pieces]
    plan = [item[1:] for item in pieces]
    _, piece_rows, width = arrays[0].shape
    units = width // 3
    split_out = len(pieces) > 1
    half = NF // 2

    ins = [xm] + ([gh] if bwd else []) + [routes_t, gates_t]
    in_specs = [SMEM_SPEC] + [full_spec(item.shape) for item in ins]
    for _, first, number in plan:
        in_specs.append(
            pl.BlockSpec(
                (1, piece_rows, width),
                lambda e, first=first, number=number: (jnp.clip(e - first, 0, number - 1), 0, 0),
            )
        )
    out_shape, out_specs, scratch = [], [], []
    scratch += [
        pltpu.VMEM((feature_dim, width), BF16),
        pltpu.VMEM((blocks, NF * CAP, BLOCK), BF16),
        pltpu.VMEM((NF, blocks * CAP, feature_dim), BF16),
    ]
    flops = 0
    out_count = 4 if split_out else 1
    if fwd:
        out_shape.append(jax.ShapeDtypeStruct((rows, feature_dim), BF16))
        out_specs.append(full_spec((rows, feature_dim)))
        scratch.append(pltpu.VMEM((blocks, NF * CAP, feature_dim), BF16))
        flops += 1.0e9 * NF * blocks / 2
    if bwd:
        out_shape.append(jax.ShapeDtypeStruct((rows + 16, feature_dim), BF16))
        out_specs.append(full_spec((rows + 16, feature_dim)))
        if split_out:
            for part in range(2):
                for _ in range(2):
                    out_shape.append(jax.ShapeDtypeStruct((4, half, piece_rows, width), BF16))
                    out_specs.append(
                        pl.BlockSpec(
                            (4, 1, piece_rows, width),
                            lambda e, part=part: (0, jnp.clip(e - part * half, 0, half - 1), 0, 0),
                        )
                    )
        else:
            out_shape.append(jax.ShapeDtypeStruct((NF, feature_dim, width), BF16))
            out_specs.append(pl.BlockSpec((1, feature_dim, width), lambda e: (e, 0, 0)))
        scratch += [
            pltpu.VMEM((blocks, NF * CAP, feature_dim), BF16),
            pltpu.VMEM((NF, blocks * CAP, feature_dim), BF16),
            pltpu.VMEM((blocks * 8, BLOCK), F32),
            pltpu.VMEM((feature_dim, width) if split_out else (8, 128), BF16),
        ]
        flops += 2.2e9 * NF * blocks / 2
    outs = pl.pallas_call(
        functools.partial(experts_kernel, fwd, bwd, blocks, plan, out_count, piece_rows),
        grid=(NF,),
        out_shape=tuple(out_shape),
        in_specs=in_specs,
        out_specs=tuple(out_specs),
        scratch_shapes=scratch,
        compiler_params=kernel_params(),
        cost_estimate=cost(flops, 20e6 * (2 if bwd else 1), rows * units * 8),
        name="experts",
    )(offs, *ins, *arrays)
    outs = list(outs)
    ffn = outs.pop(0) if fwd else None
    return (ffn, outs[0], outs[1:]) if bwd else (ffn, None, None)


def final_kernel(with_old, count, *refs):
    parts = refs[:count]
    gu_ref, dn_ref = refs[-2:]
    del with_old
    half = count // 2
    units = gu_ref.shape[-1]

    def write(group):
        total = group[0][...].reshape(group[0].shape[-2:]).astype(F32)
        for ref in group[1:]:
            total += ref[...].reshape(ref.shape[-2:]).astype(F32)
        gu_ref[0, 0, :, 0, :] = total[:, :units]
        gu_ref[0, 0, :, 1, :] = total[:, units : 2 * units]
        dn_ref[0, 0] = total[:, 2 * units :]

    @pl.when(pl.program_id(0) < NF // 2)
    def _():
        write(parts[:half])

    @pl.when(pl.program_id(0) >= NF // 2)
    def _():
        write(parts[half:])


def final_sums(lows, highs, old, layer, layer_count):
    half = NF // 2
    specs, arrays = [], []
    for part, group in enumerate((lows, highs)):
        for item in group:
            lead = (1,) * (item.ndim - 3)
            specs.append(
                pl.BlockSpec(
                    lead + (1,) + item.shape[-2:],
                    lambda e, part=part, lead=lead: (0,) * len(lead)
                    + (jnp.clip(e - part * half, 0, half - 1), 0, 0),
                )
            )
            arrays.append(item)
    count = len(arrays)
    rows, width = arrays[0].shape[-2:]
    units = width // 3
    aliases = {}
    if old is not None:
        specs += [pl.BlockSpec(memory_space=pl.ANY)] * 2
        arrays += list(old)
        aliases = {count: 0, count + 1: 1}
    return pl.pallas_call(
        functools.partial(final_kernel, old is not None, count),
        grid=(NF,),
        out_shape=(
            jax.ShapeDtypeStruct((layer_count, NF, rows, 2, units), F32),
            jax.ShapeDtypeStruct((layer_count, NF, rows, units), F32),
        ),
        in_specs=specs,
        out_specs=(
            pl.BlockSpec((1, 1, rows, 2, units), lambda e: (layer, e, 0, 0, 0)),
            pl.BlockSpec((1, 1, rows, units), lambda e: (layer, e, 0, 0)),
        ),
        input_output_aliases=aliases,
        compiler_params=kernel_params(),
        cost_estimate=cost(1e7, NF * rows * width * 12),
        name="final_sums",
    )(*arrays)


def hop(value, step):
    return lax.ppermute(value, "fsdp", [(i, i ^ step) for i in range(4)])


def swap(value):
    return lax.ppermute(value, "ctx", [(0, 1), (1, 0)])


def gather_small(value):
    by_x, by_y, by_d = hop(value, 1), hop(value, 2), hop(value, 3)
    out = []
    for item in (value, by_x, by_y, by_d):
        out += [item, swap(item)]
    return out


def turn(value, steps, count):
    return lax.ppermute(value, "tp", [(i, (i + steps) % count) for i in range(count)])


def share(value, count):
    return [value] + [turn(value, k, count) for k in range(1, count)]


def gather_cores(lows, highs):
    half = NF // 2
    out = []
    for first, items in ((0, lows), (half, highs)):
        for chip, item in enumerate(items):
            out += [(item, 2 * chip, first, half), (swap(item), 2 * chip + 1, first, half)]
    return out


def tie(*values):
    return lax.optimization_barrier(values)


def add_low(*terms):
    total = terms[0].astype(F32)
    for term in terms[1:]:
        total = total + term.astype(F32)
    return total.astype(BF16)


def scatter_cores(keep, send, first):
    other = swap(send)
    if first == 1:
        out = add_low(keep[1::2], other[1::2])
    else:
        out = add_low(keep[2:], other[2:])
    return keep, other, out


def scatter_first(keep, other, out, first):
    return scatter_beside(keep, other, hop(out, first), first)


def scatter_beside(keep, other, got, first):
    return keep[:1], other[:1], got[:1], add_low(keep[3 - first], other[3 - first], got[1])


def scatter_second(terms, first):
    return terms[:3] + (hop(terms[3], 3 - first),)


def per_device(
    hyper,
    axes,
    tokens,
    cotangent,
    lengths,
    routes,
    norm_attn,
    w_qkv,
    w_out,
    norm_moe,
    w_router,
    w_resid,
    w_const,
    v_const,
    w_gate_up,
    w_down,
):
    micro_count, seq_count, block_len, feature_dim = tokens.shape
    rows = micro_count * seq_count * block_len
    layer_count, shard_rows, qkv_cols = w_qkv.shape
    heads = qkv_cols // (3 * HD)
    units = w_gate_up.shape[-1]
    groups = ("fsdp", "ctx")
    shard_count = feature_dim // shard_rows
    ctx = lax.axis_index("ctx")
    me = lax.axis_index("fsdp") * axes["ctx"] + ctx
    rank = lax.axis_index("tp").reshape(1)
    if hyper:
        offs = me ^ jnp.arange(shard_count, dtype=jnp.int32)
    else:
        offs = jnp.zeros((1,), jnp.int32)
    info = jnp.concatenate([ctx.reshape(1), lengths.reshape(-1)]).astype(jnp.int32)
    resid = jnp.zeros((16, 16), F32).at[:NE, :NE].set(w_resid.astype(F32))

    tp_count = axes["tp"]
    outer = share(jnp.transpose(w_out, (0, 2, 1)), tp_count)
    small, wide = [], []
    for layer in range(layer_count):
        vec = jnp.concatenate(
            [
                w_router[layer],
                jnp.zeros((shard_rows, ROW_CONST - NE), BF16),
                w_const[layer, 0],
                w_const[layer, 1],
                v_const[layer].T,
                norm_attn[layer][:, None],
                norm_moe[layer][:, None],
                jnp.zeros((shard_rows, PACK - ROW_GM - 1), BF16),
            ],
            axis=1,
        )
        pad = jnp.zeros((shard_rows, round_up(qkv_cols, 128) - qkv_cols), BF16)
        turned = [item[layer] for item in outer]
        small.append(jnp.concatenate([w_qkv[layer], pad, vec] + turned, axis=1))
        wide.append(pack_wide(w_gate_up, jnp.swapaxes(w_down, 2, 3), layer))
    weights, wide_first = [None] * layer_count, [None] * layer_count

    def fetch_small(layer, after):
        own = small[layer]
        if hyper:
            own, _ = tie(own, after)
            pieces = gather_small(own)
            fetch_first(layer, [pieces[k] for k in (2, 4, 6)])
        else:
            pieces = [lax.all_gather(own, groups, axis=0, tiled=True)]
        outs = prep_weights(pieces, offs, feature_dim, qkv_cols, heads * HD, tp_count)
        weights[layer] = [outs[0], outs[2], outs[1]]
        if hyper and layer == 0:
            weights[0][0], wide_first[0] = tie(weights[0][0], wide_first[0])

    def fetch_first(layer, after):
        (low, high), _ = tie(wide[layer], after)
        lows, highs = [low, None, hop(low, 2)], [high, hop(high, 1), None]
        if layer > 0:
            lows[1], highs[2] = hop(low, 1), hop(high, 2)
        wide_first[layer] = (lows, highs)

    def fetch_rest(layer, value):
        if hyper:
            value, (lows, highs) = tie(value, wide_first[layer])
            if layer == 0:
                lows[1], highs[2] = hop(lows[0], 1), hop(highs[0], 2)
            lows.append(hop(lows[2], 1))
            highs.append(hop(highs[1], 2))
            rests[layer] = (lows, highs)
        return value

    def fetch_cores(layer, after):
        if hyper:
            lows, highs = rests[layer]
            early = (lows[0], lows[2], highs[0], highs[1])
            early, _ = tie(early, after)
            lows = (early[0], lows[1], early[1], lows[3])
            highs = (early[2], early[3], highs[2], highs[3])
            ends[layer] = (lows[1], lows[3], highs[2], highs[3])
            rests[layer] = (lows, highs)
            if layer + 1 < layer_count:
                mid, wide[layer + 1] = tie((lows[1], highs[2]), wide[layer + 1])
                rests[layer] = ((lows[0], mid[0]) + lows[2:], highs[:2] + (mid[1], highs[3]))
        else:
            both = jnp.concatenate(wide[layer], axis=0)
            full = lax.all_gather(both, groups, axis=1, tiled=True)
            weights[layer].append([(full, 0, 0, NF)])

    def fetch_last(layer, after):
        if hyper:
            lows, highs = rests[layer]
            last, _ = tie((lows[3], highs[3]), after)
            weights[layer].append(gather_cores(lows[:3] + last[:1], highs[:3] + last[1:]))

    ends, rests = [None] * layer_count, [None] * layer_count
    fetch_small(0, info)

    routes_t = jnp.moveaxis(routes.reshape(layer_count, rows, 2), 2, 1)
    routes_t = jnp.concatenate(
        [routes_t, jnp.full((layer_count, 6, rows), -1, jnp.int32)], axis=1
    )
    position = ctx * block_len + jnp.arange(block_len, dtype=jnp.int32)
    valid = position[None, None, :] < lengths[:, :, None]
    cot = jnp.where(valid[..., None], cotangent, 0).reshape(rows, feature_dim)

    base, ffn, prev_t = tokens.reshape(rows, feature_dim), None, None
    saved = []
    for layer in range(layer_count):
        qkv_full, _, vecs = weights[layer][:3]
        outs = qkv_part(base, ffn, vecs, qkv_full)
        h_in, qkv = outs if ffn is not None else (base, outs[0])
        other = fetch_rest(layer, swap(qkv))
        context, lse = attend_forward(qkv, other, info, heads)
        ctx_all = lax.all_gather(context, "tp", axis=0)
        fetch_cores(layer, context)
        wo_all = weights[layer][1]
        middle, base, xm_low, gates_t, logits_t = middle_part(
            h_in, ctx_all, wo_all, vecs, routes_t[layer], prev_t, resid, rank
        )
        fetch_last(layer, xm_low)
        pieces = weights[layer][3]
        saved.append((h_in, qkv, other, context, lse, middle, xm_low, gates_t, prev_t))
        prev_t = logits_t
        if layer < layer_count - 1:
            fetch_small(layer + 1, ends[layer] if hyper else ctx_all)
            part, _, _ = experts(True, False, xm_low, None, routes_t[layer], gates_t, pieces, offs)
            ffn = lax.psum(part, "tp")
            if hyper:
                ffn, wide_first[layer + 1] = tie(ffn, wide_first[layer + 1])

    grad, grad_low = cot, cot
    grad_logits, wide_out, pending, small_terms, late = None, None, None, None, None
    finals = [None] * layer_count
    for layer in reversed(range(layer_count)):
        qkv_full, wo_all, vecs, pieces = weights[layer]
        h_in, qkv, other, context, lse, middle, xm_low, gates_t, prev_t = saved[layer]
        top = layer == layer_count - 1
        part, gx, grads = experts(
            top, True, xm_low, grad_low, routes_t[layer], gates_t, pieces, offs
        )
        if not top and late is not None:
            late[0] = lax.psum(late[0], "tp")
            gx, grads, late, pending = tie(gx, grads, late, pending)
        gx = lax.psum(gx, "tp")
        if hyper:
            sums = [scatter_cores(grads[2 * k], grads[2 * k + 1], k + 1) for k in range(2)]
            if pending is not None:
                wide_terms, small_parts, dres = pending
                terms = [scatter_second(wide_terms[k], k + 1) for k in range(2)]
                terms, sums = tie(terms, sums)
                wide_out = final_sums(terms[0], terms[1], wide_out, layer + 1, layer_count)
                upper = scatter_cores(*pack_grads(*small_parts, offs), 1)
                gx, sums, wide_out, upper = tie(gx, sums, wide_out, upper)
                upper_got = hop(upper[2], 1)
            else:
                gx, sums = tie(gx, sums)
            got = [hop(sums[k][2], k + 1) for k in range(2)]
        if top:
            base_top = base
        else:
            late[1], gx = tie(late[1], gx)
            late[1] = lax.psum(late[1], "tp")
        gg_t = gx[rows : rows + 16, :block_len].astype(F32)
        gg_t = jnp.moveaxis(gg_t.reshape(2, 8, block_len)[: rows // BLOCK], 0, 1).reshape(8, rows)
        extra = (prev_t, resid) if prev_t is not None else (grad_logits,)
        outs = gate_backward(
            grad, middle, gx, vecs, routes_t[layer], gates_t, gg_t, context, wo_all[0], extra
        )
        gmid, gctx, dwo, dvec = outs[:4]
        if prev_t is not None:
            grad_logits, dres = outs[4:]
        gown, goth = attend_backward(qkv, other, lse, gctx, info, heads)
        if not top:
            gown, goth, late = tie(gown, goth, late)
        goth = swap(goth)
        if hyper:
            wide_terms = [scatter_beside(*sums[k][:2], got[k], k + 1) for k in range(2)]
            if layer == 0:
                goth, wide_terms, upper_got = tie(goth, wide_terms, upper_got)
        ga_part, dqkv, dgain = qkv_backward(gown, goth, h_in, vecs, qkv_full)
        small_parts = (dqkv, dwo, dvec, dgain)
        own = None
        ga = lax.psum(ga_part, "tp")
        if hyper:
            if layer > 0:
                dres = dres + swap(dres)
                dres = dres + hop(dres, 1)
                ga, wide_terms, dres, small_parts = tie(ga, wide_terms, dres, small_parts)
                dres = dres + hop(dres, 2)
                pending = (wide_terms, small_parts, dres)
            else:
                small_terms = scatter_second(scatter_beside(*upper[:2], upper_got, 1), 1)
                terms = [scatter_second(wide_terms[k], k + 1) for k in range(2)]
                terms, small_parts = tie(terms, small_parts)
                wide_out = final_sums(terms[0], terms[1], wide_out, layer, layer_count)
                own = scatter_cores(*pack_grads(*small_parts, offs), 1)
                owns = [scatter_second(scatter_first(*own, 1), 1), small_terms]
                owns = [
                    sum(term.reshape(shard_rows, -1).astype(F32) for term in item) for item in owns
                ]
                gains = share(jnp.stack([item[:, -PACK + ROW_GA] for item in owns]), tp_count)
        if top:
            late = [part[:block_len], part[block_len:]]
            late[0], ga = tie(late[0], ga)
        outs = norm_backward(gmid, ga, h_in, vecs, layer > 0)
        grad = outs[0]
        grad_low = outs[-1]
        finals[layer] = (grads, small_parts, own)

    late = jnp.concatenate(late, axis=0)
    mixed = (base_top + late.astype(F32)).astype(BF16)

    resid_total = (dres if hyper else lax.psum(dres, groups))[:NE, :NE]
    results = [None] * layer_count
    for layer in reversed(range(layer_count)):
        grads, small_parts, own = finals[layer]
        if hyper:
            own = owns[layer]
        else:
            packed = pack_grads(*small_parts, offs)
            own = lax.psum_scatter(packed[0], groups, scatter_dimension=0, tiled=True).astype(F32)
            wide_own = lax.psum_scatter(
                grads[0], groups, scatter_dimension=1, tiled=True
            ).astype(F32)
            here = (
                wide_own[:, :, : 2 * units].reshape(NF, shard_rows, 2, units),
                wide_own[:, :, 2 * units :],
            )
            if wide_out is None:
                wide_out = ([], [])
            wide_out[0].insert(0, here[0])
            wide_out[1].insert(0, here[1])
        out_cols = heads * HD
        vec = own[:, qkv_cols + out_cols :]
        results[layer] = (
            own[:, :qkv_cols],
            own[:, qkv_cols : qkv_cols + out_cols].T,
            vec[:, ROW_GM],
            vec[:, :NE],
            jnp.stack([vec[:, ROW_CONST : ROW_CONST + 2], vec[:, ROW_CONST + 2 : ROW_CONST + 4]]),
            vec[:, ROW_VEC : ROW_VEC + 2].T,
            vec[:, ROW_GA],
        )
    if not hyper:
        wide_out = (jnp.stack(wide_out[0]), jnp.stack(wide_out[1]))
    stacked = [jnp.stack([item[member] for item in results]) for member in range(7)]
    gains = jnp.stack(gains if hyper else share(stacked[6], tp_count))
    gain_own = sum(
        lax.dynamic_index_in_dim(gains, (rank[0] + tp_count - j) % tp_count, 0, keepdims=False)
        for j in range(tp_count)
    )
    return (
        mixed.reshape(tokens.shape),
        grad.reshape(tokens.shape),
        gain_own,
        stacked[0],
        stacked[1],
        stacked[2],
        stacked[3],
        resid_total,
        stacked[4],
        stacked[5],
        wide_out[0],
        jnp.swapaxes(wide_out[1], 2, 3),
    )


def solution(mesh):
    axes = dict(mesh.shape)
    hyper = axes["fsdp"] == 4 and axes["ctx"] == 2
    in_specs = (
        P(None, "fsdp", "ctx", None),
        P(None, "fsdp", "ctx", None),
        P(None, "fsdp"),
        P(None, None, "fsdp", "ctx", None),
        P(None, ("fsdp", "ctx")),
        P(None, ("fsdp", "ctx"), "tp"),
        P(None, "tp", ("fsdp", "ctx")),
        P(None, ("fsdp", "ctx")),
        P(None, ("fsdp", "ctx"), None),
        P(),
        P(None, None, ("fsdp", "ctx"), None),
        P(None, None, ("fsdp", "ctx")),
        P(None, None, ("fsdp", "ctx"), None, "tp"),
        P(None, None, "tp", ("fsdp", "ctx")),
    )
    out_specs = (
        P(None, "fsdp", "ctx", None),
        P(None, "fsdp", "ctx", None),
        P(None, ("fsdp", "ctx")),
        P(None, ("fsdp", "ctx"), "tp"),
        P(None, "tp", ("fsdp", "ctx")),
        P(None, ("fsdp", "ctx")),
        P(None, ("fsdp", "ctx"), None),
        P(),
        P(None, None, ("fsdp", "ctx"), None),
        P(None, None, ("fsdp", "ctx")),
        P(None, None, ("fsdp", "ctx"), None, "tp"),
        P(None, None, "tp", ("fsdp", "ctx")),
    )
    return jax.shard_map(
        functools.partial(per_device, hyper, axes),
        mesh=mesh,
        in_specs=in_specs,
        out_specs=out_specs,
        check_vma=False,
    )
```

```python
import functools

import jax
import jax.numpy as jnp
from jax import lax
from jax.experimental import pallas as pl
from jax.experimental.pallas import tpu as pltpu
from jax.sharding import PartitionSpec as P

HD = 64
NF = 8
NE = 12
BLOCK = 512
CAP = 128
TILE = 256
EPSILON = 1e-06
MASKED = -1e30
F32 = jnp.float32
BF16 = jnp.bfloat16
HIGH = lax.Precision.HIGHEST
ROW_CONST, ROW_VEC, ROW_GA, ROW_GM = 16, 20, 22, 23
VMEM_LIMIT = 58 * 1024 * 1024
SCALE = 0.05
PACK = 128

NN = (((1,), (0,)), ((), ()))
NT = (((1,), (1,)), ((), ()))
TN = (((0,), (0,)), ((), ()))


def mm(left, right, dims=NN, precision=None):
    return lax.dot_general(left, right, dims, precision=precision, preferred_element_type=F32)


def kernel_params():
    return pltpu.CompilerParams(vmem_limit_bytes=VMEM_LIMIT)


def cost(flops, nbytes, trans=0):
    return pl.CostEstimate(
        flops=int(flops * SCALE), bytes_accessed=int(nbytes * SCALE), transcendentals=int(trans * SCALE)
    )


def iota(shape, dim):
    return lax.broadcasted_iota(jnp.int32, shape, dim)


def full_spec(shape):
    zeros = (0,) * len(shape)
    return pl.BlockSpec(shape, lambda *idx: zeros)


SMEM_SPEC = pl.BlockSpec(memory_space=pltpu.SMEM)


def pad_rows(rows, count, width):
    row_id = iota((count, width), 0)
    out = jnp.zeros((count, width), F32)
    for place, row in rows:
        out = jnp.where(row_id == place, row, out)
    return out


def round_up(value, unit):
    return -(-value // unit) * unit


def prep_kernel(count, rows, out_cols, offs_ref, *refs):
    qkv_ref, vec_ref, wo_refs = refs[count], refs[count + 1], refs[count + 2 : -2]
    scr_ref, wo_scr = refs[-2:]
    cols = qkv_ref.shape[1]
    for piece in range(count):
        start = pl.multiple_of(offs_ref[piece] * rows, rows)
        block = refs[piece][...]
        qkv_ref[pl.ds(start, rows), :] = block[:, :cols]
        scr_ref[pl.ds(start, rows), :] = block[:, cols : cols + PACK].astype(F32)
        for rank in range(len(wo_refs)):
            first = cols + PACK + rank * out_cols
            wo_scr[rank, pl.ds(start, rows), :out_cols] = block[:, first : first + out_cols]
    vec_ref[...] = scr_ref[...].T[:32]
    total = wo_scr.shape[1]
    rest = out_cols - 128
    for rank, ref in enumerate(wo_refs):
        ref[:total, :] = wo_scr[rank, :, :128]
        ref[total:, :rest] = wo_scr[rank, : total // 2, 128:out_cols]
        ref[total:, rest:] = wo_scr[rank, total // 2 :, 128:out_cols]


def prep_weights(pieces, offs, feature_dim, qkv_cols, out_cols, out_count):
    count = len(pieces)
    cols = round_up(qkv_cols, 128)
    vmem = pl.BlockSpec(memory_space=pltpu.VMEM)
    outs = pl.pallas_call(
        functools.partial(prep_kernel, count, feature_dim // count, out_cols),
        out_shape=tuple(
            [
                jax.ShapeDtypeStruct((feature_dim, cols), BF16),
                jax.ShapeDtypeStruct((32, feature_dim), F32),
            ]
            + [jax.ShapeDtypeStruct((feature_dim * 3 // 2, 128), BF16)] * out_count
        ),
        in_specs=[SMEM_SPEC] + [vmem] * count,
        out_specs=tuple([vmem] * (2 + out_count)),
        scratch_shapes=[
            pltpu.VMEM((feature_dim, PACK), F32),
            pltpu.VMEM((out_count, feature_dim, 256), BF16),
        ],
        compiler_params=kernel_params(),
        cost_estimate=cost(1e6, 3e6),
        name="prep",
    )(offs, *pieces)
    return outs[0], outs[1], list(outs[2:])


def pack_kernel(count, rows, offs_ref, dqkv_ref, dwo_ref, dvec_ref, dgain_ref, *refs):
    outs, scr_ref = refs[:-1], refs[-1]
    cols, out_cols = dqkv_ref.shape[1], dwo_ref.shape[1]
    scr_ref[:, :cols] = dqkv_ref[...]
    scr_ref[:, cols : cols + out_cols] = dwo_ref[...]
    vec = dvec_ref[...]
    vec = jnp.where(iota(vec.shape, 0) == ROW_GA, dgain_ref[0:1, :], vec)
    wide = jnp.concatenate([vec, jnp.zeros((PACK - vec.shape[0], vec.shape[1]), F32)], axis=0).T
    scr_ref[:, cols + out_cols :] = wide
    for piece in range(count):
        start = pl.multiple_of(offs_ref[piece] * rows, rows)
        block = scr_ref[pl.ds(start, rows), :].astype(BF16)
        if count > 1:
            outs[piece % 2][piece // 2] = block
        else:
            outs[0][...] = block


def pack_grads(dqkv, dwo, dvec, dgain, offs):
    feature_dim = dqkv.shape[0]
    count = offs.shape[0]
    rows = feature_dim // count
    width = dqkv.shape[1] + dwo.shape[1] + PACK
    shape = (count // 2, rows, width) if count > 1 else (feature_dim, width)
    vmem = pl.BlockSpec(memory_space=pltpu.VMEM)
    outs = 2 if count > 1 else 1
    return pl.pallas_call(
        functools.partial(pack_kernel, count, rows),
        out_shape=tuple([jax.ShapeDtypeStruct(shape, BF16)] * outs),
        in_specs=[SMEM_SPEC, vmem, vmem, vmem, vmem],
        out_specs=tuple([vmem] * outs),
        scratch_shapes=[pltpu.VMEM((feature_dim, width), F32)],
        compiler_params=kernel_params(),
        cost_estimate=cost(1e6, 6e6),
        name="pack_grads",
    )(offs, dqkv, dwo, dvec, dgain)


def pack_wide_kernel(gu_ref, down_ref, low_ref, high_ref):
    units = down_ref.shape[-1]

    def write(ref):
        ref[0, :, :units] = gu_ref[0, 0, :, 0, :]
        ref[0, :, units : 2 * units] = gu_ref[0, 0, :, 1, :]
        ref[0, :, 2 * units :] = down_ref[0, 0]

    @pl.when(pl.program_id(0) < NF // 2)
    def _():
        write(low_ref)

    @pl.when(pl.program_id(0) >= NF // 2)
    def _():
        write(high_ref)


def pack_wide(w_gate_up, w_down_t, layer):
    _, _, rows, _, units = w_gate_up.shape
    half = NF // 2
    specs = [
        pl.BlockSpec(
            (1, rows, 3 * units), lambda e, part=part: (jnp.clip(e - part * half, 0, half - 1), 0, 0)
        )
        for part in range(2)
    ]
    return pl.pallas_call(
        pack_wide_kernel,
        grid=(NF,),
        out_shape=tuple([jax.ShapeDtypeStruct((half, rows, 3 * units), BF16)] * 2),
        in_specs=[
            pl.BlockSpec((1, 1, rows, 2, units), lambda e: (layer, e, 0, 0, 0)),
            pl.BlockSpec((1, 1, rows, units), lambda e: (layer, e, 0, 0)),
        ],
        out_specs=tuple(specs),
        compiler_params=kernel_params(),
        cost_estimate=cost(1e6, 5e6),
        name="pack_wide",
    )(w_gate_up, w_down_t)


def qkv_kernel(with_ffn, *refs):
    if with_ffn:
        base_ref, ffn_ref, vec_ref, w_ref, h_ref, qkv_ref = refs
        hidden = base_ref[...] + ffn_ref[...].astype(F32)
        h_ref[...] = hidden
    else:
        base_ref, vec_ref, w_ref, qkv_ref = refs
        hidden = base_ref[...].astype(F32)
    gain = vec_ref[ROW_GA : ROW_GA + 1, :]
    scale = lax.rsqrt(jnp.mean(hidden * hidden, axis=-1, keepdims=True) + EPSILON)
    attn_in = (hidden * scale * gain).astype(BF16)
    qkv_ref[...] = mm(attn_in, w_ref[...]).astype(BF16)


def qkv_part(base, ffn, vecs, w_qkv):
    rows, feature_dim = base.shape
    cols = round_up(w_qkv.shape[1], 128)
    row_spec = pl.BlockSpec((TILE, feature_dim), lambda i: (i, 0))
    with_ffn = ffn is not None
    out_shape = [jax.ShapeDtypeStruct((rows, cols), BF16)]
    out_specs = [pl.BlockSpec((TILE, cols), lambda i: (i, 0))]
    if with_ffn:
        out_shape = [jax.ShapeDtypeStruct((rows, feature_dim), F32)] + out_shape
        out_specs = [row_spec] + out_specs
    ins = [base] + ([ffn] if with_ffn else []) + [vecs, w_qkv]
    in_specs = [row_spec] * (2 if with_ffn else 1) + [full_spec(vecs.shape), full_spec(w_qkv.shape)]
    return pl.pallas_call(
        functools.partial(qkv_kernel, with_ffn),
        grid=(rows // TILE,),
        out_shape=tuple(out_shape),
        in_specs=in_specs,
        out_specs=tuple(out_specs),
        compiler_params=kernel_params(),
        cost_estimate=cost(2 * rows * feature_dim * cols, rows * feature_dim * 10),
        name="qkv_part",
    )(*ins)


def attn_masks(ctx, length, tile, width):
    row = iota((TILE, width), 0) + tile * TILE
    col = iota((TILE, width), 1)
    return (col <= row) & (col + ctx * BLOCK < length)


def attn_fwd_kernel(heads, info_ref, own_ref, other_ref, ctx_ref, lse_ref):
    ctx = info_ref[0]
    length = info_ref[1 + pl.program_id(0)]
    own = own_ref[...]
    other = other_ref[...]
    for head in range(heads):
        col = head * 3 * HD
        k_own = own[:, col + HD : col + 2 * HD]
        v_own = own[:, col + 2 * HD : col + 3 * HD]
        k_oth = other[:, col + HD : col + 2 * HD]
        v_oth = other[:, col + 2 * HD : col + 3 * HD]
        for tile in range(BLOCK // TILE):
            width = (tile + 1) * TILE
            query = own[tile * TILE : (tile + 1) * TILE, col : col + HD] * BF16(HD**-0.5)
            s_own = mm(query, k_own[:width], NT)
            s_own = jnp.where(attn_masks(ctx, length, tile, width), s_own, MASKED)
            s_oth = jnp.where(ctx > 0, mm(query, k_oth, NT), MASKED)
            top = jnp.maximum(
                jnp.max(s_own, axis=-1, keepdims=True), jnp.max(s_oth, axis=-1, keepdims=True)
            )
            p_own = jnp.exp(s_own - top)
            p_oth = jnp.exp(s_oth - top)
            total = jnp.sum(p_own, axis=-1, keepdims=True) + jnp.sum(p_oth, axis=-1, keepdims=True)
            out = mm(p_own.astype(BF16), v_own[:width]) + mm(p_oth.astype(BF16), v_oth)
            out = out / total
            rows = slice(tile * TILE, (tile + 1) * TILE)
            ctx_ref[head * TILE : (head + 1) * TILE, tile * HD : (tile + 1) * HD] = out.astype(BF16)
            lse_ref[rows, head : head + 1] = top + jnp.log(total)


def attend_forward(qkv, other, info, heads):
    rows, cols = qkv.shape
    count = rows // BLOCK
    spec = pl.BlockSpec((BLOCK, cols), lambda i: (i, 0))
    return pl.pallas_call(
        functools.partial(attn_fwd_kernel, heads),
        grid=(count,),
        out_shape=(
            jax.ShapeDtypeStruct((count * heads * TILE, 2 * HD), BF16),
            jax.ShapeDtypeStruct((rows, 8), F32),
        ),
        in_specs=[SMEM_SPEC, spec, spec],
        out_specs=(
            pl.BlockSpec((heads * TILE, 2 * HD), lambda i: (i, 0)),
            pl.BlockSpec((BLOCK, 8), lambda i: (i, 0)),
        ),
        compiler_params=kernel_params(),
        cost_estimate=cost(rows * 1024 * heads * HD * 16, rows * cols * 6, rows * heads * 1024),
        name="attend_forward",
    )(info, qkv, other)


def attn_bwd_kernel(heads, info_ref, own_ref, other_ref, lse_ref, gctx_ref, gown_ref, goth_ref):
    ctx = info_ref[0]
    length = info_ref[1 + pl.program_id(0)]
    own = own_ref[...]
    other = other_ref[...]
    scale = BF16(HD**-0.5)
    for head in range(heads):
        col = head * 3 * HD
        k_own = own[:, col + HD : col + 2 * HD]
        v_own = own[:, col + 2 * HD : col + 3 * HD]
        k_oth = other[:, col + HD : col + 2 * HD]
        v_oth = other[:, col + 2 * HD : col + 3 * HD]
        goth_ref[:, col : col + HD] = jnp.zeros((BLOCK, HD), BF16)
        gk_own, gv_own, gk_oth, gv_oth = [], [], [], []
        for tile in range(BLOCK // TILE):
            width = (tile + 1) * TILE
            rows = slice(tile * TILE, (tile + 1) * TILE)
            query = own[rows, col : col + HD] * scale
            gout = gctx_ref[rows, head * HD : (head + 1) * HD]
            lse = lse_ref[rows, head : head + 1]
            s_own = mm(query, k_own[:width], NT)
            s_own = jnp.where(attn_masks(ctx, length, tile, width), s_own, MASKED)
            s_oth = jnp.where(ctx > 0, mm(query, k_oth, NT), MASKED)
            p_own = jnp.exp(s_own - lse)
            p_oth = jnp.exp(s_oth - lse)
            d_own = mm(gout, v_own[:width], NT)
            d_oth = mm(gout, v_oth, NT)
            inner = jnp.sum(p_own * d_own, axis=-1, keepdims=True) + jnp.sum(
                p_oth * d_oth, axis=-1, keepdims=True
            )
            ds_own = (p_own * (d_own - inner)).astype(BF16)
            ds_oth = (p_oth * (d_oth - inner)).astype(BF16)
            p_own = p_own.astype(BF16)
            p_oth = p_oth.astype(BF16)
            gown_ref[rows, col : col + HD] = (mm(ds_own, k_own[:width]) + mm(ds_oth, k_oth)) * (
                HD**-0.5
            )
            gk_own.append(mm(ds_own, query, TN))
            gv_own.append(mm(p_own, gout, TN))
            gk_oth.append(mm(ds_oth, query, TN))
            gv_oth.append(mm(p_oth, gout, TN))
        gown_ref[:TILE, col + HD : col + 2 * HD] = gk_own[0] + gk_own[1][:TILE]
        gown_ref[TILE:, col + HD : col + 2 * HD] = gk_own[1][TILE:]
        gown_ref[:TILE, col + 2 * HD : col + 3 * HD] = gv_own[0] + gv_own[1][:TILE]
        gown_ref[TILE:, col + 2 * HD : col + 3 * HD] = gv_own[1][TILE:]
        goth_ref[:, col + HD : col + 2 * HD] = (gk_oth[0] + gk_oth[1]).astype(BF16)
        goth_ref[:, col + 2 * HD : col + 3 * HD] = (gv_oth[0] + gv_oth[1]).astype(BF16)


def attend_backward(qkv, other, lse, grad_context, info, heads):
    rows, width = qkv.shape
    cols = heads * 3 * HD
    spec = pl.BlockSpec((BLOCK, width), lambda i: (i, 0))
    return pl.pallas_call(
        functools.partial(attn_bwd_kernel, heads),
        grid=(rows // BLOCK,),
        out_shape=(
            jax.ShapeDtypeStruct((rows, cols), F32),
            jax.ShapeDtypeStruct((rows, width), BF16),
        ),
        in_specs=[
            SMEM_SPEC,
            spec,
            spec,
            pl.BlockSpec((BLOCK, 8), lambda i: (i, 0)),
            pl.BlockSpec((BLOCK, heads * HD), lambda i: (i, 0)),
        ],
        out_specs=(pl.BlockSpec((BLOCK, cols), lambda i: (i, 0)), spec),
        compiler_params=kernel_params(),
        cost_estimate=cost(rows * 1024 * heads * HD * 40, rows * cols * 12, rows * heads * 1024),
        name="attend_backward",
    )(info, qkv, other, lse, grad_context)


def alpha_rows(gate_in, const_idx):
    first = gate_in[ROW_CONST + 2 * const_idx : ROW_CONST + 2 * const_idx + 1]
    second = gate_in[ROW_CONST + 2 * const_idx + 1 : ROW_CONST + 2 * const_idx + 2]
    return pair(first, second)


def pair(first, second):
    top = jnp.maximum(first, second)
    exp_first = jnp.exp(first - top)
    exp_second = jnp.exp(second - top)
    total = exp_first + exp_second
    return exp_first / total, exp_second / total


def picks(route, value):
    return (route == value).astype(F32)


def gate_coefs(routes, gates, alphas):
    copy = picks(routes[0], NF + 1) * gates[0] + picks(routes[1], NF + 1) * gates[1]
    const = [
        picks(routes[0], NF + 2 + j) * gates[0] + picks(routes[1], NF + 2 + j) * gates[1]
        for j in range(2)
    ]
    on_normed = copy + const[0] * alphas[0][0] + const[1] * alphas[1][0]
    on_vec = [const[j] * alphas[j][1] for j in range(2)]
    return const, on_normed, on_vec


def to_columns(rows):
    width = rows[0].shape[1]
    return pad_rows(list(enumerate(rows)), 128, width).T


def unpack_context(both):
    heads = both.shape[0] // TILE
    side = lax.rem(pl.program_id(0), 2) == 0
    both = jnp.where(side, both[:, :HD], both[:, HD:])
    parts = [both[head * TILE : (head + 1) * TILE] for head in range(heads)]
    return jnp.concatenate(parts, axis=1)


def middle_kernel(with_prev, rank_ref, *refs):
    h_ref, ctx_ref, refs = refs[0], refs[1], refs[2:]
    count = ctx_ref.shape[0]
    wo_refs, refs = refs[:count], refs[count:]
    if with_prev:
        vec_ref, route_ref, prev_ref, resid_ref = refs[:4]
        refs = refs[4:]
    else:
        vec_ref, route_ref = refs[:2]
        refs = refs[2:]
    mid_ref, base_ref, xm_ref, gate_ref, logit_ref = refs
    attn_out = 0.0
    for back, ref in enumerate(wo_refs):
        context = unpack_context(ctx_ref[lax.rem(rank_ref[0] + count - back, count)])
        total = ref.shape[0] * 2 // 3
        rest = context[:, 128:]
        attn_out += mm(context[:, :128], ref[:total], NT) + jnp.concatenate(
            [mm(rest, ref[total:, :HD], NT), mm(rest, ref[total:, HD:], NT)], axis=1
        )
    middle = h_ref[...].astype(F32) + attn_out
    mid_ref[...] = middle
    vecs = vec_ref[...]
    scale = lax.rsqrt(jnp.mean(middle * middle, axis=-1, keepdims=True) + EPSILON)
    normed = middle * scale * vecs[ROW_GM : ROW_GM + 1]
    xm_low = normed.astype(BF16)
    xm_ref[...] = xm_low
    gate_in = mm(vecs[:32].astype(BF16), xm_low, NT)
    logits = gate_in[:16]
    if with_prev:
        logits = logits + mm(resid_ref[...], prev_ref[...], TN, HIGH)
    logit_ref[...] = logits
    routes = (route_ref[0:1], route_ref[1:2])
    expert = iota(logits.shape, 0)
    chosen = [
        jnp.sum(jnp.where(expert == route, logits, 0.0), axis=0, keepdims=True) for route in routes
    ]
    gates = pair(chosen[0], chosen[1])
    gate_ref[...] = pad_rows(list(enumerate(gates)), 8, logits.shape[1])
    alphas = [alpha_rows(gate_in, j) for j in range(2)]
    const, on_normed, on_vec = gate_coefs(routes, gates, alphas)
    cols = to_columns([on_normed, on_vec[0], on_vec[1]])
    base_ref[...] = (
        middle
        + cols[:, 0:1] * normed
        + cols[:, 1:2] * vecs[ROW_VEC : ROW_VEC + 1]
        + cols[:, 2:3] * vecs[ROW_VEC + 1 : ROW_VEC + 2]
    )


def middle_part(h, ctx_all, wo_all, vecs, routes_t, prev_t, resid, rank):
    rows, feature_dim = h.shape
    tp_count, packed, lanes = ctx_all.shape
    packed = packed * BLOCK // rows
    row_spec = pl.BlockSpec((TILE, feature_dim), lambda i: (i, 0))
    lane8 = pl.BlockSpec((8, TILE), lambda i: (0, i))
    lane16 = pl.BlockSpec((16, TILE), lambda i: (0, i))
    ins = [rank, h, ctx_all, *wo_all, vecs, routes_t]
    in_specs = [
        SMEM_SPEC,
        row_spec,
        pl.BlockSpec((tp_count, packed, lanes), lambda i: (0, i // 2, 0)),
        *[full_spec(item.shape) for item in wo_all],
        full_spec(vecs.shape),
        lane8,
    ]
    with_prev = prev_t is not None
    if with_prev:
        ins += [prev_t, resid]
        in_specs += [lane16, full_spec(resid.shape)]
    return pl.pallas_call(
        functools.partial(middle_kernel, with_prev),
        grid=(rows // TILE,),
        out_shape=(
            jax.ShapeDtypeStruct((rows, feature_dim), F32),
            jax.ShapeDtypeStruct((rows, feature_dim), F32),
            jax.ShapeDtypeStruct((rows, feature_dim), BF16),
            jax.ShapeDtypeStruct((8, rows), F32),
            jax.ShapeDtypeStruct((16, rows), F32),
        ),
        in_specs=in_specs,
        out_specs=(row_spec, row_spec, row_spec, lane8, lane16),
        compiler_params=kernel_params(),
        cost_estimate=cost(2 * rows * feature_dim * feature_dim, rows * feature_dim * 16),
        name="middle_part",
    )(*ins)


def split(value):
    high = value.astype(BF16)
    return high, (value - high.astype(F32)).astype(BF16)


def gate_bwd_kernel(with_prev, *refs):
    gh_ref, mid_ref, gxm_ref, vec_ref, route_ref, gate_ref, gg_ref, ctx_ref, wo_ref = refs[:9]
    refs = refs[9:]
    if with_prev:
        prev_ref, resid_ref = refs[:2]
        gmid_ref, gctx_ref, dwo_ref, dvec_ref, gprev_ref, dres_ref = refs[2:]
    else:
        gl_ref = refs[0]
        gmid_ref, gctx_ref, dwo_ref, dvec_ref = refs[1:]
    step = pl.program_id(0)
    grad = gh_ref[...].astype(F32)
    middle = mid_ref[...]
    vecs = vec_ref[...]
    gain = vecs[ROW_GM : ROW_GM + 1]
    scale = lax.rsqrt(jnp.mean(middle * middle, axis=-1, keepdims=True) + EPSILON)
    unit = middle * scale
    normed = unit * gain
    xm_low = normed.astype(BF16)
    low_vecs = vecs[:32].astype(BF16)
    gate_in = mm(low_vecs, xm_low, NT)
    alphas = [alpha_rows(gate_in, j) for j in range(2)]
    routes = (route_ref[0:1], route_ref[1:2])
    gates = (gate_ref[0:1], gate_ref[1:2])
    const, on_normed, on_vec = gate_coefs(routes, gates, alphas)
    grad_hi, grad_lo = split(grad)
    vec_dots = mm(low_vecs[16:32], grad_hi, NT) + mm(low_vecs[16:32], grad_lo, NT)
    dot_vec = [vec_dots[ROW_VEC - 16 + j : ROW_VEC - 15 + j] for j in range(2)]
    dot_col = jnp.sum(grad * normed, axis=-1, keepdims=True)
    dot_normed = jnp.broadcast_to(dot_col, (dot_col.shape[0], 128)).T[0:1]
    term = [alphas[j][0] * dot_normed + alphas[j][1] * dot_vec[j] for j in range(2)]
    gate_grads = []
    for slot in range(2):
        fixed = (
            picks(routes[slot], NF + 1) * dot_normed
            + picks(routes[slot], NF + 2) * term[0]
            + picks(routes[slot], NF + 3) * term[1]
        )
        gate_grads.append(jnp.where(routes[slot] < NF, gg_ref[slot : slot + 1], fixed))
    inner = gates[0] * gate_grads[0] + gates[1] * gate_grads[1]
    chosen_grads = [gates[slot] * (gate_grads[slot] - inner) for slot in range(2)]
    expert = iota((16, TILE), 0)
    grad_logits = jnp.where(expert == routes[0], chosen_grads[0], 0.0) + jnp.where(
        expert == routes[1], chosen_grads[1], 0.0
    )
    if not with_prev:
        grad_logits = grad_logits + gl_ref[...]
    alpha_grads = []
    for j in range(2):
        grad_first = const[j] * dot_normed
        grad_second = const[j] * dot_vec[j]
        mean = alphas[j][0] * grad_first + alphas[j][1] * grad_second
        alpha_grads.append((2 * j, alphas[j][0] * (grad_first - mean)))
        alpha_grads.append((2 * j + 1, alphas[j][1] * (grad_second - mean)))
    grad_in = jnp.concatenate([grad_logits, pad_rows(alpha_grads, 16, TILE)], axis=0)
    in_hi, in_lo = split(grad_in)
    low_gate = jnp.where(iota(low_vecs.shape, 0) < ROW_VEC, low_vecs, 0)
    grad_xm = mm(in_hi, low_gate, TN) + mm(in_lo, low_gate, TN)
    cols = to_columns([on_normed])
    grad_y = cols[:, 0:1] * grad + grad_xm + gxm_ref[...].astype(F32)
    weighted = grad_y * gain
    mean = jnp.mean(weighted * unit, axis=-1, keepdims=True)
    grad_mid = grad + scale * (weighted - unit * mean)
    gmid_ref[...] = grad_mid
    low_mid = grad_mid.astype(BF16)
    total = low_mid.shape[1]
    gctx_ref[:, :128] = mm(low_mid, wo_ref[:total]).astype(BF16)
    gctx_ref[:, 128:] = (
        mm(low_mid[:, : total // 2], wo_ref[total:, :HD])
        + mm(low_mid[:, total // 2 :], wo_ref[total:, HD:])
    ).astype(BF16)
    dwo = mm(low_mid, unpack_context(ctx_ref[...]), TN)
    vec_rows = pad_rows([(ROW_VEC - 16 + j, on_vec[j]) for j in range(2)], 16, TILE)
    vec_hi, vec_lo = split(vec_rows)
    dvec_low = mm(vec_hi, grad_hi) + mm(vec_lo, grad_hi)
    dvec_gate = mm(in_hi, xm_low) + mm(in_lo, xm_low)
    dgain = jnp.sum(grad_y * unit, axis=0, keepdims=True)
    row_id = iota(dvec_gate.shape, 0)
    dvec = dvec_gate + jnp.concatenate([jnp.zeros_like(dvec_low), dvec_low], axis=0)
    dvec = jnp.where(row_id == ROW_GM, dgain, dvec)

    @pl.when(step == 0)
    def _():
        dwo_ref[...] = dwo
        dvec_ref[...] = dvec

    @pl.when(step > 0)
    def _():
        dwo_ref[...] += dwo
        dvec_ref[...] += dvec

    if with_prev:
        gprev_ref[...] = mm(resid_ref[...], grad_logits, NN, HIGH)
        dres = mm(prev_ref[...], grad_logits, NT, HIGH)

        @pl.when(step == 0)
        def _():
            dres_ref[...] = dres

        @pl.when(step > 0)
        def _():
            dres_ref[...] += dres


def gate_backward(grad, middle, gxm, vecs, routes_t, gates_t, gg_t, context, wo_own, extra):
    rows, feature_dim = middle.shape
    out_cols = context.shape[0] * BLOCK // rows // TILE * HD
    with_prev = len(extra) == 2
    row_spec = pl.BlockSpec((TILE, feature_dim), lambda i: (i, 0))
    lane8 = pl.BlockSpec((8, TILE), lambda i: (0, i))
    lane16 = pl.BlockSpec((16, TILE), lambda i: (0, i))
    ctx_spec = pl.BlockSpec((context.shape[0] * BLOCK // rows, 2 * HD), lambda i: (i // 2, 0))
    out_spec = pl.BlockSpec((TILE, out_cols), lambda i: (i, 0))
    wo_spec = full_spec(wo_own.shape)
    in_specs = [row_spec, row_spec, row_spec, full_spec(vecs.shape), lane8, lane8, lane8]
    in_specs += [ctx_spec, wo_spec, lane16]
    out_shape = [
        jax.ShapeDtypeStruct((rows, feature_dim), F32),
        jax.ShapeDtypeStruct((rows, out_cols), BF16),
        jax.ShapeDtypeStruct((feature_dim, out_cols), F32),
        jax.ShapeDtypeStruct((32, feature_dim), F32),
    ]
    out_specs = [row_spec, out_spec, full_spec((feature_dim, out_cols)), full_spec((32, feature_dim))]
    if with_prev:
        in_specs.append(full_spec(extra[1].shape))
        out_shape += [jax.ShapeDtypeStruct((16, rows), F32), jax.ShapeDtypeStruct((16, 16), F32)]
        out_specs += [lane16, full_spec((16, 16))]
    return pl.pallas_call(
        functools.partial(gate_bwd_kernel, with_prev),
        grid=(rows // TILE,),
        out_shape=tuple(out_shape),
        in_specs=in_specs,
        out_specs=tuple(out_specs),
        compiler_params=kernel_params(),
        cost_estimate=cost(4 * rows * feature_dim * out_cols, rows * feature_dim * 18),
        name="gate_backward",
    )(grad, middle, gxm, vecs, routes_t, gates_t, gg_t, context, wo_own, *extra)


def qkv_bwd_kernel(gown_ref, goth_ref, h_ref, vec_ref, w_ref, part_ref, dw_ref, dgain_ref):
    step = pl.program_id(0)
    cols = gown_ref.shape[1]
    grad = (gown_ref[...] + goth_ref[:, :cols].astype(F32)).astype(BF16)
    part = mm(grad, w_ref[:, :cols], NT)
    part_ref[...] = part.astype(BF16)
    hidden = h_ref[...].astype(F32)
    gain = vec_ref[ROW_GA : ROW_GA + 1, :]
    scale = lax.rsqrt(jnp.mean(hidden * hidden, axis=-1, keepdims=True) + EPSILON)
    unit = hidden * scale
    attn_in = (unit * gain).astype(BF16)
    dw = mm(attn_in, grad, TN)
    dgain = jnp.broadcast_to(jnp.sum(part * unit, axis=0, keepdims=True), dgain_ref.shape)

    @pl.when(step == 0)
    def _():
        dw_ref[...] = dw
        dgain_ref[...] = dgain

    @pl.when(step > 0)
    def _():
        dw_ref[...] += dw
        dgain_ref[...] += dgain


def qkv_backward(gown, goth, h, vecs, w_qkv):
    rows, feature_dim = h.shape
    cols = gown.shape[1]
    row_spec = pl.BlockSpec((TILE, feature_dim), lambda i: (i, 0))
    col_spec = pl.BlockSpec((TILE, cols), lambda i: (i, 0))
    oth_spec = pl.BlockSpec((TILE, goth.shape[1]), lambda i: (i, 0))
    return pl.pallas_call(
        qkv_bwd_kernel,
        grid=(rows // TILE,),
        out_shape=(
            jax.ShapeDtypeStruct((rows, feature_dim), BF16),
            jax.ShapeDtypeStruct((feature_dim, cols), F32),
            jax.ShapeDtypeStruct((8, feature_dim), F32),
        ),
        in_specs=[col_spec, oth_spec, row_spec, full_spec(vecs.shape), full_spec(w_qkv.shape)],
        out_specs=(row_spec, full_spec((feature_dim, cols)), full_spec((8, feature_dim))),
        compiler_params=kernel_params(),
        cost_estimate=cost(4 * rows * feature_dim * cols, rows * feature_dim * 10),
        name="qkv_backward",
    )(gown, goth, h, vecs, w_qkv)


def norm_bwd_kernel(with_low, gmid_ref, ga_ref, h_ref, vec_ref, out_ref, *rest):
    hidden = h_ref[...].astype(F32)
    gain = vec_ref[ROW_GA : ROW_GA + 1, :]
    scale = lax.rsqrt(jnp.mean(hidden * hidden, axis=-1, keepdims=True) + EPSILON)
    unit = hidden * scale
    grad_y = ga_ref[...].astype(F32)
    weighted = grad_y * gain
    mean = jnp.mean(weighted * unit, axis=-1, keepdims=True)
    grad = gmid_ref[...] + scale * (weighted - unit * mean)
    out_ref[...] = grad
    if with_low:
        rest[0][...] = grad.astype(BF16)


def norm_backward(gmid, ga, h, vecs, with_low):
    rows, feature_dim = gmid.shape
    row_spec = pl.BlockSpec((TILE, feature_dim), lambda i: (i, 0))
    out_shape = [jax.ShapeDtypeStruct((rows, feature_dim), F32)]
    out_specs = [row_spec]
    if with_low:
        out_shape.append(jax.ShapeDtypeStruct((rows, feature_dim), BF16))
        out_specs.append(row_spec)
    return pl.pallas_call(
        functools.partial(norm_bwd_kernel, with_low),
        grid=(rows // TILE,),
        out_shape=tuple(out_shape),
        in_specs=[row_spec, row_spec, row_spec, full_spec(vecs.shape)],
        out_specs=tuple(out_specs),
        compiler_params=kernel_params(),
        cost_estimate=cost(rows * feature_dim * 10, rows * feature_dim * 16),
        name="norm_backward",
    )(gmid, ga, h, vecs)


def experts_kernel(fwd, bwd, blocks, plan, out_count, rows, offs_ref, *refs):
    refs = list(refs)
    xm_ref = refs.pop(0)
    gh_ref = refs.pop(0) if bwd else None
    route_ref, gate_ref = refs.pop(0), refs.pop(0)
    w_refs = [refs.pop(0) for _ in plan]
    ffn_ref = refs.pop(0) if fwd else None
    if bwd:
        gx_ref = refs.pop(0)
        dw_refs = [refs.pop(0) for _ in range(out_count)]
    w_scr, hot_scr, pick_scr = refs.pop(0), refs.pop(0), refs.pop(0)
    part_scr = refs.pop(0) if fwd else None
    if bwd:
        gpart_scr, raw_scr, gg_scr, dw_scr = refs
    expert = pl.program_id(0)
    last = pl.num_programs(0) - 1
    width = w_scr.shape[1]
    units = width // 3

    @pl.when(expert == 0)
    def _():
        order = (iota((BLOCK, BLOCK), 0) < iota((BLOCK, BLOCK), 1)).astype(BF16)
        ids = iota((NF, BLOCK), 0)
        row_ids = iota((CAP, BLOCK), 0).astype(F32)
        for block in range(blocks):
            lanes = slice(block * BLOCK, (block + 1) * BLOCK)
            hits = (ids == route_ref[0:1, lanes]) | (ids == route_ref[1:2, lanes])
            place = jnp.where(hits, mm(hits.astype(BF16), order), -1.0)
            for each in range(NF):
                hot_scr[block, each * CAP : (each + 1) * CAP, :] = (
                    (row_ids == place[each : each + 1]).astype(F32).astype(BF16)
                )
            hot = hot_scr[block]
            for source, target in ((xm_ref, pick_scr),) + (((gh_ref, raw_scr),) if bwd else ()):
                rows_all = mm(hot, source[lanes, :]).astype(BF16)
                for each in range(NF):
                    target[each, block * CAP : (block + 1) * CAP, :] = rows_all[
                        each * CAP : (each + 1) * CAP
                    ]
        if bwd:
            gg_scr[...] = jnp.zeros_like(gg_scr)

    def combine(source, block):
        return mm(hot_scr[block], source[block], TN)

    def fill(ref, off):
        start = pl.multiple_of(offs_ref[off] * rows, rows)
        w_scr[pl.ds(start, rows), :] = ref[0]

    for ref, (off, first, number) in zip(w_refs, plan):
        if number == NF:
            fill(ref, off)
        else:
            pl.when((expert >= first) & (expert < first + number))(
                functools.partial(fill, ref, off)
            )

    hot, gate_cols, masks = [], [], []
    first_row = pl.multiple_of(expert * CAP, CAP)
    for block in range(blocks):
        lanes = slice(block * BLOCK, (block + 1) * BLOCK)
        one_hot = hot_scr[block, pl.ds(first_row, CAP), :].astype(F32)
        mask = [route_ref[slot : slot + 1, lanes] == expert for slot in range(2)]
        gate_row = jnp.where(mask[0], gate_ref[0:1, lanes], 0.0) + jnp.where(
            mask[1], gate_ref[1:2, lanes], 0.0
        )
        gate_cols.append(jnp.sum(one_hot * gate_row, axis=1, keepdims=True))
        hot.append(one_hot)
        masks.append(mask)
    gate_col = jnp.concatenate(gate_cols, axis=0)
    picked = pick_scr[expert]
    gate_up = mm(picked, w_scr[:, : 2 * units])
    gate_in, up_in = gate_up[:, :units], gate_up[:, units:]
    sigmoid = lax.logistic(gate_in)
    silu = gate_in * sigmoid
    hidden = (silu * up_in).astype(BF16)
    if fwd:
        scaled = (mm(hidden, w_scr[:, 2 * units :], NT) * gate_col).astype(BF16)
        for block in range(blocks):
            part_scr[block, pl.ds(first_row, CAP), :] = scaled[block * CAP : (block + 1) * CAP]

        @pl.when(expert == last)
        def _():
            for block in range(blocks):
                ffn_ref[block * BLOCK : (block + 1) * BLOCK, :] = combine(part_scr, block).astype(
                    BF16
                )

    if bwd:
        raw = raw_scr[expert]
        grad_raw = mm(raw, w_scr[:, 2 * units :])
        gate_dot = jnp.sum(hidden.astype(F32) * grad_raw, axis=1, keepdims=True)
        for block in range(blocks):
            row = jnp.sum(
                hot[block] * gate_dot[block * CAP : (block + 1) * CAP],
                axis=0,
                keepdims=True,
            )
            for slot in range(2):
                gg_scr[8 * block + slot : 8 * block + slot + 1, :] += jnp.where(
                    masks[block][slot], row, 0.0
                )
        grad_hidden = grad_raw * gate_col
        grad_gate = grad_hidden * up_in * sigmoid * (1.0 + gate_in * (1.0 - sigmoid))
        grad_up = grad_hidden * silu
        grad_gu = jnp.concatenate([grad_gate.astype(BF16), grad_up.astype(BF16)], axis=1)
        grad_pick = mm(grad_gu, w_scr[:, : 2 * units], NT).astype(BF16)
        for block in range(blocks):
            gpart_scr[block, pl.ds(first_row, CAP), :] = grad_pick[block * CAP : (block + 1) * CAP]
        grad_result = (raw.astype(F32) * gate_col).astype(BF16)
        if out_count == 1:
            dw_refs[0][0, :, : 2 * units] = mm(picked, grad_gu, TN).astype(BF16)
            dw_refs[0][0, :, 2 * units :] = mm(grad_result, hidden, TN).astype(BF16)
        else:
            dw_scr[:, : 2 * units] = mm(picked, grad_gu, TN).astype(BF16)
            dw_scr[:, 2 * units :] = mm(grad_result, hidden, TN).astype(BF16)
            half = NF // 2
            for part in range(2):

                @pl.when((expert >= part * half) & (expert < (part + 1) * half))
                def _(part=part):
                    for off in range(8):
                        start = pl.multiple_of(offs_ref[off] * rows, rows)
                        dw_refs[2 * part + off % 2][off // 2, 0] = dw_scr[pl.ds(start, rows), :]

        @pl.when(expert == last)
        def _():
            total = blocks * BLOCK
            for block in range(blocks):
                gx_ref[block * BLOCK : (block + 1) * BLOCK, :] = combine(gpart_scr, block).astype(
                    BF16
                )
            gx_ref[total : total + 16, :] = jnp.zeros((16, gx_ref.shape[1]), BF16)
            gx_ref[total : total + gg_scr.shape[0], :BLOCK] = gg_scr[...].astype(BF16)


def experts(fwd, bwd, xm, gh, routes_t, gates_t, pieces, offs):
    rows, feature_dim = xm.shape
    blocks = rows // BLOCK
    arrays = [item[0] for item in pieces]
    plan = [item[1:] for item in pieces]
    _, piece_rows, width = arrays[0].shape
    units = width // 3
    split_out = len(pieces) > 1
    half = NF // 2

    ins = [xm] + ([gh] if bwd else []) + [routes_t, gates_t]
    in_specs = [SMEM_SPEC] + [full_spec(item.shape) for item in ins]
    for _, first, number in plan:
        in_specs.append(
            pl.BlockSpec(
                (1, piece_rows, width),
                lambda e, first=first, number=number: (jnp.clip(e - first, 0, number - 1), 0, 0),
            )
        )
    out_shape, out_specs, scratch = [], [], []
    scratch += [
        pltpu.VMEM((feature_dim, width), BF16),
        pltpu.VMEM((blocks, NF * CAP, BLOCK), BF16),
        pltpu.VMEM((NF, blocks * CAP, feature_dim), BF16),
    ]
    flops = 0
    out_count = 4 if split_out else 1
    if fwd:
        out_shape.append(jax.ShapeDtypeStruct((rows, feature_dim), BF16))
        out_specs.append(full_spec((rows, feature_dim)))
        scratch.append(pltpu.VMEM((blocks, NF * CAP, feature_dim), BF16))
        flops += 1.0e9 * NF * blocks / 2
    if bwd:
        out_shape.append(jax.ShapeDtypeStruct((rows + 16, feature_dim), BF16))
        out_specs.append(full_spec((rows + 16, feature_dim)))
        if split_out:
            for part in range(2):
                for _ in range(2):
                    out_shape.append(jax.ShapeDtypeStruct((4, half, piece_rows, width), BF16))
                    out_specs.append(
                        pl.BlockSpec(
                            (4, 1, piece_rows, width),
                            lambda e, part=part: (0, jnp.clip(e - part * half, 0, half - 1), 0, 0),
                        )
                    )
        else:
            out_shape.append(jax.ShapeDtypeStruct((NF, feature_dim, width), BF16))
            out_specs.append(pl.BlockSpec((1, feature_dim, width), lambda e: (e, 0, 0)))
        scratch += [
            pltpu.VMEM((blocks, NF * CAP, feature_dim), BF16),
            pltpu.VMEM((NF, blocks * CAP, feature_dim), BF16),
            pltpu.VMEM((blocks * 8, BLOCK), F32),
            pltpu.VMEM((feature_dim, width) if split_out else (8, 128), BF16),
        ]
        flops += 2.2e9 * NF * blocks / 2
    outs = pl.pallas_call(
        functools.partial(experts_kernel, fwd, bwd, blocks, plan, out_count, piece_rows),
        grid=(NF,),
        out_shape=tuple(out_shape),
        in_specs=in_specs,
        out_specs=tuple(out_specs),
        scratch_shapes=scratch,
        compiler_params=kernel_params(),
        cost_estimate=cost(flops, 20e6 * (2 if bwd else 1), rows * units * 8),
        name="experts",
    )(offs, *ins, *arrays)
    outs = list(outs)
    ffn = outs.pop(0) if fwd else None
    return (ffn, outs[0], outs[1:]) if bwd else (ffn, None, None)


def final_kernel(with_old, count, *refs):
    parts = refs[:count]
    gu_ref, dn_ref = refs[-2:]
    del with_old
    half = count // 2
    units = gu_ref.shape[-1]

    def write(group):
        total = group[0][...].reshape(group[0].shape[-2:]).astype(F32)
        for ref in group[1:]:
            total += ref[...].reshape(ref.shape[-2:]).astype(F32)
        gu_ref[0, 0, :, 0, :] = total[:, :units]
        gu_ref[0, 0, :, 1, :] = total[:, units : 2 * units]
        dn_ref[0, 0] = total[:, 2 * units :]

    @pl.when(pl.program_id(0) < NF // 2)
    def _():
        write(parts[:half])

    @pl.when(pl.program_id(0) >= NF // 2)
    def _():
        write(parts[half:])


def final_sums(lows, highs, old, layer, layer_count):
    half = NF // 2
    specs, arrays = [], []
    for part, group in enumerate((lows, highs)):
        for item in group:
            lead = (1,) * (item.ndim - 3)
            specs.append(
                pl.BlockSpec(
                    lead + (1,) + item.shape[-2:],
                    lambda e, part=part, lead=lead: (0,) * len(lead)
                    + (jnp.clip(e - part * half, 0, half - 1), 0, 0),
                )
            )
            arrays.append(item)
    count = len(arrays)
    rows, width = arrays[0].shape[-2:]
    units = width // 3
    aliases = {}
    if old is not None:
        specs += [pl.BlockSpec(memory_space=pl.ANY)] * 2
        arrays += list(old)
        aliases = {count: 0, count + 1: 1}
    return pl.pallas_call(
        functools.partial(final_kernel, old is not None, count),
        grid=(NF,),
        out_shape=(
            jax.ShapeDtypeStruct((layer_count, NF, rows, 2, units), F32),
            jax.ShapeDtypeStruct((layer_count, NF, rows, units), F32),
        ),
        in_specs=specs,
        out_specs=(
            pl.BlockSpec((1, 1, rows, 2, units), lambda e: (layer, e, 0, 0, 0)),
            pl.BlockSpec((1, 1, rows, units), lambda e: (layer, e, 0, 0)),
        ),
        input_output_aliases=aliases,
        compiler_params=kernel_params(),
        cost_estimate=cost(1e7, NF * rows * width * 12),
        name="final_sums",
    )(*arrays)


def hop(value, step):
    return lax.ppermute(value, "fsdp", [(i, i ^ step) for i in range(4)])


def swap(value):
    return lax.ppermute(value, "ctx", [(0, 1), (1, 0)])


def gather_small(value):
    by_x, by_y, by_d = hop(value, 1), hop(value, 2), hop(value, 3)
    out = []
    for item in (value, by_x, by_y, by_d):
        out += [item, swap(item)]
    return out


def turn(value, steps, count):
    return lax.ppermute(value, "tp", [(i, (i + steps) % count) for i in range(count)])


def share(value, count):
    return [value] + [turn(value, k, count) for k in range(1, count)]


def gather_cores(lows, highs, swapped):
    half = NF // 2
    out = []
    for first, items, done in ((0, lows, swapped[0]), (half, highs, swapped[1])):
        for chip, item in enumerate(items):
            other = done[chip] if chip in done else swap(item)
            out += [(item, 2 * chip, first, half), (other, 2 * chip + 1, first, half)]
    return out


def tie(*values):
    return lax.optimization_barrier(values)


def add_low(*terms):
    total = terms[0].astype(F32)
    for term in terms[1:]:
        total = total + term.astype(F32)
    return total.astype(BF16)


def scatter_cores(keep, send, first):
    other = swap(send)
    if first == 1:
        out = add_low(keep[1::2], other[1::2])
    else:
        out = add_low(keep[2:], other[2:])
    return keep, other, out


def scatter_first(keep, other, out, first):
    return scatter_beside(keep, other, hop(out, first), first)


def scatter_beside(keep, other, got, first):
    return keep, other, got, add_low(keep[3 - first], other[3 - first], got[1])


def scatter_second(terms, first):
    return terms[:3] + (hop(terms[3], 3 - first),)


def per_device(
    hyper,
    axes,
    tokens,
    cotangent,
    lengths,
    routes,
    norm_attn,
    w_qkv,
    w_out,
    norm_moe,
    w_router,
    w_resid,
    w_const,
    v_const,
    w_gate_up,
    w_down,
):
    micro_count, seq_count, block_len, feature_dim = tokens.shape
    rows = micro_count * seq_count * block_len
    layer_count, shard_rows, qkv_cols = w_qkv.shape
    heads = qkv_cols // (3 * HD)
    units = w_gate_up.shape[-1]
    groups = ("fsdp", "ctx")
    shard_count = feature_dim // shard_rows
    ctx = lax.axis_index("ctx")
    me = lax.axis_index("fsdp") * axes["ctx"] + ctx
    rank = lax.axis_index("tp").reshape(1)
    if hyper:
        offs = me ^ jnp.arange(shard_count, dtype=jnp.int32)
    else:
        offs = jnp.zeros((1,), jnp.int32)
    info = jnp.concatenate([ctx.reshape(1), lengths.reshape(-1)]).astype(jnp.int32)
    resid = jnp.zeros((16, 16), F32).at[:NE, :NE].set(w_resid.astype(F32))

    tp_count = axes["tp"]
    outer = share(jnp.transpose(w_out, (0, 2, 1)), tp_count)
    small, wide = [], []
    for layer in range(layer_count):
        vec = jnp.concatenate(
            [
                w_router[layer],
                jnp.zeros((shard_rows, ROW_CONST - NE), BF16),
                w_const[layer, 0],
                w_const[layer, 1],
                v_const[layer].T,
                norm_attn[layer][:, None],
                norm_moe[layer][:, None],
                jnp.zeros((shard_rows, PACK - ROW_GM - 1), BF16),
            ],
            axis=1,
        )
        pad = jnp.zeros((shard_rows, round_up(qkv_cols, 128) - qkv_cols), BF16)
        turned = [item[layer] for item in outer]
        small.append(jnp.concatenate([w_qkv[layer], pad, vec] + turned, axis=1))
        wide.append(pack_wide(w_gate_up, jnp.swapaxes(w_down, 2, 3), layer))
    weights, wide_first = [None] * layer_count, [None] * layer_count

    def fetch_small(layer, after):
        own = small[layer]
        if hyper:
            own, _ = tie(own, after)
            pieces = gather_small(own)
            fetch_first(layer, [pieces[k] for k in (2, 4, 6)])
        else:
            pieces = [lax.all_gather(own, groups, axis=0, tiled=True)]
        outs = prep_weights(pieces, offs, feature_dim, qkv_cols, heads * HD, tp_count)
        weights[layer] = [outs[0], outs[2], outs[1]]

    def fetch_first(layer, after):
        (low, high), _ = tie(wide[layer], after)
        lows, highs = [low, None, hop(low, 2)], [high, hop(high, 1), None]
        if layer > 0:
            lows[1], highs[2] = hop(low, 1), hop(high, 2)
        wide_first[layer] = (lows, highs, [swap(low), swap(high)] if layer == 0 else [])

    def fetch_rest(layer, value):
        if hyper:
            value, (lows, highs, own) = tie(value, wide_first[layer])
            swapped[layer] = ({0: own[0]}, {0: own[1]}) if own else ({}, {})
            value = swap(value)
            if layer == 0:
                lows[1], highs[2] = hop(lows[0], 1), hop(highs[0], 2)
            lows.append(hop(lows[2], 1))
            highs.append(hop(highs[1], 2))
            rests[layer] = (lows, highs)
        else:
            value = swap(value)
        return value

    def fetch_cores(layer, after):
        if hyper:
            lows, highs = rests[layer]
            if layer == 0:
                swapped[0][0][2], swapped[0][1][1] = swap(lows[2]), swap(highs[1])
                after, swapped[0] = tie(after, swapped[0])
                if layer + 1 < layer_count:
                    mid, wide[layer + 1] = tie((lows[1], highs[2]), wide[layer + 1])
                    lows[1], highs[2] = mid
            else:
                (lows, highs), _ = tie((lows, highs), after)
            rests[layer] = (lows, highs)
        else:
            both = jnp.concatenate(wide[layer], axis=0)
            full = lax.all_gather(both, groups, axis=1, tiled=True)
            weights[layer].append([(full, 0, 0, NF)])
        return after

    def fetch_last(layer, after):
        if hyper:
            lows, highs = rests[layer]
            if layer == 0:
                (lows[3], highs[3]), _ = tie((lows[3], highs[3]), after)
            weights[layer].append(gather_cores(lows, highs, swapped[layer]))

    rests, swapped = [None] * layer_count, [None] * layer_count
    fetch_small(0, info)

    routes_t = jnp.moveaxis(routes.reshape(layer_count, rows, 2), 2, 1)
    routes_t = jnp.concatenate(
        [routes_t, jnp.full((layer_count, 6, rows), -1, jnp.int32)], axis=1
    )
    position = ctx * block_len + jnp.arange(block_len, dtype=jnp.int32)
    valid = position[None, None, :] < lengths[:, :, None]
    cot = jnp.where(valid[..., None], cotangent, 0).reshape(rows, feature_dim)

    base, ffn, prev_t = tokens.reshape(rows, feature_dim), None, None
    saved = []
    for layer in range(layer_count):
        qkv_full, _, vecs = weights[layer][:3]
        outs = qkv_part(base, ffn, vecs, qkv_full)
        h_in, qkv = outs if ffn is not None else (base, outs[0])
        other = fetch_rest(layer, qkv)
        context, lse = attend_forward(qkv, other, info, heads)
        ctx_all = lax.all_gather(fetch_cores(layer, context), "tp", axis=0)
        wo_all = weights[layer][1]
        middle, base, xm_low, gates_t, logits_t = middle_part(
            h_in, ctx_all, wo_all, vecs, routes_t[layer], prev_t, resid, rank
        )
        fetch_last(layer, xm_low)
        pieces = weights[layer][3]
        saved.append((h_in, qkv, other, context, lse, middle, xm_low, gates_t, prev_t))
        prev_t = logits_t
        if layer < layer_count - 1:
            part, _, _ = experts(True, False, xm_low, None, routes_t[layer], gates_t, pieces, offs)
            fetch_small(layer + 1, part)
            ffn = lax.psum(part, "tp")
            if hyper:
                ffn, wide_first[layer + 1] = tie(ffn, wide_first[layer + 1])

    grad, grad_low = cot, cot
    grad_logits, wide_out, pending, small_terms, late = None, None, None, None, None
    finals = [None] * layer_count
    for layer in reversed(range(layer_count)):
        qkv_full, wo_all, vecs, pieces = weights[layer]
        h_in, qkv, other, context, lse, middle, xm_low, gates_t, prev_t = saved[layer]
        top = layer == layer_count - 1
        part, gx, grads = experts(
            top, True, xm_low, grad_low, routes_t[layer], gates_t, pieces, offs
        )
        if not top and late is not None:
            late[0] = lax.psum(late[0], "tp")
            gx, grads, late, pending = tie(gx, grads, late, pending)
        gx = lax.psum(gx, "tp")
        if hyper:
            sums = [scatter_cores(grads[2 * k], grads[2 * k + 1], k + 1) for k in range(2)]
            got = [hop(sums[k][2], k + 1) for k in range(2)]
            if pending is not None:
                wide_terms, small_parts, dres = pending
                terms = [scatter_second(wide_terms[k], k + 1) for k in range(2)]
                terms, sums = tie(terms, sums)
                wide_out = final_sums(terms[0], terms[1], wide_out, layer + 1, layer_count)
                upper = scatter_cores(*pack_grads(*small_parts, offs), 1)
                gx, sums, wide_out, upper = tie(gx, sums, wide_out, upper)
                upper_got = hop(upper[2], 1)
            else:
                gx, sums = tie(gx, sums)
        if top:
            base_top = base
        else:
            late[1], gx = tie(late[1], gx)
            late[1] = lax.psum(late[1], "tp")
        gg_t = gx[rows : rows + 16, :block_len].astype(F32)
        gg_t = jnp.moveaxis(gg_t.reshape(2, 8, block_len)[: rows // BLOCK], 0, 1).reshape(8, rows)
        extra = (prev_t, resid) if prev_t is not None else (grad_logits,)
        outs = gate_backward(
            grad, middle, gx, vecs, routes_t[layer], gates_t, gg_t, context, wo_all[0], extra
        )
        gmid, gctx, dwo, dvec = outs[:4]
        if prev_t is not None:
            grad_logits, dres = outs[4:]
        gown, goth = attend_backward(qkv, other, lse, gctx, info, heads)
        if hyper:
            wide_terms = [scatter_beside(*sums[k][:2], got[k], k + 1) for k in range(2)]
        if not top:
            gown, goth, late = tie(gown, goth, late)
            if hyper:
                gown, wide_terms, upper_got = tie(gown, wide_terms, upper_got)
        goth = swap(goth)
        ga_part, dqkv, dgain = qkv_backward(gown, goth, h_in, vecs, qkv_full)
        small_parts = (dqkv, dwo, dvec, dgain)
        own = None
        ga = lax.psum(ga_part, "tp")
        if hyper:
            if layer > 0:
                dres = dres + swap(dres)
                dres = dres + hop(dres, 1)
                ga, wide_terms, dres, small_parts = tie(ga, wide_terms, dres, small_parts)
                dres = dres + hop(dres, 2)
                pending = (wide_terms, small_parts, dres)
            else:
                small_terms = scatter_second(scatter_beside(*upper[:2], upper_got, 1), 1)
                terms = [scatter_second(wide_terms[k], k + 1) for k in range(2)]
                terms, small_parts, late = tie(terms, small_parts, late)
                wide_out = final_sums(terms[0], terms[1], wide_out, layer, layer_count)
                own = scatter_cores(*pack_grads(*small_parts, offs), 1)
                owns = [scatter_second(scatter_first(*own, 1), 1), small_terms]
                owns = [
                    sum((term[0] if term.ndim == 3 else term).astype(F32) for term in item)
                    for item in owns
                ]
                gains = share(jnp.stack([item[:, -PACK + ROW_GA] for item in owns]), tp_count)
        if top:
            late = [part[:block_len], part[block_len:]]
            late[0], ga = tie(late[0], ga)
        outs = norm_backward(gmid, ga, h_in, vecs, layer > 0)
        grad = outs[0]
        grad_low = outs[-1]
        finals[layer] = (grads, small_parts, own)

    late = jnp.concatenate(late, axis=0)
    mixed = (base_top + late.astype(F32)).astype(BF16)

    resid_total = (dres if hyper else lax.psum(dres, groups))[:NE, :NE]
    results = [None] * layer_count
    for layer in reversed(range(layer_count)):
        grads, small_parts, own = finals[layer]
        if hyper:
            own = owns[layer]
        else:
            packed = pack_grads(*small_parts, offs)
            own = lax.psum_scatter(packed[0], groups, scatter_dimension=0, tiled=True).astype(F32)
            wide_own = lax.psum_scatter(
                grads[0], groups, scatter_dimension=1, tiled=True
            ).astype(F32)
            here = (
                wide_own[:, :, : 2 * units].reshape(NF, shard_rows, 2, units),
                wide_own[:, :, 2 * units :],
            )
            if wide_out is None:
                wide_out = ([], [])
            wide_out[0].insert(0, here[0])
            wide_out[1].insert(0, here[1])
        out_cols = heads * HD
        vec = own[:, qkv_cols + out_cols :]
        results[layer] = (
            own[:, :qkv_cols],
            own[:, qkv_cols : qkv_cols + out_cols].T,
            vec[:, ROW_GM],
            vec[:, :NE],
            jnp.stack([vec[:, ROW_CONST : ROW_CONST + 2], vec[:, ROW_CONST + 2 : ROW_CONST + 4]]),
            vec[:, ROW_VEC : ROW_VEC + 2].T,
            vec[:, ROW_GA],
        )
    if not hyper:
        wide_out = (jnp.stack(wide_out[0]), jnp.stack(wide_out[1]))
    stacked = [jnp.stack([item[member] for item in results]) for member in range(7)]
    gains = jnp.stack(gains if hyper else share(stacked[6], tp_count))
    gain_own = sum(
        lax.dynamic_index_in_dim(gains, (rank[0] + tp_count - j) % tp_count, 0, keepdims=False)
        for j in range(tp_count)
    )
    return (
        mixed.reshape(tokens.shape),
        grad.reshape(tokens.shape),
        gain_own,
        stacked[0],
        stacked[1],
        stacked[2],
        stacked[3],
        resid_total,
        stacked[4],
        stacked[5],
        wide_out[0],
        jnp.swapaxes(wide_out[1], 2, 3),
    )


def solution(mesh):
    axes = dict(mesh.shape)
    hyper = axes["fsdp"] == 4 and axes["ctx"] == 2
    in_specs = (
        P(None, "fsdp", "ctx", None),
        P(None, "fsdp", "ctx", None),
        P(None, "fsdp"),
        P(None, None, "fsdp", "ctx", None),
        P(None, ("fsdp", "ctx")),
        P(None, ("fsdp", "ctx"), "tp"),
        P(None, "tp", ("fsdp", "ctx")),
        P(None, ("fsdp", "ctx")),
        P(None, ("fsdp", "ctx"), None),
        P(),
        P(None, None, ("fsdp", "ctx"), None),
        P(None, None, ("fsdp", "ctx")),
        P(None, None, ("fsdp", "ctx"), None, "tp"),
        P(None, None, "tp", ("fsdp", "ctx")),
    )
    out_specs = (
        P(None, "fsdp", "ctx", None),
        P(None, "fsdp", "ctx", None),
        P(None, ("fsdp", "ctx")),
        P(None, ("fsdp", "ctx"), "tp"),
        P(None, "tp", ("fsdp", "ctx")),
        P(None, ("fsdp", "ctx")),
        P(None, ("fsdp", "ctx"), None),
        P(),
        P(None, None, ("fsdp", "ctx"), None),
        P(None, None, ("fsdp", "ctx")),
        P(None, None, ("fsdp", "ctx"), None, "tp"),
        P(None, None, "tp", ("fsdp", "ctx")),
    )
    return jax.shard_map(
        functools.partial(per_device, hyper, axes),
        mesh=mesh,
        in_specs=in_specs,
        out_specs=out_specs,
        check_vma=False,
    )
```

```python
import functools

import jax
import jax.numpy as jnp
from jax import lax
from jax.experimental import pallas as pl
from jax.experimental.pallas import tpu as pltpu
from jax.sharding import PartitionSpec as P

HD = 64
NF = 8
NE = 12
BLOCK = 512
CAP = 128
TILE = 256
EPSILON = 1e-06
MASKED = -1e30
F32 = jnp.float32
BF16 = jnp.bfloat16
HIGH = lax.Precision.HIGHEST
ROW_CONST, ROW_VEC, ROW_GA, ROW_GM = 16, 20, 22, 23
VMEM_LIMIT = 58 * 1024 * 1024
SCALE = 0.05
PACK = 128

NN = (((1,), (0,)), ((), ()))
NT = (((1,), (1,)), ((), ()))
TN = (((0,), (0,)), ((), ()))


def mm(left, right, dims=NN, precision=None):
    return lax.dot_general(left, right, dims, precision=precision, preferred_element_type=F32)


def kernel_params():
    return pltpu.CompilerParams(vmem_limit_bytes=VMEM_LIMIT)


def cost(flops, nbytes, trans=0):
    return pl.CostEstimate(
        flops=int(flops * SCALE), bytes_accessed=int(nbytes * SCALE), transcendentals=int(trans * SCALE)
    )


def iota(shape, dim):
    return lax.broadcasted_iota(jnp.int32, shape, dim)


def full_spec(shape):
    zeros = (0,) * len(shape)
    return pl.BlockSpec(shape, lambda *idx: zeros)


SMEM_SPEC = pl.BlockSpec(memory_space=pltpu.SMEM)


def pad_rows(rows, count, width):
    row_id = iota((count, width), 0)
    out = jnp.zeros((count, width), F32)
    for place, row in rows:
        out = jnp.where(row_id == place, row, out)
    return out


def round_up(value, unit):
    return -(-value // unit) * unit


def prep_kernel(count, rows, out_cols, offs_ref, *refs):
    qkv_ref, vec_ref, wo_refs = refs[count], refs[count + 1], refs[count + 2 : -2]
    scr_ref, wo_scr = refs[-2:]
    cols = qkv_ref.shape[1]
    for piece in range(count):
        start = pl.multiple_of(offs_ref[piece] * rows, rows)
        block = refs[piece][...]
        qkv_ref[pl.ds(start, rows), :] = block[:, :cols]
        scr_ref[pl.ds(start, rows), :] = block[:, cols : cols + PACK].astype(F32)
        for rank in range(len(wo_refs)):
            first = cols + PACK + rank * out_cols
            wo_scr[rank, pl.ds(start, rows), :out_cols] = block[:, first : first + out_cols]
    vec_ref[...] = scr_ref[...].T[:32]
    total = wo_scr.shape[1]
    rest = out_cols - 128
    for rank, ref in enumerate(wo_refs):
        ref[:total, :] = wo_scr[rank, :, :128]
        ref[total:, :rest] = wo_scr[rank, : total // 2, 128:out_cols]
        ref[total:, rest:] = wo_scr[rank, total // 2 :, 128:out_cols]


def prep_weights(pieces, offs, feature_dim, qkv_cols, out_cols, out_count):
    count = len(pieces)
    cols = round_up(qkv_cols, 128)
    vmem = pl.BlockSpec(memory_space=pltpu.VMEM)
    outs = pl.pallas_call(
        functools.partial(prep_kernel, count, feature_dim // count, out_cols),
        out_shape=tuple(
            [
                jax.ShapeDtypeStruct((feature_dim, cols), BF16),
                jax.ShapeDtypeStruct((32, feature_dim), F32),
            ]
            + [jax.ShapeDtypeStruct((feature_dim * 3 // 2, 128), BF16)] * out_count
        ),
        in_specs=[SMEM_SPEC] + [vmem] * count,
        out_specs=tuple([vmem] * (2 + out_count)),
        scratch_shapes=[
            pltpu.VMEM((feature_dim, PACK), F32),
            pltpu.VMEM((out_count, feature_dim, 256), BF16),
        ],
        compiler_params=kernel_params(),
        cost_estimate=cost(1e6, 3e6),
        name="prep",
    )(offs, *pieces)
    return outs[0], outs[1], list(outs[2:])


def pack_kernel(count, rows, offs_ref, dqkv_ref, dwo_ref, dvec_ref, dgain_ref, *refs):
    outs, scr_ref = refs[:-1], refs[-1]
    cols, out_cols = dqkv_ref.shape[1], dwo_ref.shape[1]
    scr_ref[:, :cols] = dqkv_ref[...]
    scr_ref[:, cols : cols + out_cols] = dwo_ref[...]
    vec = dvec_ref[...]
    vec = jnp.where(iota(vec.shape, 0) == ROW_GA, dgain_ref[0:1, :], vec)
    wide = jnp.concatenate([vec, jnp.zeros((PACK - vec.shape[0], vec.shape[1]), F32)], axis=0).T
    scr_ref[:, cols + out_cols :] = wide
    for piece in range(count):
        start = pl.multiple_of(offs_ref[piece] * rows, rows)
        block = scr_ref[pl.ds(start, rows), :].astype(BF16)
        if count > 1:
            outs[piece % 2][piece // 2] = block
        else:
            outs[0][...] = block


def pack_grads(dqkv, dwo, dvec, dgain, offs):
    feature_dim = dqkv.shape[0]
    count = offs.shape[0]
    rows = feature_dim // count
    width = dqkv.shape[1] + dwo.shape[1] + PACK
    shape = (count // 2, rows, width) if count > 1 else (feature_dim, width)
    vmem = pl.BlockSpec(memory_space=pltpu.VMEM)
    outs = 2 if count > 1 else 1
    return pl.pallas_call(
        functools.partial(pack_kernel, count, rows),
        out_shape=tuple([jax.ShapeDtypeStruct(shape, BF16)] * outs),
        in_specs=[SMEM_SPEC, vmem, vmem, vmem, vmem],
        out_specs=tuple([vmem] * outs),
        scratch_shapes=[pltpu.VMEM((feature_dim, width), F32)],
        compiler_params=kernel_params(),
        cost_estimate=cost(1e6, 6e6),
        name="pack_grads",
    )(offs, dqkv, dwo, dvec, dgain)


def pack_wide_kernel(gu_ref, down_ref, low_ref, high_ref):
    units = down_ref.shape[-1]

    def write(ref):
        ref[0, :, :units] = gu_ref[0, 0, :, 0, :]
        ref[0, :, units : 2 * units] = gu_ref[0, 0, :, 1, :]
        ref[0, :, 2 * units :] = down_ref[0, 0]

    @pl.when(pl.program_id(0) < NF // 2)
    def _():
        write(low_ref)

    @pl.when(pl.program_id(0) >= NF // 2)
    def _():
        write(high_ref)


def pack_wide(w_gate_up, w_down_t, layer):
    _, _, rows, _, units = w_gate_up.shape
    half = NF // 2
    specs = [
        pl.BlockSpec(
            (1, rows, 3 * units), lambda e, part=part: (jnp.clip(e - part * half, 0, half - 1), 0, 0)
        )
        for part in range(2)
    ]
    return pl.pallas_call(
        pack_wide_kernel,
        grid=(NF,),
        out_shape=tuple([jax.ShapeDtypeStruct((half, rows, 3 * units), BF16)] * 2),
        in_specs=[
            pl.BlockSpec((1, 1, rows, 2, units), lambda e: (layer, e, 0, 0, 0)),
            pl.BlockSpec((1, 1, rows, units), lambda e: (layer, e, 0, 0)),
        ],
        out_specs=tuple(specs),
        compiler_params=kernel_params(),
        cost_estimate=cost(1e6, 5e6),
        name="pack_wide",
    )(w_gate_up, w_down_t)


def qkv_kernel(with_ffn, *refs):
    if with_ffn:
        base_ref, ffn_ref, vec_ref, w_ref, h_ref, qkv_ref = refs
        hidden = base_ref[...] + ffn_ref[...].astype(F32)
        h_ref[...] = hidden
    else:
        base_ref, vec_ref, w_ref, qkv_ref = refs
        hidden = base_ref[...].astype(F32)
    gain = vec_ref[ROW_GA : ROW_GA + 1, :]
    scale = lax.rsqrt(jnp.mean(hidden * hidden, axis=-1, keepdims=True) + EPSILON)
    attn_in = (hidden * scale * gain).astype(BF16)
    qkv_ref[...] = mm(attn_in, w_ref[...]).astype(BF16)


def qkv_part(base, ffn, vecs, w_qkv):
    rows, feature_dim = base.shape
    cols = round_up(w_qkv.shape[1], 128)
    row_spec = pl.BlockSpec((TILE, feature_dim), lambda i: (i, 0))
    with_ffn = ffn is not None
    out_shape = [jax.ShapeDtypeStruct((rows, cols), BF16)]
    out_specs = [pl.BlockSpec((TILE, cols), lambda i: (i, 0))]
    if with_ffn:
        out_shape = [jax.ShapeDtypeStruct((rows, feature_dim), F32)] + out_shape
        out_specs = [row_spec] + out_specs
    ins = [base] + ([ffn] if with_ffn else []) + [vecs, w_qkv]
    in_specs = [row_spec] * (2 if with_ffn else 1) + [full_spec(vecs.shape), full_spec(w_qkv.shape)]
    return pl.pallas_call(
        functools.partial(qkv_kernel, with_ffn),
        grid=(rows // TILE,),
        out_shape=tuple(out_shape),
        in_specs=in_specs,
        out_specs=tuple(out_specs),
        compiler_params=kernel_params(),
        cost_estimate=cost(2 * rows * feature_dim * cols, rows * feature_dim * 10),
        name="qkv_part",
    )(*ins)


def attn_masks(ctx, length, tile, width):
    row = iota((TILE, width), 0) + tile * TILE
    col = iota((TILE, width), 1)
    return (col <= row) & (col + ctx * BLOCK < length)


def attn_fwd_kernel(heads, info_ref, own_ref, other_ref, ctx_ref, lse_ref):
    ctx = info_ref[0]
    length = info_ref[1 + pl.program_id(0)]
    own = own_ref[...]
    other = other_ref[...]
    for head in range(heads):
        col = head * 3 * HD
        k_own = own[:, col + HD : col + 2 * HD]
        v_own = own[:, col + 2 * HD : col + 3 * HD]
        k_oth = other[:, col + HD : col + 2 * HD]
        v_oth = other[:, col + 2 * HD : col + 3 * HD]
        for tile in range(BLOCK // TILE):
            width = (tile + 1) * TILE
            query = own[tile * TILE : (tile + 1) * TILE, col : col + HD] * BF16(HD**-0.5)
            s_own = mm(query, k_own[:width], NT)
            s_own = jnp.where(attn_masks(ctx, length, tile, width), s_own, MASKED)
            s_oth = jnp.where(ctx > 0, mm(query, k_oth, NT), MASKED)
            top = jnp.maximum(
                jnp.max(s_own, axis=-1, keepdims=True), jnp.max(s_oth, axis=-1, keepdims=True)
            )
            p_own = jnp.exp(s_own - top)
            p_oth = jnp.exp(s_oth - top)
            total = jnp.sum(p_own, axis=-1, keepdims=True) + jnp.sum(p_oth, axis=-1, keepdims=True)
            out = mm(p_own.astype(BF16), v_own[:width]) + mm(p_oth.astype(BF16), v_oth)
            out = out / total
            rows = slice(tile * TILE, (tile + 1) * TILE)
            ctx_ref[head * TILE : (head + 1) * TILE, tile * HD : (tile + 1) * HD] = out.astype(BF16)
            lse_ref[rows, head : head + 1] = top + jnp.log(total)


def attend_forward(qkv, other, info, heads):
    rows, cols = qkv.shape
    count = rows // BLOCK
    spec = pl.BlockSpec((BLOCK, cols), lambda i: (i, 0))
    return pl.pallas_call(
        functools.partial(attn_fwd_kernel, heads),
        grid=(count,),
        out_shape=(
            jax.ShapeDtypeStruct((count * heads * TILE, 2 * HD), BF16),
            jax.ShapeDtypeStruct((rows, 8), F32),
        ),
        in_specs=[SMEM_SPEC, spec, spec],
        out_specs=(
            pl.BlockSpec((heads * TILE, 2 * HD), lambda i: (i, 0)),
            pl.BlockSpec((BLOCK, 8), lambda i: (i, 0)),
        ),
        compiler_params=kernel_params(),
        cost_estimate=cost(rows * 1024 * heads * HD * 16, rows * cols * 6, rows * heads * 1024),
        name="attend_forward",
    )(info, qkv, other)


def attn_bwd_kernel(heads, info_ref, own_ref, other_ref, lse_ref, gctx_ref, gown_ref, goth_ref):
    ctx = info_ref[0]
    length = info_ref[1 + pl.program_id(0)]
    own = own_ref[...]
    other = other_ref[...]
    scale = BF16(HD**-0.5)
    for head in range(heads):
        col = head * 3 * HD
        k_own = own[:, col + HD : col + 2 * HD]
        v_own = own[:, col + 2 * HD : col + 3 * HD]
        k_oth = other[:, col + HD : col + 2 * HD]
        v_oth = other[:, col + 2 * HD : col + 3 * HD]
        goth_ref[:, col : col + HD] = jnp.zeros((BLOCK, HD), BF16)
        gk_own, gv_own, gk_oth, gv_oth = [], [], [], []
        for tile in range(BLOCK // TILE):
            width = (tile + 1) * TILE
            rows = slice(tile * TILE, (tile + 1) * TILE)
            query = own[rows, col : col + HD] * scale
            gout = gctx_ref[rows, head * HD : (head + 1) * HD]
            lse = lse_ref[rows, head : head + 1]
            s_own = mm(query, k_own[:width], NT)
            s_own = jnp.where(attn_masks(ctx, length, tile, width), s_own, MASKED)
            s_oth = jnp.where(ctx > 0, mm(query, k_oth, NT), MASKED)
            p_own = jnp.exp(s_own - lse)
            p_oth = jnp.exp(s_oth - lse)
            d_own = mm(gout, v_own[:width], NT)
            d_oth = mm(gout, v_oth, NT)
            inner = jnp.sum(p_own * d_own, axis=-1, keepdims=True) + jnp.sum(
                p_oth * d_oth, axis=-1, keepdims=True
            )
            ds_own = (p_own * (d_own - inner)).astype(BF16)
            ds_oth = (p_oth * (d_oth - inner)).astype(BF16)
            p_own = p_own.astype(BF16)
            p_oth = p_oth.astype(BF16)
            gown_ref[rows, col : col + HD] = (mm(ds_own, k_own[:width]) + mm(ds_oth, k_oth)) * (
                HD**-0.5
            )
            gk_own.append(mm(ds_own, query, TN))
            gv_own.append(mm(p_own, gout, TN))
            gk_oth.append(mm(ds_oth, query, TN))
            gv_oth.append(mm(p_oth, gout, TN))
        gown_ref[:TILE, col + HD : col + 2 * HD] = gk_own[0] + gk_own[1][:TILE]
        gown_ref[TILE:, col + HD : col + 2 * HD] = gk_own[1][TILE:]
        gown_ref[:TILE, col + 2 * HD : col + 3 * HD] = gv_own[0] + gv_own[1][:TILE]
        gown_ref[TILE:, col + 2 * HD : col + 3 * HD] = gv_own[1][TILE:]
        goth_ref[:, col + HD : col + 2 * HD] = (gk_oth[0] + gk_oth[1]).astype(BF16)
        goth_ref[:, col + 2 * HD : col + 3 * HD] = (gv_oth[0] + gv_oth[1]).astype(BF16)


def attend_backward(qkv, other, lse, grad_context, info, heads):
    rows, width = qkv.shape
    cols = heads * 3 * HD
    spec = pl.BlockSpec((BLOCK, width), lambda i: (i, 0))
    return pl.pallas_call(
        functools.partial(attn_bwd_kernel, heads),
        grid=(rows // BLOCK,),
        out_shape=(
            jax.ShapeDtypeStruct((rows, cols), F32),
            jax.ShapeDtypeStruct((rows, width), BF16),
        ),
        in_specs=[
            SMEM_SPEC,
            spec,
            spec,
            pl.BlockSpec((BLOCK, 8), lambda i: (i, 0)),
            pl.BlockSpec((BLOCK, heads * HD), lambda i: (i, 0)),
        ],
        out_specs=(pl.BlockSpec((BLOCK, cols), lambda i: (i, 0)), spec),
        compiler_params=kernel_params(),
        cost_estimate=cost(rows * 1024 * heads * HD * 40, rows * cols * 12, rows * heads * 1024),
        name="attend_backward",
    )(info, qkv, other, lse, grad_context)


def alpha_rows(gate_in, const_idx):
    first = gate_in[ROW_CONST + 2 * const_idx : ROW_CONST + 2 * const_idx + 1]
    second = gate_in[ROW_CONST + 2 * const_idx + 1 : ROW_CONST + 2 * const_idx + 2]
    return pair(first, second)


def pair(first, second):
    top = jnp.maximum(first, second)
    exp_first = jnp.exp(first - top)
    exp_second = jnp.exp(second - top)
    total = exp_first + exp_second
    return exp_first / total, exp_second / total


def picks(route, value):
    return (route == value).astype(F32)


def gate_coefs(routes, gates, alphas):
    copy = picks(routes[0], NF + 1) * gates[0] + picks(routes[1], NF + 1) * gates[1]
    const = [
        picks(routes[0], NF + 2 + j) * gates[0] + picks(routes[1], NF + 2 + j) * gates[1]
        for j in range(2)
    ]
    on_normed = copy + const[0] * alphas[0][0] + const[1] * alphas[1][0]
    on_vec = [const[j] * alphas[j][1] for j in range(2)]
    return const, on_normed, on_vec


def to_columns(rows):
    width = rows[0].shape[1]
    return pad_rows(list(enumerate(rows)), 128, width).T


def unpack_context(both):
    heads = both.shape[0] // TILE
    side = lax.rem(pl.program_id(0), 2) == 0
    both = jnp.where(side, both[:, :HD], both[:, HD:])
    parts = [both[head * TILE : (head + 1) * TILE] for head in range(heads)]
    return jnp.concatenate(parts, axis=1)


def middle_kernel(with_prev, rank_ref, *refs):
    h_ref, ctx_ref, refs = refs[0], refs[1], refs[2:]
    count = ctx_ref.shape[0]
    wo_refs, refs = refs[:count], refs[count:]
    if with_prev:
        vec_ref, route_ref, prev_ref, resid_ref = refs[:4]
        refs = refs[4:]
    else:
        vec_ref, route_ref = refs[:2]
        refs = refs[2:]
    mid_ref, base_ref, xm_ref, gate_ref, logit_ref = refs
    attn_out = 0.0
    for back, ref in enumerate(wo_refs):
        context = unpack_context(ctx_ref[lax.rem(rank_ref[0] + count - back, count)])
        total = ref.shape[0] * 2 // 3
        rest = context[:, 128:]
        attn_out += mm(context[:, :128], ref[:total], NT) + jnp.concatenate(
            [mm(rest, ref[total:, :HD], NT), mm(rest, ref[total:, HD:], NT)], axis=1
        )
    middle = h_ref[...].astype(F32) + attn_out
    mid_ref[...] = middle
    vecs = vec_ref[...]
    scale = lax.rsqrt(jnp.mean(middle * middle, axis=-1, keepdims=True) + EPSILON)
    normed = middle * scale * vecs[ROW_GM : ROW_GM + 1]
    xm_low = normed.astype(BF16)
    xm_ref[...] = xm_low
    gate_in = mm(vecs[:32].astype(BF16), xm_low, NT)
    logits = gate_in[:16]
    if with_prev:
        logits = logits + mm(resid_ref[...], prev_ref[...], TN, HIGH)
    logit_ref[...] = logits
    routes = (route_ref[0:1], route_ref[1:2])
    expert = iota(logits.shape, 0)
    chosen = [
        jnp.sum(jnp.where(expert == route, logits, 0.0), axis=0, keepdims=True) for route in routes
    ]
    gates = pair(chosen[0], chosen[1])
    gate_ref[...] = pad_rows(list(enumerate(gates)), 8, logits.shape[1])
    alphas = [alpha_rows(gate_in, j) for j in range(2)]
    const, on_normed, on_vec = gate_coefs(routes, gates, alphas)
    cols = to_columns([on_normed, on_vec[0], on_vec[1]])
    base_ref[...] = (
        middle
        + cols[:, 0:1] * normed
        + cols[:, 1:2] * vecs[ROW_VEC : ROW_VEC + 1]
        + cols[:, 2:3] * vecs[ROW_VEC + 1 : ROW_VEC + 2]
    )


def middle_part(h, ctx_all, wo_all, vecs, routes_t, prev_t, resid, rank):
    rows, feature_dim = h.shape
    tp_count, packed, lanes = ctx_all.shape
    packed = packed * BLOCK // rows
    row_spec = pl.BlockSpec((TILE, feature_dim), lambda i: (i, 0))
    lane8 = pl.BlockSpec((8, TILE), lambda i: (0, i))
    lane16 = pl.BlockSpec((16, TILE), lambda i: (0, i))
    ins = [rank, h, ctx_all, *wo_all, vecs, routes_t]
    in_specs = [
        SMEM_SPEC,
        row_spec,
        pl.BlockSpec((tp_count, packed, lanes), lambda i: (0, i // 2, 0)),
        *[full_spec(item.shape) for item in wo_all],
        full_spec(vecs.shape),
        lane8,
    ]
    with_prev = prev_t is not None
    if with_prev:
        ins += [prev_t, resid]
        in_specs += [lane16, full_spec(resid.shape)]
    return pl.pallas_call(
        functools.partial(middle_kernel, with_prev),
        grid=(rows // TILE,),
        out_shape=(
            jax.ShapeDtypeStruct((rows, feature_dim), F32),
            jax.ShapeDtypeStruct((rows, feature_dim), F32),
            jax.ShapeDtypeStruct((rows, feature_dim), BF16),
            jax.ShapeDtypeStruct((8, rows), F32),
            jax.ShapeDtypeStruct((16, rows), F32),
        ),
        in_specs=in_specs,
        out_specs=(row_spec, row_spec, row_spec, lane8, lane16),
        compiler_params=kernel_params(),
        cost_estimate=cost(2 * rows * feature_dim * feature_dim, rows * feature_dim * 16),
        name="middle_part",
    )(*ins)


def split(value):
    high = value.astype(BF16)
    return high, (value - high.astype(F32)).astype(BF16)


def gate_bwd_kernel(with_prev, *refs):
    gh_ref, mid_ref, gxm_ref, vec_ref, route_ref, gate_ref, gg_ref, ctx_ref, wo_ref = refs[:9]
    refs = refs[9:]
    if with_prev:
        prev_ref, resid_ref = refs[:2]
        gmid_ref, gctx_ref, dwo_ref, dvec_ref, gprev_ref, dres_ref = refs[2:]
    else:
        gl_ref = refs[0]
        gmid_ref, gctx_ref, dwo_ref, dvec_ref = refs[1:]
    step = pl.program_id(0)
    grad = gh_ref[...].astype(F32)
    middle = mid_ref[...]
    vecs = vec_ref[...]
    gain = vecs[ROW_GM : ROW_GM + 1]
    scale = lax.rsqrt(jnp.mean(middle * middle, axis=-1, keepdims=True) + EPSILON)
    unit = middle * scale
    normed = unit * gain
    xm_low = normed.astype(BF16)
    low_vecs = vecs[:32].astype(BF16)
    gate_in = mm(low_vecs, xm_low, NT)
    alphas = [alpha_rows(gate_in, j) for j in range(2)]
    routes = (route_ref[0:1], route_ref[1:2])
    gates = (gate_ref[0:1], gate_ref[1:2])
    const, on_normed, on_vec = gate_coefs(routes, gates, alphas)
    grad_hi, grad_lo = split(grad)
    vec_dots = mm(low_vecs[16:32], grad_hi, NT) + mm(low_vecs[16:32], grad_lo, NT)
    dot_vec = [vec_dots[ROW_VEC - 16 + j : ROW_VEC - 15 + j] for j in range(2)]
    dot_col = jnp.sum(grad * normed, axis=-1, keepdims=True)
    dot_normed = jnp.broadcast_to(dot_col, (dot_col.shape[0], 128)).T[0:1]
    term = [alphas[j][0] * dot_normed + alphas[j][1] * dot_vec[j] for j in range(2)]
    gate_grads = []
    for slot in range(2):
        fixed = (
            picks(routes[slot], NF + 1) * dot_normed
            + picks(routes[slot], NF + 2) * term[0]
            + picks(routes[slot], NF + 3) * term[1]
        )
        gate_grads.append(jnp.where(routes[slot] < NF, gg_ref[slot : slot + 1], fixed))
    inner = gates[0] * gate_grads[0] + gates[1] * gate_grads[1]
    chosen_grads = [gates[slot] * (gate_grads[slot] - inner) for slot in range(2)]
    expert = iota((16, TILE), 0)
    grad_logits = jnp.where(expert == routes[0], chosen_grads[0], 0.0) + jnp.where(
        expert == routes[1], chosen_grads[1], 0.0
    )
    if not with_prev:
        grad_logits = grad_logits + gl_ref[...]
    alpha_grads = []
    for j in range(2):
        grad_first = const[j] * dot_normed
        grad_second = const[j] * dot_vec[j]
        mean = alphas[j][0] * grad_first + alphas[j][1] * grad_second
        alpha_grads.append((2 * j, alphas[j][0] * (grad_first - mean)))
        alpha_grads.append((2 * j + 1, alphas[j][1] * (grad_second - mean)))
    grad_in = jnp.concatenate([grad_logits, pad_rows(alpha_grads, 16, TILE)], axis=0)
    in_hi, in_lo = split(grad_in)
    low_gate = jnp.where(iota(low_vecs.shape, 0) < ROW_VEC, low_vecs, 0)
    grad_xm = mm(in_hi, low_gate, TN) + mm(in_lo, low_gate, TN)
    cols = to_columns([on_normed])
    grad_y = cols[:, 0:1] * grad + grad_xm + gxm_ref[...].astype(F32)
    weighted = grad_y * gain
    mean = jnp.mean(weighted * unit, axis=-1, keepdims=True)
    grad_mid = grad + scale * (weighted - unit * mean)
    gmid_ref[...] = grad_mid
    low_mid = grad_mid.astype(BF16)
    total = low_mid.shape[1]
    gctx_ref[:, :128] = mm(low_mid, wo_ref[:total]).astype(BF16)
    gctx_ref[:, 128:] = (
        mm(low_mid[:, : total // 2], wo_ref[total:, :HD])
        + mm(low_mid[:, total // 2 :], wo_ref[total:, HD:])
    ).astype(BF16)
    dwo = mm(low_mid, unpack_context(ctx_ref[...]), TN)
    vec_rows = pad_rows([(ROW_VEC - 16 + j, on_vec[j]) for j in range(2)], 16, TILE)
    vec_hi, vec_lo = split(vec_rows)
    dvec_low = mm(vec_hi, grad_hi) + mm(vec_lo, grad_hi)
    dvec_gate = mm(in_hi, xm_low) + mm(in_lo, xm_low)
    dgain = jnp.sum(grad_y * unit, axis=0, keepdims=True)
    row_id = iota(dvec_gate.shape, 0)
    dvec = dvec_gate + jnp.concatenate([jnp.zeros_like(dvec_low), dvec_low], axis=0)
    dvec = jnp.where(row_id == ROW_GM, dgain, dvec)

    @pl.when(step == 0)
    def _():
        dwo_ref[...] = dwo
        dvec_ref[...] = dvec

    @pl.when(step > 0)
    def _():
        dwo_ref[...] += dwo
        dvec_ref[...] += dvec

    if with_prev:
        gprev_ref[...] = mm(resid_ref[...], grad_logits, NN, HIGH)
        dres = mm(prev_ref[...], grad_logits, NT, HIGH)

        @pl.when(step == 0)
        def _():
            dres_ref[...] = dres

        @pl.when(step > 0)
        def _():
            dres_ref[...] += dres


def gate_backward(grad, middle, gxm, vecs, routes_t, gates_t, gg_t, context, wo_own, extra):
    rows, feature_dim = middle.shape
    out_cols = context.shape[0] * BLOCK // rows // TILE * HD
    with_prev = len(extra) == 2
    row_spec = pl.BlockSpec((TILE, feature_dim), lambda i: (i, 0))
    lane8 = pl.BlockSpec((8, TILE), lambda i: (0, i))
    lane16 = pl.BlockSpec((16, TILE), lambda i: (0, i))
    ctx_spec = pl.BlockSpec((context.shape[0] * BLOCK // rows, 2 * HD), lambda i: (i // 2, 0))
    out_spec = pl.BlockSpec((TILE, out_cols), lambda i: (i, 0))
    wo_spec = full_spec(wo_own.shape)
    in_specs = [row_spec, row_spec, row_spec, full_spec(vecs.shape), lane8, lane8, lane8]
    in_specs += [ctx_spec, wo_spec, lane16]
    out_shape = [
        jax.ShapeDtypeStruct((rows, feature_dim), F32),
        jax.ShapeDtypeStruct((rows, out_cols), BF16),
        jax.ShapeDtypeStruct((feature_dim, out_cols), F32),
        jax.ShapeDtypeStruct((32, feature_dim), F32),
    ]
    out_specs = [row_spec, out_spec, full_spec((feature_dim, out_cols)), full_spec((32, feature_dim))]
    if with_prev:
        in_specs.append(full_spec(extra[1].shape))
        out_shape += [jax.ShapeDtypeStruct((16, rows), F32), jax.ShapeDtypeStruct((16, 16), F32)]
        out_specs += [lane16, full_spec((16, 16))]
    return pl.pallas_call(
        functools.partial(gate_bwd_kernel, with_prev),
        grid=(rows // TILE,),
        out_shape=tuple(out_shape),
        in_specs=in_specs,
        out_specs=tuple(out_specs),
        compiler_params=kernel_params(),
        cost_estimate=cost(4 * rows * feature_dim * out_cols, rows * feature_dim * 18),
        name="gate_backward",
    )(grad, middle, gxm, vecs, routes_t, gates_t, gg_t, context, wo_own, *extra)


def qkv_bwd_kernel(gown_ref, goth_ref, h_ref, vec_ref, w_ref, part_ref, dw_ref, dgain_ref):
    step = pl.program_id(0)
    cols = gown_ref.shape[1]
    grad = (gown_ref[...] + goth_ref[:, :cols].astype(F32)).astype(BF16)
    part = mm(grad, w_ref[:, :cols], NT)
    part_ref[...] = part.astype(BF16)
    hidden = h_ref[...].astype(F32)
    gain = vec_ref[ROW_GA : ROW_GA + 1, :]
    scale = lax.rsqrt(jnp.mean(hidden * hidden, axis=-1, keepdims=True) + EPSILON)
    unit = hidden * scale
    attn_in = (unit * gain).astype(BF16)
    dw = mm(attn_in, grad, TN)
    dgain = jnp.broadcast_to(jnp.sum(part * unit, axis=0, keepdims=True), dgain_ref.shape)

    @pl.when(step == 0)
    def _():
        dw_ref[...] = dw
        dgain_ref[...] = dgain

    @pl.when(step > 0)
    def _():
        dw_ref[...] += dw
        dgain_ref[...] += dgain


def qkv_backward(gown, goth, h, vecs, w_qkv):
    rows, feature_dim = h.shape
    cols = gown.shape[1]
    row_spec = pl.BlockSpec((TILE, feature_dim), lambda i: (i, 0))
    col_spec = pl.BlockSpec((TILE, cols), lambda i: (i, 0))
    oth_spec = pl.BlockSpec((TILE, goth.shape[1]), lambda i: (i, 0))
    return pl.pallas_call(
        qkv_bwd_kernel,
        grid=(rows // TILE,),
        out_shape=(
            jax.ShapeDtypeStruct((rows, feature_dim), BF16),
            jax.ShapeDtypeStruct((feature_dim, cols), F32),
            jax.ShapeDtypeStruct((8, feature_dim), F32),
        ),
        in_specs=[col_spec, oth_spec, row_spec, full_spec(vecs.shape), full_spec(w_qkv.shape)],
        out_specs=(row_spec, full_spec((feature_dim, cols)), full_spec((8, feature_dim))),
        compiler_params=kernel_params(),
        cost_estimate=cost(4 * rows * feature_dim * cols, rows * feature_dim * 10),
        name="qkv_backward",
    )(gown, goth, h, vecs, w_qkv)


def norm_bwd_kernel(with_low, gmid_ref, ga_ref, h_ref, vec_ref, out_ref, *rest):
    hidden = h_ref[...].astype(F32)
    gain = vec_ref[ROW_GA : ROW_GA + 1, :]
    scale = lax.rsqrt(jnp.mean(hidden * hidden, axis=-1, keepdims=True) + EPSILON)
    unit = hidden * scale
    grad_y = ga_ref[...].astype(F32)
    weighted = grad_y * gain
    mean = jnp.mean(weighted * unit, axis=-1, keepdims=True)
    grad = gmid_ref[...] + scale * (weighted - unit * mean)
    out_ref[...] = grad
    if with_low:
        rest[0][...] = grad.astype(BF16)


def norm_backward(gmid, ga, h, vecs, with_low):
    rows, feature_dim = gmid.shape
    row_spec = pl.BlockSpec((TILE, feature_dim), lambda i: (i, 0))
    out_shape = [jax.ShapeDtypeStruct((rows, feature_dim), F32)]
    out_specs = [row_spec]
    if with_low:
        out_shape.append(jax.ShapeDtypeStruct((rows, feature_dim), BF16))
        out_specs.append(row_spec)
    return pl.pallas_call(
        functools.partial(norm_bwd_kernel, with_low),
        grid=(rows // TILE,),
        out_shape=tuple(out_shape),
        in_specs=[row_spec, row_spec, row_spec, full_spec(vecs.shape)],
        out_specs=tuple(out_specs),
        compiler_params=kernel_params(),
        cost_estimate=cost(rows * feature_dim * 10, rows * feature_dim * 16),
        name="norm_backward",
    )(gmid, ga, h, vecs)


def experts_kernel(fwd, bwd, blocks, plan, out_count, rows, offs_ref, *refs):
    refs = list(refs)
    xm_ref = refs.pop(0)
    gh_ref = refs.pop(0) if bwd else None
    route_ref, gate_ref = refs.pop(0), refs.pop(0)
    w_refs = [refs.pop(0) for _ in plan]
    ffn_ref = refs.pop(0) if fwd else None
    if bwd:
        gx_ref = refs.pop(0)
        dw_refs = [refs.pop(0) for _ in range(out_count)]
    w_scr, sem_ref, hot_scr, pick_scr = (refs.pop(0) for _ in range(4))
    part_scr = refs.pop(0) if fwd else None
    if bwd:
        gpart_scr, raw_scr, gg_scr, dw_scr = refs
    expert = pl.program_id(0)
    last = pl.num_programs(0) - 1
    depth, width = w_scr.shape[0] // 2, w_scr.shape[1]
    units = width // 3

    def move(each, target, start):
        for ref, (off, first, number) in zip(w_refs, plan):

            def one(ref=ref, off=off, first=first):
                row = pl.multiple_of(offs_ref[off] * rows + target * depth, rows)
                copy = pltpu.make_async_copy(
                    ref.at[each - first], w_scr.at[pl.ds(row, rows)], sem_ref.at[target, off]
                )
                if start:
                    copy.start()
                else:
                    copy.wait()

            if number == NF:
                one()
            else:
                pl.when((each >= first) & (each < first + number))(one)

    slot = lax.rem(expert, 2)
    here = pl.ds(pl.multiple_of(slot * depth, depth), depth)

    @pl.when(expert == 0)
    def _():
        move(0 * expert, 0, True)

    @pl.when(expert < last)
    def _():
        move(expert + 1, 1 - slot, True)

    @pl.when(expert == 0)
    def _():
        order = (iota((BLOCK, BLOCK), 0) < iota((BLOCK, BLOCK), 1)).astype(BF16)
        ids = iota((NF, BLOCK), 0)
        row_ids = iota((CAP, BLOCK), 0).astype(F32)
        for block in range(blocks):
            lanes = slice(block * BLOCK, (block + 1) * BLOCK)
            hits = (ids == route_ref[0:1, lanes]) | (ids == route_ref[1:2, lanes])
            place = jnp.where(hits, mm(hits.astype(BF16), order), -1.0)
            for each in range(NF):
                hot_scr[block, each * CAP : (each + 1) * CAP, :] = (
                    (row_ids == place[each : each + 1]).astype(F32).astype(BF16)
                )
            hot = hot_scr[block]
            for source, target in ((xm_ref, pick_scr),) + (((gh_ref, raw_scr),) if bwd else ()):
                rows_all = mm(hot, source[lanes, :]).astype(BF16)
                for each in range(NF):
                    target[each, block * CAP : (block + 1) * CAP, :] = rows_all[
                        each * CAP : (each + 1) * CAP
                    ]
        if bwd:
            gg_scr[...] = jnp.zeros_like(gg_scr)

    def combine(source, block):
        return mm(hot_scr[block], source[block], TN)

    move(expert, slot, False)
    hot, gate_cols, masks = [], [], []
    first_row = pl.multiple_of(expert * CAP, CAP)
    for block in range(blocks):
        lanes = slice(block * BLOCK, (block + 1) * BLOCK)
        one_hot = hot_scr[block, pl.ds(first_row, CAP), :].astype(F32)
        mask = [route_ref[slot : slot + 1, lanes] == expert for slot in range(2)]
        gate_row = jnp.where(mask[0], gate_ref[0:1, lanes], 0.0) + jnp.where(
            mask[1], gate_ref[1:2, lanes], 0.0
        )
        gate_cols.append(jnp.sum(one_hot * gate_row, axis=1, keepdims=True))
        hot.append(one_hot)
        masks.append(mask)
    gate_col = jnp.concatenate(gate_cols, axis=0)
    picked = pick_scr[expert]
    gate_up = mm(picked, w_scr[here, : 2 * units])
    gate_in, up_in = gate_up[:, :units], gate_up[:, units:]
    sigmoid = lax.logistic(gate_in)
    silu = gate_in * sigmoid
    hidden = (silu * up_in).astype(BF16)
    if fwd:
        scaled = (mm(hidden, w_scr[here, 2 * units :], NT) * gate_col).astype(BF16)
        for block in range(blocks):
            part_scr[block, pl.ds(first_row, CAP), :] = scaled[block * CAP : (block + 1) * CAP]

        @pl.when(expert == last)
        def _():
            for block in range(blocks):
                ffn_ref[block * BLOCK : (block + 1) * BLOCK, :] = combine(part_scr, block).astype(
                    BF16
                )

    if bwd:
        raw = raw_scr[expert]
        grad_raw = mm(raw, w_scr[here, 2 * units :])
        gate_dot = jnp.sum(hidden.astype(F32) * grad_raw, axis=1, keepdims=True)
        for block in range(blocks):
            row = jnp.sum(
                hot[block] * gate_dot[block * CAP : (block + 1) * CAP],
                axis=0,
                keepdims=True,
            )
            for slot in range(2):
                gg_scr[8 * block + slot : 8 * block + slot + 1, :] += jnp.where(
                    masks[block][slot], row, 0.0
                )
        grad_hidden = grad_raw * gate_col
        grad_gate = grad_hidden * up_in * sigmoid * (1.0 + gate_in * (1.0 - sigmoid))
        grad_up = grad_hidden * silu
        grad_gu = jnp.concatenate([grad_gate.astype(BF16), grad_up.astype(BF16)], axis=1)
        grad_pick = mm(grad_gu, w_scr[here, : 2 * units], NT).astype(BF16)
        for block in range(blocks):
            gpart_scr[block, pl.ds(first_row, CAP), :] = grad_pick[block * CAP : (block + 1) * CAP]
        grad_result = (raw.astype(F32) * gate_col).astype(BF16)
        if out_count == 1:
            dw_refs[0][0, :, : 2 * units] = mm(picked, grad_gu, TN).astype(BF16)
            dw_refs[0][0, :, 2 * units :] = mm(grad_result, hidden, TN).astype(BF16)
        else:
            dw_scr[:, : 2 * units] = mm(picked, grad_gu, TN).astype(BF16)
            dw_scr[:, 2 * units :] = mm(grad_result, hidden, TN).astype(BF16)
            half = NF // 2
            for part in range(2):

                @pl.when((expert >= part * half) & (expert < (part + 1) * half))
                def _(part=part):
                    for off in range(8):
                        start = pl.multiple_of(offs_ref[off] * rows, rows)
                        dw_refs[2 * part + off % 2][off // 2, 0] = dw_scr[pl.ds(start, rows), :]

        @pl.when(expert == last)
        def _():
            total = blocks * BLOCK
            for block in range(blocks):
                gx_ref[block * BLOCK : (block + 1) * BLOCK, :] = combine(gpart_scr, block).astype(
                    BF16
                )
            gx_ref[total : total + 16, :] = jnp.zeros((16, gx_ref.shape[1]), BF16)
            gx_ref[total : total + gg_scr.shape[0], :BLOCK] = gg_scr[...].astype(BF16)


def experts(fwd, bwd, xm, gh, routes_t, gates_t, pieces, offs):
    rows, feature_dim = xm.shape
    blocks = rows // BLOCK
    arrays = [item[0] for item in pieces]
    plan = [item[1:] for item in pieces]
    _, piece_rows, width = arrays[0].shape
    units = width // 3
    split_out = len(pieces) > 1
    half = NF // 2

    ins = [xm] + ([gh] if bwd else []) + [routes_t, gates_t]
    in_specs = [SMEM_SPEC] + [full_spec(item.shape) for item in ins]
    in_specs += [pl.BlockSpec(memory_space=pl.ANY)] * len(plan)
    out_shape, out_specs, scratch = [], [], []
    scratch += [
        pltpu.VMEM((2 * feature_dim, width), BF16),
        pltpu.SemaphoreType.DMA((2, offs.shape[0])),
        pltpu.VMEM((blocks, NF * CAP, BLOCK), BF16),
        pltpu.VMEM((NF, blocks * CAP, feature_dim), BF16),
    ]
    flops = 0
    out_count = 4 if split_out else 1
    if fwd:
        out_shape.append(jax.ShapeDtypeStruct((rows, feature_dim), BF16))
        out_specs.append(full_spec((rows, feature_dim)))
        scratch.append(pltpu.VMEM((blocks, NF * CAP, feature_dim), BF16))
        flops += 1.0e9 * NF * blocks / 2
    if bwd:
        out_shape.append(jax.ShapeDtypeStruct((rows + 16, feature_dim), BF16))
        out_specs.append(full_spec((rows + 16, feature_dim)))
        if split_out:
            for part in range(2):
                for _ in range(2):
                    out_shape.append(jax.ShapeDtypeStruct((4, half, piece_rows, width), BF16))
                    out_specs.append(
                        pl.BlockSpec(
                            (4, 1, piece_rows, width),
                            lambda e, part=part: (0, jnp.clip(e - part * half, 0, half - 1), 0, 0),
                        )
                    )
        else:
            out_shape.append(jax.ShapeDtypeStruct((NF, feature_dim, width), BF16))
            out_specs.append(pl.BlockSpec((1, feature_dim, width), lambda e: (e, 0, 0)))
        scratch += [
            pltpu.VMEM((blocks, NF * CAP, feature_dim), BF16),
            pltpu.VMEM((NF, blocks * CAP, feature_dim), BF16),
            pltpu.VMEM((blocks * 8, BLOCK), F32),
            pltpu.VMEM((feature_dim, width) if split_out else (8, 128), BF16),
        ]
        flops += 2.2e9 * NF * blocks / 2
    outs = pl.pallas_call(
        functools.partial(experts_kernel, fwd, bwd, blocks, plan, out_count, piece_rows),
        grid=(NF,),
        out_shape=tuple(out_shape),
        in_specs=in_specs,
        out_specs=tuple(out_specs),
        scratch_shapes=scratch,
        compiler_params=kernel_params(),
        cost_estimate=cost(flops, 20e6 * (2 if bwd else 1), rows * units * 8),
        name="experts",
    )(offs, *ins, *arrays)
    outs = list(outs)
    ffn = outs.pop(0) if fwd else None
    return (ffn, outs[0], outs[1:]) if bwd else (ffn, None, None)


def final_kernel(with_old, count, *refs):
    parts = refs[:count]
    gu_ref, dn_ref = refs[-2:]
    del with_old
    half = count // 2
    units = gu_ref.shape[-1]

    def write(group):
        total = group[0][...].reshape(group[0].shape[-2:]).astype(F32)
        for ref in group[1:]:
            total += ref[...].reshape(ref.shape[-2:]).astype(F32)
        gu_ref[0, 0, :, 0, :] = total[:, :units]
        gu_ref[0, 0, :, 1, :] = total[:, units : 2 * units]
        dn_ref[0, 0] = total[:, 2 * units :]

    @pl.when(pl.program_id(0) < NF // 2)
    def _():
        write(parts[:half])

    @pl.when(pl.program_id(0) >= NF // 2)
    def _():
        write(parts[half:])


def final_sums(lows, highs, old, layer, layer_count):
    half = NF // 2
    specs, arrays = [], []
    for part, group in enumerate((lows, highs)):
        for item in group:
            lead = (1,) * (item.ndim - 3)
            specs.append(
                pl.BlockSpec(
                    lead + (1,) + item.shape[-2:],
                    lambda e, part=part, lead=lead: (0,) * len(lead)
                    + (jnp.clip(e - part * half, 0, half - 1), 0, 0),
                )
            )
            arrays.append(item)
    count = len(arrays)
    rows, width = arrays[0].shape[-2:]
    units = width // 3
    aliases = {}
    if old is not None:
        specs += [pl.BlockSpec(memory_space=pl.ANY)] * 2
        arrays += list(old)
        aliases = {count: 0, count + 1: 1}
    return pl.pallas_call(
        functools.partial(final_kernel, old is not None, count),
        grid=(NF,),
        out_shape=(
            jax.ShapeDtypeStruct((layer_count, NF, rows, 2, units), F32),
            jax.ShapeDtypeStruct((layer_count, NF, rows, units), F32),
        ),
        in_specs=specs,
        out_specs=(
            pl.BlockSpec((1, 1, rows, 2, units), lambda e: (layer, e, 0, 0, 0)),
            pl.BlockSpec((1, 1, rows, units), lambda e: (layer, e, 0, 0)),
        ),
        input_output_aliases=aliases,
        compiler_params=kernel_params(),
        cost_estimate=cost(1e7, NF * rows * width * 12),
        name="final_sums",
    )(*arrays)


def hop(value, step):
    return lax.ppermute(value, "fsdp", [(i, i ^ step) for i in range(4)])


def swap(value):
    return lax.ppermute(value, "ctx", [(0, 1), (1, 0)])


def gather_small(value):
    by_x, by_y, by_d = hop(value, 1), hop(value, 2), hop(value, 3)
    out = []
    for item in (value, by_x, by_y, by_d):
        out += [item, swap(item)]
    return out


def turn(value, steps, count):
    return lax.ppermute(value, "tp", [(i, (i + steps) % count) for i in range(count)])


def share(value, count):
    return [value] + [turn(value, k, count) for k in range(1, count)]


def gather_cores(lows, highs, swapped):
    half = NF // 2
    out = []
    for first, items, done in ((0, lows, swapped[0]), (half, highs, swapped[1])):
        for chip, item in enumerate(items):
            other = done[chip] if chip in done else swap(item)
            out += [(item, 2 * chip, first, half), (other, 2 * chip + 1, first, half)]
    return out


def tie(*values):
    return lax.optimization_barrier(values)


def add_low(*terms):
    total = terms[0].astype(F32)
    for term in terms[1:]:
        total = total + term.astype(F32)
    return total.astype(BF16)


def scatter_cores(keep, send, first):
    other = swap(send)
    if first == 1:
        out = add_low(keep[1::2], other[1::2])
    else:
        out = add_low(keep[2:], other[2:])
    return keep, other, out


def scatter_first(keep, other, out, first):
    return scatter_beside(keep, other, hop(out, first), first)


def scatter_beside(keep, other, got, first):
    return keep, other, got, add_low(keep[3 - first], other[3 - first], got[1])


def scatter_second(terms, first):
    return terms[:3] + (hop(terms[3], 3 - first),)


def per_device(
    hyper,
    axes,
    tokens,
    cotangent,
    lengths,
    routes,
    norm_attn,
    w_qkv,
    w_out,
    norm_moe,
    w_router,
    w_resid,
    w_const,
    v_const,
    w_gate_up,
    w_down,
):
    micro_count, seq_count, block_len, feature_dim = tokens.shape
    rows = micro_count * seq_count * block_len
    layer_count, shard_rows, qkv_cols = w_qkv.shape
    heads = qkv_cols // (3 * HD)
    units = w_gate_up.shape[-1]
    groups = ("fsdp", "ctx")
    shard_count = feature_dim // shard_rows
    ctx = lax.axis_index("ctx")
    me = lax.axis_index("fsdp") * axes["ctx"] + ctx
    rank = lax.axis_index("tp").reshape(1)
    if hyper:
        offs = me ^ jnp.arange(shard_count, dtype=jnp.int32)
    else:
        offs = jnp.zeros((1,), jnp.int32)
    info = jnp.concatenate([ctx.reshape(1), lengths.reshape(-1)]).astype(jnp.int32)
    resid = jnp.zeros((16, 16), F32).at[:NE, :NE].set(w_resid.astype(F32))

    tp_count = axes["tp"]
    outer = share(jnp.transpose(w_out, (0, 2, 1)), tp_count)
    small, wide = [], []
    for layer in range(layer_count):
        vec = jnp.concatenate(
            [
                w_router[layer],
                jnp.zeros((shard_rows, ROW_CONST - NE), BF16),
                w_const[layer, 0],
                w_const[layer, 1],
                v_const[layer].T,
                norm_attn[layer][:, None],
                norm_moe[layer][:, None],
                jnp.zeros((shard_rows, PACK - ROW_GM - 1), BF16),
            ],
            axis=1,
        )
        pad = jnp.zeros((shard_rows, round_up(qkv_cols, 128) - qkv_cols), BF16)
        turned = [item[layer] for item in outer]
        small.append(jnp.concatenate([w_qkv[layer], pad, vec] + turned, axis=1))
        wide.append(pack_wide(w_gate_up, jnp.swapaxes(w_down, 2, 3), layer))
    weights, wide_first = [None] * layer_count, [None] * layer_count

    def fetch_small(layer, after):
        own = small[layer]
        if hyper:
            own, _ = tie(own, after)
            pieces = gather_small(own)
            fetch_first(layer, [pieces[k] for k in (2, 4, 6)])
        else:
            pieces = [lax.all_gather(own, groups, axis=0, tiled=True)]
        outs = prep_weights(pieces, offs, feature_dim, qkv_cols, heads * HD, tp_count)
        weights[layer] = [outs[0], outs[2], outs[1]]

    def fetch_first(layer, after):
        (low, high), _ = tie(wide[layer], after)
        lows, highs = [low, None, hop(low, 2)], [high, hop(high, 1), None]
        if layer > 0:
            lows[1], highs[2] = hop(low, 1), hop(high, 2)
        wide_first[layer] = (lows, highs, [swap(low), swap(high)] if layer == 0 else [])

    def fetch_rest(layer, value):
        if hyper:
            value, (lows, highs, own) = tie(value, wide_first[layer])
            swapped[layer] = ({0: own[0]}, {0: own[1]}) if own else ({}, {})
            value = swap(value)
            if layer == 0:
                lows[1], highs[2] = hop(lows[0], 1), hop(highs[0], 2)
            lows.append(hop(lows[2], 1))
            highs.append(hop(highs[1], 2))
            rests[layer] = (lows, highs)
        else:
            value = swap(value)
        return value

    def fetch_cores(layer, after):
        if hyper:
            lows, highs = rests[layer]
            if layer == 0:
                swapped[0][0][2], swapped[0][1][1] = swap(lows[2]), swap(highs[1])
                after, swapped[0] = tie(after, swapped[0])
                if layer + 1 < layer_count:
                    mid, wide[layer + 1], small[layer + 1] = tie(
                        (lows[1], highs[2]), wide[layer + 1], small[layer + 1]
                    )
                    lows[1], highs[2] = mid
            else:
                (lows, highs), _ = tie((lows, highs), after)
            rests[layer] = (lows, highs)
        else:
            both = jnp.concatenate(wide[layer], axis=0)
            full = lax.all_gather(both, groups, axis=1, tiled=True)
            weights[layer].append([(full, 0, 0, NF)])
        return after

    def fetch_last(layer, after):
        if hyper:
            lows, highs = rests[layer]
            if layer == 0:
                (lows[3], highs[3]), _ = tie((lows[3], highs[3]), after)
            weights[layer].append(gather_cores(lows, highs, swapped[layer]))

    rests, swapped = [None] * layer_count, [None] * layer_count
    fetch_small(0, info)

    routes_t = jnp.moveaxis(routes.reshape(layer_count, rows, 2), 2, 1)
    routes_t = jnp.concatenate(
        [routes_t, jnp.full((layer_count, 6, rows), -1, jnp.int32)], axis=1
    )
    position = ctx * block_len + jnp.arange(block_len, dtype=jnp.int32)
    valid = position[None, None, :] < lengths[:, :, None]
    cot = jnp.where(valid[..., None], cotangent, 0).reshape(rows, feature_dim)

    base, ffn, prev_t = tokens.reshape(rows, feature_dim), None, None
    saved = []
    for layer in range(layer_count):
        qkv_full, _, vecs = weights[layer][:3]
        outs = qkv_part(base, ffn, vecs, qkv_full)
        h_in, qkv = outs if ffn is not None else (base, outs[0])
        other = fetch_rest(layer, qkv)
        context, lse = attend_forward(qkv, other, info, heads)
        ctx_all = lax.all_gather(fetch_cores(layer, context), "tp", axis=0)
        wo_all = weights[layer][1]
        middle, base, xm_low, gates_t, logits_t = middle_part(
            h_in, ctx_all, wo_all, vecs, routes_t[layer], prev_t, resid, rank
        )
        fetch_last(layer, xm_low)
        pieces = weights[layer][3]
        saved.append((h_in, qkv, other, context, lse, middle, xm_low, gates_t, prev_t))
        prev_t = logits_t
        if layer < layer_count - 1:
            part, _, _ = experts(True, False, xm_low, None, routes_t[layer], gates_t, pieces, offs)
            fetch_small(layer + 1, part)
            ffn = lax.psum(part, "tp")
            if hyper:
                ffn, wide_first[layer + 1] = tie(ffn, wide_first[layer + 1])

    grad, grad_low = cot, cot
    grad_logits, wide_out, pending, small_terms, late = None, None, None, None, None
    finals = [None] * layer_count
    for layer in reversed(range(layer_count)):
        qkv_full, wo_all, vecs, pieces = weights[layer]
        h_in, qkv, other, context, lse, middle, xm_low, gates_t, prev_t = saved[layer]
        top = layer == layer_count - 1
        part, gx, grads = experts(
            top, True, xm_low, grad_low, routes_t[layer], gates_t, pieces, offs
        )
        if not top and late is not None:
            late[0] = lax.psum(late[0], "tp")
            gx, grads, late, pending = tie(gx, grads, late, pending)
        gx = lax.psum(gx, "tp")
        if hyper:
            sums = [scatter_cores(grads[2 * k], grads[2 * k + 1], k + 1) for k in range(2)]
            got = [hop(sums[k][2], k + 1) for k in range(2)]
            if pending is not None:
                wide_terms, small_parts, dres = pending
                terms = [scatter_second(wide_terms[k], k + 1) for k in range(2)]
                terms, sums = tie(terms, sums)
                wide_out = final_sums(terms[0], terms[1], wide_out, layer + 1, layer_count)
                upper = scatter_cores(*pack_grads(*small_parts, offs), 1)
                gx, sums, wide_out, upper = tie(gx, sums, wide_out, upper)
                upper_got = hop(upper[2], 1)
            else:
                gx, sums = tie(gx, sums)
        if top:
            base_top = base
        else:
            late[1], gx = tie(late[1], gx)
            late[1] = lax.psum(late[1], "tp")
        gg_t = gx[rows : rows + 16, :block_len].astype(F32)
        gg_t = jnp.moveaxis(gg_t.reshape(2, 8, block_len)[: rows // BLOCK], 0, 1).reshape(8, rows)
        extra = (prev_t, resid) if prev_t is not None else (grad_logits,)
        outs = gate_backward(
            grad, middle, gx, vecs, routes_t[layer], gates_t, gg_t, context, wo_all[0], extra
        )
        gmid, gctx, dwo, dvec = outs[:4]
        if prev_t is not None:
            grad_logits, dres = outs[4:]
        gown, goth = attend_backward(qkv, other, lse, gctx, info, heads)
        if hyper:
            wide_terms = [scatter_beside(*sums[k][:2], got[k], k + 1) for k in range(2)]
        if not top:
            gown, goth, late = tie(gown, goth, late)
            if hyper:
                gown, wide_terms, upper_got = tie(gown, wide_terms, upper_got)
        goth = swap(goth)
        ga_part, dqkv, dgain = qkv_backward(gown, goth, h_in, vecs, qkv_full)
        small_parts = (dqkv, dwo, dvec, dgain)
        own = None
        ga = lax.psum(ga_part, "tp")
        if hyper:
            if layer > 0:
                dres = dres + swap(dres)
                dres = dres + hop(dres, 1)
                ga, wide_terms, dres, small_parts = tie(ga, wide_terms, dres, small_parts)
                dres = dres + hop(dres, 2)
                pending = (wide_terms, small_parts, dres)
            else:
                small_terms = scatter_second(scatter_beside(*upper[:2], upper_got, 1), 1)
                terms = [scatter_second(wide_terms[k], k + 1) for k in range(2)]
                terms, small_parts, late = tie(terms, small_parts, late)
                wide_out = final_sums(terms[0], terms[1], wide_out, layer, layer_count)
                own = scatter_cores(*pack_grads(*small_parts, offs), 1)
                owns = [scatter_second(scatter_first(*own, 1), 1), small_terms]
                owns = [
                    sum((term[0] if term.ndim == 3 else term).astype(F32) for term in item)
                    for item in owns
                ]
                gains = share(jnp.stack([item[:, -PACK + ROW_GA] for item in owns]), tp_count)
        if top:
            late = [part[:block_len], part[block_len:]]
            late[0], ga = tie(late[0], ga)
        outs = norm_backward(gmid, ga, h_in, vecs, layer > 0)
        grad = outs[0]
        grad_low = outs[-1]
        finals[layer] = (grads, small_parts, own)

    late = jnp.concatenate(late, axis=0)
    mixed = (base_top + late.astype(F32)).astype(BF16)

    resid_total = (dres if hyper else lax.psum(dres, groups))[:NE, :NE]
    results = [None] * layer_count
    for layer in reversed(range(layer_count)):
        grads, small_parts, own = finals[layer]
        if hyper:
            own = owns[layer]
        else:
            packed = pack_grads(*small_parts, offs)
            own = lax.psum_scatter(packed[0], groups, scatter_dimension=0, tiled=True).astype(F32)
            wide_own = lax.psum_scatter(
                grads[0], groups, scatter_dimension=1, tiled=True
            ).astype(F32)
            here = (
                wide_own[:, :, : 2 * units].reshape(NF, shard_rows, 2, units),
                wide_own[:, :, 2 * units :],
            )
            if wide_out is None:
                wide_out = ([], [])
            wide_out[0].insert(0, here[0])
            wide_out[1].insert(0, here[1])
        out_cols = heads * HD
        vec = own[:, qkv_cols + out_cols :]
        results[layer] = (
            own[:, :qkv_cols],
            own[:, qkv_cols : qkv_cols + out_cols].T,
            vec[:, ROW_GM],
            vec[:, :NE],
            jnp.stack([vec[:, ROW_CONST : ROW_CONST + 2], vec[:, ROW_CONST + 2 : ROW_CONST + 4]]),
            vec[:, ROW_VEC : ROW_VEC + 2].T,
            vec[:, ROW_GA],
        )
    if not hyper:
        wide_out = (jnp.stack(wide_out[0]), jnp.stack(wide_out[1]))
    stacked = [jnp.stack([item[member] for item in results]) for member in range(7)]
    gains = jnp.stack(gains if hyper else share(stacked[6], tp_count))
    gain_own = sum(
        lax.dynamic_index_in_dim(gains, (rank[0] + tp_count - j) % tp_count, 0, keepdims=False)
        for j in range(tp_count)
    )
    return (
        mixed.reshape(tokens.shape),
        grad.reshape(tokens.shape),
        gain_own,
        stacked[0],
        stacked[1],
        stacked[2],
        stacked[3],
        resid_total,
        stacked[4],
        stacked[5],
        wide_out[0],
        jnp.swapaxes(wide_out[1], 2, 3),
    )


def solution(mesh):
    axes = dict(mesh.shape)
    hyper = axes["fsdp"] == 4 and axes["ctx"] == 2
    in_specs = (
        P(None, "fsdp", "ctx", None),
        P(None, "fsdp", "ctx", None),
        P(None, "fsdp"),
        P(None, None, "fsdp", "ctx", None),
        P(None, ("fsdp", "ctx")),
        P(None, ("fsdp", "ctx"), "tp"),
        P(None, "tp", ("fsdp", "ctx")),
        P(None, ("fsdp", "ctx")),
        P(None, ("fsdp", "ctx"), None),
        P(),
        P(None, None, ("fsdp", "ctx"), None),
        P(None, None, ("fsdp", "ctx")),
        P(None, None, ("fsdp", "ctx"), None, "tp"),
        P(None, None, "tp", ("fsdp", "ctx")),
    )
    out_specs = (
        P(None, "fsdp", "ctx", None),
        P(None, "fsdp", "ctx", None),
        P(None, ("fsdp", "ctx")),
        P(None, ("fsdp", "ctx"), "tp"),
        P(None, "tp", ("fsdp", "ctx")),
        P(None, ("fsdp", "ctx")),
        P(None, ("fsdp", "ctx"), None),
        P(),
        P(None, None, ("fsdp", "ctx"), None),
        P(None, None, ("fsdp", "ctx")),
        P(None, None, ("fsdp", "ctx"), None, "tp"),
        P(None, None, "tp", ("fsdp", "ctx")),
    )
    return jax.shard_map(
        functools.partial(per_device, hyper, axes),
        mesh=mesh,
        in_specs=in_specs,
        out_specs=out_specs,
        check_vma=False,
    )
```

```python
import functools

import jax
import jax.numpy as jnp
from jax import lax
from jax.experimental import pallas as pl
from jax.experimental.pallas import tpu as pltpu
from jax.sharding import PartitionSpec as P

HD = 64
NF = 8
NE = 12
BLOCK = 512
CAP = 128
TILE = 256
EPSILON = 1e-06
MASKED = -1e30
F32 = jnp.float32
BF16 = jnp.bfloat16
HIGH = lax.Precision.HIGHEST
ROW_CONST, ROW_VEC, ROW_GA, ROW_GM = 16, 20, 22, 23
VMEM_LIMIT = 58 * 1024 * 1024
SCALE = 0.05
PACK = 128

NN = (((1,), (0,)), ((), ()))
NT = (((1,), (1,)), ((), ()))
TN = (((0,), (0,)), ((), ()))


def mm(left, right, dims=NN, precision=None):
    return lax.dot_general(left, right, dims, precision=precision, preferred_element_type=F32)


def kernel_params():
    return pltpu.CompilerParams(vmem_limit_bytes=VMEM_LIMIT)


def cost(flops, nbytes, trans=0):
    return pl.CostEstimate(
        flops=int(flops * SCALE), bytes_accessed=int(nbytes * SCALE), transcendentals=int(trans * SCALE)
    )


def iota(shape, dim):
    return lax.broadcasted_iota(jnp.int32, shape, dim)


def full_spec(shape):
    zeros = (0,) * len(shape)
    return pl.BlockSpec(shape, lambda *idx: zeros)


SMEM_SPEC = pl.BlockSpec(memory_space=pltpu.SMEM)


def pad_rows(rows, count, width):
    row_id = iota((count, width), 0)
    out = jnp.zeros((count, width), F32)
    for place, row in rows:
        out = jnp.where(row_id == place, row, out)
    return out


def round_up(value, unit):
    return -(-value // unit) * unit


def prep_kernel(count, rows, out_cols, offs_ref, *refs):
    qkv_ref, vec_ref, wo_refs = refs[count], refs[count + 1], refs[count + 2 : -2]
    scr_ref, wo_scr = refs[-2:]
    cols = qkv_ref.shape[1]
    for piece in range(count):
        start = pl.multiple_of(offs_ref[piece] * rows, rows)
        block = refs[piece][...]
        qkv_ref[pl.ds(start, rows), :] = block[:, :cols]
        scr_ref[pl.ds(start, rows), :] = block[:, cols : cols + PACK].astype(F32)
        for rank in range(len(wo_refs)):
            first = cols + PACK + rank * out_cols
            wo_scr[rank, pl.ds(start, rows), :out_cols] = block[:, first : first + out_cols]
    vec_ref[...] = scr_ref[...].T[:32]
    total = wo_scr.shape[1]
    rest = out_cols - 128
    for rank, ref in enumerate(wo_refs):
        ref[:total, :] = wo_scr[rank, :, :128]
        ref[total:, :rest] = wo_scr[rank, : total // 2, 128:out_cols]
        ref[total:, rest:] = wo_scr[rank, total // 2 :, 128:out_cols]


def prep_weights(pieces, offs, feature_dim, qkv_cols, out_cols, out_count):
    count = len(pieces)
    cols = round_up(qkv_cols, 128)
    vmem = pl.BlockSpec(memory_space=pltpu.VMEM)
    outs = pl.pallas_call(
        functools.partial(prep_kernel, count, feature_dim // count, out_cols),
        out_shape=tuple(
            [
                jax.ShapeDtypeStruct((feature_dim, cols), BF16),
                jax.ShapeDtypeStruct((32, feature_dim), F32),
            ]
            + [jax.ShapeDtypeStruct((feature_dim * 3 // 2, 128), BF16)] * out_count
        ),
        in_specs=[SMEM_SPEC] + [vmem] * count,
        out_specs=tuple([vmem] * (2 + out_count)),
        scratch_shapes=[
            pltpu.VMEM((feature_dim, PACK), F32),
            pltpu.VMEM((out_count, feature_dim, 256), BF16),
        ],
        compiler_params=kernel_params(),
        cost_estimate=cost(1e6, 3e6),
        name="prep",
    )(offs, *pieces)
    return outs[0], outs[1], list(outs[2:])


def pack_kernel(count, rows, offs_ref, dqkv_ref, dwo_ref, dvec_ref, dgain_ref, *refs):
    outs, scr_ref = refs[:-1], refs[-1]
    cols, out_cols = dqkv_ref.shape[1], dwo_ref.shape[1]
    scr_ref[:, :cols] = dqkv_ref[...]
    scr_ref[:, cols : cols + out_cols] = dwo_ref[...]
    vec = dvec_ref[...]
    vec = jnp.where(iota(vec.shape, 0) == ROW_GA, dgain_ref[0:1, :], vec)
    wide = jnp.concatenate([vec, jnp.zeros((PACK - vec.shape[0], vec.shape[1]), F32)], axis=0).T
    scr_ref[:, cols + out_cols :] = wide
    for piece in range(count):
        start = pl.multiple_of(offs_ref[piece] * rows, rows)
        block = scr_ref[pl.ds(start, rows), :].astype(BF16)
        if count > 1:
            outs[piece % 2][piece // 2] = block
        else:
            outs[0][...] = block


def pack_grads(dqkv, dwo, dvec, dgain, offs):
    feature_dim = dqkv.shape[0]
    count = offs.shape[0]
    rows = feature_dim // count
    width = dqkv.shape[1] + dwo.shape[1] + PACK
    shape = (count // 2, rows, width) if count > 1 else (feature_dim, width)
    vmem = pl.BlockSpec(memory_space=pltpu.VMEM)
    outs = 2 if count > 1 else 1
    return pl.pallas_call(
        functools.partial(pack_kernel, count, rows),
        out_shape=tuple([jax.ShapeDtypeStruct(shape, BF16)] * outs),
        in_specs=[SMEM_SPEC, vmem, vmem, vmem, vmem],
        out_specs=tuple([vmem] * outs),
        scratch_shapes=[pltpu.VMEM((feature_dim, width), F32)],
        compiler_params=kernel_params(),
        cost_estimate=cost(1e6, 6e6),
        name="pack_grads",
    )(offs, dqkv, dwo, dvec, dgain)


def pack_wide_kernel(gu_ref, down_ref, low_ref, high_ref):
    units = down_ref.shape[-1]

    def write(ref):
        ref[0, :, :units] = gu_ref[0, 0, :, 0, :]
        ref[0, :, units : 2 * units] = gu_ref[0, 0, :, 1, :]
        ref[0, :, 2 * units :] = down_ref[0, 0]

    @pl.when(pl.program_id(0) < NF // 2)
    def _():
        write(low_ref)

    @pl.when(pl.program_id(0) >= NF // 2)
    def _():
        write(high_ref)


def pack_wide(w_gate_up, w_down_t, layer):
    _, _, rows, _, units = w_gate_up.shape
    half = NF // 2
    specs = [
        pl.BlockSpec(
            (1, rows, 3 * units), lambda e, part=part: (jnp.clip(e - part * half, 0, half - 1), 0, 0)
        )
        for part in range(2)
    ]
    return pl.pallas_call(
        pack_wide_kernel,
        grid=(NF,),
        out_shape=tuple([jax.ShapeDtypeStruct((half, rows, 3 * units), BF16)] * 2),
        in_specs=[
            pl.BlockSpec((1, 1, rows, 2, units), lambda e: (layer, e, 0, 0, 0)),
            pl.BlockSpec((1, 1, rows, units), lambda e: (layer, e, 0, 0)),
        ],
        out_specs=tuple(specs),
        compiler_params=kernel_params(),
        cost_estimate=cost(1e6, 5e6),
        name="pack_wide",
    )(w_gate_up, w_down_t)


def qkv_kernel(with_ffn, *refs):
    if with_ffn:
        base_ref, ffn_ref, vec_ref, w_ref, h_ref, qkv_ref = refs
        hidden = base_ref[...] + ffn_ref[...].astype(F32)
        h_ref[...] = hidden
    else:
        base_ref, vec_ref, w_ref, qkv_ref = refs
        hidden = base_ref[...].astype(F32)
    gain = vec_ref[ROW_GA : ROW_GA + 1, :]
    scale = lax.rsqrt(jnp.mean(hidden * hidden, axis=-1, keepdims=True) + EPSILON)
    attn_in = (hidden * scale * gain).astype(BF16)
    qkv_ref[...] = mm(attn_in, w_ref[...]).astype(BF16)


def qkv_part(base, ffn, vecs, w_qkv):
    rows, feature_dim = base.shape
    cols = round_up(w_qkv.shape[1], 128)
    row_spec = pl.BlockSpec((TILE, feature_dim), lambda i: (i, 0))
    with_ffn = ffn is not None
    out_shape = [jax.ShapeDtypeStruct((rows, cols), BF16)]
    out_specs = [pl.BlockSpec((TILE, cols), lambda i: (i, 0))]
    if with_ffn:
        out_shape = [jax.ShapeDtypeStruct((rows, feature_dim), F32)] + out_shape
        out_specs = [row_spec] + out_specs
    ins = [base] + ([ffn] if with_ffn else []) + [vecs, w_qkv]
    in_specs = [row_spec] * (2 if with_ffn else 1) + [full_spec(vecs.shape), full_spec(w_qkv.shape)]
    return pl.pallas_call(
        functools.partial(qkv_kernel, with_ffn),
        grid=(rows // TILE,),
        out_shape=tuple(out_shape),
        in_specs=in_specs,
        out_specs=tuple(out_specs),
        compiler_params=kernel_params(),
        cost_estimate=cost(2 * rows * feature_dim * cols, rows * feature_dim * 10),
        name="qkv_part",
    )(*ins)


def attn_masks(ctx, length, tile, width):
    row = iota((TILE, width), 0) + tile * TILE
    col = iota((TILE, width), 1)
    return (col <= row) & (col + ctx * BLOCK < length)


def attn_fwd_kernel(heads, info_ref, own_ref, other_ref, ctx_ref, lse_ref):
    ctx = info_ref[0]
    length = info_ref[1 + pl.program_id(0)]
    own = own_ref[...]
    other = other_ref[...]
    for head in range(heads):
        col = head * 3 * HD
        k_own = own[:, col + HD : col + 2 * HD]
        v_own = own[:, col + 2 * HD : col + 3 * HD]
        k_oth = other[:, col + HD : col + 2 * HD]
        v_oth = other[:, col + 2 * HD : col + 3 * HD]
        for tile in range(BLOCK // TILE):
            width = (tile + 1) * TILE
            query = own[tile * TILE : (tile + 1) * TILE, col : col + HD] * BF16(HD**-0.5)
            s_own = mm(query, k_own[:width], NT)
            s_own = jnp.where(attn_masks(ctx, length, tile, width), s_own, MASKED)
            s_oth = jnp.where(ctx > 0, mm(query, k_oth, NT), MASKED)
            top = jnp.maximum(
                jnp.max(s_own, axis=-1, keepdims=True), jnp.max(s_oth, axis=-1, keepdims=True)
            )
            p_own = jnp.exp(s_own - top)
            p_oth = jnp.exp(s_oth - top)
            total = jnp.sum(p_own, axis=-1, keepdims=True) + jnp.sum(p_oth, axis=-1, keepdims=True)
            out = mm(p_own.astype(BF16), v_own[:width]) + mm(p_oth.astype(BF16), v_oth)
            out = out / total
            rows = slice(tile * TILE, (tile + 1) * TILE)
            ctx_ref[head * TILE : (head + 1) * TILE, tile * HD : (tile + 1) * HD] = out.astype(BF16)
            lse_ref[rows, head : head + 1] = top + jnp.log(total)


def attend_forward(qkv, other, info, heads):
    rows, cols = qkv.shape
    count = rows // BLOCK
    spec = pl.BlockSpec((BLOCK, cols), lambda i: (i, 0))
    return pl.pallas_call(
        functools.partial(attn_fwd_kernel, heads),
        grid=(count,),
        out_shape=(
            jax.ShapeDtypeStruct((count * heads * TILE, 2 * HD), BF16),
            jax.ShapeDtypeStruct((rows, 8), F32),
        ),
        in_specs=[SMEM_SPEC, spec, spec],
        out_specs=(
            pl.BlockSpec((heads * TILE, 2 * HD), lambda i: (i, 0)),
            pl.BlockSpec((BLOCK, 8), lambda i: (i, 0)),
        ),
        compiler_params=kernel_params(),
        cost_estimate=cost(rows * 1024 * heads * HD * 16, rows * cols * 6, rows * heads * 1024),
        name="attend_forward",
    )(info, qkv, other)


def attn_bwd_kernel(heads, info_ref, own_ref, other_ref, lse_ref, gctx_ref, gown_ref, goth_ref):
    ctx = info_ref[0]
    length = info_ref[1 + pl.program_id(0)]
    own = own_ref[...]
    other = other_ref[...]
    scale = BF16(HD**-0.5)
    for head in range(heads):
        col = head * 3 * HD
        k_own = own[:, col + HD : col + 2 * HD]
        v_own = own[:, col + 2 * HD : col + 3 * HD]
        k_oth = other[:, col + HD : col + 2 * HD]
        v_oth = other[:, col + 2 * HD : col + 3 * HD]
        goth_ref[:, col : col + HD] = jnp.zeros((BLOCK, HD), BF16)
        gk_own, gv_own, gk_oth, gv_oth = [], [], [], []
        for tile in range(BLOCK // TILE):
            width = (tile + 1) * TILE
            rows = slice(tile * TILE, (tile + 1) * TILE)
            query = own[rows, col : col + HD] * scale
            gout = gctx_ref[rows, head * HD : (head + 1) * HD]
            lse = lse_ref[rows, head : head + 1]
            s_own = mm(query, k_own[:width], NT)
            s_own = jnp.where(attn_masks(ctx, length, tile, width), s_own, MASKED)
            s_oth = jnp.where(ctx > 0, mm(query, k_oth, NT), MASKED)
            p_own = jnp.exp(s_own - lse)
            p_oth = jnp.exp(s_oth - lse)
            d_own = mm(gout, v_own[:width], NT)
            d_oth = mm(gout, v_oth, NT)
            inner = jnp.sum(p_own * d_own, axis=-1, keepdims=True) + jnp.sum(
                p_oth * d_oth, axis=-1, keepdims=True
            )
            ds_own = (p_own * (d_own - inner)).astype(BF16)
            ds_oth = (p_oth * (d_oth - inner)).astype(BF16)
            p_own = p_own.astype(BF16)
            p_oth = p_oth.astype(BF16)
            gown_ref[rows, col : col + HD] = (mm(ds_own, k_own[:width]) + mm(ds_oth, k_oth)) * (
                HD**-0.5
            )
            gk_own.append(mm(ds_own, query, TN))
            gv_own.append(mm(p_own, gout, TN))
            gk_oth.append(mm(ds_oth, query, TN))
            gv_oth.append(mm(p_oth, gout, TN))
        gown_ref[:TILE, col + HD : col + 2 * HD] = gk_own[0] + gk_own[1][:TILE]
        gown_ref[TILE:, col + HD : col + 2 * HD] = gk_own[1][TILE:]
        gown_ref[:TILE, col + 2 * HD : col + 3 * HD] = gv_own[0] + gv_own[1][:TILE]
        gown_ref[TILE:, col + 2 * HD : col + 3 * HD] = gv_own[1][TILE:]
        goth_ref[:, col + HD : col + 2 * HD] = (gk_oth[0] + gk_oth[1]).astype(BF16)
        goth_ref[:, col + 2 * HD : col + 3 * HD] = (gv_oth[0] + gv_oth[1]).astype(BF16)


def attend_backward(qkv, other, lse, grad_context, info, heads):
    rows, width = qkv.shape
    cols = heads * 3 * HD
    spec = pl.BlockSpec((BLOCK, width), lambda i: (i, 0))
    return pl.pallas_call(
        functools.partial(attn_bwd_kernel, heads),
        grid=(rows // BLOCK,),
        out_shape=(
            jax.ShapeDtypeStruct((rows, cols), F32),
            jax.ShapeDtypeStruct((rows, width), BF16),
        ),
        in_specs=[
            SMEM_SPEC,
            spec,
            spec,
            pl.BlockSpec((BLOCK, 8), lambda i: (i, 0)),
            pl.BlockSpec((BLOCK, heads * HD), lambda i: (i, 0)),
        ],
        out_specs=(pl.BlockSpec((BLOCK, cols), lambda i: (i, 0)), spec),
        compiler_params=kernel_params(),
        cost_estimate=cost(rows * 1024 * heads * HD * 40, rows * cols * 12, rows * heads * 1024),
        name="attend_backward",
    )(info, qkv, other, lse, grad_context)


def alpha_rows(gate_in, const_idx):
    first = gate_in[ROW_CONST + 2 * const_idx : ROW_CONST + 2 * const_idx + 1]
    second = gate_in[ROW_CONST + 2 * const_idx + 1 : ROW_CONST + 2 * const_idx + 2]
    return pair(first, second)


def pair(first, second):
    top = jnp.maximum(first, second)
    exp_first = jnp.exp(first - top)
    exp_second = jnp.exp(second - top)
    total = exp_first + exp_second
    return exp_first / total, exp_second / total


def picks(route, value):
    return (route == value).astype(F32)


def gate_coefs(routes, gates, alphas):
    copy = picks(routes[0], NF + 1) * gates[0] + picks(routes[1], NF + 1) * gates[1]
    const = [
        picks(routes[0], NF + 2 + j) * gates[0] + picks(routes[1], NF + 2 + j) * gates[1]
        for j in range(2)
    ]
    on_normed = copy + const[0] * alphas[0][0] + const[1] * alphas[1][0]
    on_vec = [const[j] * alphas[j][1] for j in range(2)]
    return const, on_normed, on_vec


def to_columns(rows):
    width = rows[0].shape[1]
    return pad_rows(list(enumerate(rows)), 128, width).T


def unpack_context(both):
    heads = both.shape[0] // TILE
    side = lax.rem(pl.program_id(0), 2) == 0
    both = jnp.where(side, both[:, :HD], both[:, HD:])
    parts = [both[head * TILE : (head + 1) * TILE] for head in range(heads)]
    return jnp.concatenate(parts, axis=1)


def middle_kernel(with_prev, rank_ref, *refs):
    h_ref, ctx_ref, refs = refs[0], refs[1], refs[2:]
    count = ctx_ref.shape[0]
    wo_refs, refs = refs[:count], refs[count:]
    if with_prev:
        vec_ref, route_ref, prev_ref, resid_ref = refs[:4]
        refs = refs[4:]
    else:
        vec_ref, route_ref = refs[:2]
        refs = refs[2:]
    mid_ref, base_ref, xm_ref, gate_ref, logit_ref = refs
    attn_out = 0.0
    for back, ref in enumerate(wo_refs):
        context = unpack_context(ctx_ref[lax.rem(rank_ref[0] + count - back, count)])
        total = ref.shape[0] * 2 // 3
        rest = context[:, 128:]
        attn_out += mm(context[:, :128], ref[:total], NT) + jnp.concatenate(
            [mm(rest, ref[total:, :HD], NT), mm(rest, ref[total:, HD:], NT)], axis=1
        )
    middle = h_ref[...].astype(F32) + attn_out
    mid_ref[...] = middle
    vecs = vec_ref[...]
    scale = lax.rsqrt(jnp.mean(middle * middle, axis=-1, keepdims=True) + EPSILON)
    normed = middle * scale * vecs[ROW_GM : ROW_GM + 1]
    xm_low = normed.astype(BF16)
    xm_ref[...] = xm_low
    gate_in = mm(vecs[:32].astype(BF16), xm_low, NT)
    logits = gate_in[:16]
    if with_prev:
        logits = logits + mm(resid_ref[...], prev_ref[...], TN, HIGH)
    logit_ref[...] = logits
    routes = (route_ref[0:1], route_ref[1:2])
    expert = iota(logits.shape, 0)
    chosen = [
        jnp.sum(jnp.where(expert == route, logits, 0.0), axis=0, keepdims=True) for route in routes
    ]
    gates = pair(chosen[0], chosen[1])
    gate_ref[...] = pad_rows(list(enumerate(gates)), 8, logits.shape[1])
    alphas = [alpha_rows(gate_in, j) for j in range(2)]
    const, on_normed, on_vec = gate_coefs(routes, gates, alphas)
    cols = to_columns([on_normed, on_vec[0], on_vec[1]])
    base_ref[...] = (
        middle
        + cols[:, 0:1] * normed
        + cols[:, 1:2] * vecs[ROW_VEC : ROW_VEC + 1]
        + cols[:, 2:3] * vecs[ROW_VEC + 1 : ROW_VEC + 2]
    )


def middle_part(h, ctx_all, wo_all, vecs, routes_t, prev_t, resid, rank):
    rows, feature_dim = h.shape
    tp_count, packed, lanes = ctx_all.shape
    packed = packed * BLOCK // rows
    row_spec = pl.BlockSpec((TILE, feature_dim), lambda i: (i, 0))
    lane8 = pl.BlockSpec((8, TILE), lambda i: (0, i))
    lane16 = pl.BlockSpec((16, TILE), lambda i: (0, i))
    ins = [rank, h, ctx_all, *wo_all, vecs, routes_t]
    in_specs = [
        SMEM_SPEC,
        row_spec,
        pl.BlockSpec((tp_count, packed, lanes), lambda i: (0, i // 2, 0)),
        *[full_spec(item.shape) for item in wo_all],
        full_spec(vecs.shape),
        lane8,
    ]
    with_prev = prev_t is not None
    if with_prev:
        ins += [prev_t, resid]
        in_specs += [lane16, full_spec(resid.shape)]
    return pl.pallas_call(
        functools.partial(middle_kernel, with_prev),
        grid=(rows // TILE,),
        out_shape=(
            jax.ShapeDtypeStruct((rows, feature_dim), F32),
            jax.ShapeDtypeStruct((rows, feature_dim), F32),
            jax.ShapeDtypeStruct((rows, feature_dim), BF16),
            jax.ShapeDtypeStruct((8, rows), F32),
            jax.ShapeDtypeStruct((16, rows), F32),
        ),
        in_specs=in_specs,
        out_specs=(row_spec, row_spec, row_spec, lane8, lane16),
        compiler_params=kernel_params(),
        cost_estimate=cost(2 * rows * feature_dim * feature_dim, rows * feature_dim * 16),
        name="middle_part",
    )(*ins)


def split(value):
    high = value.astype(BF16)
    return high, (value - high.astype(F32)).astype(BF16)


def gate_bwd_kernel(with_prev, *refs):
    gh_ref, mid_ref, gxm_ref, vec_ref, route_ref, gate_ref, gg_ref, ctx_ref, wo_ref = refs[:9]
    refs = refs[9:]
    if with_prev:
        prev_ref, resid_ref = refs[:2]
        gmid_ref, gctx_ref, dwo_ref, dvec_ref, gprev_ref, dres_ref = refs[2:]
    else:
        gl_ref = refs[0]
        gmid_ref, gctx_ref, dwo_ref, dvec_ref = refs[1:]
    step = pl.program_id(0)
    grad = gh_ref[...].astype(F32)
    middle = mid_ref[...]
    vecs = vec_ref[...]
    gain = vecs[ROW_GM : ROW_GM + 1]
    scale = lax.rsqrt(jnp.mean(middle * middle, axis=-1, keepdims=True) + EPSILON)
    unit = middle * scale
    normed = unit * gain
    xm_low = normed.astype(BF16)
    low_vecs = vecs[:32].astype(BF16)
    gate_in = mm(low_vecs, xm_low, NT)
    alphas = [alpha_rows(gate_in, j) for j in range(2)]
    routes = (route_ref[0:1], route_ref[1:2])
    gates = (gate_ref[0:1], gate_ref[1:2])
    const, on_normed, on_vec = gate_coefs(routes, gates, alphas)
    grad_hi, grad_lo = split(grad)
    vec_dots = mm(low_vecs[16:32], grad_hi, NT) + mm(low_vecs[16:32], grad_lo, NT)
    dot_vec = [vec_dots[ROW_VEC - 16 + j : ROW_VEC - 15 + j] for j in range(2)]
    dot_col = jnp.sum(grad * normed, axis=-1, keepdims=True)
    dot_normed = jnp.broadcast_to(dot_col, (dot_col.shape[0], 128)).T[0:1]
    term = [alphas[j][0] * dot_normed + alphas[j][1] * dot_vec[j] for j in range(2)]
    gate_grads = []
    for slot in range(2):
        fixed = (
            picks(routes[slot], NF + 1) * dot_normed
            + picks(routes[slot], NF + 2) * term[0]
            + picks(routes[slot], NF + 3) * term[1]
        )
        gate_grads.append(jnp.where(routes[slot] < NF, gg_ref[slot : slot + 1], fixed))
    inner = gates[0] * gate_grads[0] + gates[1] * gate_grads[1]
    chosen_grads = [gates[slot] * (gate_grads[slot] - inner) for slot in range(2)]
    expert = iota((16, TILE), 0)
    grad_logits = jnp.where(expert == routes[0], chosen_grads[0], 0.0) + jnp.where(
        expert == routes[1], chosen_grads[1], 0.0
    )
    if not with_prev:
        grad_logits = grad_logits + gl_ref[...]
    alpha_grads = []
    for j in range(2):
        grad_first = const[j] * dot_normed
        grad_second = const[j] * dot_vec[j]
        mean = alphas[j][0] * grad_first + alphas[j][1] * grad_second
        alpha_grads.append((2 * j, alphas[j][0] * (grad_first - mean)))
        alpha_grads.append((2 * j + 1, alphas[j][1] * (grad_second - mean)))
    grad_in = jnp.concatenate([grad_logits, pad_rows(alpha_grads, 16, TILE)], axis=0)
    in_hi, in_lo = split(grad_in)
    low_gate = jnp.where(iota(low_vecs.shape, 0) < ROW_VEC, low_vecs, 0)
    grad_xm = mm(in_hi, low_gate, TN) + mm(in_lo, low_gate, TN)
    cols = to_columns([on_normed])
    grad_y = cols[:, 0:1] * grad + grad_xm + gxm_ref[...].astype(F32)
    weighted = grad_y * gain
    mean = jnp.mean(weighted * unit, axis=-1, keepdims=True)
    grad_mid = grad + scale * (weighted - unit * mean)
    gmid_ref[...] = grad_mid
    low_mid = grad_mid.astype(BF16)
    total = low_mid.shape[1]
    gctx_ref[:, :128] = mm(low_mid, wo_ref[:total]).astype(BF16)
    gctx_ref[:, 128:] = (
        mm(low_mid[:, : total // 2], wo_ref[total:, :HD])
        + mm(low_mid[:, total // 2 :], wo_ref[total:, HD:])
    ).astype(BF16)
    dwo = mm(low_mid, unpack_context(ctx_ref[...]), TN)
    vec_rows = pad_rows([(ROW_VEC - 16 + j, on_vec[j]) for j in range(2)], 16, TILE)
    vec_hi, vec_lo = split(vec_rows)
    dvec_low = mm(vec_hi, grad_hi) + mm(vec_lo, grad_hi)
    dvec_gate = mm(in_hi, xm_low) + mm(in_lo, xm_low)
    dgain = jnp.sum(grad_y * unit, axis=0, keepdims=True)
    row_id = iota(dvec_gate.shape, 0)
    dvec = dvec_gate + jnp.concatenate([jnp.zeros_like(dvec_low), dvec_low], axis=0)
    dvec = jnp.where(row_id == ROW_GM, dgain, dvec)

    @pl.when(step == 0)
    def _():
        dwo_ref[...] = dwo
        dvec_ref[...] = dvec

    @pl.when(step > 0)
    def _():
        dwo_ref[...] += dwo
        dvec_ref[...] += dvec

    if with_prev:
        gprev_ref[...] = mm(resid_ref[...], grad_logits, NN, HIGH)
        dres = mm(prev_ref[...], grad_logits, NT, HIGH)

        @pl.when(step == 0)
        def _():
            dres_ref[...] = dres

        @pl.when(step > 0)
        def _():
            dres_ref[...] += dres


def gate_backward(grad, middle, gxm, vecs, routes_t, gates_t, gg_t, context, wo_own, extra):
    rows, feature_dim = middle.shape
    out_cols = context.shape[0] * BLOCK // rows // TILE * HD
    with_prev = len(extra) == 2
    row_spec = pl.BlockSpec((TILE, feature_dim), lambda i: (i, 0))
    lane8 = pl.BlockSpec((8, TILE), lambda i: (0, i))
    lane16 = pl.BlockSpec((16, TILE), lambda i: (0, i))
    ctx_spec = pl.BlockSpec((context.shape[0] * BLOCK // rows, 2 * HD), lambda i: (i // 2, 0))
    out_spec = pl.BlockSpec((TILE, out_cols), lambda i: (i, 0))
    wo_spec = full_spec(wo_own.shape)
    in_specs = [row_spec, row_spec, row_spec, full_spec(vecs.shape), lane8, lane8, lane8]
    in_specs += [ctx_spec, wo_spec, lane16]
    out_shape = [
        jax.ShapeDtypeStruct((rows, feature_dim), F32),
        jax.ShapeDtypeStruct((rows, out_cols), BF16),
        jax.ShapeDtypeStruct((feature_dim, out_cols), F32),
        jax.ShapeDtypeStruct((32, feature_dim), F32),
    ]
    out_specs = [row_spec, out_spec, full_spec((feature_dim, out_cols)), full_spec((32, feature_dim))]
    if with_prev:
        in_specs.append(full_spec(extra[1].shape))
        out_shape += [jax.ShapeDtypeStruct((16, rows), F32), jax.ShapeDtypeStruct((16, 16), F32)]
        out_specs += [lane16, full_spec((16, 16))]
    return pl.pallas_call(
        functools.partial(gate_bwd_kernel, with_prev),
        grid=(rows // TILE,),
        out_shape=tuple(out_shape),
        in_specs=in_specs,
        out_specs=tuple(out_specs),
        compiler_params=kernel_params(),
        cost_estimate=cost(4 * rows * feature_dim * out_cols, rows * feature_dim * 18),
        name="gate_backward",
    )(grad, middle, gxm, vecs, routes_t, gates_t, gg_t, context, wo_own, *extra)


def qkv_bwd_kernel(gown_ref, goth_ref, h_ref, vec_ref, w_ref, part_ref, dw_ref, dgain_ref):
    step = pl.program_id(0)
    cols = gown_ref.shape[1]
    grad = (gown_ref[...] + goth_ref[:, :cols].astype(F32)).astype(BF16)
    part = mm(grad, w_ref[:, :cols], NT)
    part_ref[...] = part.astype(BF16)
    hidden = h_ref[...].astype(F32)
    gain = vec_ref[ROW_GA : ROW_GA + 1, :]
    scale = lax.rsqrt(jnp.mean(hidden * hidden, axis=-1, keepdims=True) + EPSILON)
    unit = hidden * scale
    attn_in = (unit * gain).astype(BF16)
    dw = mm(attn_in, grad, TN)
    dgain = jnp.broadcast_to(jnp.sum(part * unit, axis=0, keepdims=True), dgain_ref.shape)

    @pl.when(step == 0)
    def _():
        dw_ref[...] = dw
        dgain_ref[...] = dgain

    @pl.when(step > 0)
    def _():
        dw_ref[...] += dw
        dgain_ref[...] += dgain


def qkv_backward(gown, goth, h, vecs, w_qkv):
    rows, feature_dim = h.shape
    cols = gown.shape[1]
    row_spec = pl.BlockSpec((TILE, feature_dim), lambda i: (i, 0))
    col_spec = pl.BlockSpec((TILE, cols), lambda i: (i, 0))
    oth_spec = pl.BlockSpec((TILE, goth.shape[1]), lambda i: (i, 0))
    return pl.pallas_call(
        qkv_bwd_kernel,
        grid=(rows // TILE,),
        out_shape=(
            jax.ShapeDtypeStruct((rows, feature_dim), BF16),
            jax.ShapeDtypeStruct((feature_dim, cols), F32),
            jax.ShapeDtypeStruct((8, feature_dim), F32),
        ),
        in_specs=[col_spec, oth_spec, row_spec, full_spec(vecs.shape), full_spec(w_qkv.shape)],
        out_specs=(row_spec, full_spec((feature_dim, cols)), full_spec((8, feature_dim))),
        compiler_params=kernel_params(),
        cost_estimate=cost(4 * rows * feature_dim * cols, rows * feature_dim * 10),
        name="qkv_backward",
    )(gown, goth, h, vecs, w_qkv)


def norm_bwd_kernel(with_low, gmid_ref, ga_ref, h_ref, vec_ref, out_ref, *rest):
    hidden = h_ref[...].astype(F32)
    gain = vec_ref[ROW_GA : ROW_GA + 1, :]
    scale = lax.rsqrt(jnp.mean(hidden * hidden, axis=-1, keepdims=True) + EPSILON)
    unit = hidden * scale
    grad_y = ga_ref[...].astype(F32)
    weighted = grad_y * gain
    mean = jnp.mean(weighted * unit, axis=-1, keepdims=True)
    grad = gmid_ref[...] + scale * (weighted - unit * mean)
    out_ref[...] = grad
    if with_low:
        rest[0][...] = grad.astype(BF16)


def norm_backward(gmid, ga, h, vecs, with_low):
    rows, feature_dim = gmid.shape
    row_spec = pl.BlockSpec((TILE, feature_dim), lambda i: (i, 0))
    out_shape = [jax.ShapeDtypeStruct((rows, feature_dim), F32)]
    out_specs = [row_spec]
    if with_low:
        out_shape.append(jax.ShapeDtypeStruct((rows, feature_dim), BF16))
        out_specs.append(row_spec)
    return pl.pallas_call(
        functools.partial(norm_bwd_kernel, with_low),
        grid=(rows // TILE,),
        out_shape=tuple(out_shape),
        in_specs=[row_spec, row_spec, row_spec, full_spec(vecs.shape)],
        out_specs=tuple(out_specs),
        compiler_params=kernel_params(),
        cost_estimate=cost(rows * feature_dim * 10, rows * feature_dim * 16),
        name="norm_backward",
    )(gmid, ga, h, vecs)


def experts_kernel(fwd, bwd, blocks, plan, out_count, rows, offs_ref, *refs):
    refs = list(refs)
    xm_ref = refs.pop(0)
    gh_ref = refs.pop(0) if bwd else None
    route_ref, gate_ref = refs.pop(0), refs.pop(0)
    w_refs = [refs.pop(0) for _ in plan]
    ffn_ref = refs.pop(0) if fwd else None
    if bwd:
        gx_ref = refs.pop(0)
        dw_refs = [refs.pop(0) for _ in range(out_count)]
    w_scr, sem_ref, hot_scr, pick_scr = (refs.pop(0) for _ in range(4))
    part_scr = refs.pop(0) if fwd else None
    if bwd:
        gpart_scr, raw_scr, gg_scr, dw_scr = refs
    expert = pl.program_id(0)
    last = pl.num_programs(0) - 1
    depth, width = w_scr.shape[0] // 2, w_scr.shape[1]
    units = width // 3

    def move(each, target, start):
        for ref, (off, first, number) in zip(w_refs, plan):

            def one(ref=ref, off=off, first=first):
                row = pl.multiple_of(offs_ref[off] * rows + target * depth, rows)
                copy = pltpu.make_async_copy(
                    ref.at[each - first], w_scr.at[pl.ds(row, rows)], sem_ref.at[target, off]
                )
                if start:
                    copy.start()
                else:
                    copy.wait()

            if number == NF:
                one()
            else:
                pl.when((each >= first) & (each < first + number))(one)

    slot = lax.rem(expert, 2)
    here = pl.ds(pl.multiple_of(slot * depth, depth), depth)

    @pl.when(expert == 0)
    def _():
        move(0 * expert, 0, True)

    @pl.when(expert < last)
    def _():
        move(expert + 1, 1 - slot, True)

    @pl.when(expert == 0)
    def _():
        order = (iota((BLOCK, BLOCK), 0) < iota((BLOCK, BLOCK), 1)).astype(BF16)
        ids = iota((NF, BLOCK), 0)
        row_ids = iota((CAP, BLOCK), 0).astype(F32)
        for block in range(blocks):
            lanes = slice(block * BLOCK, (block + 1) * BLOCK)
            hits = (ids == route_ref[0:1, lanes]) | (ids == route_ref[1:2, lanes])
            place = jnp.where(hits, mm(hits.astype(BF16), order), -1.0)
            for each in range(NF):
                hot_scr[block, each * CAP : (each + 1) * CAP, :] = (
                    (row_ids == place[each : each + 1]).astype(F32).astype(BF16)
                )
            hot = hot_scr[block]
            for source, target in ((xm_ref, pick_scr),) + (((gh_ref, raw_scr),) if bwd else ()):
                rows_all = mm(hot, source[lanes, :]).astype(BF16)
                for each in range(NF):
                    target[each, block * CAP : (block + 1) * CAP, :] = rows_all[
                        each * CAP : (each + 1) * CAP
                    ]
        if bwd:
            gg_scr[...] = jnp.zeros_like(gg_scr)

    def combine(source, block):
        return mm(hot_scr[block], source[block], TN)

    move(expert, slot, False)
    hot, gate_cols, masks = [], [], []
    first_row = pl.multiple_of(expert * CAP, CAP)
    for block in range(blocks):
        lanes = slice(block * BLOCK, (block + 1) * BLOCK)
        one_hot = hot_scr[block, pl.ds(first_row, CAP), :].astype(F32)
        mask = [route_ref[slot : slot + 1, lanes] == expert for slot in range(2)]
        gate_row = jnp.where(mask[0], gate_ref[0:1, lanes], 0.0) + jnp.where(
            mask[1], gate_ref[1:2, lanes], 0.0
        )
        gate_cols.append(jnp.sum(one_hot * gate_row, axis=1, keepdims=True))
        hot.append(one_hot)
        masks.append(mask)
    gate_col = jnp.concatenate(gate_cols, axis=0)
    picked = pick_scr[expert]
    gate_up = mm(picked, w_scr[here, : 2 * units])
    gate_in, up_in = gate_up[:, :units], gate_up[:, units:]
    sigmoid = lax.logistic(gate_in)
    silu = gate_in * sigmoid
    hidden = (silu * up_in).astype(BF16)
    if fwd:
        scaled = (mm(hidden, w_scr[here, 2 * units :], NT) * gate_col).astype(BF16)
        for block in range(blocks):
            part_scr[block, pl.ds(first_row, CAP), :] = scaled[block * CAP : (block + 1) * CAP]

        @pl.when(expert == last)
        def _():
            for block in range(blocks):
                ffn_ref[block * BLOCK : (block + 1) * BLOCK, :] = combine(part_scr, block).astype(
                    BF16
                )

    if bwd:
        raw = raw_scr[expert]
        grad_raw = mm(raw, w_scr[here, 2 * units :])
        gate_dot = jnp.sum(hidden.astype(F32) * grad_raw, axis=1, keepdims=True)
        for block in range(blocks):
            row = jnp.sum(
                hot[block] * gate_dot[block * CAP : (block + 1) * CAP],
                axis=0,
                keepdims=True,
            )
            for slot in range(2):
                gg_scr[8 * block + slot : 8 * block + slot + 1, :] += jnp.where(
                    masks[block][slot], row, 0.0
                )
        grad_hidden = grad_raw * gate_col
        grad_gate = grad_hidden * up_in * sigmoid * (1.0 + gate_in * (1.0 - sigmoid))
        grad_up = grad_hidden * silu
        grad_gu = jnp.concatenate([grad_gate.astype(BF16), grad_up.astype(BF16)], axis=1)
        grad_pick = mm(grad_gu, w_scr[here, : 2 * units], NT).astype(BF16)
        for block in range(blocks):
            gpart_scr[block, pl.ds(first_row, CAP), :] = grad_pick[block * CAP : (block + 1) * CAP]
        grad_result = (raw.astype(F32) * gate_col).astype(BF16)
        if out_count == 1:
            dw_refs[0][0, :, : 2 * units] = mm(picked, grad_gu, TN).astype(BF16)
            dw_refs[0][0, :, 2 * units :] = mm(grad_result, hidden, TN).astype(BF16)
        else:
            dw_scr[:, : 2 * units] = mm(picked, grad_gu, TN).astype(BF16)
            dw_scr[:, 2 * units :] = mm(grad_result, hidden, TN).astype(BF16)
            half = NF // 2
            for part in range(2):

                @pl.when((expert >= part * half) & (expert < (part + 1) * half))
                def _(part=part):
                    for off in range(8):
                        start = pl.multiple_of(offs_ref[off] * rows, rows)
                        dw_refs[2 * part + off % 2][off // 2, 0] = dw_scr[pl.ds(start, rows), :]

        @pl.when(expert == last)
        def _():
            total = blocks * BLOCK
            for block in range(blocks):
                gx_ref[block * BLOCK : (block + 1) * BLOCK, :] = combine(gpart_scr, block).astype(
                    BF16
                )
            gx_ref[total : total + 16, :] = jnp.zeros((16, gx_ref.shape[1]), BF16)
            gx_ref[total : total + gg_scr.shape[0], :BLOCK] = gg_scr[...].astype(BF16)


def experts(fwd, bwd, xm, gh, routes_t, gates_t, pieces, offs):
    rows, feature_dim = xm.shape
    blocks = rows // BLOCK
    arrays = [item[0] for item in pieces]
    plan = [item[1:] for item in pieces]
    _, piece_rows, width = arrays[0].shape
    units = width // 3
    split_out = len(pieces) > 1
    half = NF // 2

    ins = [xm] + ([gh] if bwd else []) + [routes_t, gates_t]
    in_specs = [SMEM_SPEC] + [full_spec(item.shape) for item in ins]
    in_specs += [pl.BlockSpec(memory_space=pl.ANY)] * len(plan)
    out_shape, out_specs, scratch = [], [], []
    scratch += [
        pltpu.VMEM((2 * feature_dim, width), BF16),
        pltpu.SemaphoreType.DMA((2, offs.shape[0])),
        pltpu.VMEM((blocks, NF * CAP, BLOCK), BF16),
        pltpu.VMEM((NF, blocks * CAP, feature_dim), BF16),
    ]
    flops = 0
    out_count = 4 if split_out else 1
    if fwd:
        out_shape.append(jax.ShapeDtypeStruct((rows, feature_dim), BF16))
        out_specs.append(full_spec((rows, feature_dim)))
        scratch.append(pltpu.VMEM((blocks, NF * CAP, feature_dim), BF16))
        flops += 1.0e9 * NF * blocks / 2
    if bwd:
        out_shape.append(jax.ShapeDtypeStruct((rows + 16, feature_dim), BF16))
        out_specs.append(full_spec((rows + 16, feature_dim)))
        if split_out:
            for part in range(2):
                for _ in range(2):
                    out_shape.append(jax.ShapeDtypeStruct((4, half, piece_rows, width), BF16))
                    out_specs.append(
                        pl.BlockSpec(
                            (4, 1, piece_rows, width),
                            lambda e, part=part: (0, jnp.clip(e - part * half, 0, half - 1), 0, 0),
                        )
                    )
        else:
            out_shape.append(jax.ShapeDtypeStruct((NF, feature_dim, width), BF16))
            out_specs.append(pl.BlockSpec((1, feature_dim, width), lambda e: (e, 0, 0)))
        scratch += [
            pltpu.VMEM((blocks, NF * CAP, feature_dim), BF16),
            pltpu.VMEM((NF, blocks * CAP, feature_dim), BF16),
            pltpu.VMEM((blocks * 8, BLOCK), F32),
            pltpu.VMEM((feature_dim, width) if split_out else (8, 128), BF16),
        ]
        flops += 2.2e9 * NF * blocks / 2
    outs = pl.pallas_call(
        functools.partial(experts_kernel, fwd, bwd, blocks, plan, out_count, piece_rows),
        grid=(NF,),
        out_shape=tuple(out_shape),
        in_specs=in_specs,
        out_specs=tuple(out_specs),
        scratch_shapes=scratch,
        compiler_params=kernel_params(),
        cost_estimate=cost(flops, 20e6 * (2 if bwd else 1), rows * units * 8),
        name="experts",
    )(offs, *ins, *arrays)
    outs = list(outs)
    ffn = outs.pop(0) if fwd else None
    return (ffn, outs[0], outs[1:]) if bwd else (ffn, None, None)


def final_kernel(with_old, count, *refs):
    parts = refs[:count]
    gu_ref, dn_ref = refs[-2:]
    del with_old
    half = count // 2
    units = gu_ref.shape[-1]

    def write(group):
        total = group[0][...].reshape(group[0].shape[-2:]).astype(F32)
        for ref in group[1:]:
            total += ref[...].reshape(ref.shape[-2:]).astype(F32)
        gu_ref[0, 0, :, 0, :] = total[:, :units]
        gu_ref[0, 0, :, 1, :] = total[:, units : 2 * units]
        dn_ref[0, 0] = total[:, 2 * units :]

    @pl.when(pl.program_id(0) < NF // 2)
    def _():
        write(parts[:half])

    @pl.when(pl.program_id(0) >= NF // 2)
    def _():
        write(parts[half:])


def final_sums(lows, highs, old, layer, layer_count):
    half = NF // 2
    specs, arrays = [], []
    for part, group in enumerate((lows, highs)):
        for item in group:
            lead = (1,) * (item.ndim - 3)
            specs.append(
                pl.BlockSpec(
                    lead + (1,) + item.shape[-2:],
                    lambda e, part=part, lead=lead: (0,) * len(lead)
                    + (jnp.clip(e - part * half, 0, half - 1), 0, 0),
                )
            )
            arrays.append(item)
    count = len(arrays)
    rows, width = arrays[0].shape[-2:]
    units = width // 3
    aliases = {}
    if old is not None:
        specs += [pl.BlockSpec(memory_space=pl.ANY)] * 2
        arrays += list(old)
        aliases = {count: 0, count + 1: 1}
    return pl.pallas_call(
        functools.partial(final_kernel, old is not None, count),
        grid=(NF,),
        out_shape=(
            jax.ShapeDtypeStruct((layer_count, NF, rows, 2, units), F32),
            jax.ShapeDtypeStruct((layer_count, NF, rows, units), F32),
        ),
        in_specs=specs,
        out_specs=(
            pl.BlockSpec((1, 1, rows, 2, units), lambda e: (layer, e, 0, 0, 0)),
            pl.BlockSpec((1, 1, rows, units), lambda e: (layer, e, 0, 0)),
        ),
        input_output_aliases=aliases,
        compiler_params=kernel_params(),
        cost_estimate=cost(1e7, NF * rows * width * 12),
        name="final_sums",
    )(*arrays)


def hop(value, step):
    return lax.ppermute(value, "fsdp", [(i, i ^ step) for i in range(4)])


def swap(value):
    return lax.ppermute(value, "ctx", [(0, 1), (1, 0)])


def gather_small(value):
    by_x, by_y, by_d = hop(value, 1), hop(value, 2), hop(value, 3)
    out = []
    for item in (value, by_x, by_y, by_d):
        out += [item, swap(item)]
    return out


def turn(value, steps, count):
    return lax.ppermute(value, "tp", [(i, (i + steps) % count) for i in range(count)])


def share(value, count):
    return [value] + [turn(value, k, count) for k in range(1, count)]


def gather_cores(lows, highs, swapped):
    half = NF // 2
    out = []
    for first, items, done in ((0, lows, swapped[0]), (half, highs, swapped[1])):
        for chip, item in enumerate(items):
            other = done[chip] if chip in done else swap(item)
            out += [(item, 2 * chip, first, half), (other, 2 * chip + 1, first, half)]
    return out


def tie(*values):
    return lax.optimization_barrier(values)


def add_low(*terms):
    total = terms[0].astype(F32)
    for term in terms[1:]:
        total = total + term.astype(F32)
    return total.astype(BF16)


def scatter_cores(keep, send, first):
    other = swap(send)
    if first == 1:
        out = add_low(keep[1::2], other[1::2])
    else:
        out = add_low(keep[2:], other[2:])
    return keep, other, out


def scatter_first(keep, other, out, first):
    return scatter_beside(keep, other, hop(out, first), first)


def scatter_beside(keep, other, got, first):
    return keep, other, got, add_low(keep[3 - first], other[3 - first], got[1])


def scatter_second(terms, first):
    return terms[:3] + (hop(terms[3], 3 - first),)


def per_device(
    hyper,
    axes,
    tokens,
    cotangent,
    lengths,
    routes,
    norm_attn,
    w_qkv,
    w_out,
    norm_moe,
    w_router,
    w_resid,
    w_const,
    v_const,
    w_gate_up,
    w_down,
):
    micro_count, seq_count, block_len, feature_dim = tokens.shape
    rows = micro_count * seq_count * block_len
    layer_count, shard_rows, qkv_cols = w_qkv.shape
    heads = qkv_cols // (3 * HD)
    units = w_gate_up.shape[-1]
    groups = ("fsdp", "ctx")
    shard_count = feature_dim // shard_rows
    ctx = lax.axis_index("ctx")
    me = lax.axis_index("fsdp") * axes["ctx"] + ctx
    rank = lax.axis_index("tp").reshape(1)
    if hyper:
        offs = me ^ jnp.arange(shard_count, dtype=jnp.int32)
    else:
        offs = jnp.zeros((1,), jnp.int32)
    info = jnp.concatenate([ctx.reshape(1), lengths.reshape(-1)]).astype(jnp.int32)
    resid = jnp.zeros((16, 16), F32).at[:NE, :NE].set(w_resid.astype(F32))

    tp_count = axes["tp"]
    outer = share(jnp.transpose(w_out, (0, 2, 1)), tp_count)
    small, wide = [], []
    for layer in range(layer_count):
        vec = jnp.concatenate(
            [
                w_router[layer],
                jnp.zeros((shard_rows, ROW_CONST - NE), BF16),
                w_const[layer, 0],
                w_const[layer, 1],
                v_const[layer].T,
                norm_attn[layer][:, None],
                norm_moe[layer][:, None],
                jnp.zeros((shard_rows, PACK - ROW_GM - 1), BF16),
            ],
            axis=1,
        )
        pad = jnp.zeros((shard_rows, round_up(qkv_cols, 128) - qkv_cols), BF16)
        turned = [item[layer] for item in outer]
        small.append(jnp.concatenate([w_qkv[layer], pad, vec] + turned, axis=1))
        wide.append(pack_wide(w_gate_up, jnp.swapaxes(w_down, 2, 3), layer))
    weights, wide_first = [None] * layer_count, [None] * layer_count

    def fetch_small(layer, after):
        own = small[layer]
        if hyper:
            own, _ = tie(own, after)
            pieces = gather_small(own)
            fetch_first(layer, [pieces[k] for k in (2, 4, 6)])
        else:
            pieces = [lax.all_gather(own, groups, axis=0, tiled=True)]
        outs = prep_weights(pieces, offs, feature_dim, qkv_cols, heads * HD, tp_count)
        weights[layer] = [outs[0], outs[2], outs[1]]

    def fetch_first(layer, after):
        (low, high), _ = tie(wide[layer], after)
        lows, highs = [low, None, hop(low, 2)], [high, hop(high, 1), None]
        if layer > 0:
            lows[1], highs[2] = hop(low, 1), hop(high, 2)
        wide_first[layer] = (lows, highs, [swap(low), swap(high)] if layer == 0 else [])

    def fetch_rest(layer, value):
        if hyper:
            value, (lows, highs, own) = tie(value, wide_first[layer])
            swapped[layer] = ({0: own[0]}, {0: own[1]}) if own else ({}, {})
            value = swap(value)
            if layer == 0:
                lows[1], highs[2] = hop(lows[0], 1), hop(highs[0], 2)
            lows.append(hop(lows[2], 1))
            highs.append(hop(highs[1], 2))
            rests[layer] = (lows, highs)
        else:
            value = swap(value)
        return value

    def fetch_cores(layer, after):
        if hyper:
            lows, highs = rests[layer]
            if layer == 0:
                swapped[0][0][2], swapped[0][1][1] = swap(lows[2]), swap(highs[1])
                after, swapped[0] = tie(after, swapped[0])
                if layer + 1 < layer_count:
                    mid, wide[layer + 1], small[layer + 1] = tie(
                        (lows[1], highs[2]), wide[layer + 1], small[layer + 1]
                    )
                    lows[1], highs[2] = mid
            else:
                (lows, highs), _ = tie((lows, highs), after)
            rests[layer] = (lows, highs)
        else:
            both = jnp.concatenate(wide[layer], axis=0)
            full = lax.all_gather(both, groups, axis=1, tiled=True)
            weights[layer].append([(full, 0, 0, NF)])
        return after

    def fetch_last(layer, after):
        if hyper:
            lows, highs = rests[layer]
            if layer == 0:
                (lows[3], highs[3]), _ = tie((lows[3], highs[3]), after)
            weights[layer].append(gather_cores(lows, highs, swapped[layer]))

    rests, swapped = [None] * layer_count, [None] * layer_count
    fetch_small(0, info)

    routes_t = jnp.moveaxis(routes.reshape(layer_count, rows, 2), 2, 1)
    routes_t = jnp.concatenate(
        [routes_t, jnp.full((layer_count, 6, rows), -1, jnp.int32)], axis=1
    )
    position = ctx * block_len + jnp.arange(block_len, dtype=jnp.int32)
    valid = position[None, None, :] < lengths[:, :, None]
    cot = jnp.where(valid[..., None], cotangent, 0).reshape(rows, feature_dim)

    base, ffn, prev_t = tokens.reshape(rows, feature_dim), None, None
    saved = []
    for layer in range(layer_count):
        qkv_full, _, vecs = weights[layer][:3]
        outs = qkv_part(base, ffn, vecs, qkv_full)
        h_in, qkv = outs if ffn is not None else (base, outs[0])
        other = fetch_rest(layer, qkv)
        context, lse = attend_forward(qkv, other, info, heads)
        ctx_all = lax.all_gather(fetch_cores(layer, context), "tp", axis=0)
        if hyper and layer == 0:
            lows, highs = rests[0]
            swapped[0][0][1], swapped[0][1][2] = swap(lows[1]), swap(highs[2])
            ctx_all, swapped[0] = tie(ctx_all, swapped[0])
        wo_all = weights[layer][1]
        middle, base, xm_low, gates_t, logits_t = middle_part(
            h_in, ctx_all, wo_all, vecs, routes_t[layer], prev_t, resid, rank
        )
        fetch_last(layer, xm_low)
        pieces = weights[layer][3]
        saved.append((h_in, qkv, other, context, lse, middle, xm_low, gates_t, prev_t))
        prev_t = logits_t
        if layer < layer_count - 1:
            part, _, _ = experts(True, False, xm_low, None, routes_t[layer], gates_t, pieces, offs)
            fetch_small(layer + 1, part)
            ffn = lax.psum(part, "tp")
            if hyper:
                ffn, wide_first[layer + 1] = tie(ffn, wide_first[layer + 1])

    grad, grad_low = cot, cot
    grad_logits, wide_out, pending, small_terms, late = None, None, None, None, None
    finals = [None] * layer_count
    for layer in reversed(range(layer_count)):
        qkv_full, wo_all, vecs, pieces = weights[layer]
        h_in, qkv, other, context, lse, middle, xm_low, gates_t, prev_t = saved[layer]
        top = layer == layer_count - 1
        part, gx, grads = experts(
            top, True, xm_low, grad_low, routes_t[layer], gates_t, pieces, offs
        )
        if not top and late is not None:
            late[0] = lax.psum(late[0], "tp")
            gx, grads, late, pending = tie(gx, grads, late, pending)
        gx = lax.psum(gx, "tp")
        if hyper:
            sums = [scatter_cores(grads[2 * k], grads[2 * k + 1], k + 1) for k in range(2)]
            got = [hop(sums[k][2], k + 1) for k in range(2)]
            if pending is not None:
                wide_terms, small_parts, dres = pending
                terms = [scatter_second(wide_terms[k], k + 1) for k in range(2)]
                terms, sums = tie(terms, sums)
                wide_out = final_sums(terms[0], terms[1], wide_out, layer + 1, layer_count)
                upper = scatter_cores(*pack_grads(*small_parts, offs), 1)
                gx, sums, wide_out, upper = tie(gx, sums, wide_out, upper)
                upper_got = hop(upper[2], 1)
            else:
                gx, sums = tie(gx, sums)
        if top:
            base_top = base
        else:
            late[1], gx = tie(late[1], gx)
            late[1] = lax.psum(late[1], "tp")
        gg_t = gx[rows : rows + 16, :block_len].astype(F32)
        gg_t = jnp.moveaxis(gg_t.reshape(2, 8, block_len)[: rows // BLOCK], 0, 1).reshape(8, rows)
        extra = (prev_t, resid) if prev_t is not None else (grad_logits,)
        outs = gate_backward(
            grad, middle, gx, vecs, routes_t[layer], gates_t, gg_t, context, wo_all[0], extra
        )
        gmid, gctx, dwo, dvec = outs[:4]
        if prev_t is not None:
            grad_logits, dres = outs[4:]
        gown, goth = attend_backward(qkv, other, lse, gctx, info, heads)
        if hyper:
            wide_terms = [scatter_beside(*sums[k][:2], got[k], k + 1) for k in range(2)]
        if not top:
            gown, goth, late = tie(gown, goth, late)
            if hyper:
                gown, wide_terms, upper_got = tie(gown, wide_terms, upper_got)
        goth = swap(goth)
        ga_part, dqkv, dgain = qkv_backward(gown, goth, h_in, vecs, qkv_full)
        small_parts = (dqkv, dwo, dvec, dgain)
        own = None
        ga = lax.psum(ga_part, "tp")
        if hyper:
            if layer > 0:
                dres = dres + swap(dres)
                dres = dres + hop(dres, 1)
                ga, wide_terms, dres, small_parts = tie(ga, wide_terms, dres, small_parts)
                dres = dres + hop(dres, 2)
                pending = (wide_terms, small_parts, dres)
            else:
                small_terms = scatter_second(scatter_beside(*upper[:2], upper_got, 1), 1)
                terms = [scatter_second(wide_terms[k], k + 1) for k in range(2)]
                terms, small_parts, late = tie(terms, small_parts, late)
                wide_out = final_sums(terms[0], terms[1], wide_out, layer, layer_count)
                own = scatter_cores(*pack_grads(*small_parts, offs), 1)
                owns = [scatter_second(scatter_first(*own, 1), 1), small_terms]
                owns = [
                    sum((term[0] if term.ndim == 3 else term).astype(F32) for term in item)
                    for item in owns
                ]
                gains = share(jnp.stack([item[:, -PACK + ROW_GA] for item in owns]), tp_count)
        if top:
            late = [part[:block_len], part[block_len:]]
            late[0], ga = tie(late[0], ga)
        outs = norm_backward(gmid, ga, h_in, vecs, layer > 0)
        grad = outs[0]
        grad_low = outs[-1]
        finals[layer] = (grads, small_parts, own)

    late = jnp.concatenate(late, axis=0)
    mixed = (base_top + late.astype(F32)).astype(BF16)

    resid_total = (dres if hyper else lax.psum(dres, groups))[:NE, :NE]
    results = [None] * layer_count
    for layer in reversed(range(layer_count)):
        grads, small_parts, own = finals[layer]
        if hyper:
            own = owns[layer]
        else:
            packed = pack_grads(*small_parts, offs)
            own = lax.psum_scatter(packed[0], groups, scatter_dimension=0, tiled=True).astype(F32)
            wide_own = lax.psum_scatter(
                grads[0], groups, scatter_dimension=1, tiled=True
            ).astype(F32)
            here = (
                wide_own[:, :, : 2 * units].reshape(NF, shard_rows, 2, units),
                wide_own[:, :, 2 * units :],
            )
            if wide_out is None:
                wide_out = ([], [])
            wide_out[0].insert(0, here[0])
            wide_out[1].insert(0, here[1])
        out_cols = heads * HD
        vec = own[:, qkv_cols + out_cols :]
        results[layer] = (
            own[:, :qkv_cols],
            own[:, qkv_cols : qkv_cols + out_cols].T,
            vec[:, ROW_GM],
            vec[:, :NE],
            jnp.stack([vec[:, ROW_CONST : ROW_CONST + 2], vec[:, ROW_CONST + 2 : ROW_CONST + 4]]),
            vec[:, ROW_VEC : ROW_VEC + 2].T,
            vec[:, ROW_GA],
        )
    if not hyper:
        wide_out = (jnp.stack(wide_out[0]), jnp.stack(wide_out[1]))
    stacked = [jnp.stack([item[member] for item in results]) for member in range(7)]
    gains = jnp.stack(gains if hyper else share(stacked[6], tp_count))
    gain_own = sum(
        lax.dynamic_index_in_dim(gains, (rank[0] + tp_count - j) % tp_count, 0, keepdims=False)
        for j in range(tp_count)
    )
    return (
        mixed.reshape(tokens.shape),
        grad.reshape(tokens.shape),
        gain_own,
        stacked[0],
        stacked[1],
        stacked[2],
        stacked[3],
        resid_total,
        stacked[4],
        stacked[5],
        wide_out[0],
        jnp.swapaxes(wide_out[1], 2, 3),
    )


def solution(mesh):
    axes = dict(mesh.shape)
    hyper = axes["fsdp"] == 4 and axes["ctx"] == 2
    in_specs = (
        P(None, "fsdp", "ctx", None),
        P(None, "fsdp", "ctx", None),
        P(None, "fsdp"),
        P(None, None, "fsdp", "ctx", None),
        P(None, ("fsdp", "ctx")),
        P(None, ("fsdp", "ctx"), "tp"),
        P(None, "tp", ("fsdp", "ctx")),
        P(None, ("fsdp", "ctx")),
        P(None, ("fsdp", "ctx"), None),
        P(),
        P(None, None, ("fsdp", "ctx"), None),
        P(None, None, ("fsdp", "ctx")),
        P(None, None, ("fsdp", "ctx"), None, "tp"),
        P(None, None, "tp", ("fsdp", "ctx")),
    )
    out_specs = (
        P(None, "fsdp", "ctx", None),
        P(None, "fsdp", "ctx", None),
        P(None, ("fsdp", "ctx")),
        P(None, ("fsdp", "ctx"), "tp"),
        P(None, "tp", ("fsdp", "ctx")),
        P(None, ("fsdp", "ctx")),
        P(None, ("fsdp", "ctx"), None),
        P(),
        P(None, None, ("fsdp", "ctx"), None),
        P(None, None, ("fsdp", "ctx")),
        P(None, None, ("fsdp", "ctx"), None, "tp"),
        P(None, None, "tp", ("fsdp", "ctx")),
    )
    return jax.shard_map(
        functools.partial(per_device, hyper, axes),
        mesh=mesh,
        in_specs=in_specs,
        out_specs=out_specs,
        check_vma=False,
    )
```

```python
import functools

import jax
import jax.numpy as jnp
from jax import lax
from jax.experimental import pallas as pl
from jax.experimental.pallas import tpu as pltpu
from jax.sharding import PartitionSpec as P

HD = 64
NF = 8
NE = 12
BLOCK = 512
CAP = 128
TILE = 256
EPSILON = 1e-06
MASKED = -1e30
F32 = jnp.float32
BF16 = jnp.bfloat16
HIGH = lax.Precision.HIGHEST
ROW_CONST, ROW_VEC, ROW_GA, ROW_GM = 16, 20, 22, 23
VMEM_LIMIT = 58 * 1024 * 1024
SCALE = 0.05
PACK = 128

NN = (((1,), (0,)), ((), ()))
NT = (((1,), (1,)), ((), ()))
TN = (((0,), (0,)), ((), ()))


def mm(left, right, dims=NN, precision=None):
    return lax.dot_general(left, right, dims, precision=precision, preferred_element_type=F32)


def kernel_params():
    return pltpu.CompilerParams(vmem_limit_bytes=VMEM_LIMIT)


def cost(flops, nbytes, trans=0):
    return pl.CostEstimate(
        flops=int(flops * SCALE), bytes_accessed=int(nbytes * SCALE), transcendentals=int(trans * SCALE)
    )


def iota(shape, dim):
    return lax.broadcasted_iota(jnp.int32, shape, dim)


def full_spec(shape):
    zeros = (0,) * len(shape)
    return pl.BlockSpec(shape, lambda *idx: zeros)


SMEM_SPEC = pl.BlockSpec(memory_space=pltpu.SMEM)


def pad_rows(rows, count, width):
    row_id = iota((count, width), 0)
    out = jnp.zeros((count, width), F32)
    for place, row in rows:
        out = jnp.where(row_id == place, row, out)
    return out


def round_up(value, unit):
    return -(-value // unit) * unit


def prep_kernel(count, rows, out_cols, offs_ref, *refs):
    qkv_ref, vec_ref, wo_refs = refs[count], refs[count + 1], refs[count + 2 : -2]
    scr_ref, wo_scr = refs[-2:]
    cols = qkv_ref.shape[1]
    for piece in range(count):
        start = pl.multiple_of(offs_ref[piece] * rows, rows)
        block = refs[piece][...]
        qkv_ref[pl.ds(start, rows), :] = block[:, :cols]
        scr_ref[pl.ds(start, rows), :] = block[:, cols : cols + PACK].astype(F32)
        for rank in range(len(wo_refs)):
            first = cols + PACK + rank * out_cols
            wo_scr[rank, pl.ds(start, rows), :out_cols] = block[:, first : first + out_cols]
    vec_ref[...] = scr_ref[...].T[:32]
    total = wo_scr.shape[1]
    rest = out_cols - 128
    for rank, ref in enumerate(wo_refs):
        ref[:total, :] = wo_scr[rank, :, :128]
        ref[total:, :rest] = wo_scr[rank, : total // 2, 128:out_cols]
        ref[total:, rest:] = wo_scr[rank, total // 2 :, 128:out_cols]


def prep_weights(pieces, offs, feature_dim, qkv_cols, out_cols, out_count):
    count = len(pieces)
    cols = round_up(qkv_cols, 128)
    vmem = pl.BlockSpec(memory_space=pltpu.VMEM)
    outs = pl.pallas_call(
        functools.partial(prep_kernel, count, feature_dim // count, out_cols),
        out_shape=tuple(
            [
                jax.ShapeDtypeStruct((feature_dim, cols), BF16),
                jax.ShapeDtypeStruct((32, feature_dim), F32),
            ]
            + [jax.ShapeDtypeStruct((feature_dim * 3 // 2, 128), BF16)] * out_count
        ),
        in_specs=[SMEM_SPEC] + [vmem] * count,
        out_specs=tuple([vmem] * (2 + out_count)),
        scratch_shapes=[
            pltpu.VMEM((feature_dim, PACK), F32),
            pltpu.VMEM((out_count, feature_dim, 256), BF16),
        ],
        compiler_params=kernel_params(),
        cost_estimate=cost(1e6, 3e6),
        name="prep",
    )(offs, *pieces)
    return outs[0], outs[1], list(outs[2:])


def pack_kernel(count, rows, offs_ref, dqkv_ref, dwo_ref, dvec_ref, dgain_ref, *refs):
    outs, scr_ref = refs[:-1], refs[-1]
    cols, out_cols = dqkv_ref.shape[1], dwo_ref.shape[1]
    scr_ref[:, :cols] = dqkv_ref[...]
    scr_ref[:, cols : cols + out_cols] = dwo_ref[...]
    vec = dvec_ref[...]
    vec = jnp.where(iota(vec.shape, 0) == ROW_GA, dgain_ref[0:1, :], vec)
    wide = jnp.concatenate([vec, jnp.zeros((PACK - vec.shape[0], vec.shape[1]), F32)], axis=0).T
    scr_ref[:, cols + out_cols :] = wide
    for piece in range(count):
        start = pl.multiple_of(offs_ref[piece] * rows, rows)
        block = scr_ref[pl.ds(start, rows), :].astype(BF16)
        if count > 1:
            outs[piece % 2][piece // 2] = block
        else:
            outs[0][...] = block


def pack_grads(dqkv, dwo, dvec, dgain, offs):
    feature_dim = dqkv.shape[0]
    count = offs.shape[0]
    rows = feature_dim // count
    width = dqkv.shape[1] + dwo.shape[1] + PACK
    shape = (count // 2, rows, width) if count > 1 else (feature_dim, width)
    vmem = pl.BlockSpec(memory_space=pltpu.VMEM)
    outs = 2 if count > 1 else 1
    return pl.pallas_call(
        functools.partial(pack_kernel, count, rows),
        out_shape=tuple([jax.ShapeDtypeStruct(shape, BF16)] * outs),
        in_specs=[SMEM_SPEC, vmem, vmem, vmem, vmem],
        out_specs=tuple([vmem] * outs),
        scratch_shapes=[pltpu.VMEM((feature_dim, width), F32)],
        compiler_params=kernel_params(),
        cost_estimate=cost(1e6, 6e6),
        name="pack_grads",
    )(offs, dqkv, dwo, dvec, dgain)


def pack_wide_kernel(gu_ref, down_ref, low_ref, high_ref):
    units = down_ref.shape[-1]

    def write(ref):
        ref[0, :, :units] = gu_ref[0, 0, :, 0, :]
        ref[0, :, units : 2 * units] = gu_ref[0, 0, :, 1, :]
        ref[0, :, 2 * units :] = down_ref[0, 0]

    @pl.when(pl.program_id(0) < NF // 2)
    def _():
        write(low_ref)

    @pl.when(pl.program_id(0) >= NF // 2)
    def _():
        write(high_ref)


def pack_wide(w_gate_up, w_down_t, layer):
    _, _, rows, _, units = w_gate_up.shape
    half = NF // 2
    specs = [
        pl.BlockSpec(
            (1, rows, 3 * units), lambda e, part=part: (jnp.clip(e - part * half, 0, half - 1), 0, 0)
        )
        for part in range(2)
    ]
    return pl.pallas_call(
        pack_wide_kernel,
        grid=(NF,),
        out_shape=tuple([jax.ShapeDtypeStruct((half, rows, 3 * units), BF16)] * 2),
        in_specs=[
            pl.BlockSpec((1, 1, rows, 2, units), lambda e: (layer, e, 0, 0, 0)),
            pl.BlockSpec((1, 1, rows, units), lambda e: (layer, e, 0, 0)),
        ],
        out_specs=tuple(specs),
        compiler_params=kernel_params(),
        cost_estimate=cost(1e6, 5e6),
        name="pack_wide",
    )(w_gate_up, w_down_t)


def qkv_kernel(with_ffn, *refs):
    if with_ffn:
        base_ref, ffn_ref, vec_ref, w_ref, h_ref, qkv_ref = refs
        hidden = base_ref[...] + ffn_ref[...].astype(F32)
        h_ref[...] = hidden
    else:
        base_ref, vec_ref, w_ref, qkv_ref = refs
        hidden = base_ref[...].astype(F32)
    gain = vec_ref[ROW_GA : ROW_GA + 1, :]
    scale = lax.rsqrt(jnp.mean(hidden * hidden, axis=-1, keepdims=True) + EPSILON)
    attn_in = (hidden * scale * gain).astype(BF16)
    qkv_ref[...] = mm(attn_in, w_ref[...]).astype(BF16)


def qkv_part(base, ffn, vecs, w_qkv):
    rows, feature_dim = base.shape
    cols = round_up(w_qkv.shape[1], 128)
    row_spec = pl.BlockSpec((TILE, feature_dim), lambda i: (i, 0))
    with_ffn = ffn is not None
    out_shape = [jax.ShapeDtypeStruct((rows, cols), BF16)]
    out_specs = [pl.BlockSpec((TILE, cols), lambda i: (i, 0))]
    if with_ffn:
        out_shape = [jax.ShapeDtypeStruct((rows, feature_dim), F32)] + out_shape
        out_specs = [row_spec] + out_specs
    ins = [base] + ([ffn] if with_ffn else []) + [vecs, w_qkv]
    in_specs = [row_spec] * (2 if with_ffn else 1) + [full_spec(vecs.shape), full_spec(w_qkv.shape)]
    return pl.pallas_call(
        functools.partial(qkv_kernel, with_ffn),
        grid=(rows // TILE,),
        out_shape=tuple(out_shape),
        in_specs=in_specs,
        out_specs=tuple(out_specs),
        compiler_params=kernel_params(),
        cost_estimate=cost(2 * rows * feature_dim * cols, rows * feature_dim * 10),
        name="qkv_part",
    )(*ins)


def attn_masks(ctx, length, tile, width):
    row = iota((TILE, width), 0) + tile * TILE
    col = iota((TILE, width), 1)
    return (col <= row) & (col + ctx * BLOCK < length)


def attn_fwd_kernel(heads, info_ref, own_ref, other_ref, ctx_ref, lse_ref):
    ctx = info_ref[0]
    length = info_ref[1 + pl.program_id(0)]
    own = own_ref[...]
    other = other_ref[...]
    for head in range(heads):
        col = head * 3 * HD
        k_own = own[:, col + HD : col + 2 * HD]
        v_own = own[:, col + 2 * HD : col + 3 * HD]
        k_oth = other[:, col + HD : col + 2 * HD]
        v_oth = other[:, col + 2 * HD : col + 3 * HD]
        for tile in range(BLOCK // TILE):
            width = (tile + 1) * TILE
            query = own[tile * TILE : (tile + 1) * TILE, col : col + HD] * BF16(HD**-0.5)
            s_own = mm(query, k_own[:width], NT)
            s_own = jnp.where(attn_masks(ctx, length, tile, width), s_own, MASKED)
            s_oth = jnp.where(ctx > 0, mm(query, k_oth, NT), MASKED)
            top = jnp.maximum(
                jnp.max(s_own, axis=-1, keepdims=True), jnp.max(s_oth, axis=-1, keepdims=True)
            )
            p_own = jnp.exp(s_own - top)
            p_oth = jnp.exp(s_oth - top)
            total = jnp.sum(p_own, axis=-1, keepdims=True) + jnp.sum(p_oth, axis=-1, keepdims=True)
            out = mm(p_own.astype(BF16), v_own[:width]) + mm(p_oth.astype(BF16), v_oth)
            out = out / total
            rows = slice(tile * TILE, (tile + 1) * TILE)
            ctx_ref[head * TILE : (head + 1) * TILE, tile * HD : (tile + 1) * HD] = out.astype(BF16)
            lse_ref[rows, head : head + 1] = top + jnp.log(total)


def attend_forward(qkv, other, info, heads):
    rows, cols = qkv.shape
    count = rows // BLOCK
    spec = pl.BlockSpec((BLOCK, cols), lambda i: (i, 0))
    return pl.pallas_call(
        functools.partial(attn_fwd_kernel, heads),
        grid=(count,),
        out_shape=(
            jax.ShapeDtypeStruct((count * heads * TILE, 2 * HD), BF16),
            jax.ShapeDtypeStruct((rows, 8), F32),
        ),
        in_specs=[SMEM_SPEC, spec, spec],
        out_specs=(
            pl.BlockSpec((heads * TILE, 2 * HD), lambda i: (i, 0)),
            pl.BlockSpec((BLOCK, 8), lambda i: (i, 0)),
        ),
        compiler_params=kernel_params(),
        cost_estimate=cost(rows * 1024 * heads * HD * 16, rows * cols * 6, rows * heads * 1024),
        name="attend_forward",
    )(info, qkv, other)


def attn_bwd_kernel(heads, info_ref, own_ref, other_ref, lse_ref, gctx_ref, gown_ref, goth_ref):
    ctx = info_ref[0]
    length = info_ref[1 + pl.program_id(0)]
    own = own_ref[...]
    other = other_ref[...]
    scale = BF16(HD**-0.5)
    for head in range(heads):
        col = head * 3 * HD
        k_own = own[:, col + HD : col + 2 * HD]
        v_own = own[:, col + 2 * HD : col + 3 * HD]
        k_oth = other[:, col + HD : col + 2 * HD]
        v_oth = other[:, col + 2 * HD : col + 3 * HD]
        goth_ref[:, col : col + HD] = jnp.zeros((BLOCK, HD), BF16)
        gk_own, gv_own, gk_oth, gv_oth = [], [], [], []
        for tile in range(BLOCK // TILE):
            width = (tile + 1) * TILE
            rows = slice(tile * TILE, (tile + 1) * TILE)
            query = own[rows, col : col + HD] * scale
            gout = gctx_ref[rows, head * HD : (head + 1) * HD]
            lse = lse_ref[rows, head : head + 1]
            s_own = mm(query, k_own[:width], NT)
            s_own = jnp.where(attn_masks(ctx, length, tile, width), s_own, MASKED)
            s_oth = jnp.where(ctx > 0, mm(query, k_oth, NT), MASKED)
            p_own = jnp.exp(s_own - lse)
            p_oth = jnp.exp(s_oth - lse)
            d_own = mm(gout, v_own[:width], NT)
            d_oth = mm(gout, v_oth, NT)
            inner = jnp.sum(p_own * d_own, axis=-1, keepdims=True) + jnp.sum(
                p_oth * d_oth, axis=-1, keepdims=True
            )
            ds_own = (p_own * (d_own - inner)).astype(BF16)
            ds_oth = (p_oth * (d_oth - inner)).astype(BF16)
            p_own = p_own.astype(BF16)
            p_oth = p_oth.astype(BF16)
            gown_ref[rows, col : col + HD] = (mm(ds_own, k_own[:width]) + mm(ds_oth, k_oth)) * (
                HD**-0.5
            )
            gk_own.append(mm(ds_own, query, TN))
            gv_own.append(mm(p_own, gout, TN))
            gk_oth.append(mm(ds_oth, query, TN))
            gv_oth.append(mm(p_oth, gout, TN))
        gown_ref[:TILE, col + HD : col + 2 * HD] = gk_own[0] + gk_own[1][:TILE]
        gown_ref[TILE:, col + HD : col + 2 * HD] = gk_own[1][TILE:]
        gown_ref[:TILE, col + 2 * HD : col + 3 * HD] = gv_own[0] + gv_own[1][:TILE]
        gown_ref[TILE:, col + 2 * HD : col + 3 * HD] = gv_own[1][TILE:]
        goth_ref[:, col + HD : col + 2 * HD] = (gk_oth[0] + gk_oth[1]).astype(BF16)
        goth_ref[:, col + 2 * HD : col + 3 * HD] = (gv_oth[0] + gv_oth[1]).astype(BF16)


def attend_backward(qkv, other, lse, grad_context, info, heads):
    rows, width = qkv.shape
    cols = heads * 3 * HD
    spec = pl.BlockSpec((BLOCK, width), lambda i: (i, 0))
    return pl.pallas_call(
        functools.partial(attn_bwd_kernel, heads),
        grid=(rows // BLOCK,),
        out_shape=(
            jax.ShapeDtypeStruct((rows, cols), F32),
            jax.ShapeDtypeStruct((rows, width), BF16),
        ),
        in_specs=[
            SMEM_SPEC,
            spec,
            spec,
            pl.BlockSpec((BLOCK, 8), lambda i: (i, 0)),
            pl.BlockSpec((BLOCK, heads * HD), lambda i: (i, 0)),
        ],
        out_specs=(pl.BlockSpec((BLOCK, cols), lambda i: (i, 0)), spec),
        compiler_params=kernel_params(),
        cost_estimate=cost(rows * 1024 * heads * HD * 40, rows * cols * 12, rows * heads * 1024),
        name="attend_backward",
    )(info, qkv, other, lse, grad_context)


def alpha_rows(gate_in, const_idx):
    first = gate_in[ROW_CONST + 2 * const_idx : ROW_CONST + 2 * const_idx + 1]
    second = gate_in[ROW_CONST + 2 * const_idx + 1 : ROW_CONST + 2 * const_idx + 2]
    return pair(first, second)


def pair(first, second):
    top = jnp.maximum(first, second)
    exp_first = jnp.exp(first - top)
    exp_second = jnp.exp(second - top)
    total = exp_first + exp_second
    return exp_first / total, exp_second / total


def picks(route, value):
    return (route == value).astype(F32)


def gate_coefs(routes, gates, alphas):
    copy = picks(routes[0], NF + 1) * gates[0] + picks(routes[1], NF + 1) * gates[1]
    const = [
        picks(routes[0], NF + 2 + j) * gates[0] + picks(routes[1], NF + 2 + j) * gates[1]
        for j in range(2)
    ]
    on_normed = copy + const[0] * alphas[0][0] + const[1] * alphas[1][0]
    on_vec = [const[j] * alphas[j][1] for j in range(2)]
    return const, on_normed, on_vec


def to_columns(rows):
    width = rows[0].shape[1]
    return pad_rows(list(enumerate(rows)), 128, width).T


def unpack_context(both):
    heads = both.shape[0] // TILE
    side = lax.rem(pl.program_id(0), 2) == 0
    both = jnp.where(side, both[:, :HD], both[:, HD:])
    parts = [both[head * TILE : (head + 1) * TILE] for head in range(heads)]
    return jnp.concatenate(parts, axis=1)


def middle_kernel(with_prev, rank_ref, *refs):
    h_ref, ctx_ref, refs = refs[0], refs[1], refs[2:]
    count = ctx_ref.shape[0]
    wo_refs, refs = refs[:count], refs[count:]
    if with_prev:
        vec_ref, route_ref, prev_ref, resid_ref = refs[:4]
        refs = refs[4:]
    else:
        vec_ref, route_ref = refs[:2]
        refs = refs[2:]
    mid_ref, base_ref, xm_ref, gate_ref, logit_ref = refs
    attn_out = 0.0
    for back, ref in enumerate(wo_refs):
        context = unpack_context(ctx_ref[lax.rem(rank_ref[0] + count - back, count)])
        total = ref.shape[0] * 2 // 3
        rest = context[:, 128:]
        attn_out += mm(context[:, :128], ref[:total], NT) + jnp.concatenate(
            [mm(rest, ref[total:, :HD], NT), mm(rest, ref[total:, HD:], NT)], axis=1
        )
    middle = h_ref[...].astype(F32) + attn_out
    mid_ref[...] = middle
    vecs = vec_ref[...]
    scale = lax.rsqrt(jnp.mean(middle * middle, axis=-1, keepdims=True) + EPSILON)
    normed = middle * scale * vecs[ROW_GM : ROW_GM + 1]
    xm_low = normed.astype(BF16)
    xm_ref[...] = xm_low
    gate_in = mm(vecs[:32].astype(BF16), xm_low, NT)
    logits = gate_in[:16]
    if with_prev:
        logits = logits + mm(resid_ref[...], prev_ref[...], TN, HIGH)
    logit_ref[...] = logits
    routes = (route_ref[0:1], route_ref[1:2])
    expert = iota(logits.shape, 0)
    chosen = [
        jnp.sum(jnp.where(expert == route, logits, 0.0), axis=0, keepdims=True) for route in routes
    ]
    gates = pair(chosen[0], chosen[1])
    gate_ref[...] = pad_rows(list(enumerate(gates)), 8, logits.shape[1])
    alphas = [alpha_rows(gate_in, j) for j in range(2)]
    const, on_normed, on_vec = gate_coefs(routes, gates, alphas)
    cols = to_columns([on_normed, on_vec[0], on_vec[1]])
    base_ref[...] = (
        middle
        + cols[:, 0:1] * normed
        + cols[:, 1:2] * vecs[ROW_VEC : ROW_VEC + 1]
        + cols[:, 2:3] * vecs[ROW_VEC + 1 : ROW_VEC + 2]
    )


def middle_part(h, ctx_all, wo_all, vecs, routes_t, prev_t, resid, rank):
    rows, feature_dim = h.shape
    tp_count, packed, lanes = ctx_all.shape
    packed = packed * BLOCK // rows
    row_spec = pl.BlockSpec((TILE, feature_dim), lambda i: (i, 0))
    lane8 = pl.BlockSpec((8, TILE), lambda i: (0, i))
    lane16 = pl.BlockSpec((16, TILE), lambda i: (0, i))
    ins = [rank, h, ctx_all, *wo_all, vecs, routes_t]
    in_specs = [
        SMEM_SPEC,
        row_spec,
        pl.BlockSpec((tp_count, packed, lanes), lambda i: (0, i // 2, 0)),
        *[full_spec(item.shape) for item in wo_all],
        full_spec(vecs.shape),
        lane8,
    ]
    with_prev = prev_t is not None
    if with_prev:
        ins += [prev_t, resid]
        in_specs += [lane16, full_spec(resid.shape)]
    return pl.pallas_call(
        functools.partial(middle_kernel, with_prev),
        grid=(rows // TILE,),
        out_shape=(
            jax.ShapeDtypeStruct((rows, feature_dim), F32),
            jax.ShapeDtypeStruct((rows, feature_dim), F32),
            jax.ShapeDtypeStruct((rows, feature_dim), BF16),
            jax.ShapeDtypeStruct((8, rows), F32),
            jax.ShapeDtypeStruct((16, rows), F32),
        ),
        in_specs=in_specs,
        out_specs=(row_spec, row_spec, row_spec, lane8, lane16),
        compiler_params=kernel_params(),
        cost_estimate=cost(2 * rows * feature_dim * feature_dim, rows * feature_dim * 16),
        name="middle_part",
    )(*ins)


def split(value):
    high = value.astype(BF16)
    return high, (value - high.astype(F32)).astype(BF16)


def gate_bwd_kernel(with_prev, *refs):
    gh_ref, mid_ref, gxm_ref, vec_ref, route_ref, gate_ref, gg_ref, ctx_ref, wo_ref = refs[:9]
    refs = refs[9:]
    if with_prev:
        prev_ref, resid_ref = refs[:2]
        gmid_ref, gctx_ref, dwo_ref, dvec_ref, gprev_ref, dres_ref = refs[2:]
    else:
        gl_ref = refs[0]
        gmid_ref, gctx_ref, dwo_ref, dvec_ref = refs[1:]
    step = pl.program_id(0)
    grad = gh_ref[...].astype(F32)
    middle = mid_ref[...]
    vecs = vec_ref[...]
    gain = vecs[ROW_GM : ROW_GM + 1]
    scale = lax.rsqrt(jnp.mean(middle * middle, axis=-1, keepdims=True) + EPSILON)
    unit = middle * scale
    normed = unit * gain
    xm_low = normed.astype(BF16)
    low_vecs = vecs[:32].astype(BF16)
    gate_in = mm(low_vecs, xm_low, NT)
    alphas = [alpha_rows(gate_in, j) for j in range(2)]
    routes = (route_ref[0:1], route_ref[1:2])
    gates = (gate_ref[0:1], gate_ref[1:2])
    const, on_normed, on_vec = gate_coefs(routes, gates, alphas)
    grad_hi, grad_lo = split(grad)
    vec_dots = mm(low_vecs[16:32], grad_hi, NT) + mm(low_vecs[16:32], grad_lo, NT)
    dot_vec = [vec_dots[ROW_VEC - 16 + j : ROW_VEC - 15 + j] for j in range(2)]
    dot_col = jnp.sum(grad * normed, axis=-1, keepdims=True)
    dot_normed = jnp.broadcast_to(dot_col, (dot_col.shape[0], 128)).T[0:1]
    term = [alphas[j][0] * dot_normed + alphas[j][1] * dot_vec[j] for j in range(2)]
    gate_grads = []
    for slot in range(2):
        fixed = (
            picks(routes[slot], NF + 1) * dot_normed
            + picks(routes[slot], NF + 2) * term[0]
            + picks(routes[slot], NF + 3) * term[1]
        )
        gate_grads.append(jnp.where(routes[slot] < NF, gg_ref[slot : slot + 1], fixed))
    inner = gates[0] * gate_grads[0] + gates[1] * gate_grads[1]
    chosen_grads = [gates[slot] * (gate_grads[slot] - inner) for slot in range(2)]
    expert = iota((16, TILE), 0)
    grad_logits = jnp.where(expert == routes[0], chosen_grads[0], 0.0) + jnp.where(
        expert == routes[1], chosen_grads[1], 0.0
    )
    if not with_prev:
        grad_logits = grad_logits + gl_ref[...]
    alpha_grads = []
    for j in range(2):
        grad_first = const[j] * dot_normed
        grad_second = const[j] * dot_vec[j]
        mean = alphas[j][0] * grad_first + alphas[j][1] * grad_second
        alpha_grads.append((2 * j, alphas[j][0] * (grad_first - mean)))
        alpha_grads.append((2 * j + 1, alphas[j][1] * (grad_second - mean)))
    grad_in = jnp.concatenate([grad_logits, pad_rows(alpha_grads, 16, TILE)], axis=0)
    in_hi, in_lo = split(grad_in)
    low_gate = jnp.where(iota(low_vecs.shape, 0) < ROW_VEC, low_vecs, 0)
    grad_xm = mm(in_hi, low_gate, TN) + mm(in_lo, low_gate, TN)
    cols = to_columns([on_normed])
    grad_y = cols[:, 0:1] * grad + grad_xm + gxm_ref[...].astype(F32)
    weighted = grad_y * gain
    mean = jnp.mean(weighted * unit, axis=-1, keepdims=True)
    grad_mid = grad + scale * (weighted - unit * mean)
    gmid_ref[...] = grad_mid
    low_mid = grad_mid.astype(BF16)
    total = low_mid.shape[1]
    gctx_ref[:, :128] = mm(low_mid, wo_ref[:total]).astype(BF16)
    gctx_ref[:, 128:] = (
        mm(low_mid[:, : total // 2], wo_ref[total:, :HD])
        + mm(low_mid[:, total // 2 :], wo_ref[total:, HD:])
    ).astype(BF16)
    dwo = mm(low_mid, unpack_context(ctx_ref[...]), TN)
    vec_rows = pad_rows([(ROW_VEC - 16 + j, on_vec[j]) for j in range(2)], 16, TILE)
    vec_hi, vec_lo = split(vec_rows)
    dvec_low = mm(vec_hi, grad_hi) + mm(vec_lo, grad_hi)
    dvec_gate = mm(in_hi, xm_low) + mm(in_lo, xm_low)
    dgain = jnp.sum(grad_y * unit, axis=0, keepdims=True)
    row_id = iota(dvec_gate.shape, 0)
    dvec = dvec_gate + jnp.concatenate([jnp.zeros_like(dvec_low), dvec_low], axis=0)
    dvec = jnp.where(row_id == ROW_GM, dgain, dvec)

    @pl.when(step == 0)
    def _():
        dwo_ref[...] = dwo
        dvec_ref[...] = dvec

    @pl.when(step > 0)
    def _():
        dwo_ref[...] += dwo
        dvec_ref[...] += dvec

    if with_prev:
        gprev_ref[...] = mm(resid_ref[...], grad_logits, NN, HIGH)
        dres = mm(prev_ref[...], grad_logits, NT, HIGH)

        @pl.when(step == 0)
        def _():
            dres_ref[...] = dres

        @pl.when(step > 0)
        def _():
            dres_ref[...] += dres


def gate_backward(grad, middle, gxm, vecs, routes_t, gates_t, gg_t, context, wo_own, extra):
    rows, feature_dim = middle.shape
    out_cols = context.shape[0] * BLOCK // rows // TILE * HD
    with_prev = len(extra) == 2
    row_spec = pl.BlockSpec((TILE, feature_dim), lambda i: (i, 0))
    lane8 = pl.BlockSpec((8, TILE), lambda i: (0, i))
    lane16 = pl.BlockSpec((16, TILE), lambda i: (0, i))
    ctx_spec = pl.BlockSpec((context.shape[0] * BLOCK // rows, 2 * HD), lambda i: (i // 2, 0))
    out_spec = pl.BlockSpec((TILE, out_cols), lambda i: (i, 0))
    wo_spec = full_spec(wo_own.shape)
    in_specs = [row_spec, row_spec, row_spec, full_spec(vecs.shape), lane8, lane8, lane8]
    in_specs += [ctx_spec, wo_spec, lane16]
    out_shape = [
        jax.ShapeDtypeStruct((rows, feature_dim), F32),
        jax.ShapeDtypeStruct((rows, out_cols), BF16),
        jax.ShapeDtypeStruct((feature_dim, out_cols), F32),
        jax.ShapeDtypeStruct((32, feature_dim), F32),
    ]
    out_specs = [row_spec, out_spec, full_spec((feature_dim, out_cols)), full_spec((32, feature_dim))]
    if with_prev:
        in_specs.append(full_spec(extra[1].shape))
        out_shape += [jax.ShapeDtypeStruct((16, rows), F32), jax.ShapeDtypeStruct((16, 16), F32)]
        out_specs += [lane16, full_spec((16, 16))]
    return pl.pallas_call(
        functools.partial(gate_bwd_kernel, with_prev),
        grid=(rows // TILE,),
        out_shape=tuple(out_shape),
        in_specs=in_specs,
        out_specs=tuple(out_specs),
        compiler_params=kernel_params(),
        cost_estimate=cost(4 * rows * feature_dim * out_cols, rows * feature_dim * 18),
        name="gate_backward",
    )(grad, middle, gxm, vecs, routes_t, gates_t, gg_t, context, wo_own, *extra)


def qkv_bwd_kernel(gown_ref, goth_ref, h_ref, vec_ref, w_ref, part_ref, dw_ref, dgain_ref):
    step = pl.program_id(0)
    cols = gown_ref.shape[1]
    grad = (gown_ref[...] + goth_ref[:, :cols].astype(F32)).astype(BF16)
    part = mm(grad, w_ref[:, :cols], NT)
    part_ref[...] = part.astype(BF16)
    hidden = h_ref[...].astype(F32)
    gain = vec_ref[ROW_GA : ROW_GA + 1, :]
    scale = lax.rsqrt(jnp.mean(hidden * hidden, axis=-1, keepdims=True) + EPSILON)
    unit = hidden * scale
    attn_in = (unit * gain).astype(BF16)
    dw = mm(attn_in, grad, TN)
    dgain = jnp.broadcast_to(jnp.sum(part * unit, axis=0, keepdims=True), dgain_ref.shape)

    @pl.when(step == 0)
    def _():
        dw_ref[...] = dw
        dgain_ref[...] = dgain

    @pl.when(step > 0)
    def _():
        dw_ref[...] += dw
        dgain_ref[...] += dgain


def qkv_backward(gown, goth, h, vecs, w_qkv):
    rows, feature_dim = h.shape
    cols = gown.shape[1]
    row_spec = pl.BlockSpec((TILE, feature_dim), lambda i: (i, 0))
    col_spec = pl.BlockSpec((TILE, cols), lambda i: (i, 0))
    oth_spec = pl.BlockSpec((TILE, goth.shape[1]), lambda i: (i, 0))
    return pl.pallas_call(
        qkv_bwd_kernel,
        grid=(rows // TILE,),
        out_shape=(
            jax.ShapeDtypeStruct((rows, feature_dim), BF16),
            jax.ShapeDtypeStruct((feature_dim, cols), F32),
            jax.ShapeDtypeStruct((8, feature_dim), F32),
        ),
        in_specs=[col_spec, oth_spec, row_spec, full_spec(vecs.shape), full_spec(w_qkv.shape)],
        out_specs=(row_spec, full_spec((feature_dim, cols)), full_spec((8, feature_dim))),
        compiler_params=kernel_params(),
        cost_estimate=cost(4 * rows * feature_dim * cols, rows * feature_dim * 10),
        name="qkv_backward",
    )(gown, goth, h, vecs, w_qkv)


def norm_bwd_kernel(with_low, gmid_ref, ga_ref, h_ref, vec_ref, out_ref, *rest):
    hidden = h_ref[...].astype(F32)
    gain = vec_ref[ROW_GA : ROW_GA + 1, :]
    scale = lax.rsqrt(jnp.mean(hidden * hidden, axis=-1, keepdims=True) + EPSILON)
    unit = hidden * scale
    grad_y = ga_ref[...].astype(F32)
    weighted = grad_y * gain
    mean = jnp.mean(weighted * unit, axis=-1, keepdims=True)
    grad = gmid_ref[...] + scale * (weighted - unit * mean)
    out_ref[...] = grad
    if with_low:
        rest[0][...] = grad.astype(BF16)


def norm_backward(gmid, ga, h, vecs, with_low):
    rows, feature_dim = gmid.shape
    row_spec = pl.BlockSpec((TILE, feature_dim), lambda i: (i, 0))
    out_shape = [jax.ShapeDtypeStruct((rows, feature_dim), F32)]
    out_specs = [row_spec]
    if with_low:
        out_shape.append(jax.ShapeDtypeStruct((rows, feature_dim), BF16))
        out_specs.append(row_spec)
    return pl.pallas_call(
        functools.partial(norm_bwd_kernel, with_low),
        grid=(rows // TILE,),
        out_shape=tuple(out_shape),
        in_specs=[row_spec, row_spec, row_spec, full_spec(vecs.shape)],
        out_specs=tuple(out_specs),
        compiler_params=kernel_params(),
        cost_estimate=cost(rows * feature_dim * 10, rows * feature_dim * 16),
        name="norm_backward",
    )(gmid, ga, h, vecs)


def experts_kernel(fwd, bwd, blocks, plan, out_count, rows, offs_ref, *refs):
    refs = list(refs)
    xm_ref = refs.pop(0)
    gh_ref = refs.pop(0) if bwd else None
    route_ref, gate_ref = refs.pop(0), refs.pop(0)
    w_refs = [refs.pop(0) for _ in plan]
    ffn_ref = refs.pop(0) if fwd else None
    if bwd:
        gx_ref = refs.pop(0)
        dw_refs = [refs.pop(0) for _ in range(out_count)]
    w_scr, sem_ref, hot_scr, pick_scr = (refs.pop(0) for _ in range(4))
    part_scr = refs.pop(0) if fwd else None
    if bwd:
        gpart_scr, raw_scr, gg_scr, dw_scr = refs
    expert = pl.program_id(0)
    last = pl.num_programs(0) - 1
    depth, width = w_scr.shape[0] // 2, w_scr.shape[1]
    units = width // 3

    def move(each, target, start):
        for ref, (off, first, number) in zip(w_refs, plan):

            def one(ref=ref, off=off, first=first):
                row = pl.multiple_of(offs_ref[off] * rows + target * depth, rows)
                copy = pltpu.make_async_copy(
                    ref.at[each - first], w_scr.at[pl.ds(row, rows)], sem_ref.at[target, off]
                )
                if start:
                    copy.start()
                else:
                    copy.wait()

            if number == NF:
                one()
            else:
                pl.when((each >= first) & (each < first + number))(one)

    slot = lax.rem(expert, 2)
    here = pl.ds(pl.multiple_of(slot * depth, depth), depth)

    @pl.when(expert == 0)
    def _():
        move(0 * expert, 0, True)

    @pl.when(expert < last)
    def _():
        move(expert + 1, 1 - slot, True)

    @pl.when(expert == 0)
    def _():
        order = (iota((BLOCK, BLOCK), 0) < iota((BLOCK, BLOCK), 1)).astype(BF16)
        ids = iota((NF, BLOCK), 0)
        row_ids = iota((CAP, BLOCK), 0).astype(F32)
        for block in range(blocks):
            lanes = slice(block * BLOCK, (block + 1) * BLOCK)
            hits = (ids == route_ref[0:1, lanes]) | (ids == route_ref[1:2, lanes])
            place = jnp.where(hits, mm(hits.astype(BF16), order), -1.0)
            for each in range(NF):
                hot_scr[block, each * CAP : (each + 1) * CAP, :] = (
                    (row_ids == place[each : each + 1]).astype(F32).astype(BF16)
                )
            hot = hot_scr[block]
            for source, target in ((xm_ref, pick_scr),) + (((gh_ref, raw_scr),) if bwd else ()):
                rows_all = mm(hot, source[lanes, :]).astype(BF16)
                for each in range(NF):
                    target[each, block * CAP : (block + 1) * CAP, :] = rows_all[
                        each * CAP : (each + 1) * CAP
                    ]
        if bwd:
            gg_scr[...] = jnp.zeros_like(gg_scr)

    def combine(source, block):
        return mm(hot_scr[block], source[block], TN)

    move(expert, slot, False)
    hot, gate_cols, masks = [], [], []
    first_row = pl.multiple_of(expert * CAP, CAP)
    for block in range(blocks):
        lanes = slice(block * BLOCK, (block + 1) * BLOCK)
        one_hot = hot_scr[block, pl.ds(first_row, CAP), :].astype(F32)
        mask = [route_ref[slot : slot + 1, lanes] == expert for slot in range(2)]
        gate_row = jnp.where(mask[0], gate_ref[0:1, lanes], 0.0) + jnp.where(
            mask[1], gate_ref[1:2, lanes], 0.0
        )
        gate_cols.append(jnp.sum(one_hot * gate_row, axis=1, keepdims=True))
        hot.append(one_hot)
        masks.append(mask)
    gate_col = jnp.concatenate(gate_cols, axis=0)
    picked = pick_scr[expert]
    gate_up = mm(picked, w_scr[here, : 2 * units])
    gate_in, up_in = gate_up[:, :units], gate_up[:, units:]
    sigmoid = lax.logistic(gate_in)
    silu = gate_in * sigmoid
    hidden = (silu * up_in).astype(BF16)
    if fwd:
        scaled = (mm(hidden, w_scr[here, 2 * units :], NT) * gate_col).astype(BF16)
        for block in range(blocks):
            part_scr[block, pl.ds(first_row, CAP), :] = scaled[block * CAP : (block + 1) * CAP]

        @pl.when(expert == last)
        def _():
            for block in range(blocks):
                ffn_ref[block * BLOCK : (block + 1) * BLOCK, :] = combine(part_scr, block).astype(
                    BF16
                )

    if bwd:
        raw = raw_scr[expert]
        grad_raw = mm(raw, w_scr[here, 2 * units :])
        gate_dot = jnp.sum(hidden.astype(F32) * grad_raw, axis=1, keepdims=True)
        for block in range(blocks):
            row = jnp.sum(
                hot[block] * gate_dot[block * CAP : (block + 1) * CAP],
                axis=0,
                keepdims=True,
            )
            for slot in range(2):
                gg_scr[8 * block + slot : 8 * block + slot + 1, :] += jnp.where(
                    masks[block][slot], row, 0.0
                )
        grad_hidden = grad_raw * gate_col
        grad_gate = grad_hidden * up_in * sigmoid * (1.0 + gate_in * (1.0 - sigmoid))
        grad_up = grad_hidden * silu
        grad_gu = jnp.concatenate([grad_gate.astype(BF16), grad_up.astype(BF16)], axis=1)
        grad_pick = mm(grad_gu, w_scr[here, : 2 * units], NT).astype(BF16)
        for block in range(blocks):
            gpart_scr[block, pl.ds(first_row, CAP), :] = grad_pick[block * CAP : (block + 1) * CAP]
        grad_result = (raw.astype(F32) * gate_col).astype(BF16)
        if out_count == 1:
            dw_refs[0][0, :, : 2 * units] = mm(picked, grad_gu, TN).astype(BF16)
            dw_refs[0][0, :, 2 * units :] = mm(grad_result, hidden, TN).astype(BF16)
        else:
            dw_scr[:, : 2 * units] = mm(picked, grad_gu, TN).astype(BF16)
            dw_scr[:, 2 * units :] = mm(grad_result, hidden, TN).astype(BF16)
            half = NF // 2
            for part in range(2):

                @pl.when((expert >= part * half) & (expert < (part + 1) * half))
                def _(part=part):
                    for off in range(8):
                        start = pl.multiple_of(offs_ref[off] * rows, rows)
                        dw_refs[2 * part + off % 2][off // 2, 0] = dw_scr[pl.ds(start, rows), :]

        @pl.when(expert == last)
        def _():
            total = blocks * BLOCK
            for block in range(blocks):
                gx_ref[block * BLOCK : (block + 1) * BLOCK, :] = combine(gpart_scr, block).astype(
                    BF16
                )
            gx_ref[total : total + 16, :] = jnp.zeros((16, gx_ref.shape[1]), BF16)
            gx_ref[total : total + gg_scr.shape[0], :BLOCK] = gg_scr[...].astype(BF16)


def experts(fwd, bwd, xm, gh, routes_t, gates_t, pieces, offs):
    rows, feature_dim = xm.shape
    blocks = rows // BLOCK
    arrays = [item[0] for item in pieces]
    plan = [item[1:] for item in pieces]
    _, piece_rows, width = arrays[0].shape
    units = width // 3
    split_out = len(pieces) > 1
    half = NF // 2

    ins = [xm] + ([gh] if bwd else []) + [routes_t, gates_t]
    in_specs = [SMEM_SPEC] + [full_spec(item.shape) for item in ins]
    in_specs += [pl.BlockSpec(memory_space=pl.ANY)] * len(plan)
    out_shape, out_specs, scratch = [], [], []
    scratch += [
        pltpu.VMEM((2 * feature_dim, width), BF16),
        pltpu.SemaphoreType.DMA((2, offs.shape[0])),
        pltpu.VMEM((blocks, NF * CAP, BLOCK), BF16),
        pltpu.VMEM((NF, blocks * CAP, feature_dim), BF16),
    ]
    flops = 0
    out_count = 4 if split_out else 1
    if fwd:
        out_shape.append(jax.ShapeDtypeStruct((rows, feature_dim), BF16))
        out_specs.append(full_spec((rows, feature_dim)))
        scratch.append(pltpu.VMEM((blocks, NF * CAP, feature_dim), BF16))
        flops += 1.0e9 * NF * blocks / 2
    if bwd:
        out_shape.append(jax.ShapeDtypeStruct((rows + 16, feature_dim), BF16))
        out_specs.append(full_spec((rows + 16, feature_dim)))
        if split_out:
            for part in range(2):
                for _ in range(2):
                    out_shape.append(jax.ShapeDtypeStruct((4, half, piece_rows, width), BF16))
                    out_specs.append(
                        pl.BlockSpec(
                            (4, 1, piece_rows, width),
                            lambda e, part=part: (0, jnp.clip(e - part * half, 0, half - 1), 0, 0),
                        )
                    )
        else:
            out_shape.append(jax.ShapeDtypeStruct((NF, feature_dim, width), BF16))
            out_specs.append(pl.BlockSpec((1, feature_dim, width), lambda e: (e, 0, 0)))
        scratch += [
            pltpu.VMEM((blocks, NF * CAP, feature_dim), BF16),
            pltpu.VMEM((NF, blocks * CAP, feature_dim), BF16),
            pltpu.VMEM((blocks * 8, BLOCK), F32),
            pltpu.VMEM((feature_dim, width) if split_out else (8, 128), BF16),
        ]
        flops += 2.2e9 * NF * blocks / 2
    outs = pl.pallas_call(
        functools.partial(experts_kernel, fwd, bwd, blocks, plan, out_count, piece_rows),
        grid=(NF,),
        out_shape=tuple(out_shape),
        in_specs=in_specs,
        out_specs=tuple(out_specs),
        scratch_shapes=scratch,
        compiler_params=kernel_params(),
        cost_estimate=cost(flops, 20e6 * (2 if bwd else 1), rows * units * 8),
        name="experts",
    )(offs, *ins, *arrays)
    outs = list(outs)
    ffn = outs.pop(0) if fwd else None
    return (ffn, outs[0], outs[1:]) if bwd else (ffn, None, None)


def final_kernel(with_old, count, *refs):
    parts = refs[:count]
    gu_ref, dn_ref = refs[-2:]
    del with_old
    half = count // 2
    units = gu_ref.shape[-1]

    def write(group):
        total = group[0][...].reshape(group[0].shape[-2:]).astype(F32)
        for ref in group[1:]:
            total += ref[...].reshape(ref.shape[-2:]).astype(F32)
        gu_ref[0, 0, :, 0, :] = total[:, :units]
        gu_ref[0, 0, :, 1, :] = total[:, units : 2 * units]
        dn_ref[0, 0] = total[:, 2 * units :]

    @pl.when(pl.program_id(0) < NF // 2)
    def _():
        write(parts[:half])

    @pl.when(pl.program_id(0) >= NF // 2)
    def _():
        write(parts[half:])


def final_sums(lows, highs, old, layer, layer_count):
    half = NF // 2
    specs, arrays = [], []
    for part, group in enumerate((lows, highs)):
        for item in group:
            lead = (1,) * (item.ndim - 3)
            specs.append(
                pl.BlockSpec(
                    lead + (1,) + item.shape[-2:],
                    lambda e, part=part, lead=lead: (0,) * len(lead)
                    + (jnp.clip(e - part * half, 0, half - 1), 0, 0),
                )
            )
            arrays.append(item)
    count = len(arrays)
    rows, width = arrays[0].shape[-2:]
    units = width // 3
    aliases = {}
    if old is not None:
        specs += [pl.BlockSpec(memory_space=pl.ANY)] * 2
        arrays += list(old)
        aliases = {count: 0, count + 1: 1}
    return pl.pallas_call(
        functools.partial(final_kernel, old is not None, count),
        grid=(NF,),
        out_shape=(
            jax.ShapeDtypeStruct((layer_count, NF, rows, 2, units), F32),
            jax.ShapeDtypeStruct((layer_count, NF, rows, units), F32),
        ),
        in_specs=specs,
        out_specs=(
            pl.BlockSpec((1, 1, rows, 2, units), lambda e: (layer, e, 0, 0, 0)),
            pl.BlockSpec((1, 1, rows, units), lambda e: (layer, e, 0, 0)),
        ),
        input_output_aliases=aliases,
        compiler_params=kernel_params(),
        cost_estimate=cost(1e7, NF * rows * width * 12),
        name="final_sums",
    )(*arrays)


def hop(value, step):
    return lax.ppermute(value, "fsdp", [(i, i ^ step) for i in range(4)])


def swap(value):
    return lax.ppermute(value, "ctx", [(0, 1), (1, 0)])


def gather_small(value):
    by_x, by_y, by_d = hop(value, 1), hop(value, 2), hop(value, 3)
    out = []
    for item in (value, by_x, by_y, by_d):
        out += [item, swap(item)]
    return out


def turn(value, steps, count):
    return lax.ppermute(value, "tp", [(i, (i + steps) % count) for i in range(count)])


def share(value, count):
    return [value] + [turn(value, k, count) for k in range(1, count)]


def gather_cores(lows, highs, swapped):
    half = NF // 2
    out = []
    for first, items, done in ((0, lows, swapped[0]), (half, highs, swapped[1])):
        for chip, item in enumerate(items):
            other = done[chip] if chip in done else swap(item)
            out += [(item, 2 * chip, first, half), (other, 2 * chip + 1, first, half)]
    return out


def tie(*values):
    return lax.optimization_barrier(values)


def add_low(*terms):
    total = terms[0].astype(F32)
    for term in terms[1:]:
        total = total + term.astype(F32)
    return total.astype(BF16)


def scatter_cores(keep, send, first):
    other = swap(send)
    if first == 1:
        out = add_low(keep[1::2], other[1::2])
    else:
        out = add_low(keep[2:], other[2:])
    return keep, other, out


def scatter_first(keep, other, out, first):
    return scatter_beside(keep, other, hop(out, first), first)


def scatter_beside(keep, other, got, first):
    return keep, other, got, add_low(keep[3 - first], other[3 - first], got[1])


def scatter_second(terms, first):
    return terms[:3] + (hop(terms[3], 3 - first),)


def per_device(
    hyper,
    axes,
    tokens,
    cotangent,
    lengths,
    routes,
    norm_attn,
    w_qkv,
    w_out,
    norm_moe,
    w_router,
    w_resid,
    w_const,
    v_const,
    w_gate_up,
    w_down,
):
    micro_count, seq_count, block_len, feature_dim = tokens.shape
    rows = micro_count * seq_count * block_len
    layer_count, shard_rows, qkv_cols = w_qkv.shape
    heads = qkv_cols // (3 * HD)
    units = w_gate_up.shape[-1]
    groups = ("fsdp", "ctx")
    shard_count = feature_dim // shard_rows
    ctx = lax.axis_index("ctx")
    me = lax.axis_index("fsdp") * axes["ctx"] + ctx
    rank = lax.axis_index("tp").reshape(1)
    if hyper:
        offs = me ^ jnp.arange(shard_count, dtype=jnp.int32)
    else:
        offs = jnp.zeros((1,), jnp.int32)
    info = jnp.concatenate([ctx.reshape(1), lengths.reshape(-1)]).astype(jnp.int32)
    resid = jnp.zeros((16, 16), F32).at[:NE, :NE].set(w_resid.astype(F32))

    tp_count = axes["tp"]
    outer = share(jnp.transpose(w_out, (0, 2, 1)), tp_count)
    small, wide = [], []
    for layer in range(layer_count):
        vec = jnp.concatenate(
            [
                w_router[layer],
                jnp.zeros((shard_rows, ROW_CONST - NE), BF16),
                w_const[layer, 0],
                w_const[layer, 1],
                v_const[layer].T,
                norm_attn[layer][:, None],
                norm_moe[layer][:, None],
                jnp.zeros((shard_rows, PACK - ROW_GM - 1), BF16),
            ],
            axis=1,
        )
        pad = jnp.zeros((shard_rows, round_up(qkv_cols, 128) - qkv_cols), BF16)
        turned = [item[layer] for item in outer]
        small.append(jnp.concatenate([w_qkv[layer], pad, vec] + turned, axis=1))
        wide.append(pack_wide(w_gate_up, jnp.swapaxes(w_down, 2, 3), layer))
    weights, wide_first = [None] * layer_count, [None] * layer_count

    def fetch_small(layer, after):
        own = small[layer]
        if hyper:
            own, _ = tie(own, after)
            pieces = gather_small(own)
            fetch_first(layer, [pieces[k] for k in (2, 4, 6)])
        else:
            pieces = [lax.all_gather(own, groups, axis=0, tiled=True)]
        outs = prep_weights(pieces, offs, feature_dim, qkv_cols, heads * HD, tp_count)
        weights[layer] = [outs[0], outs[2], outs[1]]

    def fetch_first(layer, after):
        (low, high), _ = tie(wide[layer], after)
        lows, highs = [low, None, hop(low, 2)], [high, hop(high, 1), None]
        if layer > 0:
            lows[1], highs[2] = hop(low, 1), hop(high, 2)
        wide_first[layer] = (lows, highs, [swap(low), swap(high)] if layer == 0 else [])

    def fetch_rest(layer, value):
        if hyper:
            value, (lows, highs, own) = tie(value, wide_first[layer])
            swapped[layer] = ({0: own[0]}, {0: own[1]}) if own else ({}, {})
            value = swap(value)
            if layer == 0:
                lows[1], highs[2] = hop(lows[0], 1), hop(highs[0], 2)
            lows.append(hop(lows[2], 1))
            highs.append(hop(highs[1], 2))
            rests[layer] = (lows, highs)
        else:
            value = swap(value)
        return value

    def fetch_cores(layer, after):
        if hyper:
            lows, highs = rests[layer]
            if layer == 0:
                swapped[0][0][2], swapped[0][1][1] = swap(lows[2]), swap(highs[1])
                after, swapped[0] = tie(after, swapped[0])
                if layer + 1 < layer_count:
                    mid, wide[layer + 1] = tie((lows[1], highs[2]), wide[layer + 1])
                    lows[1], highs[2] = mid
            else:
                (lows, highs), _ = tie((lows, highs), after)
            rests[layer] = (lows, highs)
        else:
            both = jnp.concatenate(wide[layer], axis=0)
            full = lax.all_gather(both, groups, axis=1, tiled=True)
            weights[layer].append([(full, 0, 0, NF)])
        return after

    def fetch_last(layer, after):
        if hyper:
            lows, highs = rests[layer]
            if layer == 0:
                (lows[3], highs[3]), _ = tie((lows[3], highs[3]), after)
            weights[layer].append(gather_cores(lows, highs, swapped[layer]))

    rests, swapped = [None] * layer_count, [None] * layer_count
    fetch_small(0, info)

    routes_t = jnp.moveaxis(routes.reshape(layer_count, rows, 2), 2, 1)
    routes_t = jnp.concatenate(
        [routes_t, jnp.full((layer_count, 6, rows), -1, jnp.int32)], axis=1
    )
    position = ctx * block_len + jnp.arange(block_len, dtype=jnp.int32)
    valid = position[None, None, :] < lengths[:, :, None]
    cot = jnp.where(valid[..., None], cotangent, 0).reshape(rows, feature_dim)

    base, ffn, prev_t = tokens.reshape(rows, feature_dim), None, None
    saved = []
    for layer in range(layer_count):
        qkv_full, _, vecs = weights[layer][:3]
        outs = qkv_part(base, ffn, vecs, qkv_full)
        h_in, qkv = outs if ffn is not None else (base, outs[0])
        other = fetch_rest(layer, qkv)
        context, lse = attend_forward(qkv, other, info, heads)
        ctx_all = lax.all_gather(fetch_cores(layer, context), "tp", axis=0)
        if hyper and layer == 0:
            lows, highs = rests[0]
            swapped[0][0][1], swapped[0][1][2] = swap(lows[1]), swap(highs[2])
            ctx_all, swapped[0], small[1:] = tie(ctx_all, swapped[0], small[1:])
        wo_all = weights[layer][1]
        middle, base, xm_low, gates_t, logits_t = middle_part(
            h_in, ctx_all, wo_all, vecs, routes_t[layer], prev_t, resid, rank
        )
        fetch_last(layer, xm_low)
        pieces = weights[layer][3]
        saved.append((h_in, qkv, other, context, lse, middle, xm_low, gates_t, prev_t))
        prev_t = logits_t
        if layer < layer_count - 1:
            part, _, _ = experts(True, False, xm_low, None, routes_t[layer], gates_t, pieces, offs)
            fetch_small(layer + 1, part)
            ffn = lax.psum(part, "tp")
            if hyper:
                ffn, wide_first[layer + 1] = tie(ffn, wide_first[layer + 1])

    grad, grad_low = cot, cot
    grad_logits, wide_out, pending, small_terms, late = None, None, None, None, None
    finals = [None] * layer_count
    for layer in reversed(range(layer_count)):
        qkv_full, wo_all, vecs, pieces = weights[layer]
        h_in, qkv, other, context, lse, middle, xm_low, gates_t, prev_t = saved[layer]
        top = layer == layer_count - 1
        part, gx, grads = experts(
            top, True, xm_low, grad_low, routes_t[layer], gates_t, pieces, offs
        )
        if not top and late is not None:
            late[0] = lax.psum(late[0], "tp")
            gx, grads, late, pending = tie(gx, grads, late, pending)
        gx = lax.psum(gx, "tp")
        if hyper:
            sums = [scatter_cores(grads[2 * k], grads[2 * k + 1], k + 1) for k in range(2)]
            got = [hop(sums[k][2], k + 1) for k in range(2)]
            if pending is not None:
                wide_terms, small_parts, dres = pending
                terms = [scatter_second(wide_terms[k], k + 1) for k in range(2)]
                terms, sums = tie(terms, sums)
                wide_out = final_sums(terms[0], terms[1], wide_out, layer + 1, layer_count)
                upper = scatter_cores(*pack_grads(*small_parts, offs), 1)
                gx, sums, wide_out, upper = tie(gx, sums, wide_out, upper)
                upper_got = hop(upper[2], 1)
            else:
                gx, sums = tie(gx, sums)
        if top:
            base_top = base
        else:
            late[1], gx = tie(late[1], gx)
            late[1] = lax.psum(late[1], "tp")
        gg_t = gx[rows : rows + 16, :block_len].astype(F32)
        gg_t = jnp.moveaxis(gg_t.reshape(2, 8, block_len)[: rows // BLOCK], 0, 1).reshape(8, rows)
        extra = (prev_t, resid) if prev_t is not None else (grad_logits,)
        outs = gate_backward(
            grad, middle, gx, vecs, routes_t[layer], gates_t, gg_t, context, wo_all[0], extra
        )
        gmid, gctx, dwo, dvec = outs[:4]
        if prev_t is not None:
            grad_logits, dres = outs[4:]
        gown, goth = attend_backward(qkv, other, lse, gctx, info, heads)
        if hyper:
            wide_terms = [scatter_beside(*sums[k][:2], got[k], k + 1) for k in range(2)]
        if not top:
            gown, goth, late = tie(gown, goth, late)
            if hyper:
                gown, wide_terms, upper_got = tie(gown, wide_terms, upper_got)
        goth = swap(goth)
        ga_part, dqkv, dgain = qkv_backward(gown, goth, h_in, vecs, qkv_full)
        small_parts = (dqkv, dwo, dvec, dgain)
        own = None
        ga = lax.psum(ga_part, "tp")
        if hyper:
            if layer > 0:
                dres = dres + swap(dres)
                dres = dres + hop(dres, 1)
                ga, wide_terms, dres, small_parts = tie(ga, wide_terms, dres, small_parts)
                dres = dres + hop(dres, 2)
                pending = (wide_terms, small_parts, dres)
            else:
                small_terms = scatter_second(scatter_beside(*upper[:2], upper_got, 1), 1)
                terms = [scatter_second(wide_terms[k], k + 1) for k in range(2)]
                terms, small_parts, late = tie(terms, small_parts, late)
                wide_out = final_sums(terms[0], terms[1], wide_out, layer, layer_count)
                own = scatter_cores(*pack_grads(*small_parts, offs), 1)
                owns = [scatter_second(scatter_first(*own, 1), 1), small_terms]
                owns = [
                    sum((term[0] if term.ndim == 3 else term).astype(F32) for term in item)
                    for item in owns
                ]
                gains = share(jnp.stack([item[:, -PACK + ROW_GA] for item in owns]), tp_count)
        if top:
            late = [part[:block_len], part[block_len:]]
            late[0], ga = tie(late[0], ga)
        outs = norm_backward(gmid, ga, h_in, vecs, layer > 0)
        grad = outs[0]
        grad_low = outs[-1]
        finals[layer] = (grads, small_parts, own)

    late = jnp.concatenate(late, axis=0)
    mixed = (base_top + late.astype(F32)).astype(BF16)

    resid_total = (dres if hyper else lax.psum(dres, groups))[:NE, :NE]
    results = [None] * layer_count
    for layer in reversed(range(layer_count)):
        grads, small_parts, own = finals[layer]
        if hyper:
            own = owns[layer]
        else:
            packed = pack_grads(*small_parts, offs)
            own = lax.psum_scatter(packed[0], groups, scatter_dimension=0, tiled=True).astype(F32)
            wide_own = lax.psum_scatter(
                grads[0], groups, scatter_dimension=1, tiled=True
            ).astype(F32)
            here = (
                wide_own[:, :, : 2 * units].reshape(NF, shard_rows, 2, units),
                wide_own[:, :, 2 * units :],
            )
            if wide_out is None:
                wide_out = ([], [])
            wide_out[0].insert(0, here[0])
            wide_out[1].insert(0, here[1])
        out_cols = heads * HD
        vec = own[:, qkv_cols + out_cols :]
        results[layer] = (
            own[:, :qkv_cols],
            own[:, qkv_cols : qkv_cols + out_cols].T,
            vec[:, ROW_GM],
            vec[:, :NE],
            jnp.stack([vec[:, ROW_CONST : ROW_CONST + 2], vec[:, ROW_CONST + 2 : ROW_CONST + 4]]),
            vec[:, ROW_VEC : ROW_VEC + 2].T,
            vec[:, ROW_GA],
        )
    if not hyper:
        wide_out = (jnp.stack(wide_out[0]), jnp.stack(wide_out[1]))
    stacked = [jnp.stack([item[member] for item in results]) for member in range(7)]
    gains = jnp.stack(gains if hyper else share(stacked[6], tp_count))
    gain_own = sum(
        lax.dynamic_index_in_dim(gains, (rank[0] + tp_count - j) % tp_count, 0, keepdims=False)
        for j in range(tp_count)
    )
    return (
        mixed.reshape(tokens.shape),
        grad.reshape(tokens.shape),
        gain_own,
        stacked[0],
        stacked[1],
        stacked[2],
        stacked[3],
        resid_total,
        stacked[4],
        stacked[5],
        wide_out[0],
        jnp.swapaxes(wide_out[1], 2, 3),
    )


def solution(mesh):
    axes = dict(mesh.shape)
    hyper = axes["fsdp"] == 4 and axes["ctx"] == 2
    in_specs = (
        P(None, "fsdp", "ctx", None),
        P(None, "fsdp", "ctx", None),
        P(None, "fsdp"),
        P(None, None, "fsdp", "ctx", None),
        P(None, ("fsdp", "ctx")),
        P(None, ("fsdp", "ctx"), "tp"),
        P(None, "tp", ("fsdp", "ctx")),
        P(None, ("fsdp", "ctx")),
        P(None, ("fsdp", "ctx"), None),
        P(),
        P(None, None, ("fsdp", "ctx"), None),
        P(None, None, ("fsdp", "ctx")),
        P(None, None, ("fsdp", "ctx"), None, "tp"),
        P(None, None, "tp", ("fsdp", "ctx")),
    )
    out_specs = (
        P(None, "fsdp", "ctx", None),
        P(None, "fsdp", "ctx", None),
        P(None, ("fsdp", "ctx")),
        P(None, ("fsdp", "ctx"), "tp"),
        P(None, "tp", ("fsdp", "ctx")),
        P(None, ("fsdp", "ctx")),
        P(None, ("fsdp", "ctx"), None),
        P(),
        P(None, None, ("fsdp", "ctx"), None),
        P(None, None, ("fsdp", "ctx")),
        P(None, None, ("fsdp", "ctx"), None, "tp"),
        P(None, None, "tp", ("fsdp", "ctx")),
    )
    return jax.shard_map(
        functools.partial(per_device, hyper, axes),
        mesh=mesh,
        in_specs=in_specs,
        out_specs=out_specs,
        check_vma=False,
    )
```
